32 devices in a mesh: dp: 16 (over z, y, x), fsdp: 2 (over core).
Axes of the slice: x: 2, y: 2, z: 4, core: 2. Of those that a mesh axis runs over, the one named last changes fastest.
Arguments:
- hidden_in: bfloat16 [32, 704, 1024], P(('dp', 'fsdp')), may hold values from -6 to 6
- cluster_lengths: int32 [32, 8], P(('dp', 'fsdp')), may hold values from 1 to 192, 704 in all within a row
- norm_gain: bfloat16 [1024], P('fsdp'), may hold values from 0.099609375 to 1.8984375
- in_proj: bfloat16 [1024, 4096], P('fsdp'), may hold values from -0.1875 to 0.1875
- conv_weight: bfloat16 [4, 2048], P(None, 'fsdp'), may hold values from -3 to 3
- conv_bias: bfloat16 [2048], P('fsdp'), may hold values from -3 to 3
- x_proj: bfloat16 [2048, 96], P('fsdp'), may hold values from -0.125 to 0.125
- dt_proj: bfloat16 [64, 2048], P(None, 'fsdp'), may hold values from -0.75 to 0.75
- dt_bias: bfloat16 [2048], P('fsdp'), may hold values from -6 to -2.5
- a_log: bfloat16 [16, 2048], P(None, 'fsdp'), may hold values from 0 to 2.765625
- skip_gain: bfloat16 [2048], P('fsdp'), may hold values from 0.5 to 1.5
- out_proj: bfloat16 [2048, 1024], P('fsdp'), may hold values from -0.125 to 0.125
- out_grad: bfloat16 [32, 704, 1024], P(('dp', 'fsdp')), may hold values from -6 to 6
Outputs:
- layer_out: bfloat16 [32, 704, 1024], P(('dp', 'fsdp'))
- input_grad: float32 [32, 704, 1024], P(('dp', 'fsdp'))
- grad_norm_gain: float32 [1024], P('fsdp')
- grad_in_proj: float32 [1024, 4096], P('fsdp')
- grad_conv_weight: float32 [4, 2048], P(None, 'fsdp')
- grad_conv_bias: float32 [2048], P('fsdp')
- grad_x_proj: float32 [2048, 96], P('fsdp')
- grad_dt_proj: float32 [64, 2048], P(None, 'fsdp')
- grad_dt_bias: float32 [2048], P('fsdp')
- grad_a_log: float32 [16, 2048], P(None, 'fsdp')
- grad_skip_gain: float32 [2048], P('fsdp')
- grad_out_proj: float32 [2048, 1024], P('fsdp')
The draws below stay inside these ranges and needn't reach their ends.
Inputs may be any that keep to these rules, and one draw needn't show every extreme that they name: `cluster_lengths`: each row lists the 8 cluster lengths of one context; they sum to 704, and each context's longest cluster has exactly 192 tokens.
All inputs are finite; a program needn't handle non-finite values.
Results may differ from the reference program's by a relative error of at most 0.011.
Values may be sent and summed in bfloat16 or wider, within the bound.
A program may use at most 256 MiB of HBM per device.

```python
import math
import jax
import jax.numpy as jnp
import numpy as np
from jax import lax

D = 1024
DI = 2048
N = 16
R = 64
K = 4
XW = 96
SPAN = 64
LEN = 704
CLUSTERS = 8
MOST = 192
CONTEXTS = 32


def level_of(stream_key, shape, shards, low, high):
    level = 1.0
    for position, blocks in shards:
        heights = jax.random.uniform(jax.random.fold_in(jax.random.fold_in(stream_key, 6), position), (blocks,), jnp.float32, low / len(shards), high / len(shards))
        level = level * jnp.repeat(jnp.exp(heights), shape[position] // blocks).reshape((-1,) + (1,) * (len(shape) - 1 - position))
    return level


def length_profile(number_of, total, reach, lean):
    weights = [(1 << 20) // math.isqrt(grade ** lean) + 1 for grade in range(2, number_of + 1)]
    rest, counts = total - reach - (number_of - 1), [1] * (number_of - 1)
    while rest > 0:
        candidates = [i for i in range(number_of - 1) if counts[i] < reach]
        whole, budget = sum([weights[i] for i in candidates]), rest
        for i in candidates:
            addition = min(reach - counts[i], max(1, budget * weights[i] // whole), rest)
            counts[i] = counts[i] + addition
            rest = rest - addition
    return np.array([reach] + counts)


def ragged(stream_key, amount, total, limit, skew):
    if amount == 2:
        one = jax.random.randint(stream_key, (), max(1, total - limit), min(limit, total - 1) + 1)
        return jnp.stack([one, total - one])
    sizes = jnp.asarray(length_profile(amount, total, limit, skew), jnp.int32)
    twos = (amount - 1) // 2
    source_of, receiver = sizes[1:1 + 2 * twos:2], sizes[2:2 + 2 * twos:2]
    room = jnp.minimum(source_of - 1, limit - receiver)
    moved = jax.random.randint(jax.random.fold_in(stream_key, 1), (twos,), 0, 1 << 20) % (room + 1)
    sizes = sizes.at[1:1 + 2 * twos:2].set(source_of - moved).at[2:2 + 2 * twos:2].set(receiver + moved)
    return sizes[jax.random.permutation(jax.random.fold_in(stream_key, 2), amount)]


def gaussian(own_key, shape, width, limit, split=(), held_as=jnp.bfloat16):
    loudness = level_of(own_key, shape, split, -0.22, 0.18) if split else 1.0
    array = jax.random.normal(own_key, shape, jnp.float32) * width * loudness
    return jnp.minimum(jnp.maximum(array, -limit), limit).astype(held_as)


def setup_inputs(seed: int = 0) -> dict:
    seeds = jax.random.split(jax.random.key(seed), 14)
    hidden_in = gaussian(seeds[0], (CONTEXTS, LEN, D), 1.0, 6.0, ((0, 32),))
    cluster_lengths = jax.vmap(lambda own: ragged(own, CLUSTERS, LEN, MOST, 2))(jax.random.split(seeds[1], CONTEXTS)).reshape((CONTEXTS, CLUSTERS)).astype(jnp.int32)
    norm_gain = jnp.clip(1.0 + 0.18 * jax.random.normal(seeds[2], (D,), jnp.float32), 0.099609375, 1.8984375).astype(jnp.bfloat16)
    in_proj = gaussian(seeds[3], (D, 2 * DI), D ** -0.5, 0.1875, ((0, 2),))
    conv_weight = gaussian(seeds[4], (K, DI), K ** -0.5, 3.0, ((1, 2),))
    conv_bias = gaussian(seeds[5], (DI,), 0.5, 3.0, ((0, 2),))
    x_proj = gaussian(seeds[6], (DI, XW), DI ** -0.5, 0.125, ((0, 2),))
    dt_proj = gaussian(seeds[7], (R, DI), R ** -0.5, 0.75, ((1, 2),))
    dt_bias = jnp.clip(-6.0 + 3.5 * jax.random.uniform(seeds[8], (DI,), jnp.float32) ** level_of(seeds[8], (DI,), ((0, 2),), -0.2, 0.2), -6.0, -2.5).astype(jnp.bfloat16)
    a_log = jnp.clip(2.765625 * jax.random.uniform(seeds[9], (N, DI), jnp.float32) ** level_of(seeds[9], (N, DI), ((1, 2),), -0.2, 0.2), 0.0, 2.765625).astype(jnp.bfloat16)
    skip_gain = jnp.clip(0.5 + 1.0 * jax.random.uniform(seeds[10], (DI,), jnp.float32) ** level_of(seeds[10], (DI,), ((0, 2),), -0.2, 0.2), 0.5, 1.5).astype(jnp.bfloat16)
    out_proj = gaussian(seeds[11], (DI, D), DI ** -0.5, 0.125, ((0, 2),))
    out_grad = gaussian(seeds[12], (CONTEXTS, LEN, D), 1.0, 6.0, ((0, 32),))
    return dict(hidden_in=hidden_in, cluster_lengths=cluster_lengths, norm_gain=norm_gain, in_proj=in_proj, conv_weight=conv_weight, conv_bias=conv_bias, x_proj=x_proj, dt_proj=dt_proj, dt_bias=dt_bias, a_log=a_log, skip_gain=skip_gain, out_proj=out_proj, out_grad=out_grad)


@jax.custom_vjp
def low(v):
    return lax.optimization_barrier(v.astype(jnp.bfloat16)).astype(jnp.float32)

@jax.custom_vjp
def low_back(v):
    return v

def low_keep(v):
    return (low(v), None)

def low_pass(kept, grad):
    return (grad,)

def back_keep(v):
    return (v, None)

def back_low(kept, grad):
    return (low(grad),)
low.defvjp(low_keep, low_pass)
low_back.defvjp(back_keep, back_low)
norm_eps = 1e-05

def matmul_hi(left, right):
    return jnp.dot(left, right, precision=lax.Precision.HIGHEST)

def cluster_offsets(lengths, total_len):
    end_points = jnp.cumsum(lengths, axis=1, dtype=jnp.int32)
    start_points = end_points - lengths
    where_at = jnp.arange(total_len, dtype=jnp.int32)
    inside = (where_at[None, None, :] >= start_points[:, :, None]) & (where_at[None, None, :] < end_points[:, :, None])
    first_spot = lax.optimization_barrier(jnp.sum(jnp.where(inside, start_points[:, :, None], 0), axis=1, dtype=jnp.int32))
    return where_at[None, :] - first_spot

def rms_piece(inputs, gain_vec):
    mean_sq = lax.optimization_barrier(jnp.mean(inputs * inputs, axis=-1, keepdims=True))
    return inputs * lax.rsqrt(mean_sq + norm_eps) * gain_vec

def conv_piece(upper_part, conv_taps, conv_shift, offsets):
    tap_count = conv_taps.shape[0]
    total_len = upper_part.shape[1]
    summed = conv_shift + conv_taps[tap_count - 1] * upper_part
    for lag_steps in range(1, tap_count):
        shifted = jnp.pad(upper_part, ((0, 0), (lag_steps, 0), (0, 0)))[:, :total_len]
        summed = summed + conv_taps[tap_count - 1 - lag_steps] * jnp.where((offsets >= lag_steps)[..., None], shifted, 0.0)
    return summed * jax.nn.sigmoid(summed)

def gate_piece(y_full, gate_z):
    return y_full * gate_z * jax.nn.sigmoid(gate_z)

def scan_block(state_now, decay_rate, pieces):

    def token_step(carried, item_now):
        step_dt, step_b, step_c, step_u, step_keep = item_now
        carried = jnp.exp(step_dt[:, None, :] * decay_rate) * step_keep[:, None, None] * carried + (step_dt * step_u)[:, None, :] * step_b[:, :, None]
        return (carried, lax.optimization_barrier(jnp.sum(step_c[:, :, None] * carried, axis=1)))
    return lax.scan(token_step, state_now, pieces)

def run_scan(delta_t, b_in, c_out, inner_act, keep_mask, decay_rate):
    groups, total_len, channels = delta_t.shape
    blocks = total_len // SPAN

    def to_time(array_in):
        return jnp.moveaxis(array_in.reshape((groups, blocks, SPAN) + array_in.shape[2:]), 0, 2)
    pieces = (to_time(delta_t), to_time(b_in), to_time(c_out), to_time(inner_act), to_time(keep_mask))
    saved_fn = jax.checkpoint(scan_block)

    def outer_step(state_now, span_items):
        return saved_fn(state_now, decay_rate, span_items)
    zero_state = jnp.zeros((groups, N, channels), jnp.float32)
    _, outputs = lax.scan(outer_step, zero_state, pieces)
    return jnp.moveaxis(outputs, 2, 0).reshape(groups, total_len, channels)

def layer_block(inputs, offsets, norm_gain, in_proj, conv_weight, conv_bias, x_proj, dt_proj, dt_bias, a_log, skip_gain, out_proj):
    groups = inputs.shape[0]
    normed = low(rms_piece(inputs, norm_gain))
    both = low_back(matmul_hi(normed.reshape(-1, D), in_proj)).reshape(groups, LEN, 2 * DI)
    upper_part = both[..., :DI]
    gate_z = both[..., DI:]
    inner_act = conv_piece(upper_part, conv_weight, conv_bias, offsets)
    projected = low_back(matmul_hi(low(inner_act).reshape(-1, DI), x_proj)).reshape(groups, LEN, XW)
    rank_part = low(projected[..., :R])
    b_in = projected[..., R:R + N]
    c_out = projected[..., R + N:]
    dt_pre = low_back(matmul_hi(rank_part.reshape(-1, R), dt_proj).reshape(groups, LEN, DI) + dt_bias)
    delta_t = jax.nn.softplus(dt_pre)
    decay_rate = -jnp.exp(a_log)
    keep_mask = jnp.where(offsets > 0, 1.0, 0.0).astype(jnp.float32)
    scan_out = run_scan(delta_t, b_in, c_out, inner_act, keep_mask, decay_rate)
    gated = low(gate_piece(scan_out + skip_gain * inner_act, gate_z))
    return inputs + matmul_hi(gated.reshape(-1, DI), out_proj).reshape(groups, LEN, D)

def reference(hidden_in, cluster_lengths, norm_gain, in_proj, conv_weight, conv_bias, x_proj, dt_proj, dt_bias, a_log, skip_gain, out_proj, out_grad):
    offsets = cluster_offsets(cluster_lengths, LEN)
    placed = offsets.reshape(CONTEXTS // 4, 4, LEN)
    saved_fn = jax.checkpoint(layer_block)

    def forward(inputs, w_gain, w_in, w_conv, b_conv, w_x, w_dt, b_dt, w_alog, w_skip, w_out):
        shaped = inputs.reshape(CONTEXTS // 4, 4, LEN, D)
        result = lax.map(lambda group_item: saved_fn(group_item[0], group_item[1], w_gain, w_in, w_conv, b_conv, w_x, w_dt, b_dt, w_alog, w_skip, w_out), (shaped, placed))
        return result.reshape(CONTEXTS, LEN, D)
    result, pull_back = jax.vjp(forward, hidden_in.astype(jnp.float32), norm_gain.astype(jnp.float32), in_proj.astype(jnp.float32), conv_weight.astype(jnp.float32), conv_bias.astype(jnp.float32), x_proj.astype(jnp.float32), dt_proj.astype(jnp.float32), dt_bias.astype(jnp.float32), a_log.astype(jnp.float32), skip_gain.astype(jnp.float32), out_proj.astype(jnp.float32))
    gradients = pull_back(out_grad.astype(jnp.float32))
    return (result.astype(jnp.bfloat16), gradients[0], gradients[1], gradients[2], gradients[3], gradients[4], gradients[5], gradients[6], gradients[7], gradients[8], gradients[9], gradients[10])
```

```python
import functools
import math

import jax
import jax.numpy as jnp
from jax import lax
from jax.experimental import pallas as pl
from jax.experimental.pallas import tpu as pltpu
from jax.sharding import PartitionSpec as P

CHUNK = 64
WIDTH = 4
norm_eps = 1e-05

BIG = 1e30
LN2 = math.log(2.0)
LOG2E = 1.0 / LN2

def bcast(ref, row, lanes, width):
    return [ref[j, pl.ds(row, 8, stride=0), :] for j in range(width)]

def forward_kernel(dt_ref, u_ref, keep_ref, b_ref, c_ref, a_ref, y_ref, bound_ref, hs, dtm, dtu, ybuf, *, width):
    rows, inner = dt_ref.shape
    lanes_step = 128 * width
    @pl.when(pl.program_id(0) == 0)
    def _():
        hs[...] = jnp.zeros_like(hs)
    bound_ref[0] = hs[...]
    def chan(cb, _):
        base = pl.multiple_of(cb * lanes_step, lanes_step)
        for j in range(width):
            from_ = pl.ds(base + 128 * j, 128)
            d = dt_ref[:, from_]
            dtm[j] = jnp.where(keep_ref[...] > 0, d, BIG)
            dtu[j] = d * u_ref[:, from_]
        A = [[a_ref[pl.ds(8 * s, 8), pl.ds(base + 128 * j, 128)] for s in range(2)] for j in range(width)]
        def body(g, h):
            h = [list(p) for p in zip(h[:width], h[width:])]
            r0 = pl.multiple_of(g * 8, 8)
            for t in range(8):
                d = bcast(dtm, r0 + t, base, width)
                x = bcast(dtu, r0 + t, base, width)
                bt = [b_ref[pl.ds((r0 + t) * 16 + 8 * s, 8), :] for s in range(2)]
                ct = [c_ref[pl.ds((r0 + t) * 16 + 8 * s, 8), :] for s in range(2)]
                for j in range(width):
                    for s in range(2):
                        h[j][s] = jnp.exp2(d[j] * A[j][s]) * h[j][s] + x[j] * bt[s]
                    ybuf[j, pl.ds(t * 8, 8), :] = ct[0] * h[j][0] + ct[1] * h[j][1]
            for j in range(width):
                acc = ybuf[j, pl.ds(0, 8, stride=8), :]
                for s in range(1, 8):
                    acc = acc + ybuf[j, pl.ds(s, 8, stride=8), :]
                y_ref[pl.ds(r0, 8), pl.ds(base + 128 * j, 128)] = acc
            return tuple(p[0] for p in h) + tuple(p[1] for p in h)
        h0 = tuple(hs[pl.ds(8 * s, 8), pl.ds(base + 128 * j, 128)] for s in range(2) for j in range(width))
        h = lax.fori_loop(0, rows // 8, body, h0)
        for s in range(2):
            for j in range(width):
                hs[pl.ds(8 * s, 8), pl.ds(base + 128 * j, 128)] = h[s * width + j]
        return _
    lax.fori_loop(0, inner // lanes_step, chan, 0)

def scan_forward(dt, u, keep, b, c, a, chunk, width):
    T, DI = dt.shape
    n = T // chunk
    row = lambda w: pl.BlockSpec((chunk, w), lambda i: (i, 0))
    return pl.pallas_call(
        functools.partial(forward_kernel, width=width),
        grid=(n,),
        in_specs=[row(DI), row(DI), row(128), pl.BlockSpec((chunk * 16, 128), lambda i: (i, 0)), pl.BlockSpec((chunk * 16, 128), lambda i: (i, 0)),
                  pl.BlockSpec((16, DI), lambda i: (0, 0))],
        out_specs=[row(DI), pl.BlockSpec((1, 16, DI), lambda i: (i, 0, 0))],
        out_shape=[jax.ShapeDtypeStruct((T, DI), jnp.float32), jax.ShapeDtypeStruct((n, 16, DI), jnp.float32)],
        scratch_shapes=[pltpu.VMEM((16, DI), jnp.float32), pltpu.VMEM((width, chunk, 128), jnp.float32), pltpu.VMEM((width, chunk, 128), jnp.float32),
                        pltpu.VMEM((width, 64, 128), jnp.float32)],
        compiler_params=pltpu.CompilerParams(dimension_semantics=("arbitrary",), vmem_limit_bytes=56 << 20),
        name="scan_forward",
    )(dt, u, keep, b, c, a)

def backward_kernel(dt_ref, u_ref, dy_ref, keep_ref, b_ref, c_ref, a_ref, bound_ref, dd_ref, di_ref, db_ref, dc_ref, ga_ref,
               ws, dtm, dtu, dyb, hbuf, sbuf, qbuf, *, width):
    rows, inner = dt_ref.shape
    lanes_step = 128 * width
    @pl.when(pl.program_id(0) == 0)
    def _():
        ws[...] = jnp.zeros_like(ws)
        ga_ref[...] = jnp.zeros_like(ga_ref)
    db_ref[...] = jnp.zeros_like(db_ref)
    dc_ref[...] = jnp.zeros_like(dc_ref)
    def chan(cb, _):
        base = pl.multiple_of(cb * lanes_step, lanes_step)
        for j in range(width):
            from_ = pl.ds(base + 128 * j, 128)
            d = dt_ref[:, from_]
            dtm[j] = jnp.where(keep_ref[...] > 0, d, BIG)
            dtu[j] = d * u_ref[:, from_]
            dyb[j] = dy_ref[:, from_]
        A = [[a_ref[pl.ds(8 * s, 8), pl.ds(base + 128 * j, 128)] for s in range(2)] for j in range(width)]
        def again(g, h):
            h = [list(p) for p in zip(h[:width], h[width:])]
            r0 = pl.multiple_of(g * 8, 8)
            for t in range(8):
                d = bcast(dtm, r0 + t, base, width)
                x = bcast(dtu, r0 + t, base, width)
                bt = [b_ref[pl.ds((r0 + t) * 16 + 8 * s, 8), :] for s in range(2)]
                for j in range(width):
                    for s in range(2):
                        hbuf[pl.ds((r0 + t) * 16 + 8 * s, 8), pl.ds(128 * j, 128)] = h[j][s]
                        h[j][s] = jnp.exp2(d[j] * A[j][s]) * h[j][s] + x[j] * bt[s]
            return tuple(p[0] for p in h) + tuple(p[1] for p in h)
        h0 = tuple(bound_ref[0, pl.ds(8 * s, 8), pl.ds(base + 128 * j, 128)] for s in range(2) for j in range(width))
        h = lax.fori_loop(0, rows // 8, again, h0)
        for s in range(2):
            for j in range(width):
                hbuf[pl.ds(rows * 16 + 8 * s, 8), pl.ds(128 * j, 128)] = h[s * width + j]
        def body(k, carry):
            g_ = rows // 8 - 1 - k
            r0 = pl.multiple_of(g_ * 8, 8)
            w = [[carry[s * width + j] for s in range(2)] for j in range(width)]
            ga = [[carry[2 * width + s * width + j] for s in range(2)] for j in range(width)]
            for t in range(7, -1, -1):
                d = bcast(dtm, r0 + t, base, width)
                x = bcast(dtu, r0 + t, base, width)
                v = bcast(dyb, r0 + t, base, width)
                bt = [b_ref[pl.ds((r0 + t) * 16 + 8 * s, 8), :] for s in range(2)]
                ct = [c_ref[pl.ds((r0 + t) * 16 + 8 * s, 8), :] for s in range(2)]
                db = [None, None]
                dc = [None, None]
                for j in range(width):
                    qs, ss = None, None
                    for s in range(2):
                        hn = hbuf[pl.ds((r0 + t + 1) * 16 + 8 * s, 8), pl.ds(128 * j, 128)]
                        hp = hbuf[pl.ds((r0 + t) * 16 + 8 * s, 8), pl.ds(128 * j, 128)]
                        g = ct[s] * v[j] + w[j][s]
                        w[j][s] = jnp.exp2(d[j] * A[j][s]) * g
                        q = w[j][s] * hp
                        ga[j][s] = ga[j][s] + q * d[j]
                        qa = q * A[j][s]
                        sb = g * bt[s]
                        qs = qa if qs is None else qs + qa
                        ss = sb if ss is None else ss + sb
                        gx = g * x[j]
                        vh = v[j] * hn
                        db[s] = gx if db[s] is None else db[s] + gx
                        dc[s] = vh if dc[s] is None else dc[s] + vh
                    qbuf[j, pl.ds(t * 8, 8), :] = qs
                    sbuf[j, pl.ds(t * 8, 8), :] = ss
                for s in range(2):
                    rr = pl.ds((r0 + t) * 16 + 8 * s, 8)
                    db_ref[rr, :] = db_ref[rr, :] + db[s]
                    dc_ref[rr, :] = dc_ref[rr, :] + dc[s]
            for j in range(width):
                here = pl.ds(base + 128 * j, 128)
                q8 = qbuf[j, pl.ds(0, 8, stride=8), :]
                s8 = sbuf[j, pl.ds(0, 8, stride=8), :]
                for s in range(1, 8):
                    q8 = q8 + qbuf[j, pl.ds(s, 8, stride=8), :]
                    s8 = s8 + sbuf[j, pl.ds(s, 8, stride=8), :]
                dd_ref[pl.ds(r0, 8), here] = LN2 * q8 + u_ref[pl.ds(r0, 8), here] * s8
                di_ref[pl.ds(r0, 8), here] = dt_ref[pl.ds(r0, 8), here] * s8
            return tuple(w[j][s] for s in range(2) for j in range(width)) + tuple(ga[j][s] for s in range(2) for j in range(width))
        c0 = tuple(r[pl.ds(8 * s, 8), pl.ds(base + 128 * j, 128)] for r in (ws, ga_ref) for s in range(2) for j in range(width))
        out = lax.fori_loop(0, rows // 8, body, c0)
        k = 0
        for r in (ws, ga_ref):
            for s in range(2):
                for j in range(width):
                    r[pl.ds(8 * s, 8), pl.ds(base + 128 * j, 128)] = out[k]
                    k += 1
        return _
    lax.fori_loop(0, inner // lanes_step, chan, 0)

def scan_backward(dt, u, dy, keep, b, c, a, bound, chunk, width):
    T, DI = dt.shape
    n = T // chunk
    rev = lambda i: (n - 1 - i, 0)
    row = lambda w: pl.BlockSpec((chunk, w), rev)
    tall = pl.BlockSpec((chunk * 16, 128), rev)
    f32 = jnp.float32
    return pl.pallas_call(
        functools.partial(backward_kernel, width=width),
        grid=(n,),
        in_specs=[row(DI), row(DI), row(DI), row(128), tall, tall, pl.BlockSpec((16, DI), lambda i: (0, 0)),
                  pl.BlockSpec((1, 16, DI), lambda i: (n - 1 - i, 0, 0))],
        out_specs=[row(DI), row(DI), tall, tall, pl.BlockSpec((16, DI), lambda i: (0, 0))],
        out_shape=[jax.ShapeDtypeStruct((T, DI), f32)] * 2 + [jax.ShapeDtypeStruct((T * 16, 128), f32)] * 2 + [jax.ShapeDtypeStruct((16, DI), f32)],
        scratch_shapes=[pltpu.VMEM((16, DI), f32), pltpu.VMEM((width, chunk, 128), f32), pltpu.VMEM((width, chunk, 128), f32), pltpu.VMEM((width, chunk, 128), f32),
                        pltpu.VMEM((chunk * 16 + 16, 128 * width), f32), pltpu.VMEM((width, 64, 128), f32), pltpu.VMEM((width, 64, 128), f32)],
        compiler_params=pltpu.CompilerParams(dimension_semantics=("arbitrary",), vmem_limit_bytes=56 << 20),
        name="scan_backward",
    )(dt, u, dy, keep, b, c, a, bound)


def cluster_offsets(lengths, total_len):
    count = lengths.shape[1]
    ahead = jnp.arange(count)[:, None] < jnp.arange(count)[None, :]
    start_points = jnp.sum(jnp.where(ahead[None], lengths[:, :, None], 0), axis=1, dtype=jnp.int32)
    end_points = start_points + lengths
    where_at = jnp.arange(total_len, dtype=jnp.int32)
    inside = (where_at[None, None, :] >= start_points[:, :, None]) & (
        where_at[None, None, :] < end_points[:, :, None]
    )
    first_spot = jnp.sum(jnp.where(inside, start_points[:, :, None], 0), axis=1, dtype=jnp.int32)
    return where_at[None, :] - first_spot


def rms_piece(inputs, gain_vec):
    mean_sq = jnp.mean(inputs * inputs, axis=-1, keepdims=True)
    return inputs * lax.rsqrt(mean_sq + norm_eps) * gain_vec


def conv_piece(upper_part, conv_taps, conv_shift, offsets):
    tap_count = conv_taps.shape[0]
    total_len = upper_part.shape[0]
    summed = conv_shift + conv_taps[tap_count - 1] * upper_part
    for lag_steps in range(1, tap_count):
        shifted = jnp.pad(upper_part, ((lag_steps, 0), (0, 0)))[:total_len]
        summed = summed + conv_taps[tap_count - 1 - lag_steps] * jnp.where(
            (offsets >= lag_steps)[:, None], shifted, 0.0
        )
    return summed * jax.nn.sigmoid(summed)


def gate_piece(y_full, gate_z):
    return y_full * gate_z * jax.nn.sigmoid(gate_z)


def dot32(left, right, contract):
    return lax.dot_general(left, right, (contract, ((), ())), preferred_element_type=jnp.float32)


def reduced(grad, dim):
    share = lax.psum_scatter(grad.astype(jnp.bfloat16), "fsdp", scatter_dimension=dim, tiled=True)
    return lax.psum(share, "dp").astype(jnp.float32)


def shards(
    hidden_in,
    cluster_lengths,
    norm_gain,
    in_proj,
    conv_weight,
    conv_bias,
    x_proj,
    dt_proj,
    dt_bias,
    a_log,
    skip_gain,
    out_proj,
    out_grad,
):
    f32, bf16 = jnp.float32, jnp.bfloat16
    w_in = lax.all_gather(in_proj, "fsdp", axis=0, tiled=True)
    w_out = lax.all_gather(out_proj, "fsdp", axis=0, tiled=True)
    w_x = lax.all_gather(x_proj, "fsdp", axis=0, tiled=True)
    w_gain = lax.all_gather(norm_gain, "fsdp", axis=0, tiled=True)
    taps = conv_weight.shape[0]
    rank_dim = dt_proj.shape[0]
    state_dim = a_log.shape[0]
    packed = jnp.concatenate(
        [dt_proj, a_log, conv_weight, conv_bias[None], dt_bias[None], skip_gain[None]], axis=0
    )
    packed = lax.all_gather(packed, "fsdp", axis=1, tiled=True)
    w_dt = packed[:rank_dim]
    w_alog = packed[rank_dim : rank_dim + state_dim].astype(f32)
    rest = packed[rank_dim + state_dim :].astype(f32)
    conv_taps, conv_shift, b_dt, w_skip = rest[:taps], rest[taps], rest[taps + 1], rest[taps + 2]

    contexts_here, total_len, model_dim = hidden_in.shape
    inner_dim = conv_taps.shape[1]
    rows = contexts_here * total_len
    offsets = cluster_offsets(cluster_lengths, total_len).reshape(rows)
    keep = jnp.broadcast_to(jnp.where(offsets > 0, 1.0, 0.0).astype(f32)[:, None], (rows, 128))
    inputs = hidden_in.reshape(rows, model_dim).astype(f32)
    grad_rows = out_grad.reshape(rows, model_dim)
    gain_full = w_gain.astype(f32)
    normed16 = rms_piece(inputs, gain_full).astype(bf16)
    both = dot32(normed16, w_in, ((1,), (0,)))
    upper_part = both[:, :inner_dim]
    gate_z = both[:, inner_dim:]
    inner_act = conv_piece(upper_part, conv_taps, conv_shift, offsets)
    inner16 = inner_act.astype(bf16)
    projected = dot32(inner16, w_x, ((1,), (0,)))
    rank16 = projected[:, :rank_dim].astype(bf16)
    b_in = projected[:, rank_dim : rank_dim + state_dim]
    c_out = projected[:, rank_dim + state_dim :]
    dt_pre = dot32(rank16, w_dt, ((1,), (0,))) + b_dt
    delta_t = jax.nn.softplus(dt_pre)
    decay_rate = -jnp.exp(w_alog)
    spread = lambda v: jnp.broadcast_to(v[:, :, None], (rows, state_dim, 128)).reshape(rows * state_dim, 128)
    b_wide, c_wide = spread(b_in), spread(c_out)
    rate2 = decay_rate * LOG2E
    scan_y, boundary = scan_forward(delta_t, inner_act, keep, b_wide, c_wide, rate2, CHUNK, WIDTH)
    d_gated = dot32(grad_rows, w_out, ((1,), (1,)))
    y_full = scan_y + w_skip * inner_act
    gated16 = gate_piece(y_full, gate_z).astype(bf16)
    layer_out = (inputs + dot32(gated16, w_out, ((1,), (0,)))).astype(bf16)
    g_w_out = dot32(gated16, grad_rows, ((0,), (0,)))
    _, gate_pull = jax.vjp(gate_piece, y_full, gate_z)
    d_y, d_gate_z = gate_pull(d_gated)
    gate16 = d_gate_z.astype(bf16)
    g_w_gate = dot32(normed16, gate16, ((0,), (0,)))
    g_skip = jnp.sum(d_y * inner_act, axis=0)
    d_delta, d_inner_scan, d_bin, d_cout, rate_sum = scan_backward(
        delta_t, inner_act, d_y, keep, b_wide, c_wide, rate2, boundary, CHUNK, WIDTH
    )
    d_bin = jnp.sum(d_bin.reshape(rows, state_dim, 128), axis=-1)
    d_cout = jnp.sum(d_cout.reshape(rows, state_dim, 128), axis=-1)
    g_alog = rate_sum * decay_rate
    dt16 = (d_delta * jax.nn.sigmoid(dt_pre)).astype(bf16)
    g_b_dt = jnp.sum(dt16.astype(f32), axis=0)
    g_w_dt = dot32(rank16, dt16, ((0,), (0,)))
    d_rank = dot32(dt16, w_dt, ((1,), (1,)))
    proj16 = jnp.concatenate([d_rank, d_bin, d_cout], axis=-1).astype(bf16)
    g_w_x = dot32(proj16, inner16, ((0,), (0,)))
    d_inner = dot32(proj16, w_x, ((1,), (1,))) + d_inner_scan + d_y * w_skip
    _, conv_pull = jax.vjp(
        lambda part_u, taps_in, shift_in: conv_piece(part_u, taps_in, shift_in, offsets),
        upper_part,
        conv_taps,
        conv_shift,
    )
    d_upper, g_conv, g_b_conv = conv_pull(d_inner)
    upper16 = d_upper.astype(bf16)
    g_w_upper = dot32(normed16, upper16, ((0,), (0,)))
    d_normed = dot32(upper16, w_in[:, :inner_dim], ((1,), (1,))) + dot32(
        gate16, w_in[:, inner_dim:], ((1,), (1,))
    )
    _, norm_pull = jax.vjp(rms_piece, inputs, gain_full)
    d_inputs, g_gain = norm_pull(d_normed)
    input_grad = grad_rows.astype(f32) + d_inputs

    parts = lax.axis_size("fsdp")
    gain_row = jnp.pad(
        g_gain.reshape(parts, model_dim // parts), ((0, 0), (0, (inner_dim - model_dim) // parts))
    ).reshape(1, inner_dim)
    small = jnp.concatenate(
        [g_w_x, g_w_dt, g_alog, g_conv, g_b_conv[None], g_b_dt[None], g_skip[None], gain_row], axis=0
    )
    t_out = reduced(g_w_out, 0)
    t_gate = reduced(g_w_gate, 0)
    t_upper = reduced(g_w_upper, 0)
    t_small = reduced(small, 1)
    t_in = jnp.concatenate([t_upper, t_gate], axis=1)
    columns = rank_dim + 2 * state_dim
    at = 0
    picked = []
    for size in (columns, rank_dim, state_dim, taps, 1, 1, 1, 1):
        picked.append(t_small[at : at + size])
        at += size
    t_x, t_dt, t_alog, t_conv, t_b_conv, t_b_dt, t_skip, t_gain = picked
    return (
        layer_out.reshape(hidden_in.shape),
        input_grad.reshape(hidden_in.shape),
        t_gain[0, : model_dim // parts],
        t_in,
        t_conv,
        t_b_conv[0],
        t_x.T,
        t_dt,
        t_b_dt[0],
        t_alog,
        t_skip[0],
        t_out,
    )


def solution(mesh):
    placed = (
        P(("dp", "fsdp"), None, None),
        P(("dp", "fsdp"), None),
        P("fsdp"),
        P("fsdp", None),
        P(None, "fsdp"),
        P("fsdp"),
        P("fsdp", None),
        P(None, "fsdp"),
        P("fsdp"),
        P(None, "fsdp"),
        P("fsdp"),
        P("fsdp", None),
        P(("dp", "fsdp"), None, None),
    )
    return jax.shard_map(
        shards,
        mesh=mesh,
        in_specs=placed,
        out_specs=(
            P(("dp", "fsdp"), None, None),
            P(("dp", "fsdp"), None, None),
            P("fsdp"),
            P("fsdp", None),
            P(None, "fsdp"),
            P("fsdp"),
            P("fsdp", None),
            P(None, "fsdp"),
            P("fsdp"),
            P(None, "fsdp"),
            P("fsdp"),
            P("fsdp", None),
        ),
        check_vma=False,
    )
```

```python
import functools
import math

import jax
import jax.numpy as jnp
from jax import lax
from jax.experimental import pallas as pl
from jax.experimental.pallas import tpu as pltpu
from jax.sharding import PartitionSpec as P

CHUNK = 64
WIDTH = 4
norm_eps = 1e-05

BIG = 1e30
LN2 = math.log(2.0)
LOG2E = 1.0 / LN2

def bcast(ref, row, lanes, width):
    return [ref[j, pl.ds(row, 8, stride=0), :] for j in range(width)]

def bits_of(size):
    return size.bit_length() - 1


ORDERS = ((0, 1, 2, 3), (1, 2, 0, 3), (2, 0, 1, 3))


class Reduction:
    def __init__(self, outer, inner, shapes, parts):
        self.outer_bits, self.inner_bits = bits_of(outer), bits_of(inner)
        self.blocks, self.inner = outer * inner, inner
        self.shapes = [(self.blocks, s[0] // self.blocks, s[1]) for s in shapes]
        self.stages = self.outer_bits + self.inner_bits
        self.steps = self.stages + self.inner_bits
        self.pieces = []
        for i, s in enumerate(shapes):
            at = 0
            for columns, order in parts[i]:
                order = [b for b in order if b < self.inner_bits] + list(range(len(order), self.inner_bits))
                self.pieces.append((i, pl.ds(at, columns), order))
                at += columns
            assert at == s[1]

    def axis_bit(self, piece, stage):
        if stage < self.outer_bits:
            return "fsdp", self.outer_bits - 1 - stage
        return "dp", self.pieces[piece][2][stage - self.outer_bits]

    def mine(self, piece, stage):
        axis, bit = self.axis_bit(piece, stage)
        return (lax.axis_index(axis) // (1 << bit)) % 2

    def partner(self, axis, bit):
        here = lax.axis_index(axis)
        return {axis: here + (1 << bit) - (here // (1 << bit)) % 2 * (2 << bit)}

    def barrier(self):
        sem = pltpu.get_barrier_semaphore()
        for axis, bits in (("fsdp", self.outer_bits), ("dp", self.inner_bits)):
            for bit in range(bits):
                pl.semaphore_signal(sem, inc=1, device_id=self.partner(axis, bit), device_id_type=pl.DeviceIdType.MESH)
        pl.semaphore_wait(sem, self.stages)

    def low(self, piece, stage):
        low = 0
        for s in range(1, stage):
            low = low + self.mine(piece, s) * (self.blocks >> (s + 1))
        return low

    def place(self, piece, stages):
        at = 0
        for j in range(stages):
            at = at + self.mine(piece, self.outer_bits + j) * (1 << (self.inner_bits - 1 - j))
        return at

    def bind(self, given, out, scratch):
        n = len(self.shapes)
        self.given, self.out = given, out
        self.work, self.inbox, self.result = scratch[:n], scratch[n : 2 * n], scratch[2 * n : 3 * n]
        self.send, self.recv, self.near = scratch[3 * n :]

    def scratch(self):
        b16, k = jnp.bfloat16, len(self.pieces)
        return (
            [pltpu.VMEM((b // 2, r, c), b16) for b, r, c in self.shapes]
            + [pltpu.VMEM((b, r, c), b16) for b, r, c in self.shapes]
            + [pltpu.VMEM((self.inner, r, c), b16) for b, r, c in self.shapes]
            + [pltpu.SemaphoreType.DMA((k, self.steps)), pltpu.SemaphoreType.DMA((k, self.steps)), pltpu.SemaphoreType.DMA((k,))]
        )

    def copy(self, piece, step):
        i, columns, _ = self.pieces[piece]
        if step < self.stages:
            stage = step
            half = self.blocks >> (step + 1)
            other = (1 - self.mine(piece, step)) * half
            if step == 0:
                source = self.given[i].at[pl.ds(other, half), :, columns]
            else:
                source = self.work[i].at[pl.ds(self.low(piece, step) + other, half), :, columns]
            target = self.inbox[i].at[pl.ds(self.blocks - 2 * half, half), :, columns]
        else:
            stage = self.steps - 1 - step + self.outer_bits
            j = stage - self.outer_bits
            many = 1 << (self.inner_bits - 1 - j)
            source = target = self.result[i].at[pl.ds(self.place(piece, j + 1), many), :, columns]
        return pltpu.make_async_remote_copy(
            src_ref=source,
            dst_ref=target,
            send_sem=self.send.at[piece, step],
            recv_sem=self.recv.at[piece, step],
            device_id=self.partner(*self.axis_bit(piece, stage)),
            device_id_type=pl.DeviceIdType.MESH,
        )

    def own(self, piece):
        i, columns, _ = self.pieces[piece]
        half = self.blocks // 2
        source = self.given[i].at[pl.ds(self.mine(piece, 0) * half, half), :, columns]
        return pltpu.make_async_copy(source, self.work[i].at[:, :, columns], self.near.at[piece])

    def leave(self, piece):
        i, columns, _ = self.pieces[piece]
        return pltpu.make_async_copy(self.result[i].at[:, :, columns], self.out[i].at[:, :, columns], self.near.at[piece])

    def add(self, piece, stage):
        i, columns, _ = self.pieces[piece]
        work, inbox, result = self.work[i], self.inbox[i], self.result[i]
        half = self.blocks >> (stage + 1)
        arrived = self.blocks - 2 * half
        base = 0 if stage == 0 else self.low(piece, stage) + self.mine(piece, stage) * half

        @pl.loop(0, half)
        def _(k):
            new = work[base + k, :, columns].astype(jnp.float32) + inbox[arrived + k, :, columns].astype(jnp.float32)
            if stage == self.stages - 1:
                result[self.place(piece, self.inner_bits), :, columns] = new.astype(jnp.bfloat16)
            else:
                work[base + k, :, columns] = new.astype(jnp.bfloat16)

    def begin(self):
        self.barrier()
        for p in range(len(self.pieces)):
            self.copy(p, 0).start()
        for p in range(len(self.pieces)):
            self.own(p).start()

    def finish(self, step):
        for p in range(len(self.pieces)):
            if step == 0:
                self.own(p).wait()
            self.copy(p, step).wait()
            if step < self.stages:
                self.add(p, step)
            if step + 1 < self.steps:
                self.copy(p, step + 1).start()
            else:
                self.leave(p).start()
        if step + 1 == self.steps:
            for p in range(len(self.pieces)):
                self.leave(p).wait()

    def times(self, count):
        heavy = (2.0, 1.3)
        there = [heavy[j] if j < len(heavy) else 1.0 for j in range(self.inner_bits)]
        loads = [1.2] * self.outer_bits + there + there[::-1]
        total, at, out = sum(loads), 0.0, []
        for load in loads[:-1]:
            at += load
            out.append(max(1, min(count - 1, round(at / total * count))))
        return out


def reduce_kernel(*refs, plan):
    n = len(plan.shapes)
    plan.bind(refs[:n], refs[n : 2 * n], refs[2 * n :])
    plan.begin()
    for step in range(plan.steps):
        plan.finish(step)


def reduction_of(arrays, parts):
    plan = Reduction(lax.axis_size("fsdp"), lax.axis_size("dp"), [a.shape for a in arrays], parts)
    shaped = [a.reshape(s) for a, s in zip(arrays, plan.shapes)]
    out = [jax.ShapeDtypeStruct((plan.inner,) + s[1:], jnp.bfloat16) for s in plan.shapes]
    return plan, shaped, out


def reduce_all(arrays, parts, ident):
    plan, shaped, out = reduction_of(arrays, parts)
    anywhere = pl.BlockSpec(memory_space=pl.ANY)
    out = pl.pallas_call(
        functools.partial(reduce_kernel, plan=plan),
        out_shape=out,
        in_specs=[anywhere] * len(arrays),
        out_specs=[anywhere] * len(arrays),
        scratch_shapes=plan.scratch(),
        compiler_params=pltpu.CompilerParams(collective_id=ident, has_side_effects=True, vmem_limit_bytes=56 << 20),
        name="reduce_all",
    )(*shaped)
    return [o.reshape(-1, o.shape[-1]) for o in out]


def forward_kernel(dt_ref, u_ref, keep_ref, b_ref, c_ref, a_ref, y_ref, bound_ref, hs, dtm, dtu, ybuf, *, width):
    rows, inner = dt_ref.shape
    lanes_step = 128 * width
    @pl.when(pl.program_id(0) == 0)
    def _():
        hs[...] = jnp.zeros_like(hs)
    bound_ref[0] = hs[...]
    def chan(cb, _):
        base = pl.multiple_of(cb * lanes_step, lanes_step)
        for j in range(width):
            from_ = pl.ds(base + 128 * j, 128)
            d = dt_ref[:, from_]
            dtm[j] = jnp.where(keep_ref[...] > 0, d, BIG)
            dtu[j] = d * u_ref[:, from_]
        A = [[a_ref[pl.ds(8 * s, 8), pl.ds(base + 128 * j, 128)] for s in range(2)] for j in range(width)]
        def body(g, h):
            h = [list(p) for p in zip(h[:width], h[width:])]
            r0 = pl.multiple_of(g * 8, 8)
            for t in range(8):
                d = bcast(dtm, r0 + t, base, width)
                x = bcast(dtu, r0 + t, base, width)
                bt = [b_ref[pl.ds((r0 + t) * 16 + 8 * s, 8), :] for s in range(2)]
                ct = [c_ref[pl.ds((r0 + t) * 16 + 8 * s, 8), :] for s in range(2)]
                for j in range(width):
                    for s in range(2):
                        h[j][s] = jnp.exp2(d[j] * A[j][s]) * h[j][s] + x[j] * bt[s]
                    ybuf[j, pl.ds(t * 8, 8), :] = ct[0] * h[j][0] + ct[1] * h[j][1]
            for j in range(width):
                acc = ybuf[j, pl.ds(0, 8, stride=8), :]
                for s in range(1, 8):
                    acc = acc + ybuf[j, pl.ds(s, 8, stride=8), :]
                y_ref[pl.ds(r0, 8), pl.ds(base + 128 * j, 128)] = acc
            return tuple(p[0] for p in h) + tuple(p[1] for p in h)
        h0 = tuple(hs[pl.ds(8 * s, 8), pl.ds(base + 128 * j, 128)] for s in range(2) for j in range(width))
        h = lax.fori_loop(0, rows // 8, body, h0)
        for s in range(2):
            for j in range(width):
                hs[pl.ds(8 * s, 8), pl.ds(base + 128 * j, 128)] = h[s * width + j]
        return _
    lax.fori_loop(0, inner // lanes_step, chan, 0)

def scan_forward(dt, u, keep, b, c, a, chunk, width):
    T, DI = dt.shape
    n = T // chunk
    row = lambda w: pl.BlockSpec((chunk, w), lambda i: (i, 0))
    return pl.pallas_call(
        functools.partial(forward_kernel, width=width),
        grid=(n,),
        in_specs=[row(DI), row(DI), row(128), pl.BlockSpec((chunk * 16, 128), lambda i: (i, 0)), pl.BlockSpec((chunk * 16, 128), lambda i: (i, 0)),
                  pl.BlockSpec((16, DI), lambda i: (0, 0))],
        out_specs=[row(DI), pl.BlockSpec((1, 16, DI), lambda i: (i, 0, 0))],
        out_shape=[jax.ShapeDtypeStruct((T, DI), jnp.float32), jax.ShapeDtypeStruct((n, 16, DI), jnp.float32)],
        scratch_shapes=[pltpu.VMEM((16, DI), jnp.float32), pltpu.VMEM((width, chunk, 128), jnp.float32), pltpu.VMEM((width, chunk, 128), jnp.float32),
                        pltpu.VMEM((width, 64, 128), jnp.float32)],
        compiler_params=pltpu.CompilerParams(dimension_semantics=("arbitrary",), vmem_limit_bytes=56 << 20),
        name="scan_forward",
    )(dt, u, keep, b, c, a)

def backward_kernel(dt_ref, u_ref, dy_ref, keep_ref, b_ref, c_ref, a_ref, bound_ref, *rest, width, plan, total):
    n = len(plan.shapes)
    given, rest = rest[:n], rest[n:]
    (dd_ref, di_ref, db_ref, dc_ref, ga_ref), out, rest = rest[:5], rest[5 : 5 + n], rest[5 + n :]
    ws, dtm, dtu, dyb, hbuf, sbuf, qbuf = rest[:7]
    plan.bind(given, out, rest[7:])
    times = plan.times(total // dt_ref.shape[0])
    rows, inner = dt_ref.shape
    lanes_step = 128 * width
    @pl.when(pl.program_id(0) == 0)
    def _():
        ws[...] = jnp.zeros_like(ws)
        ga_ref[...] = jnp.zeros_like(ga_ref)
        plan.begin()
    for at in sorted(set(times)):
        @pl.when(pl.program_id(0) == at)
        def _():
            for step in range(plan.steps - 1):
                if times[step] == at:
                    plan.finish(step)
    db_ref[...] = jnp.zeros_like(db_ref)
    dc_ref[...] = jnp.zeros_like(dc_ref)
    def chan(cb, _):
        base = pl.multiple_of(cb * lanes_step, lanes_step)
        for j in range(width):
            from_ = pl.ds(base + 128 * j, 128)
            d = dt_ref[:, from_]
            dtm[j] = jnp.where(keep_ref[...] > 0, d, BIG)
            dtu[j] = d * u_ref[:, from_]
            dyb[j] = dy_ref[:, from_]
        A = [[a_ref[pl.ds(8 * s, 8), pl.ds(base + 128 * j, 128)] for s in range(2)] for j in range(width)]
        def again(g, h):
            h = [list(p) for p in zip(h[:width], h[width:])]
            r0 = pl.multiple_of(g * 8, 8)
            for t in range(8):
                d = bcast(dtm, r0 + t, base, width)
                x = bcast(dtu, r0 + t, base, width)
                bt = [b_ref[pl.ds((r0 + t) * 16 + 8 * s, 8), :] for s in range(2)]
                for j in range(width):
                    for s in range(2):
                        hbuf[pl.ds((r0 + t) * 16 + 8 * s, 8), pl.ds(128 * j, 128)] = h[j][s]
                        h[j][s] = jnp.exp2(d[j] * A[j][s]) * h[j][s] + x[j] * bt[s]
            return tuple(p[0] for p in h) + tuple(p[1] for p in h)
        h0 = tuple(bound_ref[0, pl.ds(8 * s, 8), pl.ds(base + 128 * j, 128)] for s in range(2) for j in range(width))
        h = lax.fori_loop(0, rows // 8, again, h0)
        for s in range(2):
            for j in range(width):
                hbuf[pl.ds(rows * 16 + 8 * s, 8), pl.ds(128 * j, 128)] = h[s * width + j]
        def body(k, carry):
            g_ = rows // 8 - 1 - k
            r0 = pl.multiple_of(g_ * 8, 8)
            w = [[carry[s * width + j] for s in range(2)] for j in range(width)]
            ga = [[carry[2 * width + s * width + j] for s in range(2)] for j in range(width)]
            for t in range(7, -1, -1):
                d = bcast(dtm, r0 + t, base, width)
                x = bcast(dtu, r0 + t, base, width)
                v = bcast(dyb, r0 + t, base, width)
                bt = [b_ref[pl.ds((r0 + t) * 16 + 8 * s, 8), :] for s in range(2)]
                ct = [c_ref[pl.ds((r0 + t) * 16 + 8 * s, 8), :] for s in range(2)]
                db = [None, None]
                dc = [None, None]
                for j in range(width):
                    qs, ss = None, None
                    for s in range(2):
                        hn = hbuf[pl.ds((r0 + t + 1) * 16 + 8 * s, 8), pl.ds(128 * j, 128)]
                        hp = hbuf[pl.ds((r0 + t) * 16 + 8 * s, 8), pl.ds(128 * j, 128)]
                        g = ct[s] * v[j] + w[j][s]
                        w[j][s] = jnp.exp2(d[j] * A[j][s]) * g
                        q = w[j][s] * hp
                        ga[j][s] = ga[j][s] + q * d[j]
                        qa = q * A[j][s]
                        sb = g * bt[s]
                        qs = qa if qs is None else qs + qa
                        ss = sb if ss is None else ss + sb
                        gx = g * x[j]
                        vh = v[j] * hn
                        db[s] = gx if db[s] is None else db[s] + gx
                        dc[s] = vh if dc[s] is None else dc[s] + vh
                    qbuf[j, pl.ds(t * 8, 8), :] = qs
                    sbuf[j, pl.ds(t * 8, 8), :] = ss
                for s in range(2):
                    rr = pl.ds((r0 + t) * 16 + 8 * s, 8)
                    db_ref[rr, :] = db_ref[rr, :] + db[s]
                    dc_ref[rr, :] = dc_ref[rr, :] + dc[s]
            for j in range(width):
                here = pl.ds(base + 128 * j, 128)
                q8 = qbuf[j, pl.ds(0, 8, stride=8), :]
                s8 = sbuf[j, pl.ds(0, 8, stride=8), :]
                for s in range(1, 8):
                    q8 = q8 + qbuf[j, pl.ds(s, 8, stride=8), :]
                    s8 = s8 + sbuf[j, pl.ds(s, 8, stride=8), :]
                dd_ref[pl.ds(r0, 8), here] = LN2 * q8 + u_ref[pl.ds(r0, 8), here] * s8
                di_ref[pl.ds(r0, 8), here] = dt_ref[pl.ds(r0, 8), here] * s8
            return tuple(w[j][s] for s in range(2) for j in range(width)) + tuple(ga[j][s] for s in range(2) for j in range(width))
        c0 = tuple(r[pl.ds(8 * s, 8), pl.ds(base + 128 * j, 128)] for r in (ws, ga_ref) for s in range(2) for j in range(width))
        out = lax.fori_loop(0, rows // 8, body, c0)
        k = 0
        for r in (ws, ga_ref):
            for s in range(2):
                for j in range(width):
                    r[pl.ds(8 * s, 8), pl.ds(base + 128 * j, 128)] = out[k]
                    k += 1
        return _
    lax.fori_loop(0, inner // lanes_step, chan, 0)
    @pl.when(pl.program_id(0) == pl.num_programs(0) - 1)
    def _():
        plan.finish(plan.steps - 1)


def scan_backward(dt, u, dy, keep, b, c, a, bound, chunk, width, grads, parts):
    T, DI = dt.shape
    n = T // chunk
    rev = lambda i: (n - 1 - i, 0)
    row = lambda w: pl.BlockSpec((chunk, w), rev)
    tall = pl.BlockSpec((chunk * 16, 128), rev)
    fixed = pl.BlockSpec((16, DI), lambda i: (0, 0))
    anywhere = pl.BlockSpec(memory_space=pl.ANY)
    f32 = jnp.float32
    plan, shaped, summed = reduction_of(grads, parts)
    out = pl.pallas_call(
        functools.partial(backward_kernel, width=width, plan=plan, total=T),
        grid=(n,),
        in_specs=[row(DI), row(DI), row(DI), row(128), tall, tall, fixed, pl.BlockSpec((1, 16, DI), lambda i: (n - 1 - i, 0, 0))]
        + [anywhere] * len(grads),
        out_specs=[row(DI), row(DI), tall, tall, fixed] + [anywhere] * len(grads),
        out_shape=[jax.ShapeDtypeStruct((T, DI), f32)] * 2 + [jax.ShapeDtypeStruct((T * 16, 128), f32)] * 2
        + [jax.ShapeDtypeStruct((16, DI), f32)] + summed,
        scratch_shapes=[pltpu.VMEM((16, DI), f32)] + [pltpu.VMEM((width, chunk, 128), f32)] * 3
        + [pltpu.VMEM((chunk * 16 + 16, 128 * width), f32)] + [pltpu.VMEM((width, 64, 128), f32)] * 2 + plan.scratch(),
        compiler_params=pltpu.CompilerParams(
            dimension_semantics=("arbitrary",), collective_id=0, has_side_effects=True, vmem_limit_bytes=56 << 20
        ),
        name="scan_backward",
    )(dt, u, dy, keep, b, c, a, bound, *shaped)
    return out[:5], [o.reshape(-1, o.shape[-1]) for o in out[5:]]


def cluster_offsets(lengths, total_len):
    count = lengths.shape[1]
    ahead = jnp.arange(count)[:, None] < jnp.arange(count)[None, :]
    start_points = jnp.sum(jnp.where(ahead[None], lengths[:, :, None], 0), axis=1, dtype=jnp.int32)
    end_points = start_points + lengths
    where_at = jnp.arange(total_len, dtype=jnp.int32)
    inside = (where_at[None, None, :] >= start_points[:, :, None]) & (
        where_at[None, None, :] < end_points[:, :, None]
    )
    first_spot = jnp.sum(jnp.where(inside, start_points[:, :, None], 0), axis=1, dtype=jnp.int32)
    return where_at[None, :] - first_spot


def rms_piece(inputs, gain_vec):
    mean_sq = jnp.mean(inputs * inputs, axis=-1, keepdims=True)
    return inputs * lax.rsqrt(mean_sq + norm_eps) * gain_vec


def conv_piece(upper_part, conv_taps, conv_shift, offsets):
    tap_count = conv_taps.shape[0]
    total_len = upper_part.shape[0]
    summed = conv_shift + conv_taps[tap_count - 1] * upper_part
    for lag_steps in range(1, tap_count):
        shifted = jnp.pad(upper_part, ((lag_steps, 0), (0, 0)))[:total_len]
        summed = summed + conv_taps[tap_count - 1 - lag_steps] * jnp.where(
            (offsets >= lag_steps)[:, None], shifted, 0.0
        )
    return summed * jax.nn.sigmoid(summed)


def gate_piece(y_full, gate_z):
    return y_full * gate_z * jax.nn.sigmoid(gate_z)


def dot32(left, right, contract):
    return lax.dot_general(left, right, (contract, ((), ())), preferred_element_type=jnp.float32)


def thirds(columns, times=1):
    wide = columns // times // 1024 * 384
    return list(zip((wide, wide, columns // times - 2 * wide) * times, ORDERS * times))


def shards(
    hidden_in,
    cluster_lengths,
    norm_gain,
    in_proj,
    conv_weight,
    conv_bias,
    x_proj,
    dt_proj,
    dt_bias,
    a_log,
    skip_gain,
    out_proj,
    out_grad,
):
    f32, bf16 = jnp.float32, jnp.bfloat16
    w_in = lax.all_gather(in_proj, "fsdp", axis=0, tiled=True)
    w_out = lax.all_gather(out_proj, "fsdp", axis=0, tiled=True)
    w_x = lax.all_gather(x_proj, "fsdp", axis=0, tiled=True)
    w_gain = lax.all_gather(norm_gain, "fsdp", axis=0, tiled=True)
    taps = conv_weight.shape[0]
    rank_dim = dt_proj.shape[0]
    state_dim = a_log.shape[0]
    packed = jnp.concatenate(
        [dt_proj, a_log, conv_weight, conv_bias[None], dt_bias[None], skip_gain[None]], axis=0
    )
    packed = lax.all_gather(packed, "fsdp", axis=1, tiled=True)
    w_dt = packed[:rank_dim]
    w_alog = packed[rank_dim : rank_dim + state_dim].astype(f32)
    rest = packed[rank_dim + state_dim :].astype(f32)
    conv_taps, conv_shift, b_dt, w_skip = rest[:taps], rest[taps], rest[taps + 1], rest[taps + 2]

    contexts_here, total_len, model_dim = hidden_in.shape
    inner_dim = conv_taps.shape[1]
    rows = contexts_here * total_len
    offsets = cluster_offsets(cluster_lengths, total_len).reshape(rows)
    keep = jnp.broadcast_to(jnp.where(offsets > 0, 1.0, 0.0).astype(f32)[:, None], (rows, 128))
    inputs = hidden_in.reshape(rows, model_dim).astype(f32)
    grad_rows = out_grad.reshape(rows, model_dim)
    gain_full = w_gain.astype(f32)
    normed16 = rms_piece(inputs, gain_full).astype(bf16)
    both = dot32(normed16, w_in, ((1,), (0,)))
    upper_part = both[:, :inner_dim]
    gate_z = both[:, inner_dim:]
    inner_act = conv_piece(upper_part, conv_taps, conv_shift, offsets)
    inner16 = inner_act.astype(bf16)
    projected = dot32(inner16, w_x, ((1,), (0,)))
    rank16 = projected[:, :rank_dim].astype(bf16)
    b_in = projected[:, rank_dim : rank_dim + state_dim]
    c_out = projected[:, rank_dim + state_dim :]
    dt_pre = dot32(rank16, w_dt, ((1,), (0,))) + b_dt
    delta_t = jax.nn.softplus(dt_pre)
    decay_rate = -jnp.exp(w_alog)
    spread = lambda v: jnp.broadcast_to(v[:, :, None], (rows, state_dim, 128)).reshape(rows * state_dim, 128)
    b_wide, c_wide = spread(b_in), spread(c_out)
    rate2 = decay_rate * LOG2E
    scan_y, boundary = scan_forward(delta_t, inner_act, keep, b_wide, c_wide, rate2, CHUNK, WIDTH)
    d_gated = dot32(grad_rows, w_out, ((1,), (1,)))
    y_full = scan_y + w_skip * inner_act
    gated16 = gate_piece(y_full, gate_z).astype(bf16)
    layer_out = (inputs + dot32(gated16, w_out, ((1,), (0,)))).astype(bf16)
    g_w_out = dot32(gated16, grad_rows, ((0,), (0,)))
    _, gate_pull = jax.vjp(gate_piece, y_full, gate_z)
    d_y, d_gate_z = gate_pull(d_gated)
    gate16 = d_gate_z.astype(bf16)
    g_w_gate = dot32(normed16, gate16, ((0,), (0,)))
    g_skip = jnp.sum(d_y * inner_act, axis=0)
    (d_delta, d_inner_scan, d_bin, d_cout, rate_sum), (t_out, t_gate) = scan_backward(
        delta_t, inner_act, d_y, keep, b_wide, c_wide, rate2, boundary, CHUNK, WIDTH,
        [g_w_out.astype(bf16), g_w_gate.astype(bf16)], [thirds(model_dim), thirds(inner_dim)],
    )
    d_bin = jnp.sum(d_bin.reshape(rows, state_dim, 128), axis=-1)
    d_cout = jnp.sum(d_cout.reshape(rows, state_dim, 128), axis=-1)
    g_alog = rate_sum * decay_rate
    dt16 = (d_delta * jax.nn.sigmoid(dt_pre)).astype(bf16)
    g_b_dt = jnp.sum(dt16.astype(f32), axis=0)
    g_w_dt = dot32(rank16, dt16, ((0,), (0,)))
    d_rank = dot32(dt16, w_dt, ((1,), (1,)))
    proj16 = jnp.concatenate([d_rank, d_bin, d_cout], axis=-1).astype(bf16)
    g_w_x = dot32(proj16, inner16, ((0,), (0,)))
    d_inner = dot32(proj16, w_x, ((1,), (1,))) + d_inner_scan + d_y * w_skip
    _, conv_pull = jax.vjp(
        lambda part_u, taps_in, shift_in: conv_piece(part_u, taps_in, shift_in, offsets),
        upper_part,
        conv_taps,
        conv_shift,
    )
    d_upper, g_conv, g_b_conv = conv_pull(d_inner)
    upper16 = d_upper.astype(bf16)
    g_w_upper = dot32(normed16, upper16, ((0,), (0,)))
    d_normed = dot32(upper16, w_in[:, :inner_dim], ((1,), (1,))) + dot32(
        gate16, w_in[:, inner_dim:], ((1,), (1,))
    )
    _, norm_pull = jax.vjp(rms_piece, inputs, gain_full)
    d_inputs, g_gain = norm_pull(d_normed)
    input_grad = grad_rows.astype(f32) + d_inputs

    parts = lax.axis_size("fsdp")
    gain_row = jnp.pad(
        g_gain.reshape(parts, model_dim // parts), ((0, 0), (0, (inner_dim - model_dim) // parts))
    ).reshape(1, inner_dim)
    small = jnp.concatenate(
        [g_w_x, g_w_dt, g_alog, g_conv, g_b_conv[None], g_b_dt[None], g_skip[None], gain_row], axis=0
    )
    spare = -small.shape[0] % (16 * lax.axis_size("dp"))
    small = jnp.pad(small, ((0, spare), (0, 0))).astype(bf16)
    small = small.reshape(-1, parts, inner_dim // parts).transpose(1, 0, 2).reshape(-1, inner_dim // parts)
    t_upper, t_small = reduce_all(
        [g_w_upper.astype(bf16), small], [thirds(inner_dim, 2), [(inner_dim // parts, ORDERS[2])]], 1
    )
    t_small = t_small.astype(f32)
    t_in = jnp.concatenate([t_upper, t_gate], axis=1).astype(f32)
    t_out = t_out.astype(f32)
    columns = rank_dim + 2 * state_dim
    at = 0
    picked = []
    for size in (columns, rank_dim, state_dim, taps, 1, 1, 1, 1):
        picked.append(t_small[at : at + size])
        at += size
    t_x, t_dt, t_alog, t_conv, t_b_conv, t_b_dt, t_skip, t_gain = picked
    return (
        layer_out.reshape(hidden_in.shape),
        input_grad.reshape(hidden_in.shape),
        t_gain[0, : model_dim // parts],
        t_in,
        t_conv,
        t_b_conv[0],
        t_x.T,
        t_dt,
        t_b_dt[0],
        t_alog,
        t_skip[0],
        t_out,
    )


def solution(mesh):
    placed = (
        P(("dp", "fsdp"), None, None),
        P(("dp", "fsdp"), None),
        P("fsdp"),
        P("fsdp", None),
        P(None, "fsdp"),
        P("fsdp"),
        P("fsdp", None),
        P(None, "fsdp"),
        P("fsdp"),
        P(None, "fsdp"),
        P("fsdp"),
        P("fsdp", None),
        P(("dp", "fsdp"), None, None),
    )
    return jax.shard_map(
        shards,
        mesh=mesh,
        in_specs=placed,
        out_specs=(
            P(("dp", "fsdp"), None, None),
            P(("dp", "fsdp"), None, None),
            P("fsdp"),
            P("fsdp", None),
            P(None, "fsdp"),
            P("fsdp"),
            P("fsdp", None),
            P(None, "fsdp"),
            P("fsdp"),
            P(None, "fsdp"),
            P("fsdp"),
            P("fsdp", None),
        ),
        check_vma=False,
    )
```

```python
import functools
import math

import jax
import jax.numpy as jnp
from jax import lax
from jax.experimental import pallas as pl
from jax.experimental.pallas import tpu as pltpu
from jax.sharding import PartitionSpec as P

CHUNK = 64
WIDTH = 4
norm_eps = 1e-05

def bits_of(size):
    return size.bit_length() - 1


ORDERS = ((0, 1, 2, 3), (1, 2, 0, 3), (2, 0, 1, 3))


class Reduction:
    def __init__(self, outer, inner, shapes, parts):
        self.outer_bits, self.inner_bits = bits_of(outer), bits_of(inner)
        self.blocks, self.inner = outer * inner, inner
        self.shapes = [(self.blocks, s[0] // self.blocks, s[1]) for s in shapes]
        self.stages = self.outer_bits + self.inner_bits
        self.steps = self.stages + self.inner_bits
        self.pieces = []
        for i, s in enumerate(shapes):
            at = 0
            for columns, order in parts[i]:
                order = [b for b in order if b < self.inner_bits] + list(range(len(order), self.inner_bits))
                self.pieces.append((i, pl.ds(at, columns), order))
                at += columns
            assert at == s[1]

    def axis_bit(self, piece, stage):
        if stage < self.outer_bits:
            return "fsdp", self.outer_bits - 1 - stage
        return "dp", self.pieces[piece][2][stage - self.outer_bits]

    def mine(self, piece, stage):
        axis, bit = self.axis_bit(piece, stage)
        return (lax.axis_index(axis) // (1 << bit)) % 2

    def partner(self, axis, bit):
        here = lax.axis_index(axis)
        return {axis: here + (1 << bit) - (here // (1 << bit)) % 2 * (2 << bit)}

    def barrier(self):
        sem = pltpu.get_barrier_semaphore()
        for axis, bits in (("fsdp", self.outer_bits), ("dp", self.inner_bits)):
            for bit in range(bits):
                pl.semaphore_signal(sem, inc=1, device_id=self.partner(axis, bit), device_id_type=pl.DeviceIdType.MESH)
        pl.semaphore_wait(sem, self.stages)

    def low(self, piece, stage):
        low = 0
        for s in range(1, stage):
            low = low + self.mine(piece, s) * (self.blocks >> (s + 1))
        return low

    def place(self, piece, stages):
        at = 0
        for j in range(stages):
            at = at + self.mine(piece, self.outer_bits + j) * (1 << (self.inner_bits - 1 - j))
        return at

    def bind(self, given, out, scratch):
        n = len(self.shapes)
        self.given, self.out = given, out
        self.work, self.inbox, self.result = scratch[:n], scratch[n : 2 * n], scratch[2 * n : 3 * n]
        self.send, self.recv, self.near = scratch[3 * n :]

    def scratch(self):
        b16, k = jnp.bfloat16, len(self.pieces)
        return (
            [pltpu.VMEM((b // 2, r, c), b16) for b, r, c in self.shapes]
            + [pltpu.VMEM((b, r, c), b16) for b, r, c in self.shapes]
            + [pltpu.VMEM((self.inner, r, c), b16) for b, r, c in self.shapes]
            + [pltpu.SemaphoreType.DMA((k, self.steps)), pltpu.SemaphoreType.DMA((k, self.steps)), pltpu.SemaphoreType.DMA((k,))]
        )

    def copy(self, piece, step):
        i, columns, _ = self.pieces[piece]
        if step < self.stages:
            stage = step
            half = self.blocks >> (step + 1)
            other = (1 - self.mine(piece, step)) * half
            if step == 0:
                source = self.given[i].at[pl.ds(other, half), :, columns]
            else:
                source = self.work[i].at[pl.ds(self.low(piece, step) + other, half), :, columns]
            target = self.inbox[i].at[pl.ds(self.blocks - 2 * half, half), :, columns]
        else:
            stage = self.steps - 1 - step + self.outer_bits
            j = stage - self.outer_bits
            many = 1 << (self.inner_bits - 1 - j)
            source = target = self.result[i].at[pl.ds(self.place(piece, j + 1), many), :, columns]
        return pltpu.make_async_remote_copy(
            src_ref=source,
            dst_ref=target,
            send_sem=self.send.at[piece, step],
            recv_sem=self.recv.at[piece, step],
            device_id=self.partner(*self.axis_bit(piece, stage)),
            device_id_type=pl.DeviceIdType.MESH,
        )

    def own(self, piece):
        i, columns, _ = self.pieces[piece]
        half = self.blocks // 2
        source = self.given[i].at[pl.ds(self.mine(piece, 0) * half, half), :, columns]
        return pltpu.make_async_copy(source, self.work[i].at[:, :, columns], self.near.at[piece])

    def leave(self, piece):
        i, columns, _ = self.pieces[piece]
        return pltpu.make_async_copy(self.result[i].at[:, :, columns], self.out[i].at[:, :, columns], self.near.at[piece])

    def add(self, piece, stage):
        i, columns, _ = self.pieces[piece]
        work, inbox, result = self.work[i], self.inbox[i], self.result[i]
        half = self.blocks >> (stage + 1)
        arrived = self.blocks - 2 * half
        base = 0 if stage == 0 else self.low(piece, stage) + self.mine(piece, stage) * half

        @pl.loop(0, half)
        def _(k):
            new = work[base + k, :, columns].astype(jnp.float32) + inbox[arrived + k, :, columns].astype(jnp.float32)
            if stage == self.stages - 1:
                result[self.place(piece, self.inner_bits), :, columns] = new.astype(jnp.bfloat16)
            else:
                work[base + k, :, columns] = new.astype(jnp.bfloat16)

    def begin(self):
        self.barrier()
        for p in range(len(self.pieces)):
            self.copy(p, 0).start()
        for p in range(len(self.pieces)):
            self.own(p).start()

    def finish(self, step):
        for p in range(len(self.pieces)):
            if step == 0:
                self.own(p).wait()
            self.copy(p, step).wait()
            if step < self.stages:
                self.add(p, step)
            if step + 1 < self.steps:
                self.copy(p, step + 1).start()
            else:
                self.leave(p).start()
        if step + 1 == self.steps:
            for p in range(len(self.pieces)):
                self.leave(p).wait()

    def times(self, count):
        heavy = (2.0, 1.3)
        there = [heavy[j] if j < len(heavy) else 1.0 for j in range(self.inner_bits)]
        loads = [1.2] * self.outer_bits + there + there[::-1]
        total, at, out = sum(loads), 0.0, []
        for load in loads[:-1]:
            at += load
            out.append(max(1, min(count - 1, round(at / total * count))))
        return out


def reduce_kernel(*refs, plan):
    n = len(plan.shapes)
    plan.bind(refs[:n], refs[n : 2 * n], refs[2 * n :])
    plan.begin()
    for step in range(plan.steps):
        plan.finish(step)


def reduction_of(arrays, parts):
    plan = Reduction(lax.axis_size("fsdp"), lax.axis_size("dp"), [a.shape for a in arrays], parts)
    shaped = [a.reshape(s) for a, s in zip(arrays, plan.shapes)]
    out = [jax.ShapeDtypeStruct((plan.inner,) + s[1:], jnp.bfloat16) for s in plan.shapes]
    return plan, shaped, out


def reduce_all(arrays, parts, ident):
    plan, shaped, out = reduction_of(arrays, parts)
    anywhere = pl.BlockSpec(memory_space=pl.ANY)
    out = pl.pallas_call(
        functools.partial(reduce_kernel, plan=plan),
        out_shape=out,
        in_specs=[anywhere] * len(arrays),
        out_specs=[anywhere] * len(arrays),
        scratch_shapes=plan.scratch(),
        compiler_params=pltpu.CompilerParams(collective_id=ident, has_side_effects=True, vmem_limit_bytes=56 << 20),
        name="reduce_all",
    )(*shaped)
    return [o.reshape(-1, o.shape[-1]) for o in out]


BIG = 1e30
LN2 = math.log(2.0)
LOG2E = 1.0 / LN2
TAPS, SHIFT, DT_BIAS, SKIP = 0, 4, 5, 6


def rows_of(ref, tile, row, width):
    return [ref[tile + j, pl.ds(row, 8, stride=0), :] for j in range(width)]


def by_eights(ref, tile):
    total = ref[tile, pl.ds(0, 8, stride=8), :]
    for s in range(1, 8):
        total = total + ref[tile, pl.ds(s, 8, stride=8), :]
    return total


def folded(x):
    total = x[:8]
    for s in range(8, x.shape[0], 8):
        total = total + x[s : s + 8]
    return total


def spread(proj, first, wide, states):
    for t in range(proj.shape[1]):
        wide[pl.ds(t * states, states), :] = jnp.broadcast_to(proj[first : first + states, t : t + 1], (states, 128))


def forward_kernel(
    upper_ref, z_ref, dg_ref, off_ref, par_ref, xp_ref, dtw_ref, a_ref,
    u_ref, ds_ref, dt_ref, sg_ref, dy_ref, gated_ref, gate_ref, proj_ref, wide_b, wide_c, bound_ref, skip_ref,
    hs, ext, u16, dtm, dtu, ys, ybuf, *, width
):
    f32, bf16 = jnp.float32, jnp.bfloat16
    rows, inner = upper_ref.shape
    states, rank = a_ref.shape[0], dtw_ref.shape[0]
    tiles = inner // 128

    @pl.when(pl.program_id(0) == 0)
    def _():
        hs[...] = jnp.zeros_like(hs)
        skip_ref[...] = jnp.zeros_like(skip_ref)
        ext[pl.ds(0, 8), :] = jnp.zeros((8, inner), f32)

    bound_ref[0] = hs[...]

    @pl.loop(0, tiles, unroll=True)
    def _(k):
        lanes = pl.ds(pl.multiple_of(k * 128, 128), 128)
        now = upper_ref[:, lanes]
        ext[pl.ds(8, rows), lanes] = now
        conv = par_ref[SHIFT : SHIFT + 1, lanes] + par_ref[TAPS + 3 : TAPS + 4, lanes] * now
        for lag in range(1, 4):
            before = ext[pl.ds(8 - lag, rows), lanes]
            conv = conv + par_ref[TAPS + 3 - lag : TAPS + 4 - lag, lanes] * jnp.where(off_ref[...] >= lag, before, 0.0)
        sig = jax.nn.sigmoid(conv)
        act = conv * sig
        u_ref[:, lanes] = act
        u16[:, lanes] = act.astype(bf16)
        ds_ref[:, lanes] = sig * (1.0 + conv * (1.0 - sig))
        ext[pl.ds(0, 8), lanes] = now[rows - 8 :]

    proj = lax.dot_general(xp_ref[...], u16[...], (((1,), (1,)), ((), ())), preferred_element_type=f32)
    proj_ref[0] = proj
    spread(proj, rank, wide_b, states)
    spread(proj, rank + states, wide_c, states)
    rank16 = proj[:rank].astype(bf16)

    @pl.loop(0, tiles // 2, unroll=True)
    def _(k):
        pair = pl.ds(pl.multiple_of(k * 256, 256), 256)
        pre = lax.dot_general(rank16, dtw_ref[:, pair], (((0,), (0,)), ((), ())), preferred_element_type=f32)
        pre = pre + par_ref[DT_BIAS : DT_BIAS + 1, pair]
        small = jnp.exp(-jnp.abs(pre))
        delta = jnp.maximum(pre, 0.0) + jnp.log1p(small)
        dt_ref[:, pair] = delta
        sg_ref[:, pair] = jnp.where(pre >= 0, 1.0, small) / (1.0 + small)
        grown = delta * u_ref[:, pair]
        for j in range(2):
            part = slice(128 * j, 128 * j + 128)
            dtm[2 * k + j] = jnp.where(off_ref[...] > 0, delta[:, part], BIG)
            dtu[2 * k + j] = grown[:, part]

    @pl.loop(0, tiles // width)
    def _(cb):
        tile = cb * width
        base = pl.multiple_of(cb * 128 * width, 128 * width)
        rate = [[a_ref[pl.ds(8 * s, 8), pl.ds(base + 128 * j, 128)] for s in range(2)] for j in range(width)]

        def body(g, h):
            h = [list(p) for p in zip(h[:width], h[width:])]
            r0 = pl.multiple_of(g * 8, 8)
            for t in range(8):
                d = rows_of(dtm, tile, r0 + t, width)
                x = rows_of(dtu, tile, r0 + t, width)
                bt = [wide_b[pl.ds((r0 + t) * 16 + 8 * s, 8), :] for s in range(2)]
                ct = [wide_c[pl.ds((r0 + t) * 16 + 8 * s, 8), :] for s in range(2)]
                for j in range(width):
                    for s in range(2):
                        h[j][s] = jnp.exp2(d[j] * rate[j][s]) * h[j][s] + x[j] * bt[s]
                    ybuf[j, pl.ds(t * 8, 8), :] = ct[0] * h[j][0] + ct[1] * h[j][1]
            for j in range(width):
                ys[tile + j, pl.ds(r0, 8), :] = by_eights(ybuf, j)
            return tuple(p[0] for p in h) + tuple(p[1] for p in h)

        h = tuple(hs[pl.ds(8 * s, 8), pl.ds(base + 128 * j, 128)] for s in range(2) for j in range(width))
        h = lax.fori_loop(0, rows // 8, body, h, unroll=4)
        for s in range(2):
            for j in range(width):
                hs[pl.ds(8 * s, 8), pl.ds(base + 128 * j, 128)] = h[s * width + j]

    @pl.loop(0, tiles, unroll=True)
    def _(k):
        lanes = pl.ds(pl.multiple_of(k * 128, 128), 128)
        act, z, dg = u_ref[:, lanes], z_ref[:, lanes], dg_ref[:, lanes]
        full = ys[k] + par_ref[SKIP : SKIP + 1, lanes] * act
        sig = jax.nn.sigmoid(z)
        silu = z * sig
        gated_ref[:, lanes] = (full * silu).astype(bf16)
        dy = dg * silu
        dy_ref[:, lanes] = dy
        gate_ref[:, lanes] = (dg * full * sig * (1.0 + z * (1.0 - sig))).astype(bf16)
        skip_ref[:, lanes] = skip_ref[:, lanes] + folded(dy * act)


def scan_forward(both, d_gated, offset, params, xp, dtw, rate, chunk, width):
    T, DI = d_gated.shape
    n, states, cols = T // chunk, rate.shape[0], xp.shape[0]
    f32, bf16 = jnp.float32, jnp.bfloat16
    row = pl.BlockSpec((chunk, DI), lambda i: (i, 0))
    whole = lambda a: pl.BlockSpec(a.shape, lambda i: (0, 0))
    flat = lambda d: jax.ShapeDtypeStruct((T, DI), d)
    tile = lambda d: pltpu.VMEM((DI // 128, chunk, 128), d)
    return pl.pallas_call(
        functools.partial(forward_kernel, width=width),
        grid=(n,),
        in_specs=[row, pl.BlockSpec((chunk, DI), lambda i: (i, 1)), row, pl.BlockSpec((chunk, 128), lambda i: (i, 0))]
        + [whole(a) for a in (params, xp, dtw, rate)],
        out_specs=[row] * 7
        + [
            pl.BlockSpec((1, cols, chunk), lambda i: (i, 0, 0)),
            pl.BlockSpec((chunk * states, 128), lambda i: (i, 0)),
            pl.BlockSpec((chunk * states, 128), lambda i: (i, 0)),
            pl.BlockSpec((1, states, DI), lambda i: (i, 0, 0)),
            pl.BlockSpec((8, DI), lambda i: (0, 0)),
        ],
        out_shape=[flat(f32)] * 5
        + [flat(bf16)] * 2
        + [
            jax.ShapeDtypeStruct((n, cols, chunk), f32),
            jax.ShapeDtypeStruct((T * states, 128), f32),
            jax.ShapeDtypeStruct((T * states, 128), f32),
            jax.ShapeDtypeStruct((n, states, DI), f32),
            jax.ShapeDtypeStruct((8, DI), f32),
        ],
        scratch_shapes=[
            pltpu.VMEM((states, DI), f32),
            pltpu.VMEM((chunk + 8, DI), f32),
            pltpu.VMEM((chunk, DI), bf16),
            tile(f32),
            tile(f32),
            tile(f32),
            pltpu.VMEM((width, 64, 128), f32),
        ],
        compiler_params=pltpu.CompilerParams(dimension_semantics=("arbitrary",), vmem_limit_bytes=48 << 20),
        name="scan_forward",
    )(both, both, d_gated, offset, params, xp, dtw, rate)


def backward_kernel(
    u_ref, ds_ref, dt_ref, sg_ref, dy_ref, upper_ref, off_ref, proj_ref, wide_b, wide_c, bound_ref, par_ref, xp_ref, dtw_ref, a_ref,
    *rest, width, plan, total
):
    f32, bf16 = jnp.float32, jnp.bfloat16
    n = len(plan.shapes)
    given, rest = rest[:n], rest[n:]
    (du_ref, ga_ref, gdt_ref, gx_ref, sum_ref), out, rest = rest[:5], rest[5 : 5 + n], rest[5 + n :]
    ws, dtm, dtu, dyb, hbuf, sbuf, qbuf, dd, di, u16, dt16, ext, off_ext, wide_db, wide_dc, cols_ref = rest[:16]
    plan.bind(given, out, rest[16:])
    rows, inner = u_ref.shape
    states, rank = a_ref.shape[0], dtw_ref.shape[0]
    tiles = inner // 128
    times = plan.times(total // rows)

    @pl.when(pl.program_id(0) == 0)
    def _():
        for ref in (ws, ga_ref, gdt_ref, gx_ref, sum_ref):
            ref[...] = jnp.zeros_like(ref)
        ext[pl.ds(rows, 8), :] = jnp.zeros((8, inner), f32)
        off_ext[pl.ds(rows, 8), :] = jnp.full((8, 128), -1, jnp.int32)
        plan.begin()

    for at in sorted(set(times)):
        @pl.when(pl.program_id(0) == at)
        def _():
            for step in range(plan.steps - 1):
                if times[step] == at:
                    plan.finish(step)

    proj = proj_ref[0]
    wide_db[...] = jnp.zeros_like(wide_db)
    wide_dc[...] = jnp.zeros_like(wide_dc)

    @pl.loop(0, tiles // width)
    def _(cb):
        tile = cb * width
        base = pl.multiple_of(cb * 128 * width, 128 * width)
        for j in range(width):
            lanes = pl.ds(base + 128 * j, 128)
            d, act = dt_ref[:, lanes], u_ref[:, lanes]
            dtm[j] = jnp.where(off_ref[...] > 0, d, BIG)
            dtu[j] = d * act
            dyb[j] = dy_ref[:, lanes]
            u16[:, lanes] = act.astype(bf16)
        rate = [[a_ref[pl.ds(8 * s, 8), pl.ds(base + 128 * j, 128)] for s in range(2)] for j in range(width)]

        def again(g, h):
            h = [list(p) for p in zip(h[:width], h[width:])]
            r0 = pl.multiple_of(g * 8, 8)
            for t in range(8):
                d = rows_of(dtm, 0, r0 + t, width)
                x = rows_of(dtu, 0, r0 + t, width)
                bt = [wide_b[pl.ds((r0 + t) * 16 + 8 * s, 8), :] for s in range(2)]
                for j in range(width):
                    for s in range(2):
                        hbuf[pl.ds((r0 + t) * 16 + 8 * s, 8), pl.ds(128 * j, 128)] = h[j][s]
                        h[j][s] = jnp.exp2(d[j] * rate[j][s]) * h[j][s] + x[j] * bt[s]
            return tuple(p[0] for p in h) + tuple(p[1] for p in h)

        h = tuple(bound_ref[0, pl.ds(8 * s, 8), pl.ds(base + 128 * j, 128)] for s in range(2) for j in range(width))
        h = lax.fori_loop(0, rows // 8, again, h)
        for s in range(2):
            for j in range(width):
                hbuf[pl.ds(rows * 16 + 8 * s, 8), pl.ds(128 * j, 128)] = h[s * width + j]

        def body(k, carry):
            r0 = pl.multiple_of((rows // 8 - 1 - k) * 8, 8)
            w = [[carry[s * width + j] for s in range(2)] for j in range(width)]
            ga = [[carry[2 * width + s * width + j] for s in range(2)] for j in range(width)]
            newer = [[hbuf[pl.ds((r0 + 8) * 16 + 8 * s, 8), pl.ds(128 * j, 128)] for s in range(2)] for j in range(width)]
            for t in range(7, -1, -1):
                d = rows_of(dtm, 0, r0 + t, width)
                x = rows_of(dtu, 0, r0 + t, width)
                v = rows_of(dyb, 0, r0 + t, width)
                bt = [wide_b[pl.ds((r0 + t) * 16 + 8 * s, 8), :] for s in range(2)]
                ct = [wide_c[pl.ds((r0 + t) * 16 + 8 * s, 8), :] for s in range(2)]
                db = [None, None]
                dc = [None, None]
                for j in range(width):
                    qs, ss = None, None
                    for s in range(2):
                        later = newer[j][s]
                        prior = hbuf[pl.ds((r0 + t) * 16 + 8 * s, 8), pl.ds(128 * j, 128)]
                        newer[j][s] = prior
                        g = ct[s] * v[j] + w[j][s]
                        w[j][s] = jnp.exp2(d[j] * rate[j][s]) * g
                        q = w[j][s] * prior
                        ga[j][s] = ga[j][s] + q * d[j]
                        qa = q * rate[j][s]
                        sb = g * bt[s]
                        qs = qa if qs is None else qs + qa
                        ss = sb if ss is None else ss + sb
                        gx = g * x[j]
                        vh = v[j] * later
                        db[s] = gx if db[s] is None else db[s] + gx
                        dc[s] = vh if dc[s] is None else dc[s] + vh
                    qbuf[j, pl.ds(t * 8, 8), :] = qs
                    sbuf[j, pl.ds(t * 8, 8), :] = ss
                for s in range(2):
                    here = pl.ds((r0 + t) * 16 + 8 * s, 8)
                    wide_db[here, :] = wide_db[here, :] + db[s]
                    wide_dc[here, :] = wide_dc[here, :] + dc[s]
            for j in range(width):
                lanes = pl.ds(base + 128 * j, 128)
                here = pl.ds(r0, 8)
                s8 = by_eights(sbuf, j)
                dd[here, lanes] = LN2 * by_eights(qbuf, j) + u_ref[here, lanes] * s8
                di[here, lanes] = dt_ref[here, lanes] * s8
            return tuple(w[j][s] for s in range(2) for j in range(width)) + tuple(
                ga[j][s] for s in range(2) for j in range(width)
            )

        held = [(r, pl.ds(8 * s, 8), pl.ds(base + 128 * j, 128)) for r in (ws, ga_ref) for s in range(2) for j in range(width)]
        end = lax.fori_loop(0, rows // 8, body, tuple(r[a, b] for r, a, b in held))
        for (r, a, b), value in zip(held, end):
            r[a, b] = value

    for i, ref in enumerate((wide_db, wide_dc)):
        for k in range(states):
            cols_ref[pl.ds(i * rows, rows), pl.ds(128 * k, 128)] = ref[pl.ds(k, rows, stride=states), :].astype(bf16)
    owner = lax.broadcasted_iota(jnp.int32, (states, states * 128), 1) // 128
    picks = jnp.where(owner == lax.broadcasted_iota(jnp.int32, (states, states * 128), 0), 1.0, 0.0).astype(bf16)
    d_bc = lax.dot_general(picks, cols_ref[...], (((1,), (1,)), ((), ())), preferred_element_type=f32)

    @pl.loop(0, tiles, unroll=True)
    def _(k):
        lanes = pl.ds(pl.multiple_of(k * 128, 128), 128)
        low = (dd[:, lanes] * sg_ref[:, lanes]).astype(bf16)
        dt16[:, lanes] = low
        sum_ref[pl.ds(40, 8), lanes] = sum_ref[pl.ds(40, 8), lanes] + folded(low.astype(f32))

    rank16 = proj[:rank].astype(bf16)
    d_rank = lax.dot_general(dtw_ref[...], dt16[...], (((1,), (1,)), ((), ())), preferred_element_type=f32)
    proj16 = jnp.concatenate([d_rank, d_bc[:, :rows], d_bc[:, rows:]], axis=0).astype(bf16)
    off_ext[pl.ds(0, rows), :] = off_ref[...]

    @pl.loop(0, tiles // 2, unroll=True)
    def _(k):
        pair = pl.ds(pl.multiple_of(k * 256, 256), 256)
        dot = lambda a, b, c: lax.dot_general(a, b, ((c, (0,)), ((), ())), preferred_element_type=f32)
        gdt_ref[:, pair] = gdt_ref[:, pair] + dot(rank16, dt16[:, pair], (1,))
        gx_ref[:, pair] = gx_ref[:, pair] + dot(proj16, u16[:, pair], (1,))
        inner_grad = dot(proj16, xp_ref[:, pair], (0,)) + di[:, pair] + dy_ref[:, pair] * par_ref[SKIP : SKIP + 1, pair]
        ext[pl.ds(0, rows), pair] = inner_grad * ds_ref[:, pair]
        for j in range(2):
            lanes = pl.ds(pl.multiple_of(k * 256 + 128 * j, 128), 128)
            now, above = ext[pl.ds(0, rows), lanes], upper_ref[:, lanes]
            grad = par_ref[TAPS + 3 : TAPS + 4, lanes] * now
            sums = [now, now * above]
            for lag in range(1, 4):
                after = jnp.where(off_ext[pl.ds(lag, rows), :] >= lag, ext[pl.ds(lag, rows), lanes], 0.0)
                grad = grad + par_ref[TAPS + 3 - lag : TAPS + 4 - lag, lanes] * after
                sums.append(after * above)
            du_ref[:, lanes] = grad.astype(bf16)
            for at, value in zip((32, 24, 16, 8, 0), sums):
                sum_ref[pl.ds(at, 8), lanes] = sum_ref[pl.ds(at, 8), lanes] + folded(value)
            ext[pl.ds(rows, 8), lanes] = now[:8]

    off_ext[pl.ds(rows, 8), :] = off_ref[pl.ds(0, 8), :]

    @pl.when(pl.program_id(0) == pl.num_programs(0) - 1)
    def _():
        plan.finish(plan.steps - 1)


def scan_backward(saved, both, offset, proj, wide_b, wide_c, bound, params, xp, dtw, rate, chunk, width, grads, parts):
    T, DI = saved[0].shape
    n, states, cols, rank = T // chunk, rate.shape[0], xp.shape[0], dtw.shape[0]
    f32, bf16 = jnp.float32, jnp.bfloat16
    row = pl.BlockSpec((chunk, DI), lambda i: (n - 1 - i, 0))
    whole = lambda a: pl.BlockSpec(a.shape, lambda i: (0, 0))
    anywhere = pl.BlockSpec(memory_space=pl.ANY)
    plan, shaped, summed = reduction_of(grads, parts)
    sums = [jax.ShapeDtypeStruct((r, DI), f32) for r in (states, rank, cols, 48)]
    pieces = pltpu.VMEM((width, chunk, 128), f32)
    eights = pltpu.VMEM((width, 64, 128), f32)
    tall = pltpu.VMEM((chunk * states, 128), f32)
    out = pl.pallas_call(
        functools.partial(backward_kernel, width=width, plan=plan, total=T),
        grid=(n,),
        in_specs=[row] * 6
        + [
            pl.BlockSpec((chunk, 128), lambda i: (n - 1 - i, 0)),
            pl.BlockSpec((1, cols, chunk), lambda i: (n - 1 - i, 0, 0)),
            pl.BlockSpec((chunk * states, 128), lambda i: (n - 1 - i, 0)),
            pl.BlockSpec((chunk * states, 128), lambda i: (n - 1 - i, 0)),
            pl.BlockSpec((1, states, DI), lambda i: (n - 1 - i, 0, 0)),
        ]
        + [whole(a) for a in (params, xp, dtw, rate)]
        + [anywhere] * len(grads),
        out_specs=[row] + [whole(a) for a in sums] + [anywhere] * len(grads),
        out_shape=[jax.ShapeDtypeStruct((T, DI), bf16)] + sums + summed,
        scratch_shapes=[
            pltpu.VMEM((states, DI), f32),
            pieces,
            pieces,
            pieces,
            pltpu.VMEM((chunk * states + states, 128 * width), f32),
            eights,
            eights,
            pltpu.VMEM((chunk, DI), f32),
            pltpu.VMEM((chunk, DI), f32),
            pltpu.VMEM((chunk, DI), bf16),
            pltpu.VMEM((chunk, DI), bf16),
            pltpu.VMEM((chunk + 8, DI), f32),
            pltpu.VMEM((chunk + 8, 128), jnp.int32),
            tall,
            tall,
            pltpu.VMEM((2 * chunk, states * 128), bf16),
        ]
        + plan.scratch(),
        compiler_params=pltpu.CompilerParams(
            dimension_semantics=("arbitrary",), collective_id=0, has_side_effects=True, vmem_limit_bytes=56 << 20
        ),
        name="scan_backward",
    )(*saved, both, offset, proj, wide_b, wide_c, bound, params, xp, dtw, rate, *shaped)
    return out[:5], [o.reshape(-1, o.shape[-1]) for o in out[5:]]


def cluster_offsets(lengths, total_len):
    count = lengths.shape[1]
    ahead = jnp.arange(count)[:, None] < jnp.arange(count)[None, :]
    start_points = jnp.sum(jnp.where(ahead[None], lengths[:, :, None], 0), axis=1, dtype=jnp.int32)
    end_points = start_points + lengths
    where_at = jnp.arange(total_len, dtype=jnp.int32)
    inside = (where_at[None, None, :] >= start_points[:, :, None]) & (
        where_at[None, None, :] < end_points[:, :, None]
    )
    first_spot = jnp.sum(jnp.where(inside, start_points[:, :, None], 0), axis=1, dtype=jnp.int32)
    return where_at[None, :] - first_spot


def rms_piece(inputs, gain_vec):
    mean_sq = jnp.mean(inputs * inputs, axis=-1, keepdims=True)
    return inputs * lax.rsqrt(mean_sq + norm_eps) * gain_vec


def dot32(left, right, contract):
    return lax.dot_general(left, right, (contract, ((), ())), preferred_element_type=jnp.float32)


def thirds(columns, times=1):
    wide = columns // times // 1024 * 384
    return list(zip((wide, wide, columns // times - 2 * wide) * times, ORDERS * times))


def shards(
    hidden_in,
    cluster_lengths,
    norm_gain,
    in_proj,
    conv_weight,
    conv_bias,
    x_proj,
    dt_proj,
    dt_bias,
    a_log,
    skip_gain,
    out_proj,
    out_grad,
):
    f32, bf16 = jnp.float32, jnp.bfloat16
    w_in = lax.all_gather(in_proj, "fsdp", axis=0, tiled=True)
    w_out = lax.all_gather(out_proj, "fsdp", axis=0, tiled=True)
    w_x = lax.all_gather(x_proj, "fsdp", axis=0, tiled=True)
    w_gain = lax.all_gather(norm_gain, "fsdp", axis=0, tiled=True)
    taps = conv_weight.shape[0]
    rank_dim = dt_proj.shape[0]
    state_dim = a_log.shape[0]
    packed = jnp.concatenate(
        [dt_proj, a_log, conv_weight, conv_bias[None], dt_bias[None], skip_gain[None]], axis=0
    )
    packed = lax.all_gather(packed, "fsdp", axis=1, tiled=True)
    w_dt = packed[:rank_dim]
    w_alog = packed[rank_dim : rank_dim + state_dim].astype(f32)
    rest = packed[rank_dim + state_dim :].astype(f32)

    contexts_here, total_len, model_dim = hidden_in.shape
    inner_dim = packed.shape[1]
    rows = contexts_here * total_len
    offsets = cluster_offsets(cluster_lengths, total_len).reshape(rows)
    offset = jnp.broadcast_to(offsets[:, None], (rows, 128))
    inputs = hidden_in.reshape(rows, model_dim).astype(f32)
    grad_rows = out_grad.reshape(rows, model_dim)
    gain_full = w_gain.astype(f32)
    normed16 = rms_piece(inputs, gain_full).astype(bf16)
    both = dot32(normed16, w_in, ((1,), (0,)))
    decay_rate = -jnp.exp(w_alog)
    rate2 = decay_rate * LOG2E
    params = jnp.pad(rest, ((0, 8 - rest.shape[0]), (0, 0)))
    xp = w_x.T
    d_gated = dot32(grad_rows, w_out, ((1,), (1,)))
    *saved, gated16, gate16, proj, b_wide, c_wide, boundary, skip_sums = scan_forward(
        both, d_gated, offset, params, xp, w_dt, rate2, CHUNK, WIDTH
    )
    g_w_out = dot32(gated16, grad_rows, ((0,), (0,))).astype(bf16)
    g_w_gate = dot32(normed16, gate16, ((0,), (0,))).astype(bf16)
    (upper16, rate_sum, g_w_dt, g_w_x, sums), (t_out, t_gate) = scan_backward(
        saved, both, offset, proj, b_wide, c_wide, boundary, params, xp, w_dt, rate2, CHUNK, WIDTH,
        [g_w_out, g_w_gate], [thirds(model_dim), thirds(inner_dim)],
    )
    layer_out = (inputs + dot32(gated16, w_out, ((1,), (0,)))).astype(bf16)
    g_w_upper = dot32(normed16, upper16, ((0,), (0,))).astype(bf16)
    d_normed = dot32(upper16, w_in[:, :inner_dim], ((1,), (1,))) + dot32(
        gate16, w_in[:, inner_dim:], ((1,), (1,))
    )
    _, norm_pull = jax.vjp(rms_piece, inputs, gain_full)
    d_inputs, g_gain = norm_pull(d_normed)
    input_grad = grad_rows.astype(f32) + d_inputs

    parts = lax.axis_size("fsdp")
    gain_row = jnp.pad(
        g_gain.reshape(parts, model_dim // parts), ((0, 0), (0, (inner_dim - model_dim) // parts))
    ).reshape(1, inner_dim)
    row_sums = jnp.concatenate([sums, skip_sums]).reshape(7, 8, inner_dim).sum(axis=1)
    small = jnp.concatenate([g_w_x, g_w_dt, rate_sum * decay_rate, row_sums, gain_row], axis=0)
    spare = -small.shape[0] % (16 * lax.axis_size("dp"))
    small = jnp.pad(small, ((0, spare), (0, 0))).astype(bf16)
    small = small.reshape(-1, parts, inner_dim // parts).transpose(1, 0, 2).reshape(-1, inner_dim // parts)
    t_upper, t_small = reduce_all(
        [g_w_upper, small], [thirds(inner_dim, 2), [(inner_dim // parts, ORDERS[2])]], 1
    )
    t_small = t_small.astype(f32)
    t_in = jnp.concatenate([t_upper, t_gate], axis=1).astype(f32)
    t_out = t_out.astype(f32)
    columns = rank_dim + 2 * state_dim
    at = 0
    picked = []
    for size in (columns, rank_dim, state_dim, taps, 1, 1, 1, 1):
        picked.append(t_small[at : at + size])
        at += size
    t_x, t_dt, t_alog, t_conv, t_b_conv, t_b_dt, t_skip, t_gain = picked
    return (
        layer_out.reshape(hidden_in.shape),
        input_grad.reshape(hidden_in.shape),
        t_gain[0, : model_dim // parts],
        t_in,
        t_conv,
        t_b_conv[0],
        t_x.T,
        t_dt,
        t_b_dt[0],
        t_alog,
        t_skip[0],
        t_out,
    )


def solution(mesh):
    placed = (
        P(("dp", "fsdp"), None, None),
        P(("dp", "fsdp"), None),
        P("fsdp"),
        P("fsdp", None),
        P(None, "fsdp"),
        P("fsdp"),
        P("fsdp", None),
        P(None, "fsdp"),
        P("fsdp"),
        P(None, "fsdp"),
        P("fsdp"),
        P("fsdp", None),
        P(("dp", "fsdp"), None, None),
    )
    return jax.shard_map(
        shards,
        mesh=mesh,
        in_specs=placed,
        out_specs=(
            P(("dp", "fsdp"), None, None),
            P(("dp", "fsdp"), None, None),
            P("fsdp"),
            P("fsdp", None),
            P(None, "fsdp"),
            P("fsdp"),
            P("fsdp", None),
            P(None, "fsdp"),
            P("fsdp"),
            P(None, "fsdp"),
            P("fsdp"),
            P("fsdp", None),
        ),
        check_vma=False,
    )
```

```python
import functools
import math

import jax
import jax.numpy as jnp
from jax import lax
from jax.experimental import pallas as pl
from jax.experimental.pallas import tpu as pltpu
from jax.sharding import PartitionSpec as P

CHUNK = 64
WIDTH = 4
norm_eps = 1e-05

def bits_of(size):
    return size.bit_length() - 1


ORDERS = ((0, 1, 2, 3), (1, 2, 0, 3), (2, 0, 1, 3))


class Reduction:
    def __init__(self, outer, inner, shapes, parts):
        self.outer_bits, self.inner_bits = bits_of(outer), bits_of(inner)
        self.blocks, self.inner = outer * inner, inner
        self.shapes = [(self.blocks, s[0] // self.blocks, s[1]) for s in shapes]
        self.stages = self.outer_bits + self.inner_bits
        self.steps = self.stages + self.inner_bits
        self.pieces = []
        for i, s in enumerate(shapes):
            at = 0
            for columns, order in parts[i]:
                order = [b for b in order if b < self.inner_bits] + list(range(len(order), self.inner_bits))
                self.pieces.append((i, pl.ds(at, columns), order))
                at += columns
            assert at == s[1]

    def axis_bit(self, piece, stage):
        if stage < self.outer_bits:
            return "fsdp", self.outer_bits - 1 - stage
        return "dp", self.pieces[piece][2][stage - self.outer_bits]

    def mine(self, piece, stage):
        axis, bit = self.axis_bit(piece, stage)
        return (lax.axis_index(axis) // (1 << bit)) % 2

    def partner(self, axis, bit):
        here = lax.axis_index(axis)
        return {axis: here + (1 << bit) - (here // (1 << bit)) % 2 * (2 << bit)}

    def barrier(self):
        sem = pltpu.get_barrier_semaphore()
        for axis, bits in (("fsdp", self.outer_bits), ("dp", self.inner_bits)):
            for bit in range(bits):
                pl.semaphore_signal(sem, inc=1, device_id=self.partner(axis, bit), device_id_type=pl.DeviceIdType.MESH)
        pl.semaphore_wait(sem, self.stages)

    def low(self, piece, stage):
        low = 0
        for s in range(1, stage):
            low = low + self.mine(piece, s) * (self.blocks >> (s + 1))
        return low

    def place(self, piece, stages):
        at = 0
        for j in range(stages):
            at = at + self.mine(piece, self.outer_bits + j) * (1 << (self.inner_bits - 1 - j))
        return at

    def bind(self, given, out, scratch):
        n = len(self.shapes)
        self.given, self.out = given, out
        self.work, self.inbox, self.result = scratch[:n], scratch[n : 2 * n], scratch[2 * n : 3 * n]
        self.send, self.recv, self.near = scratch[3 * n :]

    def scratch(self):
        b16, k = jnp.bfloat16, len(self.pieces)
        return (
            [pltpu.VMEM((b // 2, r, c), b16) for b, r, c in self.shapes]
            + [pltpu.VMEM((b, r, c), b16) for b, r, c in self.shapes]
            + [pltpu.VMEM((self.inner, r, c), b16) for b, r, c in self.shapes]
            + [pltpu.SemaphoreType.DMA((k, self.steps)), pltpu.SemaphoreType.DMA((k, self.steps)), pltpu.SemaphoreType.DMA((k,))]
        )

    def copy(self, piece, step):
        i, columns, _ = self.pieces[piece]
        if step < self.stages:
            stage = step
            half = self.blocks >> (step + 1)
            other = (1 - self.mine(piece, step)) * half
            if step == 0:
                source = self.given[i].at[pl.ds(other, half), :, columns]
            else:
                source = self.work[i].at[pl.ds(self.low(piece, step) + other, half), :, columns]
            target = self.inbox[i].at[pl.ds(self.blocks - 2 * half, half), :, columns]
        else:
            stage = self.steps - 1 - step + self.outer_bits
            j = stage - self.outer_bits
            many = 1 << (self.inner_bits - 1 - j)
            source = target = self.result[i].at[pl.ds(self.place(piece, j + 1), many), :, columns]
        return pltpu.make_async_remote_copy(
            src_ref=source,
            dst_ref=target,
            send_sem=self.send.at[piece, step],
            recv_sem=self.recv.at[piece, step],
            device_id=self.partner(*self.axis_bit(piece, stage)),
            device_id_type=pl.DeviceIdType.MESH,
        )

    def own(self, piece):
        i, columns, _ = self.pieces[piece]
        half = self.blocks // 2
        source = self.given[i].at[pl.ds(self.mine(piece, 0) * half, half), :, columns]
        return pltpu.make_async_copy(source, self.work[i].at[:, :, columns], self.near.at[piece])

    def leave(self, piece):
        i, columns, _ = self.pieces[piece]
        return pltpu.make_async_copy(self.result[i].at[:, :, columns], self.out[i].at[:, :, columns], self.near.at[piece])

    def add(self, piece, stage):
        i, columns, _ = self.pieces[piece]
        work, inbox, result = self.work[i], self.inbox[i], self.result[i]
        half = self.blocks >> (stage + 1)
        arrived = self.blocks - 2 * half
        base = 0 if stage == 0 else self.low(piece, stage) + self.mine(piece, stage) * half

        @pl.loop(0, half)
        def _(k):
            new = work[base + k, :, columns].astype(jnp.float32) + inbox[arrived + k, :, columns].astype(jnp.float32)
            if stage == self.stages - 1:
                result[self.place(piece, self.inner_bits), :, columns] = new.astype(jnp.bfloat16)
            else:
                work[base + k, :, columns] = new.astype(jnp.bfloat16)

    def begin(self):
        self.barrier()
        for p in range(len(self.pieces)):
            self.copy(p, 0).start()
        for p in range(len(self.pieces)):
            self.own(p).start()

    def finish(self, step):
        for p in range(len(self.pieces)):
            if step == 0:
                self.own(p).wait()
            self.copy(p, step).wait()
            if step < self.stages:
                self.add(p, step)
            if step + 1 < self.steps:
                self.copy(p, step + 1).start()
            else:
                self.leave(p).start()
        if step + 1 == self.steps:
            for p in range(len(self.pieces)):
                self.leave(p).wait()

    def times(self, count):
        heavy = (18.0, 10.0, 6.5, 14.0)
        there = [heavy[min(j, 3)] for j in range(self.inner_bits)]
        loads = [11.0] * self.outer_bits + there + there[::-1]
        total, at, out = sum(loads), 0.0, []
        for load in loads[:-1]:
            at += load
            out.append(max(1, min(count - 1, round(at / total * count))))
        return out


def reduce_kernel(*refs, plan):
    n = len(plan.shapes)
    plan.bind(refs[:n], refs[n : 2 * n], refs[2 * n :])
    plan.begin()
    for step in range(plan.steps):
        plan.finish(step)


def reduction_of(arrays, parts):
    plan = Reduction(lax.axis_size("fsdp"), lax.axis_size("dp"), [a.shape for a in arrays], parts)
    shaped = [a.reshape(s) for a, s in zip(arrays, plan.shapes)]
    out = [jax.ShapeDtypeStruct((plan.inner,) + s[1:], jnp.bfloat16) for s in plan.shapes]
    return plan, shaped, out


def reduce_all(arrays, parts, ident):
    plan, shaped, out = reduction_of(arrays, parts)
    anywhere = pl.BlockSpec(memory_space=pl.ANY)
    out = pl.pallas_call(
        functools.partial(reduce_kernel, plan=plan),
        out_shape=out,
        in_specs=[anywhere] * len(arrays),
        out_specs=[anywhere] * len(arrays),
        scratch_shapes=plan.scratch(),
        compiler_params=pltpu.CompilerParams(collective_id=ident, has_side_effects=True, vmem_limit_bytes=56 << 20),
        name="reduce_all",
    )(*shaped)
    return [o.reshape(-1, o.shape[-1]) for o in out]


class Exchange:
    def __init__(self, size):
        self.size = size

    def owner(self, turn):
        return (lax.axis_index("fsdp") + self.size - turn) % self.size

    def peer(self, turn):
        return {"fsdp": (lax.axis_index("fsdp") + turn) % self.size}

    def barrier(self):
        sem = pltpu.get_barrier_semaphore()
        for turn in range(1, self.size):
            pl.semaphore_signal(sem, inc=1, device_id=self.peer(turn), device_id_type=pl.DeviceIdType.MESH)
        pl.semaphore_wait(sem, self.size - 1)

    def copy(self, source, target, sems, which, turn):
        if turn == 0:
            return pltpu.make_async_copy(source, target, sems[1].at[which, 0])
        return pltpu.make_async_remote_copy(
            src_ref=source,
            dst_ref=target,
            send_sem=sems[0].at[which, turn],
            recv_sem=sems[1].at[which, turn],
            device_id=self.peer(turn),
            device_id_type=pl.DeviceIdType.MESH,
        )


GAIN_ROW = 80


def gather_kernel(
    x_ref, go_ref, dt_ref, rate_ref, vec_ref, xp_ref, wout_ref, win_ref,
    normed_ref, pack_out, wout_out, win_out, dg_out, both_out,
    pack, wout, win, dg, both, packed, send, recv, leave, tiles, *, plan
):
    f32, bf16 = jnp.float32, jnp.bfloat16
    rows, model = x_ref.shape
    deep, wide, share = model // plan.size, both.shape[1], packed.shape[1]
    me = lax.axis_index("fsdp")
    sems = (send, recv)

    def copies(which, turn):
        source = (packed, wout_ref, win_ref)[which]
        if which == 0:
            target = pack.at[:, pl.ds(pl.multiple_of(me * share, 128), share)]
        else:
            target = (wout, win)[which - 1].at[me]
        return plan.copy(source, target, sems, which, turn)

    at = 0
    for ref in (dt_ref, rate_ref, vec_ref):
        packed[at : at + ref.shape[0], :] = ref[...]
        at += ref.shape[0]
    packed[at:, :] = xp_ref[...].astype(f32).T.astype(bf16)
    plan.barrier()
    for which in range(3):
        for turn in range(1, plan.size):
            copies(which, turn).start()
    for which in (1, 0, 2):
        copies(which, 0).start()

    def times_out(turn):
        at = plan.owner(turn)

        @pl.loop(0, share // 256)
        def _(k):
            here = pl.ds(pl.multiple_of(at * share + k * 256, 128), 256)
            dg[:, here] = lax.dot_general(
                go_ref[...], wout[at, pl.ds(pl.multiple_of(k * 256, 256), 256), :],
                (((1,), (1,)), ((), ())), preferred_element_type=f32,
            )
        pltpu.make_async_copy(wout.at[at], wout_out.at[at], leave.at[0, turn]).start()
        part = pl.ds(pl.multiple_of(at * share, 128), share)
        pltpu.make_async_copy(dg.at[:, part], dg_out.at[:, part], leave.at[2, turn]).start()

    def times_in(turn):
        at = plan.owner(turn)
        left = pl.ds(pl.multiple_of(at * deep, 128), deep)

        @pl.loop(0, wide // 256)
        def _(k):
            here = pl.ds(pl.multiple_of(k * 256, 256), 256)
            new = jnp.dot(normed_ref[:, left], win[at, :, here], preferred_element_type=f32)
            both[:, here] = new if turn == 0 else both[:, here] + new
            if turn == plan.size - 1:
                pltpu.make_async_copy(both.at[:, here], both_out.at[:, here], tiles.at[k]).start()
        pltpu.make_async_copy(win.at[at], win_out.at[at], leave.at[1, turn]).start()

    copies(1, 0).wait()
    times_out(0)
    for turn in range(plan.size):
        copies(0, turn).wait()
    whole_pack = pltpu.make_async_copy(pack, pack_out, leave.at[3, 0])
    whole_pack.start()
    gain = jnp.concatenate(
        [pack[GAIN_ROW : GAIN_ROW + 16, b * share : b * share + deep] for b in range(plan.size)], axis=1
    ).astype(f32)[:1]

    @pl.loop(0, rows // 64)
    def _(k):
        here = pl.ds(pl.multiple_of(k * 64, 64), 64)
        x = x_ref[here, :].astype(f32)
        mean_sq = jnp.mean(x * x, axis=-1, keepdims=True)
        normed_ref[here, :] = (x * lax.rsqrt(mean_sq + norm_eps) * gain).astype(bf16)

    copies(2, 0).wait()
    times_in(0)
    for turn in range(1, plan.size):
        copies(1, turn).wait()
        times_out(turn)
    for turn in range(1, plan.size):
        copies(2, turn).wait()
        times_in(turn)
    whole_pack.wait()
    for turn in range(plan.size):
        at = plan.owner(turn)
        part = pl.ds(pl.multiple_of(at * share, 128), share)
        pltpu.make_async_copy(wout.at[at], wout_out.at[at], leave.at[0, turn]).wait()
        pltpu.make_async_copy(win.at[at], win_out.at[at], leave.at[1, turn]).wait()
        pltpu.make_async_copy(dg.at[:, part], dg_out.at[:, part], leave.at[2, turn]).wait()

    @pl.loop(0, wide // 256)
    def _(k):
        here = pl.ds(pl.multiple_of(k * 256, 256), 256)
        pltpu.make_async_copy(both.at[:, here], both_out.at[:, here], tiles.at[k]).wait()


def gather_weights(x, grad_rows, small, w_out, w_in):
    f32, bf16 = jnp.float32, jnp.bfloat16
    plan = Exchange(lax.axis_size("fsdp"))
    n, (rows, model), wide = plan.size, x.shape, w_in.shape[1]
    depth, share = sum(s.shape[0] for s in small[:3]) + small[3].shape[1], small[0].shape[1]
    inner = n * share
    anywhere = pl.BlockSpec(memory_space=pl.ANY)
    near = pl.BlockSpec(memory_space=pltpu.VMEM)
    shapes = [
        ((depth, inner), bf16), ((n,) + w_out.shape, bf16), ((n,) + w_in.shape, bf16), ((rows, inner), f32), ((rows, wide), f32),
    ]
    normed, packed, out_all, in_all, d_gated, both = pl.pallas_call(
        functools.partial(gather_kernel, plan=plan),
        out_shape=[jax.ShapeDtypeStruct(x.shape, bf16)] + [jax.ShapeDtypeStruct(*s) for s in shapes],
        in_specs=[near] * 6 + [anywhere] * 2,
        out_specs=[near] + [anywhere] * 5,
        scratch_shapes=[pltpu.VMEM(*s) for s in shapes]
        + [
            pltpu.VMEM((depth, share), bf16),
            pltpu.SemaphoreType.DMA((3, n)),
            pltpu.SemaphoreType.DMA((3, n)),
            pltpu.SemaphoreType.DMA((4, n)),
            pltpu.SemaphoreType.DMA((wide // 256,)),
        ],
        compiler_params=pltpu.CompilerParams(collective_id=2, has_side_effects=True, vmem_limit_bytes=56 << 20),
        name="gather_weights",
    )(x, grad_rows, *small, w_out, w_in)
    return normed, packed, out_all.reshape(-1, w_out.shape[1]), in_all.reshape(-1, wide), d_gated, both


BIG = 1e30
LN2 = math.log(2.0)
LOG2E = 1.0 / LN2
TAPS, SHIFT, DT_BIAS, SKIP = 0, 4, 5, 6


def rows_of(ref, tile, row, width):
    return [ref[tile + j, pl.ds(row, 8, stride=0), :] for j in range(width)]


def by_eights(ref, tile):
    total = ref[tile, pl.ds(0, 8, stride=8), :]
    for s in range(1, 8):
        total = total + ref[tile, pl.ds(s, 8, stride=8), :]
    return total


def folded(x):
    total = x[:8]
    for s in range(8, x.shape[0], 8):
        total = total + x[s : s + 8]
    return total


def spread(proj, first, wide, states):
    for t in range(proj.shape[1]):
        wide[pl.ds(t * states, states), :] = jnp.broadcast_to(proj[first : first + states, t : t + 1], (states, 128))


def forward_kernel(
    upper_ref, z_ref, dg_ref, off_ref, par_ref, xp_ref, dtw_ref, a_ref,
    u_ref, ds_ref, dt_ref, sg_ref, dy_ref, gated_ref, gate_ref, proj_ref, wide_b, wide_c, bound_ref, skip_ref,
    hs, ext, u16, dtm, dtu, ys, ybuf, *, width
):
    f32, bf16 = jnp.float32, jnp.bfloat16
    rows, inner = upper_ref.shape
    states, rank = a_ref.shape[0], dtw_ref.shape[0]
    tiles = inner // 128

    @pl.when(pl.program_id(0) == 0)
    def _():
        hs[...] = jnp.zeros_like(hs)
        skip_ref[...] = jnp.zeros_like(skip_ref)
        ext[pl.ds(0, 8), :] = jnp.zeros((8, inner), f32)

    bound_ref[0] = hs[...]

    @pl.loop(0, tiles, unroll=True)
    def _(k):
        lanes = pl.ds(pl.multiple_of(k * 128, 128), 128)
        now = upper_ref[:, lanes]
        ext[pl.ds(8, rows), lanes] = now
        conv = par_ref[SHIFT : SHIFT + 1, lanes] + par_ref[TAPS + 3 : TAPS + 4, lanes] * now
        for lag in range(1, 4):
            before = ext[pl.ds(8 - lag, rows), lanes]
            conv = conv + par_ref[TAPS + 3 - lag : TAPS + 4 - lag, lanes] * jnp.where(off_ref[...] >= lag, before, 0.0)
        sig = jax.nn.sigmoid(conv)
        act = conv * sig
        u_ref[:, lanes] = act
        u16[:, lanes] = act.astype(bf16)
        ds_ref[:, lanes] = sig * (1.0 + conv * (1.0 - sig))
        ext[pl.ds(0, 8), lanes] = now[rows - 8 :]

    proj = lax.dot_general(xp_ref[...], u16[...], (((1,), (1,)), ((), ())), preferred_element_type=f32)
    proj_ref[0] = proj
    spread(proj, rank, wide_b, states)
    spread(proj, rank + states, wide_c, states)
    rank16 = proj[:rank].astype(bf16)

    @pl.loop(0, tiles // 2, unroll=True)
    def _(k):
        pair = pl.ds(pl.multiple_of(k * 256, 256), 256)
        pre = lax.dot_general(rank16, dtw_ref[:, pair], (((0,), (0,)), ((), ())), preferred_element_type=f32)
        pre = pre + par_ref[DT_BIAS : DT_BIAS + 1, pair]
        small = jnp.exp(-jnp.abs(pre))
        delta = jnp.maximum(pre, 0.0) + jnp.log1p(small)
        dt_ref[:, pair] = delta
        sg_ref[:, pair] = jnp.where(pre >= 0, 1.0, small) / (1.0 + small)
        grown = delta * u_ref[:, pair]
        for j in range(2):
            part = slice(128 * j, 128 * j + 128)
            dtm[2 * k + j] = jnp.where(off_ref[...] > 0, delta[:, part], BIG)
            dtu[2 * k + j] = grown[:, part]

    @pl.loop(0, tiles // width)
    def _(cb):
        tile = cb * width
        base = pl.multiple_of(cb * 128 * width, 128 * width)
        rate = [[a_ref[pl.ds(8 * s, 8), pl.ds(base + 128 * j, 128)] for s in range(2)] for j in range(width)]

        def body(g, h):
            h = [list(p) for p in zip(h[:width], h[width:])]
            r0 = pl.multiple_of(g * 8, 8)
            for t in range(8):
                d = rows_of(dtm, tile, r0 + t, width)
                x = rows_of(dtu, tile, r0 + t, width)
                bt = [wide_b[pl.ds((r0 + t) * 16 + 8 * s, 8), :] for s in range(2)]
                ct = [wide_c[pl.ds((r0 + t) * 16 + 8 * s, 8), :] for s in range(2)]
                for j in range(width):
                    for s in range(2):
                        h[j][s] = jnp.exp2(d[j] * rate[j][s]) * h[j][s] + x[j] * bt[s]
                    ybuf[j, pl.ds(t * 8, 8), :] = ct[0] * h[j][0] + ct[1] * h[j][1]
            for j in range(width):
                ys[tile + j, pl.ds(r0, 8), :] = by_eights(ybuf, j)
            return tuple(p[0] for p in h) + tuple(p[1] for p in h)

        h = tuple(hs[pl.ds(8 * s, 8), pl.ds(base + 128 * j, 128)] for s in range(2) for j in range(width))
        h = lax.fori_loop(0, rows // 8, body, h, unroll=4)
        for s in range(2):
            for j in range(width):
                hs[pl.ds(8 * s, 8), pl.ds(base + 128 * j, 128)] = h[s * width + j]

    @pl.loop(0, tiles, unroll=True)
    def _(k):
        lanes = pl.ds(pl.multiple_of(k * 128, 128), 128)
        act, z, dg = u_ref[:, lanes], z_ref[:, lanes], dg_ref[:, lanes]
        full = ys[k] + par_ref[SKIP : SKIP + 1, lanes] * act
        sig = jax.nn.sigmoid(z)
        silu = z * sig
        gated_ref[:, lanes] = (full * silu).astype(bf16)
        dy = dg * silu
        dy_ref[:, lanes] = dy
        gate_ref[:, lanes] = (dg * full * sig * (1.0 + z * (1.0 - sig))).astype(bf16)
        skip_ref[:, lanes] = skip_ref[:, lanes] + folded(dy * act)


def scan_forward(both, d_gated, offset, params, xp, dtw, rate, chunk, width):
    T, DI = d_gated.shape
    n, states, cols = T // chunk, rate.shape[0], xp.shape[0]
    f32, bf16 = jnp.float32, jnp.bfloat16
    row = pl.BlockSpec((chunk, DI), lambda i: (i, 0))
    whole = lambda a: pl.BlockSpec(a.shape, lambda i: (0, 0))
    flat = lambda d: jax.ShapeDtypeStruct((T, DI), d)
    tile = lambda d: pltpu.VMEM((DI // 128, chunk, 128), d)
    return pl.pallas_call(
        functools.partial(forward_kernel, width=width),
        grid=(n,),
        in_specs=[row, pl.BlockSpec((chunk, DI), lambda i: (i, 1)), row, pl.BlockSpec((chunk, 128), lambda i: (i, 0))]
        + [whole(a) for a in (params, xp, dtw, rate)],
        out_specs=[row] * 7
        + [
            pl.BlockSpec((1, cols, chunk), lambda i: (i, 0, 0)),
            pl.BlockSpec((chunk * states, 128), lambda i: (i, 0)),
            pl.BlockSpec((chunk * states, 128), lambda i: (i, 0)),
            pl.BlockSpec((1, states, DI), lambda i: (i, 0, 0)),
            pl.BlockSpec((8, DI), lambda i: (0, 0)),
        ],
        out_shape=[flat(f32)] * 5
        + [flat(bf16)] * 2
        + [
            jax.ShapeDtypeStruct((n, cols, chunk), f32),
            jax.ShapeDtypeStruct((T * states, 128), f32),
            jax.ShapeDtypeStruct((T * states, 128), f32),
            jax.ShapeDtypeStruct((n, states, DI), f32),
            jax.ShapeDtypeStruct((8, DI), f32),
        ],
        scratch_shapes=[
            pltpu.VMEM((states, DI), f32),
            pltpu.VMEM((chunk + 8, DI), f32),
            pltpu.VMEM((chunk, DI), bf16),
            tile(f32),
            tile(f32),
            tile(f32),
            pltpu.VMEM((width, 64, 128), f32),
        ],
        compiler_params=pltpu.CompilerParams(dimension_semantics=("arbitrary",), vmem_limit_bytes=48 << 20),
        name="scan_forward",
    )(both, both, d_gated, offset, params, xp, dtw, rate)


def backward_kernel(
    u_ref, ds_ref, dt_ref, sg_ref, dy_ref, upper_ref, off_ref, proj_ref, wide_b, wide_c, bound_ref, par_ref, xp_ref, dtw_ref, a_ref,
    *rest, width, plan, total
):
    f32, bf16 = jnp.float32, jnp.bfloat16
    n = len(plan.shapes)
    given, rest = rest[:n], rest[n:]
    (du_ref, ga_ref, gdt_ref, gx_ref, sum_ref), out, rest = rest[:5], rest[5 : 5 + n], rest[5 + n :]
    ws, dtm, dtu, dyb, hbuf, sbuf, qbuf, dd, di, u16, dt16, ext, off_ext, wide_db, wide_dc, cols_ref = rest[:16]
    plan.bind(given, out, rest[16:])
    rows, inner = u_ref.shape
    states, rank = a_ref.shape[0], dtw_ref.shape[0]
    tiles = inner // 128
    times = plan.times(total // rows * (tiles // width))

    @pl.when(pl.program_id(0) == 0)
    def _():
        for ref in (ws, ga_ref, gdt_ref, gx_ref, sum_ref):
            ref[...] = jnp.zeros_like(ref)
        ext[pl.ds(rows, 8), :] = jnp.zeros((8, inner), f32)
        off_ext[pl.ds(rows, 8), :] = jnp.full((8, 128), -1, jnp.int32)
        plan.begin()

    proj = proj_ref[0]
    wide_db[...] = jnp.zeros_like(wide_db)
    wide_dc[...] = jnp.zeros_like(wide_dc)

    @pl.loop(0, tiles // width)
    def _(cb):
        tile = cb * width
        base = pl.multiple_of(cb * 128 * width, 128 * width)
        for at in sorted(set(times)):
            @pl.when(pl.program_id(0) * (tiles // width) + cb == at)
            def _():
                for step in range(plan.steps - 1):
                    if times[step] == at:
                        plan.finish(step)

        for j in range(width):
            lanes = pl.ds(base + 128 * j, 128)
            d, act = dt_ref[:, lanes], u_ref[:, lanes]
            dtm[j] = jnp.where(off_ref[...] > 0, d, BIG)
            dtu[j] = d * act
            dyb[j] = dy_ref[:, lanes]
            u16[:, lanes] = act.astype(bf16)
        rate = [[a_ref[pl.ds(8 * s, 8), pl.ds(base + 128 * j, 128)] for s in range(2)] for j in range(width)]

        def again(g, h):
            h = [list(p) for p in zip(h[:width], h[width:])]
            r0 = pl.multiple_of(g * 8, 8)
            for t in range(8):
                d = rows_of(dtm, 0, r0 + t, width)
                x = rows_of(dtu, 0, r0 + t, width)
                bt = [wide_b[pl.ds((r0 + t) * 16 + 8 * s, 8), :] for s in range(2)]
                for j in range(width):
                    for s in range(2):
                        hbuf[pl.ds((r0 + t) * 16 + 8 * s, 8), pl.ds(128 * j, 128)] = h[j][s]
                        h[j][s] = jnp.exp2(d[j] * rate[j][s]) * h[j][s] + x[j] * bt[s]
            return tuple(p[0] for p in h) + tuple(p[1] for p in h)

        h = tuple(bound_ref[0, pl.ds(8 * s, 8), pl.ds(base + 128 * j, 128)] for s in range(2) for j in range(width))
        h = lax.fori_loop(0, rows // 8, again, h)
        for s in range(2):
            for j in range(width):
                hbuf[pl.ds(rows * 16 + 8 * s, 8), pl.ds(128 * j, 128)] = h[s * width + j]

        def body(k, carry):
            r0 = pl.multiple_of((rows // 8 - 1 - k) * 8, 8)
            w = [[carry[s * width + j] for s in range(2)] for j in range(width)]
            ga = [[carry[2 * width + s * width + j] for s in range(2)] for j in range(width)]
            newer = [[hbuf[pl.ds((r0 + 8) * 16 + 8 * s, 8), pl.ds(128 * j, 128)] for s in range(2)] for j in range(width)]
            for t in range(7, -1, -1):
                d = rows_of(dtm, 0, r0 + t, width)
                x = rows_of(dtu, 0, r0 + t, width)
                v = rows_of(dyb, 0, r0 + t, width)
                bt = [wide_b[pl.ds((r0 + t) * 16 + 8 * s, 8), :] for s in range(2)]
                ct = [wide_c[pl.ds((r0 + t) * 16 + 8 * s, 8), :] for s in range(2)]
                db = [None, None]
                dc = [None, None]
                for j in range(width):
                    qs, ss = None, None
                    for s in range(2):
                        later = newer[j][s]
                        prior = hbuf[pl.ds((r0 + t) * 16 + 8 * s, 8), pl.ds(128 * j, 128)]
                        newer[j][s] = prior
                        g = ct[s] * v[j] + w[j][s]
                        w[j][s] = jnp.exp2(d[j] * rate[j][s]) * g
                        q = w[j][s] * prior
                        ga[j][s] = ga[j][s] + q * d[j]
                        qa = q * rate[j][s]
                        sb = g * bt[s]
                        qs = qa if qs is None else qs + qa
                        ss = sb if ss is None else ss + sb
                        gx = g * x[j]
                        vh = v[j] * later
                        db[s] = gx if db[s] is None else db[s] + gx
                        dc[s] = vh if dc[s] is None else dc[s] + vh
                    qbuf[j, pl.ds(t * 8, 8), :] = qs
                    sbuf[j, pl.ds(t * 8, 8), :] = ss
                for s in range(2):
                    here = pl.ds((r0 + t) * 16 + 8 * s, 8)
                    wide_db[here, :] = wide_db[here, :] + db[s]
                    wide_dc[here, :] = wide_dc[here, :] + dc[s]
            for j in range(width):
                lanes = pl.ds(base + 128 * j, 128)
                here = pl.ds(r0, 8)
                s8 = by_eights(sbuf, j)
                dd[here, lanes] = LN2 * by_eights(qbuf, j) + u_ref[here, lanes] * s8
                di[here, lanes] = dt_ref[here, lanes] * s8
            return tuple(w[j][s] for s in range(2) for j in range(width)) + tuple(
                ga[j][s] for s in range(2) for j in range(width)
            )

        held = [(r, pl.ds(8 * s, 8), pl.ds(base + 128 * j, 128)) for r in (ws, ga_ref) for s in range(2) for j in range(width)]
        end = lax.fori_loop(0, rows // 8, body, tuple(r[a, b] for r, a, b in held))
        for (r, a, b), value in zip(held, end):
            r[a, b] = value

    for i, ref in enumerate((wide_db, wide_dc)):
        for k in range(states):
            cols_ref[pl.ds(i * rows, rows), pl.ds(128 * k, 128)] = ref[pl.ds(k, rows, stride=states), :].astype(bf16)
    owner = lax.broadcasted_iota(jnp.int32, (states, states * 128), 1) // 128
    picks = jnp.where(owner == lax.broadcasted_iota(jnp.int32, (states, states * 128), 0), 1.0, 0.0).astype(bf16)
    d_bc = lax.dot_general(picks, cols_ref[...], (((1,), (1,)), ((), ())), preferred_element_type=f32)

    @pl.loop(0, tiles, unroll=True)
    def _(k):
        lanes = pl.ds(pl.multiple_of(k * 128, 128), 128)
        low = (dd[:, lanes] * sg_ref[:, lanes]).astype(bf16)
        dt16[:, lanes] = low
        sum_ref[pl.ds(40, 8), lanes] = sum_ref[pl.ds(40, 8), lanes] + folded(low.astype(f32))

    rank16 = proj[:rank].astype(bf16)
    d_rank = lax.dot_general(dtw_ref[...], dt16[...], (((1,), (1,)), ((), ())), preferred_element_type=f32)
    proj16 = jnp.concatenate([d_rank, d_bc[:, :rows], d_bc[:, rows:]], axis=0).astype(bf16)
    off_ext[pl.ds(0, rows), :] = off_ref[...]

    @pl.loop(0, tiles // 2, unroll=True)
    def _(k):
        pair = pl.ds(pl.multiple_of(k * 256, 256), 256)
        dot = lambda a, b, c: lax.dot_general(a, b, ((c, (0,)), ((), ())), preferred_element_type=f32)
        gdt_ref[:, pair] = gdt_ref[:, pair] + dot(rank16, dt16[:, pair], (1,))
        gx_ref[:, pair] = gx_ref[:, pair] + dot(proj16, u16[:, pair], (1,))
        inner_grad = dot(proj16, xp_ref[:, pair], (0,)) + di[:, pair] + dy_ref[:, pair] * par_ref[SKIP : SKIP + 1, pair]
        ext[pl.ds(0, rows), pair] = inner_grad * ds_ref[:, pair]
        for j in range(2):
            lanes = pl.ds(pl.multiple_of(k * 256 + 128 * j, 128), 128)
            now, above = ext[pl.ds(0, rows), lanes], upper_ref[:, lanes]
            grad = par_ref[TAPS + 3 : TAPS + 4, lanes] * now
            sums = [now, now * above]
            for lag in range(1, 4):
                after = jnp.where(off_ext[pl.ds(lag, rows), :] >= lag, ext[pl.ds(lag, rows), lanes], 0.0)
                grad = grad + par_ref[TAPS + 3 - lag : TAPS + 4 - lag, lanes] * after
                sums.append(after * above)
            du_ref[:, lanes] = grad.astype(bf16)
            for at, value in zip((32, 24, 16, 8, 0), sums):
                sum_ref[pl.ds(at, 8), lanes] = sum_ref[pl.ds(at, 8), lanes] + folded(value)
            ext[pl.ds(rows, 8), lanes] = now[:8]

    off_ext[pl.ds(rows, 8), :] = off_ref[pl.ds(0, 8), :]

    @pl.when(pl.program_id(0) == pl.num_programs(0) - 1)
    def _():
        plan.finish(plan.steps - 1)


def scan_backward(saved, both, offset, proj, wide_b, wide_c, bound, params, xp, dtw, rate, chunk, width, grads, parts):
    T, DI = saved[0].shape
    n, states, cols, rank = T // chunk, rate.shape[0], xp.shape[0], dtw.shape[0]
    f32, bf16 = jnp.float32, jnp.bfloat16
    row = pl.BlockSpec((chunk, DI), lambda i: (n - 1 - i, 0))
    whole = lambda a: pl.BlockSpec(a.shape, lambda i: (0, 0))
    anywhere = pl.BlockSpec(memory_space=pl.ANY)
    plan, shaped, summed = reduction_of(grads, parts)
    sums = [jax.ShapeDtypeStruct((r, DI), f32) for r in (states, rank, cols, 48)]
    pieces = pltpu.VMEM((width, chunk, 128), f32)
    eights = pltpu.VMEM((width, 64, 128), f32)
    tall = pltpu.VMEM((chunk * states, 128), f32)
    out = pl.pallas_call(
        functools.partial(backward_kernel, width=width, plan=plan, total=T),
        grid=(n,),
        in_specs=[row] * 6
        + [
            pl.BlockSpec((chunk, 128), lambda i: (n - 1 - i, 0)),
            pl.BlockSpec((1, cols, chunk), lambda i: (n - 1 - i, 0, 0)),
            pl.BlockSpec((chunk * states, 128), lambda i: (n - 1 - i, 0)),
            pl.BlockSpec((chunk * states, 128), lambda i: (n - 1 - i, 0)),
            pl.BlockSpec((1, states, DI), lambda i: (n - 1 - i, 0, 0)),
        ]
        + [whole(a) for a in (params, xp, dtw, rate)]
        + [anywhere] * len(grads),
        out_specs=[row] + [whole(a) for a in sums] + [anywhere] * len(grads),
        out_shape=[jax.ShapeDtypeStruct((T, DI), bf16)] + sums + summed,
        scratch_shapes=[
            pltpu.VMEM((states, DI), f32),
            pieces,
            pieces,
            pieces,
            pltpu.VMEM((chunk * states + states, 128 * width), f32),
            eights,
            eights,
            pltpu.VMEM((chunk, DI), f32),
            pltpu.VMEM((chunk, DI), f32),
            pltpu.VMEM((chunk, DI), bf16),
            pltpu.VMEM((chunk, DI), bf16),
            pltpu.VMEM((chunk + 8, DI), f32),
            pltpu.VMEM((chunk + 8, 128), jnp.int32),
            tall,
            tall,
            pltpu.VMEM((2 * chunk, states * 128), bf16),
        ]
        + plan.scratch(),
        compiler_params=pltpu.CompilerParams(
            dimension_semantics=("arbitrary",), collective_id=0, has_side_effects=True, vmem_limit_bytes=56 << 20
        ),
        name="scan_backward",
    )(*saved, both, offset, proj, wide_b, wide_c, bound, params, xp, dtw, rate, *shaped)
    return out[:5], [o.reshape(-1, o.shape[-1]) for o in out[5:]]


def cluster_offsets(lengths, total_len):
    count = lengths.shape[1]
    ahead = jnp.arange(count)[:, None] < jnp.arange(count)[None, :]
    start_points = jnp.sum(jnp.where(ahead[None], lengths[:, :, None], 0), axis=1, dtype=jnp.int32)
    end_points = start_points + lengths
    where_at = jnp.arange(total_len, dtype=jnp.int32)
    inside = (where_at[None, None, :] >= start_points[:, :, None]) & (
        where_at[None, None, :] < end_points[:, :, None]
    )
    first_spot = jnp.sum(jnp.where(inside, start_points[:, :, None], 0), axis=1, dtype=jnp.int32)
    return where_at[None, :] - first_spot


def rms_piece(inputs, gain_vec):
    mean_sq = jnp.mean(inputs * inputs, axis=-1, keepdims=True)
    return inputs * lax.rsqrt(mean_sq + norm_eps) * gain_vec


def dot32(left, right, contract):
    return lax.dot_general(left, right, (contract, ((), ())), preferred_element_type=jnp.float32)


def thirds(columns, times=1):
    wide = columns // times // 1024 * 384
    return list(zip((wide, wide, columns // times - 2 * wide) * times, ORDERS * times))


def shards(
    hidden_in,
    cluster_lengths,
    norm_gain,
    in_proj,
    conv_weight,
    conv_bias,
    x_proj,
    dt_proj,
    dt_bias,
    a_log,
    skip_gain,
    out_proj,
    out_grad,
):
    f32, bf16 = jnp.float32, jnp.bfloat16
    taps, share = conv_weight.shape
    rank_dim = dt_proj.shape[0]
    state_dim = a_log.shape[0]
    contexts_here, total_len, model_dim = hidden_in.shape
    rows = contexts_here * total_len
    columns = rank_dim + 2 * state_dim
    offsets = cluster_offsets(cluster_lengths, total_len).reshape(rows)
    offset = jnp.broadcast_to(offsets[:, None], (rows, 128))
    grad_rows = out_grad.reshape(rows, model_dim)
    gain_part = jnp.pad(norm_gain, (0, share - norm_gain.shape[0]))
    vectors = [v[None] for v in (gain_part,)] + [conv_weight] + [v[None] for v in (conv_bias, dt_bias, skip_gain)]
    spare = columns - rank_dim - state_dim - taps - 4
    vectors = jnp.concatenate(vectors + [jnp.zeros((spare, share), bf16)], axis=0)
    normed16, packed, w_out, w_in, d_gated, both = gather_weights(
        hidden_in.reshape(rows, model_dim), grad_rows, (dt_proj, a_log, vectors, x_proj), out_proj, in_proj
    )
    inner_dim = packed.shape[1]
    decay_rate = -jnp.exp(packed[rank_dim : rank_dim + state_dim].astype(f32))
    rate2 = decay_rate * LOG2E
    params = packed[GAIN_ROW + 1 : GAIN_ROW + 9].astype(f32)
    w_dt, xp = packed[:rank_dim], packed[columns:]
    parts = lax.axis_size("fsdp")
    gain_full = packed[GAIN_ROW].reshape(parts, share)[:, : model_dim // parts].reshape(model_dim).astype(f32)
    inputs = hidden_in.reshape(rows, model_dim).astype(f32)
    *saved, gated16, gate16, proj, b_wide, c_wide, boundary, skip_sums = scan_forward(
        both, d_gated, offset, params, xp, w_dt, rate2, CHUNK, WIDTH
    )
    g_w_out = dot32(gated16, grad_rows, ((0,), (0,))).astype(bf16)
    g_w_gate = dot32(normed16, gate16, ((0,), (0,))).astype(bf16)
    (upper16, rate_sum, g_w_dt, g_w_x, sums), (t_out, t_gate) = scan_backward(
        saved, both, offset, proj, b_wide, c_wide, boundary, params, xp, w_dt, rate2, CHUNK, WIDTH,
        [g_w_out, g_w_gate], [thirds(model_dim), thirds(inner_dim)],
    )
    layer_out = (inputs + dot32(gated16, w_out, ((1,), (0,)))).astype(bf16)
    g_w_upper = dot32(normed16, upper16, ((0,), (0,))).astype(bf16)
    d_normed = dot32(upper16, w_in[:, :inner_dim], ((1,), (1,))) + dot32(
        gate16, w_in[:, inner_dim:], ((1,), (1,))
    )
    _, norm_pull = jax.vjp(rms_piece, inputs, gain_full)
    d_inputs, g_gain = norm_pull(d_normed)
    input_grad = grad_rows.astype(f32) + d_inputs

    gain_row = jnp.pad(
        g_gain.reshape(parts, model_dim // parts), ((0, 0), (0, (inner_dim - model_dim) // parts))
    ).reshape(1, inner_dim)
    row_sums = jnp.concatenate([sums, skip_sums]).reshape(7, 8, inner_dim).sum(axis=1)
    small = jnp.concatenate([g_w_x, g_w_dt, rate_sum * decay_rate, row_sums, gain_row], axis=0)
    spare = -small.shape[0] % (16 * lax.axis_size("dp"))
    small = jnp.pad(small, ((0, spare), (0, 0))).astype(bf16)
    small = small.reshape(-1, parts, inner_dim // parts).transpose(1, 0, 2).reshape(-1, inner_dim // parts)
    t_upper, t_small = reduce_all(
        [g_w_upper, small], [thirds(inner_dim, 2), [(inner_dim // parts, ORDERS[2])]], 1
    )
    t_small = t_small.astype(f32)
    t_in = jnp.concatenate([t_upper, t_gate], axis=1).astype(f32)
    t_out = t_out.astype(f32)
    at = 0
    picked = []
    for size in (columns, rank_dim, state_dim, taps, 1, 1, 1, 1):
        picked.append(t_small[at : at + size])
        at += size
    t_x, t_dt, t_alog, t_conv, t_b_conv, t_b_dt, t_skip, t_gain = picked
    return (
        layer_out.reshape(hidden_in.shape),
        input_grad.reshape(hidden_in.shape),
        t_gain[0, : model_dim // parts],
        t_in,
        t_conv,
        t_b_conv[0],
        t_x.T,
        t_dt,
        t_b_dt[0],
        t_alog,
        t_skip[0],
        t_out,
    )


def solution(mesh):
    placed = (
        P(("dp", "fsdp"), None, None),
        P(("dp", "fsdp"), None),
        P("fsdp"),
        P("fsdp", None),
        P(None, "fsdp"),
        P("fsdp"),
        P("fsdp", None),
        P(None, "fsdp"),
        P("fsdp"),
        P(None, "fsdp"),
        P("fsdp"),
        P("fsdp", None),
        P(("dp", "fsdp"), None, None),
    )
    return jax.shard_map(
        shards,
        mesh=mesh,
        in_specs=placed,
        out_specs=(
            P(("dp", "fsdp"), None, None),
            P(("dp", "fsdp"), None, None),
            P("fsdp"),
            P("fsdp", None),
            P(None, "fsdp"),
            P("fsdp"),
            P("fsdp", None),
            P(None, "fsdp"),
            P("fsdp"),
            P(None, "fsdp"),
            P("fsdp"),
            P("fsdp", None),
        ),
        check_vma=False,
    )
```

```python
import functools
import math

import jax
import jax.numpy as jnp
from jax import lax
from jax.experimental import pallas as pl
from jax.experimental.pallas import tpu as pltpu
from jax.sharding import PartitionSpec as P

CHUNK = 64
WIDTH = 4
norm_eps = 1e-05

def bits_of(size):
    return size.bit_length() - 1


ORDERS = ((0, 1, 2, 3), (1, 2, 0, 3), (2, 0, 1, 3))


class Reduction:
    def __init__(self, outer, inner, shapes, parts):
        self.outer_bits, self.inner_bits = bits_of(outer), bits_of(inner)
        self.blocks, self.inner = outer * inner, inner
        self.shapes = [(self.blocks, s[0] // self.blocks, s[1]) for s in shapes]
        self.stages = self.outer_bits + self.inner_bits
        self.steps = self.stages + self.inner_bits
        self.pieces = []
        for i, s in enumerate(shapes):
            at = 0
            for columns, order in parts[i]:
                order = [b for b in order if b < self.inner_bits] + list(range(len(order), self.inner_bits))
                self.pieces.append((i, pl.ds(at, columns), order))
                at += columns
            assert at == s[1]

    def axis_bit(self, piece, stage):
        if stage < self.outer_bits:
            return "fsdp", self.outer_bits - 1 - stage
        return "dp", self.pieces[piece][2][stage - self.outer_bits]

    def mine(self, piece, stage):
        axis, bit = self.axis_bit(piece, stage)
        return (lax.axis_index(axis) // (1 << bit)) % 2

    def partner(self, axis, bit):
        here = lax.axis_index(axis)
        return {axis: here + (1 << bit) - (here // (1 << bit)) % 2 * (2 << bit)}

    def barrier(self):
        sem = pltpu.get_barrier_semaphore()
        for axis, bits in (("fsdp", self.outer_bits), ("dp", self.inner_bits)):
            for bit in range(bits):
                pl.semaphore_signal(sem, inc=1, device_id=self.partner(axis, bit), device_id_type=pl.DeviceIdType.MESH)
        pl.semaphore_wait(sem, self.stages)

    def low(self, piece, stage):
        low = 0
        for s in range(1, stage):
            low = low + self.mine(piece, s) * (self.blocks >> (s + 1))
        return low

    def place(self, piece, stages):
        at = 0
        for j in range(stages):
            at = at + self.mine(piece, self.outer_bits + j) * (1 << (self.inner_bits - 1 - j))
        return at

    def bind(self, given, out, scratch):
        n = len(self.shapes)
        self.given, self.out = given, out
        self.work, self.inbox, self.result = scratch[:n], scratch[n : 2 * n], scratch[2 * n : 3 * n]
        self.send, self.recv, self.near = scratch[3 * n :]

    def scratch(self):
        b16, k = jnp.bfloat16, len(self.pieces)
        return (
            [pltpu.VMEM((b // 2, r, c), b16) for b, r, c in self.shapes]
            + [pltpu.VMEM((b, r, c), b16) for b, r, c in self.shapes]
            + [pltpu.VMEM((self.inner, r, c), b16) for b, r, c in self.shapes]
            + [pltpu.SemaphoreType.DMA((k, self.steps)), pltpu.SemaphoreType.DMA((k, self.steps)), pltpu.SemaphoreType.DMA((k,))]
        )

    def copy(self, piece, step):
        i, columns, _ = self.pieces[piece]
        if step < self.stages:
            stage = step
            half = self.blocks >> (step + 1)
            other = (1 - self.mine(piece, step)) * half
            if step == 0:
                source = self.given[i].at[pl.ds(other, half), :, columns]
            else:
                source = self.work[i].at[pl.ds(self.low(piece, step) + other, half), :, columns]
            target = self.inbox[i].at[pl.ds(self.blocks - 2 * half, half), :, columns]
        else:
            stage = self.steps - 1 - step + self.outer_bits
            j = stage - self.outer_bits
            many = 1 << (self.inner_bits - 1 - j)
            source = target = self.result[i].at[pl.ds(self.place(piece, j + 1), many), :, columns]
        return pltpu.make_async_remote_copy(
            src_ref=source,
            dst_ref=target,
            send_sem=self.send.at[piece, step],
            recv_sem=self.recv.at[piece, step],
            device_id=self.partner(*self.axis_bit(piece, stage)),
            device_id_type=pl.DeviceIdType.MESH,
        )

    def own(self, piece):
        i, columns, _ = self.pieces[piece]
        half = self.blocks // 2
        source = self.given[i].at[pl.ds(self.mine(piece, 0) * half, half), :, columns]
        return pltpu.make_async_copy(source, self.work[i].at[:, :, columns], self.near.at[piece])

    def leave(self, piece):
        i, columns, _ = self.pieces[piece]
        return pltpu.make_async_copy(self.result[i].at[:, :, columns], self.out[i].at[:, :, columns], self.near.at[piece])

    def add(self, piece, stage):
        i, columns, _ = self.pieces[piece]
        work, inbox, result = self.work[i], self.inbox[i], self.result[i]
        half = self.blocks >> (stage + 1)
        arrived = self.blocks - 2 * half
        base = 0 if stage == 0 else self.low(piece, stage) + self.mine(piece, stage) * half

        @pl.loop(0, half)
        def _(k):
            new = work[base + k, :, columns].astype(jnp.float32) + inbox[arrived + k, :, columns].astype(jnp.float32)
            if stage == self.stages - 1:
                result[self.place(piece, self.inner_bits), :, columns] = new.astype(jnp.bfloat16)
            else:
                work[base + k, :, columns] = new.astype(jnp.bfloat16)

    def start(self, pieces):
        for p in pieces:
            self.copy(p, 0).start()
        for p in pieces:
            self.own(p).start()

    def advance(self, pieces, step):
        for p in pieces:
            if step == 0:
                self.own(p).wait()
            self.copy(p, step).wait()
            if step < self.stages:
                self.add(p, step)
            if step + 1 < self.steps:
                self.copy(p, step + 1).start()
            else:
                self.leave(p).start()

    def gone(self, pieces):
        for p in pieces:
            self.leave(p).wait()

    def times(self, count):
        heavy = (18.0, 10.0, 6.5, 14.0)
        there = [heavy[min(j, 3)] for j in range(self.inner_bits)]
        loads = [11.0] * self.outer_bits + there + there[::-1]
        total, at, out = sum(loads), 0.0, []
        for load in loads[:-1]:
            at += load
            out.append(max(1, min(count - 1, round(at / total * count))))
        return out


def reduction_of(arrays, parts):
    plan = Reduction(lax.axis_size("fsdp"), lax.axis_size("dp"), [a.shape for a in arrays], parts)
    shaped = [a.reshape(s) for a, s in zip(arrays, plan.shapes)]
    out = [jax.ShapeDtypeStruct((plan.inner,) + s[1:], jnp.bfloat16) for s in plan.shapes]
    return plan, shaped, out


class Exchange:
    def __init__(self, size):
        self.size = size

    def owner(self, turn):
        return (lax.axis_index("fsdp") + self.size - turn) % self.size

    def peer(self, turn):
        return {"fsdp": (lax.axis_index("fsdp") + turn) % self.size}

    def barrier(self):
        sem = pltpu.get_barrier_semaphore()
        for turn in range(1, self.size):
            pl.semaphore_signal(sem, inc=1, device_id=self.peer(turn), device_id_type=pl.DeviceIdType.MESH)
        pl.semaphore_wait(sem, self.size - 1)

    def copy(self, source, target, sems, which, turn):
        if turn == 0:
            return pltpu.make_async_copy(source, target, sems[1].at[which, 0])
        return pltpu.make_async_remote_copy(
            src_ref=source,
            dst_ref=target,
            send_sem=sems[0].at[which, turn],
            recv_sem=sems[1].at[which, turn],
            device_id=self.peer(turn),
            device_id_type=pl.DeviceIdType.MESH,
        )


GAIN_ROW = 80


def gather_kernel(
    x_ref, go_ref, dt_ref, rate_ref, vec_ref, xp_ref, wout_ref, win_ref,
    normed_ref, pack_out, wout_out, win_out, dg_out, both_out,
    pack, wout, win, dg, both, packed, send, recv, leave, tiles, *, plan
):
    f32, bf16 = jnp.float32, jnp.bfloat16
    rows, model = x_ref.shape
    deep, wide, share = model // plan.size, both.shape[1], packed.shape[1]
    me = lax.axis_index("fsdp")
    sems = (send, recv)

    def copies(which, turn):
        source = (packed, wout_ref, win_ref)[which]
        if which == 0:
            target = pack.at[:, pl.ds(pl.multiple_of(me * share, 128), share)]
        else:
            target = (wout, win)[which - 1].at[me]
        return plan.copy(source, target, sems, which, turn)

    at = 0
    for ref in (dt_ref, rate_ref, vec_ref):
        packed[at : at + ref.shape[0], :] = ref[...]
        at += ref.shape[0]
    packed[at:, :] = xp_ref[...].astype(f32).T.astype(bf16)
    plan.barrier()
    for which in range(3):
        for turn in range(1, plan.size):
            copies(which, turn).start()
    for which in (1, 0, 2):
        copies(which, 0).start()

    def times_out(turn):
        at = plan.owner(turn)

        @pl.loop(0, share // 256)
        def _(k):
            here = pl.ds(pl.multiple_of(at * share + k * 256, 128), 256)
            dg[:, here] = lax.dot_general(
                go_ref[...], wout[at, pl.ds(pl.multiple_of(k * 256, 256), 256), :],
                (((1,), (1,)), ((), ())), preferred_element_type=f32,
            )
        pltpu.make_async_copy(wout.at[at], wout_out.at[at], leave.at[0, turn]).start()
        part = pl.ds(pl.multiple_of(at * share, 128), share)
        pltpu.make_async_copy(dg.at[:, part], dg_out.at[:, part], leave.at[2, turn]).start()

    def times_in(turn):
        at = plan.owner(turn)
        left = pl.ds(pl.multiple_of(at * deep, 128), deep)

        @pl.loop(0, wide // 256)
        def _(k):
            here = pl.ds(pl.multiple_of(k * 256, 256), 256)
            new = jnp.dot(normed_ref[:, left], win[at, :, here], preferred_element_type=f32)
            both[:, here] = new if turn == 0 else both[:, here] + new
            if turn == plan.size - 1:
                pltpu.make_async_copy(both.at[:, here], both_out.at[:, here], tiles.at[k]).start()
        pltpu.make_async_copy(win.at[at], win_out.at[at], leave.at[1, turn]).start()

    copies(1, 0).wait()
    times_out(0)
    for turn in range(plan.size):
        copies(0, turn).wait()
    whole_pack = pltpu.make_async_copy(pack, pack_out, leave.at[3, 0])
    whole_pack.start()
    gain = jnp.concatenate(
        [pack[GAIN_ROW : GAIN_ROW + 16, b * share : b * share + deep] for b in range(plan.size)], axis=1
    ).astype(f32)[:1]

    @pl.loop(0, rows // 64)
    def _(k):
        here = pl.ds(pl.multiple_of(k * 64, 64), 64)
        x = x_ref[here, :].astype(f32)
        mean_sq = jnp.mean(x * x, axis=-1, keepdims=True)
        normed_ref[here, :] = (x * lax.rsqrt(mean_sq + norm_eps) * gain).astype(bf16)

    copies(2, 0).wait()
    times_in(0)
    for turn in range(1, plan.size):
        copies(1, turn).wait()
        times_out(turn)
    for turn in range(1, plan.size):
        copies(2, turn).wait()
        times_in(turn)
    whole_pack.wait()
    for turn in range(plan.size):
        at = plan.owner(turn)
        part = pl.ds(pl.multiple_of(at * share, 128), share)
        pltpu.make_async_copy(wout.at[at], wout_out.at[at], leave.at[0, turn]).wait()
        pltpu.make_async_copy(win.at[at], win_out.at[at], leave.at[1, turn]).wait()
        pltpu.make_async_copy(dg.at[:, part], dg_out.at[:, part], leave.at[2, turn]).wait()

    @pl.loop(0, wide // 256)
    def _(k):
        here = pl.ds(pl.multiple_of(k * 256, 256), 256)
        pltpu.make_async_copy(both.at[:, here], both_out.at[:, here], tiles.at[k]).wait()


def gather_weights(x, grad_rows, small, w_out, w_in):
    f32, bf16 = jnp.float32, jnp.bfloat16
    plan = Exchange(lax.axis_size("fsdp"))
    n, (rows, model), wide = plan.size, x.shape, w_in.shape[1]
    depth, share = sum(s.shape[0] for s in small[:3]) + small[3].shape[1], small[0].shape[1]
    inner = n * share
    anywhere = pl.BlockSpec(memory_space=pl.ANY)
    near = pl.BlockSpec(memory_space=pltpu.VMEM)
    shapes = [
        ((depth, inner), bf16), ((n,) + w_out.shape, bf16), ((n,) + w_in.shape, bf16), ((rows, inner), f32), ((rows, wide), f32),
    ]
    normed, packed, out_all, in_all, d_gated, both = pl.pallas_call(
        functools.partial(gather_kernel, plan=plan),
        out_shape=[jax.ShapeDtypeStruct(x.shape, bf16)] + [jax.ShapeDtypeStruct(*s) for s in shapes],
        in_specs=[near] * 6 + [anywhere] * 2,
        out_specs=[near] + [anywhere] * 5,
        scratch_shapes=[pltpu.VMEM(*s) for s in shapes]
        + [
            pltpu.VMEM((depth, share), bf16),
            pltpu.SemaphoreType.DMA((3, n)),
            pltpu.SemaphoreType.DMA((3, n)),
            pltpu.SemaphoreType.DMA((4, n)),
            pltpu.SemaphoreType.DMA((wide // 256,)),
        ],
        compiler_params=pltpu.CompilerParams(collective_id=2, has_side_effects=True, vmem_limit_bytes=56 << 20),
        name="gather_weights",
    )(x, grad_rows, *small, w_out, w_in)
    return normed, packed, out_all.reshape(-1, w_out.shape[1]), in_all.reshape(-1, wide), d_gated, both


BIG = 1e30
LN2 = math.log(2.0)
LOG2E = 1.0 / LN2
TAPS, SHIFT, DT_BIAS, SKIP = 0, 4, 5, 6


def rows_of(ref, tile, row, width):
    return [ref[tile + j, pl.ds(row, 8, stride=0), :] for j in range(width)]


def by_eights(ref, tile):
    total = ref[tile, pl.ds(0, 8, stride=8), :]
    for s in range(1, 8):
        total = total + ref[tile, pl.ds(s, 8, stride=8), :]
    return total


def folded(x):
    total = x[:8]
    for s in range(8, x.shape[0], 8):
        total = total + x[s : s + 8]
    return total


def spread(proj, first, wide, states):
    for t in range(proj.shape[1]):
        wide[pl.ds(t * states, states), :] = jnp.broadcast_to(proj[first : first + states, t : t + 1], (states, 128))


def forward_kernel(
    upper_ref, z_ref, dg_ref, off_ref, par_ref, xp_ref, dtw_ref, a_ref,
    u_ref, ds_ref, dt_ref, sg_ref, dy_ref, gated_ref, gate_ref, proj_ref, wide_b, wide_c, bound_ref, skip_ref,
    hs, ext, u16, dtm, dtu, ys, ybuf, *, width
):
    f32, bf16 = jnp.float32, jnp.bfloat16
    rows, inner = upper_ref.shape
    states, rank = a_ref.shape[0], dtw_ref.shape[0]
    tiles = inner // 128

    @pl.when(pl.program_id(0) == 0)
    def _():
        hs[...] = jnp.zeros_like(hs)
        skip_ref[...] = jnp.zeros_like(skip_ref)
        ext[pl.ds(0, 8), :] = jnp.zeros((8, inner), f32)

    bound_ref[0] = hs[...]

    @pl.loop(0, tiles, unroll=True)
    def _(k):
        lanes = pl.ds(pl.multiple_of(k * 128, 128), 128)
        now = upper_ref[:, lanes]
        ext[pl.ds(8, rows), lanes] = now
        conv = par_ref[SHIFT : SHIFT + 1, lanes] + par_ref[TAPS + 3 : TAPS + 4, lanes] * now
        for lag in range(1, 4):
            before = ext[pl.ds(8 - lag, rows), lanes]
            conv = conv + par_ref[TAPS + 3 - lag : TAPS + 4 - lag, lanes] * jnp.where(off_ref[...] >= lag, before, 0.0)
        sig = jax.nn.sigmoid(conv)
        act = conv * sig
        u_ref[:, lanes] = act
        u16[:, lanes] = act.astype(bf16)
        ds_ref[:, lanes] = sig * (1.0 + conv * (1.0 - sig))
        ext[pl.ds(0, 8), lanes] = now[rows - 8 :]

    proj = lax.dot_general(xp_ref[...], u16[...], (((1,), (1,)), ((), ())), preferred_element_type=f32)
    proj_ref[0] = proj
    spread(proj, rank, wide_b, states)
    spread(proj, rank + states, wide_c, states)
    rank16 = proj[:rank].astype(bf16)

    @pl.loop(0, tiles // 2, unroll=True)
    def _(k):
        pair = pl.ds(pl.multiple_of(k * 256, 256), 256)
        pre = lax.dot_general(rank16, dtw_ref[:, pair], (((0,), (0,)), ((), ())), preferred_element_type=f32)
        pre = pre + par_ref[DT_BIAS : DT_BIAS + 1, pair]
        small = jnp.exp(-jnp.abs(pre))
        delta = jnp.maximum(pre, 0.0) + jnp.log1p(small)
        dt_ref[:, pair] = delta
        sg_ref[:, pair] = jnp.where(pre >= 0, 1.0, small) / (1.0 + small)
        grown = delta * u_ref[:, pair]
        for j in range(2):
            part = slice(128 * j, 128 * j + 128)
            dtm[2 * k + j] = jnp.where(off_ref[...] > 0, delta[:, part], BIG)
            dtu[2 * k + j] = grown[:, part]

    @pl.loop(0, tiles // width)
    def _(cb):
        tile = cb * width
        base = pl.multiple_of(cb * 128 * width, 128 * width)
        rate = [[a_ref[pl.ds(8 * s, 8), pl.ds(base + 128 * j, 128)] for s in range(2)] for j in range(width)]

        def body(g, h):
            h = [list(p) for p in zip(h[:width], h[width:])]
            r0 = pl.multiple_of(g * 8, 8)
            for t in range(8):
                d = rows_of(dtm, tile, r0 + t, width)
                x = rows_of(dtu, tile, r0 + t, width)
                bt = [wide_b[pl.ds((r0 + t) * 16 + 8 * s, 8), :] for s in range(2)]
                ct = [wide_c[pl.ds((r0 + t) * 16 + 8 * s, 8), :] for s in range(2)]
                for j in range(width):
                    for s in range(2):
                        h[j][s] = jnp.exp2(d[j] * rate[j][s]) * h[j][s] + x[j] * bt[s]
                    ybuf[j, pl.ds(t * 8, 8), :] = ct[0] * h[j][0] + ct[1] * h[j][1]
            for j in range(width):
                ys[tile + j, pl.ds(r0, 8), :] = by_eights(ybuf, j)
            return tuple(p[0] for p in h) + tuple(p[1] for p in h)

        h = tuple(hs[pl.ds(8 * s, 8), pl.ds(base + 128 * j, 128)] for s in range(2) for j in range(width))
        h = lax.fori_loop(0, rows // 8, body, h, unroll=4)
        for s in range(2):
            for j in range(width):
                hs[pl.ds(8 * s, 8), pl.ds(base + 128 * j, 128)] = h[s * width + j]

    @pl.loop(0, tiles, unroll=True)
    def _(k):
        lanes = pl.ds(pl.multiple_of(k * 128, 128), 128)
        act, z, dg = u_ref[:, lanes], z_ref[:, lanes], dg_ref[:, lanes]
        full = ys[k] + par_ref[SKIP : SKIP + 1, lanes] * act
        sig = jax.nn.sigmoid(z)
        silu = z * sig
        gated_ref[:, lanes] = (full * silu).astype(bf16)
        dy = dg * silu
        dy_ref[:, lanes] = dy
        gate_ref[:, lanes] = (dg * full * sig * (1.0 + z * (1.0 - sig))).astype(bf16)
        skip_ref[:, lanes] = skip_ref[:, lanes] + folded(dy * act)


def scan_forward(both, d_gated, offset, params, xp, dtw, rate, chunk, width):
    T, DI = d_gated.shape
    n, states, cols = T // chunk, rate.shape[0], xp.shape[0]
    f32, bf16 = jnp.float32, jnp.bfloat16
    row = pl.BlockSpec((chunk, DI), lambda i: (i, 0))
    whole = lambda a: pl.BlockSpec(a.shape, lambda i: (0, 0))
    flat = lambda d: jax.ShapeDtypeStruct((T, DI), d)
    tile = lambda d: pltpu.VMEM((DI // 128, chunk, 128), d)
    return pl.pallas_call(
        functools.partial(forward_kernel, width=width),
        grid=(n,),
        in_specs=[row, pl.BlockSpec((chunk, DI), lambda i: (i, 1)), row, pl.BlockSpec((chunk, 128), lambda i: (i, 0))]
        + [whole(a) for a in (params, xp, dtw, rate)],
        out_specs=[row] * 7
        + [
            pl.BlockSpec((1, cols, chunk), lambda i: (i, 0, 0)),
            pl.BlockSpec((chunk * states, 128), lambda i: (i, 0)),
            pl.BlockSpec((chunk * states, 128), lambda i: (i, 0)),
            pl.BlockSpec((1, states, DI), lambda i: (i, 0, 0)),
            pl.BlockSpec((8, DI), lambda i: (0, 0)),
        ],
        out_shape=[flat(f32)] * 5
        + [flat(bf16)] * 2
        + [
            jax.ShapeDtypeStruct((n, cols, chunk), f32),
            jax.ShapeDtypeStruct((T * states, 128), f32),
            jax.ShapeDtypeStruct((T * states, 128), f32),
            jax.ShapeDtypeStruct((n, states, DI), f32),
            jax.ShapeDtypeStruct((8, DI), f32),
        ],
        scratch_shapes=[
            pltpu.VMEM((states, DI), f32),
            pltpu.VMEM((chunk + 8, DI), f32),
            pltpu.VMEM((chunk, DI), bf16),
            tile(f32),
            tile(f32),
            tile(f32),
            pltpu.VMEM((width, 64, 128), f32),
        ],
        compiler_params=pltpu.CompilerParams(dimension_semantics=("arbitrary",), vmem_limit_bytes=48 << 20),
        name="scan_forward",
    )(both, both, d_gated, offset, params, xp, dtw, rate)


def backward_kernel(
    u_ref, ds_ref, dt_ref, sg_ref, dy_ref, upper_ref, off_ref, proj_ref, wide_b, wide_c, bound_ref, par_ref, xp_ref, dtw_ref, a_ref,
    *rest, width, plan, total
):
    f32, bf16 = jnp.float32, jnp.bfloat16
    n = len(plan.shapes)
    given, rest = rest[:n], rest[n:]
    (du_ref, ga_ref, gdt_ref, gx_ref, sum_ref), out, rest = rest[:5], rest[5 : 5 + n], rest[5 + n :]
    ws, dtm, dtu, dyb, hbuf, sbuf, qbuf, dd, di, u16, dt16, ext, off_ext, wide_db, wide_dc, cols_ref = rest[:16]
    plan.bind(given, out, rest[16:])
    rows, inner = u_ref.shape
    states, rank = a_ref.shape[0], dtw_ref.shape[0]
    tiles = inner // 128
    everything = range(len(plan.pieces))
    times = plan.times(total // rows * (tiles // width))

    @pl.when(pl.program_id(0) == 0)
    def _():
        for ref in (ws, ga_ref, gdt_ref, gx_ref, sum_ref):
            ref[...] = jnp.zeros_like(ref)
        ext[pl.ds(rows, 8), :] = jnp.zeros((8, inner), f32)
        off_ext[pl.ds(rows, 8), :] = jnp.full((8, 128), -1, jnp.int32)
        plan.barrier()
        plan.start(everything)

    proj = proj_ref[0]
    wide_db[...] = jnp.zeros_like(wide_db)
    wide_dc[...] = jnp.zeros_like(wide_dc)

    @pl.loop(0, tiles // width)
    def _(cb):
        tile = cb * width
        base = pl.multiple_of(cb * 128 * width, 128 * width)
        for at in sorted(set(times)):
            @pl.when(pl.program_id(0) * (tiles // width) + cb == at)
            def _():
                for step in range(plan.steps - 1):
                    if times[step] == at:
                        plan.advance(everything, step)

        for j in range(width):
            lanes = pl.ds(base + 128 * j, 128)
            d, act = dt_ref[:, lanes], u_ref[:, lanes]
            dtm[j] = jnp.where(off_ref[...] > 0, d, BIG)
            dtu[j] = d * act
            dyb[j] = dy_ref[:, lanes]
            u16[:, lanes] = act.astype(bf16)
        rate = [[a_ref[pl.ds(8 * s, 8), pl.ds(base + 128 * j, 128)] for s in range(2)] for j in range(width)]

        def again(g, h):
            h = [list(p) for p in zip(h[:width], h[width:])]
            r0 = pl.multiple_of(g * 8, 8)
            for t in range(8):
                d = rows_of(dtm, 0, r0 + t, width)
                x = rows_of(dtu, 0, r0 + t, width)
                bt = [wide_b[pl.ds((r0 + t) * 16 + 8 * s, 8), :] for s in range(2)]
                for j in range(width):
                    for s in range(2):
                        hbuf[pl.ds((r0 + t) * 16 + 8 * s, 8), pl.ds(128 * j, 128)] = h[j][s]
                        h[j][s] = jnp.exp2(d[j] * rate[j][s]) * h[j][s] + x[j] * bt[s]
            return tuple(p[0] for p in h) + tuple(p[1] for p in h)

        h = tuple(bound_ref[0, pl.ds(8 * s, 8), pl.ds(base + 128 * j, 128)] for s in range(2) for j in range(width))
        h = lax.fori_loop(0, rows // 8, again, h)
        for s in range(2):
            for j in range(width):
                hbuf[pl.ds(rows * 16 + 8 * s, 8), pl.ds(128 * j, 128)] = h[s * width + j]

        def body(k, carry):
            r0 = pl.multiple_of((rows // 8 - 1 - k) * 8, 8)
            w = [[carry[s * width + j] for s in range(2)] for j in range(width)]
            ga = [[carry[2 * width + s * width + j] for s in range(2)] for j in range(width)]
            newer = [[hbuf[pl.ds((r0 + 8) * 16 + 8 * s, 8), pl.ds(128 * j, 128)] for s in range(2)] for j in range(width)]
            for t in range(7, -1, -1):
                d = rows_of(dtm, 0, r0 + t, width)
                x = rows_of(dtu, 0, r0 + t, width)
                v = rows_of(dyb, 0, r0 + t, width)
                bt = [wide_b[pl.ds((r0 + t) * 16 + 8 * s, 8), :] for s in range(2)]
                ct = [wide_c[pl.ds((r0 + t) * 16 + 8 * s, 8), :] for s in range(2)]
                db = [None, None]
                dc = [None, None]
                for j in range(width):
                    qs, ss = None, None
                    for s in range(2):
                        later = newer[j][s]
                        prior = hbuf[pl.ds((r0 + t) * 16 + 8 * s, 8), pl.ds(128 * j, 128)]
                        newer[j][s] = prior
                        g = ct[s] * v[j] + w[j][s]
                        w[j][s] = jnp.exp2(d[j] * rate[j][s]) * g
                        q = w[j][s] * prior
                        ga[j][s] = ga[j][s] + q * d[j]
                        qa = q * rate[j][s]
                        sb = g * bt[s]
                        qs = qa if qs is None else qs + qa
                        ss = sb if ss is None else ss + sb
                        gx = g * x[j]
                        vh = v[j] * later
                        db[s] = gx if db[s] is None else db[s] + gx
                        dc[s] = vh if dc[s] is None else dc[s] + vh
                    qbuf[j, pl.ds(t * 8, 8), :] = qs
                    sbuf[j, pl.ds(t * 8, 8), :] = ss
                for s in range(2):
                    here = pl.ds((r0 + t) * 16 + 8 * s, 8)
                    wide_db[here, :] = wide_db[here, :] + db[s]
                    wide_dc[here, :] = wide_dc[here, :] + dc[s]
            for j in range(width):
                lanes = pl.ds(base + 128 * j, 128)
                here = pl.ds(r0, 8)
                s8 = by_eights(sbuf, j)
                dd[here, lanes] = LN2 * by_eights(qbuf, j) + u_ref[here, lanes] * s8
                di[here, lanes] = dt_ref[here, lanes] * s8
            return tuple(w[j][s] for s in range(2) for j in range(width)) + tuple(
                ga[j][s] for s in range(2) for j in range(width)
            )

        held = [(r, pl.ds(8 * s, 8), pl.ds(base + 128 * j, 128)) for r in (ws, ga_ref) for s in range(2) for j in range(width)]
        end = lax.fori_loop(0, rows // 8, body, tuple(r[a, b] for r, a, b in held))
        for (r, a, b), value in zip(held, end):
            r[a, b] = value

    for i, ref in enumerate((wide_db, wide_dc)):
        for k in range(states):
            cols_ref[pl.ds(i * rows, rows), pl.ds(128 * k, 128)] = ref[pl.ds(k, rows, stride=states), :].astype(bf16)
    owner = lax.broadcasted_iota(jnp.int32, (states, states * 128), 1) // 128
    picks = jnp.where(owner == lax.broadcasted_iota(jnp.int32, (states, states * 128), 0), 1.0, 0.0).astype(bf16)
    d_bc = lax.dot_general(picks, cols_ref[...], (((1,), (1,)), ((), ())), preferred_element_type=f32)

    @pl.loop(0, tiles, unroll=True)
    def _(k):
        lanes = pl.ds(pl.multiple_of(k * 128, 128), 128)
        low = (dd[:, lanes] * sg_ref[:, lanes]).astype(bf16)
        dt16[:, lanes] = low
        sum_ref[pl.ds(40, 8), lanes] = sum_ref[pl.ds(40, 8), lanes] + folded(low.astype(f32))

    rank16 = proj[:rank].astype(bf16)
    d_rank = lax.dot_general(dtw_ref[...], dt16[...], (((1,), (1,)), ((), ())), preferred_element_type=f32)
    proj16 = jnp.concatenate([d_rank, d_bc[:, :rows], d_bc[:, rows:]], axis=0).astype(bf16)
    off_ext[pl.ds(0, rows), :] = off_ref[...]

    @pl.loop(0, tiles // 2, unroll=True)
    def _(k):
        pair = pl.ds(pl.multiple_of(k * 256, 256), 256)
        dot = lambda a, b, c: lax.dot_general(a, b, ((c, (0,)), ((), ())), preferred_element_type=f32)
        gdt_ref[:, pair] = gdt_ref[:, pair] + dot(rank16, dt16[:, pair], (1,))
        gx_ref[:, pair] = gx_ref[:, pair] + dot(proj16, u16[:, pair], (1,))
        inner_grad = dot(proj16, xp_ref[:, pair], (0,)) + di[:, pair] + dy_ref[:, pair] * par_ref[SKIP : SKIP + 1, pair]
        ext[pl.ds(0, rows), pair] = inner_grad * ds_ref[:, pair]
        for j in range(2):
            lanes = pl.ds(pl.multiple_of(k * 256 + 128 * j, 128), 128)
            now, above = ext[pl.ds(0, rows), lanes], upper_ref[:, lanes]
            grad = par_ref[TAPS + 3 : TAPS + 4, lanes] * now
            sums = [now, now * above]
            for lag in range(1, 4):
                after = jnp.where(off_ext[pl.ds(lag, rows), :] >= lag, ext[pl.ds(lag, rows), lanes], 0.0)
                grad = grad + par_ref[TAPS + 3 - lag : TAPS + 4 - lag, lanes] * after
                sums.append(after * above)
            du_ref[:, lanes] = grad.astype(bf16)
            for at, value in zip((32, 24, 16, 8, 0), sums):
                sum_ref[pl.ds(at, 8), lanes] = sum_ref[pl.ds(at, 8), lanes] + folded(value)
            ext[pl.ds(rows, 8), lanes] = now[:8]

    off_ext[pl.ds(rows, 8), :] = off_ref[pl.ds(0, 8), :]

    @pl.when(pl.program_id(0) == pl.num_programs(0) - 1)
    def _():
        plan.advance(everything, plan.steps - 1)
        plan.gone(everything)


def scan_backward(saved, both, offset, proj, wide_b, wide_c, bound, params, xp, dtw, rate, chunk, width, grads, parts):
    T, DI = saved[0].shape
    n, states, cols, rank = T // chunk, rate.shape[0], xp.shape[0], dtw.shape[0]
    f32, bf16 = jnp.float32, jnp.bfloat16
    row = pl.BlockSpec((chunk, DI), lambda i: (n - 1 - i, 0))
    whole = lambda a: pl.BlockSpec(a.shape, lambda i: (0, 0))
    anywhere = pl.BlockSpec(memory_space=pl.ANY)
    plan, shaped, summed = reduction_of(grads, parts)
    sums = [jax.ShapeDtypeStruct((r, DI), f32) for r in (states, rank, cols, 48)]
    pieces = pltpu.VMEM((width, chunk, 128), f32)
    eights = pltpu.VMEM((width, 64, 128), f32)
    tall = pltpu.VMEM((chunk * states, 128), f32)
    out = pl.pallas_call(
        functools.partial(backward_kernel, width=width, plan=plan, total=T),
        grid=(n,),
        in_specs=[row] * 6
        + [
            pl.BlockSpec((chunk, 128), lambda i: (n - 1 - i, 0)),
            pl.BlockSpec((1, cols, chunk), lambda i: (n - 1 - i, 0, 0)),
            pl.BlockSpec((chunk * states, 128), lambda i: (n - 1 - i, 0)),
            pl.BlockSpec((chunk * states, 128), lambda i: (n - 1 - i, 0)),
            pl.BlockSpec((1, states, DI), lambda i: (n - 1 - i, 0, 0)),
        ]
        + [whole(a) for a in (params, xp, dtw, rate)]
        + [anywhere] * len(grads),
        out_specs=[row] + [whole(a) for a in sums] + [anywhere] * len(grads),
        out_shape=[jax.ShapeDtypeStruct((T, DI), bf16)] + sums + summed,
        scratch_shapes=[
            pltpu.VMEM((states, DI), f32),
            pieces,
            pieces,
            pieces,
            pltpu.VMEM((chunk * states + states, 128 * width), f32),
            eights,
            eights,
            pltpu.VMEM((chunk, DI), f32),
            pltpu.VMEM((chunk, DI), f32),
            pltpu.VMEM((chunk, DI), bf16),
            pltpu.VMEM((chunk, DI), bf16),
            pltpu.VMEM((chunk + 8, DI), f32),
            pltpu.VMEM((chunk + 8, 128), jnp.int32),
            tall,
            tall,
            pltpu.VMEM((2 * chunk, states * 128), bf16),
        ]
        + plan.scratch(),
        compiler_params=pltpu.CompilerParams(
            dimension_semantics=("arbitrary",), collective_id=0, has_side_effects=True, vmem_limit_bytes=56 << 20
        ),
        name="scan_backward",
    )(*saved, both, offset, proj, wide_b, wide_c, bound, params, xp, dtw, rate, *shaped)
    return out[:5], [o.reshape(-1, o.shape[-1]) for o in out[5:]]


def finish_kernel(
    grads_ref, small_ref, upper_ref, gate_ref, gated_ref, in_ref, wout_ref, x_ref, go_ref, gain_ref,
    total_ref, few_ref, layer_ref, left_ref,
    upper, gate, gated, win, wout, x, go, dn, layer, mine, gain_sum, loads, away, *rest, plan, gain_row
):
    f32, bf16 = jnp.float32, jnp.bfloat16
    rows, model = x.shape
    inner = upper.shape[1]
    plan.bind([grads_ref, mine], [total_ref, few_ref], rest)
    main = [p for p in range(len(plan.pieces)) if plan.pieces[p][0] == 0]
    late = [p for p in range(len(plan.pieces)) if plan.pieces[p][0] == 1]

    copies = [
        pltpu.make_async_copy(a, b, loads.at[i])
        for i, (a, b) in enumerate(
            (
                (upper_ref, upper), (in_ref.at[:, pl.ds(0, inner)], win.at[0]), (gate_ref, gate),
                (in_ref.at[:, pl.ds(inner, inner)], win.at[1]), (x_ref, x), (go_ref, go), (small_ref, mine),
                (gated_ref, gated), (wout_ref, wout),
            )
        )
    ]

    def product(left, k):
        @pl.loop(0, model // 256)
        def _(j):
            here = pl.ds(pl.multiple_of(j * 256, 256), 256)
            new = lax.dot_general(left[...], win[k, here, :], (((1,), (1,)), ((), ())), preferred_element_type=f32)
            dn[:, here] = new if k == 0 else dn[:, here] + new

    plan.barrier()
    plan.start(main)
    for c in copies:
        c.start()
    copies[0].wait()
    copies[1].wait()
    product(upper, 0)
    plan.advance(main, 0)
    copies[2].wait()
    copies[3].wait()
    product(gate, 1)
    copies[4].wait()
    copies[5].wait()
    gain_sum[...] = jnp.zeros_like(gain_sum)

    @pl.loop(0, rows // 32)
    def _(k):
        here = pl.ds(pl.multiple_of(k * 32, 32), 32)
        value, grad, gain = x[here, :].astype(f32), dn[here, :], gain_ref[...]
        scale = lax.rsqrt(jnp.mean(value * value, axis=-1, keepdims=True) + norm_eps)
        through = grad * value
        gain_sum[...] = gain_sum[...] + folded(through * scale)
        pull = jnp.mean(through * gain, axis=-1, keepdims=True) * (scale * scale * scale)
        dn[here, :] = go[here, :].astype(f32) + scale * (grad * gain) - value * pull

    leaving = [pltpu.make_async_copy(dn, left_ref, away.at[0]), pltpu.make_async_copy(layer, layer_ref, away.at[1])]
    leaving[0].start()
    copies[6].wait()
    gain_grad = jnp.sum(gain_sum[...], axis=0, keepdims=True)
    outer = plan.blocks // plan.inner
    deep, r = model // outer, mine.shape[1]
    for f in range(outer):
        block = f * plan.inner + gain_row // r
        old = mine[block, :, 0:deep].astype(f32)
        new = jnp.broadcast_to(gain_grad[:, f * deep : (f + 1) * deep], (r, deep))
        chosen = lax.broadcasted_iota(jnp.int32, (r, deep), 0) == gain_row % r
        mine[block, :, 0:deep] = jnp.where(chosen, new, old).astype(bf16)
    plan.start(late)
    plan.advance(main, 1)
    plan.advance(late, 0)
    copies[7].wait()
    copies[8].wait()

    @pl.loop(0, model // 256)
    def _(j):
        here = pl.ds(pl.multiple_of(j * 256, 256), 256)
        new = x[:, here].astype(f32) + jnp.dot(gated[...], wout[:, here], preferred_element_type=f32)
        layer[:, here] = new.astype(bf16)

    leaving[1].start()
    for step in range(2, plan.steps):
        plan.advance(main, step)
        plan.advance(late, step - 1)
    plan.advance(late, plan.steps - 1)
    plan.gone(main + late)
    for c in leaving:
        c.wait()


def finish(grads, small, upper16, gate16, gated16, w_in, w_out, x, go, gain, parts, gain_row):
    f32, bf16 = jnp.float32, jnp.bfloat16
    (rows, model), inner = x.shape, upper16.shape[1]
    plan, shaped, summed = reduction_of([grads, small], parts)
    anywhere = pl.BlockSpec(memory_space=pl.ANY)
    flat = pltpu.VMEM((rows, inner), bf16)
    thin = pltpu.VMEM((rows, model), bf16)
    total, few, layer_out, input_grad = pl.pallas_call(
        functools.partial(finish_kernel, plan=plan, gain_row=gain_row),
        out_shape=summed + [jax.ShapeDtypeStruct((rows, model), bf16), jax.ShapeDtypeStruct((rows, model), f32)],
        in_specs=[anywhere] * 9 + [pl.BlockSpec(memory_space=pltpu.VMEM)],
        out_specs=[anywhere] * 4,
        scratch_shapes=[
            flat,
            flat,
            flat,
            pltpu.VMEM((2, model, inner), bf16),
            pltpu.VMEM((inner, model), bf16),
            thin,
            thin,
            pltpu.VMEM((rows, model), f32),
            thin,
            pltpu.VMEM(plan.shapes[1], bf16),
            pltpu.VMEM((8, model), f32),
            pltpu.SemaphoreType.DMA((9,)),
            pltpu.SemaphoreType.DMA((2,)),
        ]
        + plan.scratch(),
        compiler_params=pltpu.CompilerParams(collective_id=1, has_side_effects=True, vmem_limit_bytes=56 << 20),
        name="finish",
    )(*shaped, upper16, gate16, gated16, w_in, w_out, x, go, gain)
    return total.reshape(-1, total.shape[-1]), few.reshape(-1, few.shape[-1]), layer_out, input_grad


def cluster_offsets(lengths, total_len):
    count = lengths.shape[1]
    ahead = jnp.arange(count)[:, None] < jnp.arange(count)[None, :]
    start_points = jnp.sum(jnp.where(ahead[None], lengths[:, :, None], 0), axis=1, dtype=jnp.int32)
    end_points = start_points + lengths
    where_at = jnp.arange(total_len, dtype=jnp.int32)
    inside = (where_at[None, None, :] >= start_points[:, :, None]) & (
        where_at[None, None, :] < end_points[:, :, None]
    )
    first_spot = jnp.sum(jnp.where(inside, start_points[:, :, None], 0), axis=1, dtype=jnp.int32)
    return where_at[None, :] - first_spot


def dot32(left, right, contract):
    return lax.dot_general(left, right, (contract, ((), ())), preferred_element_type=jnp.float32)


def thirds(columns, times=1):
    wide = columns // times // 1024 * 384
    return list(zip((wide, wide, columns // times - 2 * wide) * times, ORDERS * times))


def shards(
    hidden_in,
    cluster_lengths,
    norm_gain,
    in_proj,
    conv_weight,
    conv_bias,
    x_proj,
    dt_proj,
    dt_bias,
    a_log,
    skip_gain,
    out_proj,
    out_grad,
):
    f32, bf16 = jnp.float32, jnp.bfloat16
    taps, share = conv_weight.shape
    rank_dim = dt_proj.shape[0]
    state_dim = a_log.shape[0]
    contexts_here, total_len, model_dim = hidden_in.shape
    rows = contexts_here * total_len
    columns = rank_dim + 2 * state_dim
    offsets = cluster_offsets(cluster_lengths, total_len).reshape(rows)
    offset = jnp.broadcast_to(offsets[:, None], (rows, 128))
    grad_rows = out_grad.reshape(rows, model_dim)
    gain_part = jnp.pad(norm_gain, (0, share - norm_gain.shape[0]))
    vectors = [v[None] for v in (gain_part,)] + [conv_weight] + [v[None] for v in (conv_bias, dt_bias, skip_gain)]
    spare = columns - rank_dim - state_dim - taps - 4
    vectors = jnp.concatenate(vectors + [jnp.zeros((spare, share), bf16)], axis=0)
    normed16, packed, w_out, w_in, d_gated, both = gather_weights(
        hidden_in.reshape(rows, model_dim), grad_rows, (dt_proj, a_log, vectors, x_proj), out_proj, in_proj
    )
    inner_dim = packed.shape[1]
    decay_rate = -jnp.exp(packed[rank_dim : rank_dim + state_dim].astype(f32))
    rate2 = decay_rate * LOG2E
    params = packed[GAIN_ROW + 1 : GAIN_ROW + 9].astype(f32)
    w_dt, xp = packed[:rank_dim], packed[columns:]
    parts = lax.axis_size("fsdp")
    gain_full = packed[GAIN_ROW].reshape(parts, share)[:, : model_dim // parts].reshape(model_dim).astype(f32)
    *saved, gated16, gate16, proj, b_wide, c_wide, boundary, skip_sums = scan_forward(
        both, d_gated, offset, params, xp, w_dt, rate2, CHUNK, WIDTH
    )
    g_w_out = dot32(gated16, grad_rows, ((0,), (0,))).astype(bf16)
    g_w_gate = dot32(normed16, gate16, ((0,), (0,))).astype(bf16)
    (upper16, rate_sum, g_w_dt, g_w_x, sums), (t_out, t_gate) = scan_backward(
        saved, both, offset, proj, b_wide, c_wide, boundary, params, xp, w_dt, rate2, CHUNK, WIDTH,
        [g_w_out, g_w_gate], [thirds(model_dim), thirds(inner_dim)],
    )
    g_w_upper = dot32(normed16, upper16, ((0,), (0,))).astype(bf16)
    row_sums = jnp.concatenate([sums, skip_sums]).reshape(7, 8, inner_dim).sum(axis=1)
    small = jnp.concatenate([g_w_x, g_w_dt, rate_sum * decay_rate, row_sums], axis=0)
    gain_row = small.shape[0]
    spare = -(gain_row + 1) % (16 * lax.axis_size("dp")) + 1
    small = jnp.pad(small, ((0, spare), (0, 0))).astype(bf16)
    small = small.reshape(-1, parts, inner_dim // parts).transpose(1, 0, 2).reshape(-1, inner_dim // parts)
    t_upper, t_small, layer_out, input_grad = finish(
        g_w_upper, small, upper16, gate16, gated16, w_in, w_out, hidden_in.reshape(rows, model_dim), grad_rows,
        gain_full[None], [thirds(inner_dim, 2), [(inner_dim // parts, ORDERS[2])]], gain_row,
    )
    t_small = t_small.astype(f32)
    t_in = jnp.concatenate([t_upper, t_gate], axis=1).astype(f32)
    t_out = t_out.astype(f32)
    at = 0
    picked = []
    for size in (columns, rank_dim, state_dim, taps, 1, 1, 1, 1):
        picked.append(t_small[at : at + size])
        at += size
    t_x, t_dt, t_alog, t_conv, t_b_conv, t_b_dt, t_skip, t_gain = picked
    return (
        layer_out.reshape(hidden_in.shape),
        input_grad.reshape(hidden_in.shape),
        t_gain[0, : model_dim // parts],
        t_in,
        t_conv,
        t_b_conv[0],
        t_x.T,
        t_dt,
        t_b_dt[0],
        t_alog,
        t_skip[0],
        t_out,
    )


def solution(mesh):
    placed = (
        P(("dp", "fsdp"), None, None),
        P(("dp", "fsdp"), None),
        P("fsdp"),
        P("fsdp", None),
        P(None, "fsdp"),
        P("fsdp"),
        P("fsdp", None),
        P(None, "fsdp"),
        P("fsdp"),
        P(None, "fsdp"),
        P("fsdp"),
        P("fsdp", None),
        P(("dp", "fsdp"), None, None),
    )
    return jax.shard_map(
        shards,
        mesh=mesh,
        in_specs=placed,
        out_specs=(
            P(("dp", "fsdp"), None, None),
            P(("dp", "fsdp"), None, None),
            P("fsdp"),
            P("fsdp", None),
            P(None, "fsdp"),
            P("fsdp"),
            P("fsdp", None),
            P(None, "fsdp"),
            P("fsdp"),
            P(None, "fsdp"),
            P("fsdp"),
            P("fsdp", None),
        ),
        check_vma=False,
    )
```

```python
import functools
import math

import jax
import jax.numpy as jnp
from jax import lax
from jax.experimental import pallas as pl
from jax.experimental.pallas import tpu as pltpu
from jax.sharding import PartitionSpec as P

CHUNK = 64
WIDTH = 4
norm_eps = 1e-05
BIG = 1e30
LN2 = math.log(2.0)
LOG2E = 1.0 / LN2

def bits_of(size):
    return size.bit_length() - 1


ORDERS = ((0, 1, 2, 3), (1, 2, 0, 3), (2, 0, 1, 3))


class Reduction:
    def __init__(self, outer, inner, shapes, parts):
        self.outer_bits, self.inner_bits = bits_of(outer), bits_of(inner)
        self.blocks, self.inner = outer * inner, inner
        self.shapes = [(self.blocks, s[0] // self.blocks, s[1]) for s in shapes]
        self.stages = self.outer_bits + self.inner_bits
        self.steps = self.stages + self.inner_bits
        self.pieces = []
        for i, s in enumerate(shapes):
            at = 0
            for columns, order in parts[i]:
                order = [b for b in order if b < self.inner_bits] + list(range(len(order), self.inner_bits))
                self.pieces.append((i, pl.ds(at, columns), order))
                at += columns
            assert at == s[1]

    def axis_bit(self, piece, stage):
        if stage < self.outer_bits:
            return "fsdp", self.outer_bits - 1 - stage
        return "dp", self.pieces[piece][2][stage - self.outer_bits]

    def mine(self, piece, stage):
        axis, bit = self.axis_bit(piece, stage)
        return (lax.axis_index(axis) // (1 << bit)) % 2

    def partner(self, axis, bit):
        here = lax.axis_index(axis)
        return {axis: here + (1 << bit) - (here // (1 << bit)) % 2 * (2 << bit)}

    def barrier(self):
        sem = pltpu.get_barrier_semaphore()
        for axis, bits in (("fsdp", self.outer_bits), ("dp", self.inner_bits)):
            for bit in range(bits):
                pl.semaphore_signal(sem, inc=1, device_id=self.partner(axis, bit), device_id_type=pl.DeviceIdType.MESH)
        pl.semaphore_wait(sem, self.stages)

    def low(self, piece, stage):
        low = 0
        for s in range(1, stage):
            low = low + self.mine(piece, s) * (self.blocks >> (s + 1))
        return low

    def place(self, piece, stages):
        at = 0
        for j in range(stages):
            at = at + self.mine(piece, self.outer_bits + j) * (1 << (self.inner_bits - 1 - j))
        return at

    def bind(self, given, out, scratch):
        n = len(self.shapes)
        self.given, self.out = given, out
        self.work, self.inbox, self.result = scratch[:n], scratch[n : 2 * n], scratch[2 * n : 3 * n]
        self.send, self.recv, self.near = scratch[3 * n :]

    def scratch(self):
        b16, k = jnp.bfloat16, len(self.pieces)
        return (
            [pltpu.VMEM((b // 2, r, c), b16) for b, r, c in self.shapes]
            + [pltpu.VMEM((b, r, c), b16) for b, r, c in self.shapes]
            + [pltpu.VMEM((self.inner, r, c), b16) for b, r, c in self.shapes]
            + [pltpu.SemaphoreType.DMA((k, self.steps)), pltpu.SemaphoreType.DMA((k, self.steps)), pltpu.SemaphoreType.DMA((k,))]
        )

    def copy(self, piece, step):
        i, columns, _ = self.pieces[piece]
        if step < self.stages:
            stage = step
            half = self.blocks >> (step + 1)
            other = (1 - self.mine(piece, step)) * half
            if step == 0:
                source = self.given[i].at[pl.ds(other, half), :, columns]
            else:
                source = self.work[i].at[pl.ds(self.low(piece, step) + other, half), :, columns]
            target = self.inbox[i].at[pl.ds(self.blocks - 2 * half, half), :, columns]
        else:
            stage = self.steps - 1 - step + self.outer_bits
            j = stage - self.outer_bits
            many = 1 << (self.inner_bits - 1 - j)
            source = target = self.result[i].at[pl.ds(self.place(piece, j + 1), many), :, columns]
        return pltpu.make_async_remote_copy(
            src_ref=source,
            dst_ref=target,
            send_sem=self.send.at[piece, step],
            recv_sem=self.recv.at[piece, step],
            device_id=self.partner(*self.axis_bit(piece, stage)),
            device_id_type=pl.DeviceIdType.MESH,
        )

    def own(self, piece):
        i, columns, _ = self.pieces[piece]
        half = self.blocks // 2
        source = self.given[i].at[pl.ds(self.mine(piece, 0) * half, half), :, columns]
        return pltpu.make_async_copy(source, self.work[i].at[:, :, columns], self.near.at[piece])

    def leave(self, piece):
        i, columns, _ = self.pieces[piece]
        return pltpu.make_async_copy(self.result[i].at[:, :, columns], self.out[i].at[:, :, columns], self.near.at[piece])

    def add(self, piece, stage):
        i, columns, _ = self.pieces[piece]
        work, inbox, result = self.work[i], self.inbox[i], self.result[i]
        half = self.blocks >> (stage + 1)
        arrived = self.blocks - 2 * half
        base = 0 if stage == 0 else self.low(piece, stage) + self.mine(piece, stage) * half

        @pl.loop(0, half)
        def _(k):
            new = work[base + k, :, columns].astype(jnp.float32) + inbox[arrived + k, :, columns].astype(jnp.float32)
            if stage == self.stages - 1:
                result[self.place(piece, self.inner_bits), :, columns] = new.astype(jnp.bfloat16)
            else:
                work[base + k, :, columns] = new.astype(jnp.bfloat16)

    def start(self, pieces):
        for p in pieces:
            self.copy(p, 0).start()
        for p in pieces:
            self.own(p).start()

    def advance(self, pieces, step):
        for p in pieces:
            if step == 0:
                self.own(p).wait()
            self.copy(p, step).wait()
            if step < self.stages:
                self.add(p, step)
            if step + 1 < self.steps:
                self.copy(p, step + 1).start()
            else:
                self.leave(p).start()

    def gone(self, pieces):
        for p in pieces:
            self.leave(p).wait()

    def times(self, count):
        heavy = (18.0, 10.0, 6.5, 14.0)
        there = [heavy[min(j, 3)] for j in range(self.inner_bits)]
        loads = [11.0] * self.outer_bits + there + there[::-1]
        total, at, out = sum(loads), 0.0, []
        for load in loads[:-1]:
            at += load
            out.append(max(1, min(count - 1, round(at / total * count))))
        return out


def reduction_of(arrays, parts):
    plan = Reduction(lax.axis_size("fsdp"), lax.axis_size("dp"), [a.shape for a in arrays], parts)
    shaped = [a.reshape(s) for a, s in zip(arrays, plan.shapes)]
    out = [jax.ShapeDtypeStruct((plan.inner,) + s[1:], jnp.bfloat16) for s in plan.shapes]
    return plan, shaped, out


class Exchange:
    def __init__(self, size):
        self.size = size

    def owner(self, turn):
        return (lax.axis_index("fsdp") + self.size - turn) % self.size

    def peer(self, turn):
        return {"fsdp": (lax.axis_index("fsdp") + turn) % self.size}

    def barrier(self):
        sem = pltpu.get_barrier_semaphore()
        for turn in range(1, self.size):
            pl.semaphore_signal(sem, inc=1, device_id=self.peer(turn), device_id_type=pl.DeviceIdType.MESH)
        pl.semaphore_wait(sem, self.size - 1)

    def copy(self, source, target, sems, which, turn):
        if turn == 0:
            return pltpu.make_async_copy(source, target, sems[1].at[which, 0])
        return pltpu.make_async_remote_copy(
            src_ref=source,
            dst_ref=target,
            send_sem=sems[0].at[which, turn],
            recv_sem=sems[1].at[which, turn],
            device_id=self.peer(turn),
            device_id_type=pl.DeviceIdType.MESH,
        )


def gather_kernel(
    x_ref, go_ref, dt_ref, rate_ref, taps_ref, vec_ref, xp_ref, wout_ref, win_ref,
    normed_ref, dtw_ref, xpw_ref, decay_ref, par_ref, gain_ref, wout_out, win_out, dg_out, both_out,
    pack, wout, win, dg, both, packed, send, recv, leave, tiles, *, plan
):
    f32, bf16 = jnp.float32, jnp.bfloat16
    rows, model = x_ref.shape
    deep, wide, share = model // plan.size, both.shape[1], packed.shape[1]
    me = lax.axis_index("fsdp")
    sems = (send, recv)

    def copies(which, turn):
        source = (packed, wout_ref, win_ref)[which]
        if which == 0:
            target = pack.at[:, pl.ds(pl.multiple_of(me * share, 128), share)]
        else:
            target = (wout, win)[which - 1].at[me]
        return plan.copy(source, target, sems, which, turn)

    lines = share // 128
    vectors = vec_ref[...].astype(f32)
    line = [
        jnp.concatenate([vectors[k : k + 1] for k in range(v * lines, (v + 1) * lines)], axis=1) for v in range(4)
    ]
    few = [line[0], taps_ref[...].astype(f32)] + line[1:]
    depth, states, taps = dt_ref.shape[0], rate_ref.shape[0], taps_ref.shape[0]
    few.append(jnp.zeros((16 - 4 - taps, share), f32))
    packed[0:depth, :] = dt_ref[...]
    packed[depth : depth + states, :] = rate_ref[...]
    packed[depth + states : depth + states + 16, :] = jnp.concatenate(few, axis=0).astype(bf16)
    packed[depth + states + 16 :, :] = xp_ref[...]
    plan.barrier()
    for which in range(3):
        for turn in range(1, plan.size):
            copies(which, turn).start()
    for which in (1, 0, 2):
        copies(which, 0).start()

    def times_out(turn):
        at = plan.owner(turn)

        @pl.loop(0, share // 256)
        def _(k):
            here = pl.ds(pl.multiple_of(at * share + k * 256, 128), 256)
            dg[:, here] = lax.dot_general(
                go_ref[...], wout[at, pl.ds(pl.multiple_of(k * 256, 256), 256), :],
                (((1,), (1,)), ((), ())), preferred_element_type=f32,
            )
        pltpu.make_async_copy(wout.at[at], wout_out.at[at], leave.at[0, turn]).start()
        part = pl.ds(pl.multiple_of(at * share, 128), share)
        pltpu.make_async_copy(dg.at[:, part], dg_out.at[:, part], leave.at[2, turn]).start()

    def times_in(turn):
        at = plan.owner(turn)
        left = pl.ds(pl.multiple_of(at * deep, 128), deep)

        @pl.loop(0, wide // 256)
        def _(k):
            here = pl.ds(pl.multiple_of(k * 256, 256), 256)
            new = jnp.dot(normed_ref[:, left], win[at, :, here], preferred_element_type=f32)
            both[:, here] = new if turn == 0 else both[:, here] + new
            if turn == plan.size - 1:
                pltpu.make_async_copy(both.at[:, here], both_out.at[:, here], tiles.at[k]).start()
        pltpu.make_async_copy(win.at[at], win_out.at[at], leave.at[1, turn]).start()

    copies(1, 0).wait()
    times_out(0)
    for turn in range(plan.size):
        copies(0, turn).wait()
    dtw_ref[...] = pack[0:depth, :]
    xpw_ref[...] = pack[depth + states + 16 :, :]
    decay_ref[...] = -jnp.exp(pack[depth : depth + states, :].astype(f32)) * LOG2E
    few = pack[depth + states : depth + states + 16, :].astype(f32)
    par_ref[...] = few[1:9]
    gain = jnp.concatenate([few[:1, b * share : b * share + deep] for b in range(plan.size)], axis=1)
    gain_ref[...] = jnp.broadcast_to(gain, gain_ref.shape)

    @pl.loop(0, rows // 64)
    def _(k):
        here = pl.ds(pl.multiple_of(k * 64, 64), 64)
        x = x_ref[here, :].astype(f32)
        mean_sq = jnp.mean(x * x, axis=-1, keepdims=True)
        normed_ref[here, :] = (x * lax.rsqrt(mean_sq + norm_eps) * gain).astype(bf16)

    copies(2, 0).wait()
    times_in(0)
    for turn in range(1, plan.size):
        copies(1, turn).wait()
        times_out(turn)
    for turn in range(1, plan.size):
        copies(2, turn).wait()
        times_in(turn)
    for turn in range(plan.size):
        at = plan.owner(turn)
        part = pl.ds(pl.multiple_of(at * share, 128), share)
        pltpu.make_async_copy(wout.at[at], wout_out.at[at], leave.at[0, turn]).wait()
        pltpu.make_async_copy(win.at[at], win_out.at[at], leave.at[1, turn]).wait()
        pltpu.make_async_copy(dg.at[:, part], dg_out.at[:, part], leave.at[2, turn]).wait()

    @pl.loop(0, wide // 256)
    def _(k):
        here = pl.ds(pl.multiple_of(k * 256, 256), 256)
        pltpu.make_async_copy(both.at[:, here], both_out.at[:, here], tiles.at[k]).wait()


def gather_weights(x, grad_rows, small, w_out, w_in):
    f32, bf16 = jnp.float32, jnp.bfloat16
    plan = Exchange(lax.axis_size("fsdp"))
    n, (rows, model), wide = plan.size, x.shape, w_in.shape[1]
    (rank, share), states, cols = small[0].shape, small[1].shape[0], small[4].shape[0]
    inner = n * share
    anywhere = pl.BlockSpec(memory_space=pl.ANY)
    near = pl.BlockSpec(memory_space=pltpu.VMEM)
    shapes = [
        ((rank + states + 16 + cols, inner), bf16), ((n,) + w_out.shape, bf16), ((n,) + w_in.shape, bf16), ((rows, inner), f32), ((rows, wide), f32),
    ]
    outs = [
        (x.shape, bf16), ((rank, inner), bf16), ((cols, inner), bf16), ((states, inner), f32), ((8, inner), f32), ((8, model), f32),
    ]
    *made, out_all, in_all, d_gated, both = pl.pallas_call(
        functools.partial(gather_kernel, plan=plan),
        out_shape=[jax.ShapeDtypeStruct(*s) for s in outs + shapes[1:]],
        in_specs=[near] * 7 + [anywhere] * 2,
        out_specs=[near] * 6 + [anywhere] * 4,
        scratch_shapes=[pltpu.VMEM(*s) for s in shapes]
        + [
            pltpu.VMEM((shapes[0][0][0], share), bf16),
            pltpu.SemaphoreType.DMA((3, n)),
            pltpu.SemaphoreType.DMA((3, n)),
            pltpu.SemaphoreType.DMA((3, n)),
            pltpu.SemaphoreType.DMA((wide // 256,)),
        ],
        compiler_params=pltpu.CompilerParams(collective_id=2, has_side_effects=True, vmem_limit_bytes=56 << 20),
        name="gather_weights",
    )(x, grad_rows, *small, w_out, w_in)
    return made, out_all.reshape(-1, w_out.shape[1]), in_all.reshape(-1, wide), d_gated, both


TAPS, SHIFT, DT_BIAS, SKIP = 0, 4, 5, 6


def rows_of(ref, tile, row, width):
    return [ref[tile + j, pl.ds(row, 8, stride=0), :] for j in range(width)]


def by_eights(ref, tile):
    total = ref[tile, pl.ds(0, 8, stride=8), :]
    for s in range(1, 8):
        total = total + ref[tile, pl.ds(s, 8, stride=8), :]
    return total


def folded(x):
    total = x[:8]
    for s in range(8, x.shape[0], 8):
        total = total + x[s : s + 8]
    return total


def spread(proj, first, wide, states):
    for t in range(proj.shape[1]):
        wide[pl.ds(t * states, states), :] = jnp.broadcast_to(proj[first : first + states, t : t + 1], (states, 128))


def forward_kernel(
    upper_ref, z_ref, dg_ref, off_ref, par_ref, xp_ref, dtw_ref, a_ref,
    u_ref, ds_ref, dt_ref, sg_ref, dy_ref, gated_ref, gate_ref, proj_ref, wide_b, wide_c, bound_ref, skip_ref,
    hs, ext, u16, dtm, dtu, ys, ybuf, *, width
):
    f32, bf16 = jnp.float32, jnp.bfloat16
    rows, inner = upper_ref.shape
    states, rank = a_ref.shape[0], dtw_ref.shape[0]
    tiles = inner // 128

    @pl.when(pl.program_id(0) == 0)
    def _():
        hs[...] = jnp.zeros_like(hs)
        skip_ref[...] = jnp.zeros_like(skip_ref)
        ext[pl.ds(0, 8), :] = jnp.zeros((8, inner), f32)

    bound_ref[0] = hs[...]

    @pl.loop(0, tiles, unroll=True)
    def _(k):
        lanes = pl.ds(pl.multiple_of(k * 128, 128), 128)
        now = upper_ref[:, lanes]
        ext[pl.ds(8, rows), lanes] = now
        conv = par_ref[SHIFT : SHIFT + 1, lanes] + par_ref[TAPS + 3 : TAPS + 4, lanes] * now
        for lag in range(1, 4):
            before = ext[pl.ds(8 - lag, rows), lanes]
            conv = conv + par_ref[TAPS + 3 - lag : TAPS + 4 - lag, lanes] * jnp.where(off_ref[...] >= lag, before, 0.0)
        sig = jax.nn.sigmoid(conv)
        act = conv * sig
        u_ref[:, lanes] = act
        u16[:, lanes] = act.astype(bf16)
        ds_ref[:, lanes] = sig * (1.0 + conv * (1.0 - sig))
        ext[pl.ds(0, 8), lanes] = now[rows - 8 :]

    proj = lax.dot_general(xp_ref[...], u16[...], (((1,), (1,)), ((), ())), preferred_element_type=f32)
    proj_ref[0] = proj
    spread(proj, rank, wide_b, states)
    spread(proj, rank + states, wide_c, states)
    rank16 = proj[:rank].astype(bf16)

    @pl.loop(0, tiles // 2, unroll=True)
    def _(k):
        pair = pl.ds(pl.multiple_of(k * 256, 256), 256)
        pre = lax.dot_general(rank16, dtw_ref[:, pair], (((0,), (0,)), ((), ())), preferred_element_type=f32)
        pre = pre + par_ref[DT_BIAS : DT_BIAS + 1, pair]
        small = jnp.exp(-jnp.abs(pre))
        delta = jnp.maximum(pre, 0.0) + jnp.log1p(small)
        dt_ref[:, pair] = delta
        sg_ref[:, pair] = jnp.where(pre >= 0, 1.0, small) / (1.0 + small)
        grown = delta * u_ref[:, pair]
        for j in range(2):
            part = slice(128 * j, 128 * j + 128)
            dtm[2 * k + j] = jnp.where(off_ref[...] > 0, delta[:, part], BIG)
            dtu[2 * k + j] = grown[:, part]

    @pl.loop(0, tiles // width)
    def _(cb):
        tile = cb * width
        base = pl.multiple_of(cb * 128 * width, 128 * width)
        rate = [[a_ref[pl.ds(8 * s, 8), pl.ds(base + 128 * j, 128)] for s in range(2)] for j in range(width)]

        def body(g, h):
            h = [list(p) for p in zip(h[:width], h[width:])]
            r0 = pl.multiple_of(g * 8, 8)
            for t in range(8):
                d = rows_of(dtm, tile, r0 + t, width)
                x = rows_of(dtu, tile, r0 + t, width)
                bt = [wide_b[pl.ds((r0 + t) * 16 + 8 * s, 8), :] for s in range(2)]
                ct = [wide_c[pl.ds((r0 + t) * 16 + 8 * s, 8), :] for s in range(2)]
                for j in range(width):
                    for s in range(2):
                        h[j][s] = jnp.exp2(d[j] * rate[j][s]) * h[j][s] + x[j] * bt[s]
                    ybuf[j, pl.ds(t * 8, 8), :] = ct[0] * h[j][0] + ct[1] * h[j][1]
            for j in range(width):
                ys[tile + j, pl.ds(r0, 8), :] = by_eights(ybuf, j)
            return tuple(p[0] for p in h) + tuple(p[1] for p in h)

        h = tuple(hs[pl.ds(8 * s, 8), pl.ds(base + 128 * j, 128)] for s in range(2) for j in range(width))
        h = lax.fori_loop(0, rows // 8, body, h, unroll=4)
        for s in range(2):
            for j in range(width):
                hs[pl.ds(8 * s, 8), pl.ds(base + 128 * j, 128)] = h[s * width + j]

    @pl.loop(0, tiles, unroll=True)
    def _(k):
        lanes = pl.ds(pl.multiple_of(k * 128, 128), 128)
        act, z, dg = u_ref[:, lanes], z_ref[:, lanes], dg_ref[:, lanes]
        full = ys[k] + par_ref[SKIP : SKIP + 1, lanes] * act
        sig = jax.nn.sigmoid(z)
        silu = z * sig
        gated_ref[:, lanes] = (full * silu).astype(bf16)
        dy = dg * silu
        dy_ref[:, lanes] = dy
        gate_ref[:, lanes] = (dg * full * sig * (1.0 + z * (1.0 - sig))).astype(bf16)
        skip_ref[:, lanes] = skip_ref[:, lanes] + folded(dy * act)


def scan_forward(both, d_gated, offset, params, xp, dtw, rate, chunk, width):
    T, DI = d_gated.shape
    n, states, cols = T // chunk, rate.shape[0], xp.shape[0]
    f32, bf16 = jnp.float32, jnp.bfloat16
    row = pl.BlockSpec((chunk, DI), lambda i: (i, 0))
    whole = lambda a: pl.BlockSpec(a.shape, lambda i: (0, 0))
    flat = lambda d: jax.ShapeDtypeStruct((T, DI), d)
    tile = lambda d: pltpu.VMEM((DI // 128, chunk, 128), d)
    return pl.pallas_call(
        functools.partial(forward_kernel, width=width),
        grid=(n,),
        in_specs=[row, pl.BlockSpec((chunk, DI), lambda i: (i, 1)), row, pl.BlockSpec((chunk, 128), lambda i: (i, 0))]
        + [whole(a) for a in (params, xp, dtw, rate)],
        out_specs=[row] * 7
        + [
            pl.BlockSpec((1, cols, chunk), lambda i: (i, 0, 0)),
            pl.BlockSpec((chunk * states, 128), lambda i: (i, 0)),
            pl.BlockSpec((chunk * states, 128), lambda i: (i, 0)),
            pl.BlockSpec((1, states, DI), lambda i: (i, 0, 0)),
            pl.BlockSpec((8, DI), lambda i: (0, 0)),
        ],
        out_shape=[flat(f32)] * 5
        + [flat(bf16)] * 2
        + [
            jax.ShapeDtypeStruct((n, cols, chunk), f32),
            jax.ShapeDtypeStruct((T * states, 128), f32),
            jax.ShapeDtypeStruct((T * states, 128), f32),
            jax.ShapeDtypeStruct((n, states, DI), f32),
            jax.ShapeDtypeStruct((8, DI), f32),
        ],
        scratch_shapes=[
            pltpu.VMEM((states, DI), f32),
            pltpu.VMEM((chunk + 8, DI), f32),
            pltpu.VMEM((chunk, DI), bf16),
            tile(f32),
            tile(f32),
            tile(f32),
            pltpu.VMEM((width, 64, 128), f32),
        ],
        compiler_params=pltpu.CompilerParams(dimension_semantics=("arbitrary",), vmem_limit_bytes=62 << 20),
        name="scan_forward",
    )(both, both, d_gated, offset, params, xp, dtw, rate)


def backward_kernel(
    u_ref, ds_ref, dt_ref, sg_ref, dy_ref, upper_ref, off_ref, proj_ref, wide_b, wide_c, bound_ref, par_ref, xp_ref, dtw_ref, a_ref, skip_ref,
    *rest, width, plan, total
):
    f32, bf16 = jnp.float32, jnp.bfloat16
    n = len(plan.shapes)
    given, rest = rest[:n], rest[n:]
    (du_ref, small_ref), out, rest = rest[:2], rest[2 : 2 + n], rest[2 + n :]
    ga_ref, gdt_ref, gx_ref, sum_ref, *rest = rest
    ws, dtm, dtu, dyb, hbuf, sbuf, qbuf, dd, di, u16, dt16, ext, off_ext, wide_db, wide_dc, cols_ref = rest[:16]
    plan.bind(given, out, rest[16:])
    rows, inner = u_ref.shape
    states, rank = a_ref.shape[0], dtw_ref.shape[0]
    tiles = inner // 128
    everything = range(len(plan.pieces))
    times = plan.times(total // rows * (tiles // width))

    @pl.when(pl.program_id(0) == 0)
    def _():
        for ref in (ws, ga_ref, gdt_ref, gx_ref, sum_ref):
            ref[...] = jnp.zeros_like(ref)
        ext[pl.ds(rows, 8), :] = jnp.zeros((8, inner), f32)
        off_ext[pl.ds(rows, 8), :] = jnp.full((8, 128), -1, jnp.int32)
        plan.barrier()
        plan.start(everything)

    proj = proj_ref[0]
    wide_db[...] = jnp.zeros_like(wide_db)
    wide_dc[...] = jnp.zeros_like(wide_dc)

    @pl.loop(0, tiles // width)
    def _(cb):
        tile = cb * width
        base = pl.multiple_of(cb * 128 * width, 128 * width)
        for at in sorted(set(times)):
            @pl.when(pl.program_id(0) * (tiles // width) + cb == at)
            def _():
                for step in range(plan.steps - 1):
                    if times[step] == at:
                        plan.advance(everything, step)

        for j in range(width):
            lanes = pl.ds(base + 128 * j, 128)
            d, act = dt_ref[:, lanes], u_ref[:, lanes]
            dtm[j] = jnp.where(off_ref[...] > 0, d, BIG)
            dtu[j] = d * act
            dyb[j] = dy_ref[:, lanes]
            u16[:, lanes] = act.astype(bf16)
        rate = [[a_ref[pl.ds(8 * s, 8), pl.ds(base + 128 * j, 128)] for s in range(2)] for j in range(width)]

        def again(g, h):
            h = [list(p) for p in zip(h[:width], h[width:])]
            r0 = pl.multiple_of(g * 8, 8)
            for t in range(8):
                d = rows_of(dtm, 0, r0 + t, width)
                x = rows_of(dtu, 0, r0 + t, width)
                bt = [wide_b[pl.ds((r0 + t) * 16 + 8 * s, 8), :] for s in range(2)]
                for j in range(width):
                    for s in range(2):
                        hbuf[pl.ds((r0 + t) * 16 + 8 * s, 8), pl.ds(128 * j, 128)] = h[j][s]
                        h[j][s] = jnp.exp2(d[j] * rate[j][s]) * h[j][s] + x[j] * bt[s]
            return tuple(p[0] for p in h) + tuple(p[1] for p in h)

        h = tuple(bound_ref[0, pl.ds(8 * s, 8), pl.ds(base + 128 * j, 128)] for s in range(2) for j in range(width))
        h = lax.fori_loop(0, rows // 8, again, h)
        for s in range(2):
            for j in range(width):
                hbuf[pl.ds(rows * 16 + 8 * s, 8), pl.ds(128 * j, 128)] = h[s * width + j]

        def body(k, carry):
            r0 = pl.multiple_of((rows // 8 - 1 - k) * 8, 8)
            w = [[carry[s * width + j] for s in range(2)] for j in range(width)]
            ga = [[carry[2 * width + s * width + j] for s in range(2)] for j in range(width)]
            newer = [[hbuf[pl.ds((r0 + 8) * 16 + 8 * s, 8), pl.ds(128 * j, 128)] for s in range(2)] for j in range(width)]
            for t in range(7, -1, -1):
                d = rows_of(dtm, 0, r0 + t, width)
                x = rows_of(dtu, 0, r0 + t, width)
                v = rows_of(dyb, 0, r0 + t, width)
                bt = [wide_b[pl.ds((r0 + t) * 16 + 8 * s, 8), :] for s in range(2)]
                ct = [wide_c[pl.ds((r0 + t) * 16 + 8 * s, 8), :] for s in range(2)]
                db = [None, None]
                dc = [None, None]
                for j in range(width):
                    qs, ss = None, None
                    for s in range(2):
                        later = newer[j][s]
                        prior = hbuf[pl.ds((r0 + t) * 16 + 8 * s, 8), pl.ds(128 * j, 128)]
                        newer[j][s] = prior
                        g = ct[s] * v[j] + w[j][s]
                        w[j][s] = jnp.exp2(d[j] * rate[j][s]) * g
                        q = w[j][s] * prior
                        ga[j][s] = ga[j][s] + q * d[j]
                        qa = q * rate[j][s]
                        sb = g * bt[s]
                        qs = qa if qs is None else qs + qa
                        ss = sb if ss is None else ss + sb
                        gx = g * x[j]
                        vh = v[j] * later
                        db[s] = gx if db[s] is None else db[s] + gx
                        dc[s] = vh if dc[s] is None else dc[s] + vh
                    qbuf[j, pl.ds(t * 8, 8), :] = qs
                    sbuf[j, pl.ds(t * 8, 8), :] = ss
                for s in range(2):
                    here = pl.ds((r0 + t) * 16 + 8 * s, 8)
                    wide_db[here, :] = wide_db[here, :] + db[s]
                    wide_dc[here, :] = wide_dc[here, :] + dc[s]
            for j in range(width):
                lanes = pl.ds(base + 128 * j, 128)
                here = pl.ds(r0, 8)
                s8 = by_eights(sbuf, j)
                dd[here, lanes] = LN2 * by_eights(qbuf, j) + u_ref[here, lanes] * s8
                di[here, lanes] = dt_ref[here, lanes] * s8
            return tuple(w[j][s] for s in range(2) for j in range(width)) + tuple(
                ga[j][s] for s in range(2) for j in range(width)
            )

        held = [(r, pl.ds(8 * s, 8), pl.ds(base + 128 * j, 128)) for r in (ws, ga_ref) for s in range(2) for j in range(width)]
        end = lax.fori_loop(0, rows // 8, body, tuple(r[a, b] for r, a, b in held))
        for (r, a, b), value in zip(held, end):
            r[a, b] = value

    for i, ref in enumerate((wide_db, wide_dc)):
        for k in range(states):
            cols_ref[pl.ds(i * rows, rows), pl.ds(128 * k, 128)] = ref[pl.ds(k, rows, stride=states), :].astype(bf16)
    owner = lax.broadcasted_iota(jnp.int32, (states, states * 128), 1) // 128
    picks = jnp.where(owner == lax.broadcasted_iota(jnp.int32, (states, states * 128), 0), 1.0, 0.0).astype(bf16)
    d_bc = lax.dot_general(picks, cols_ref[...], (((1,), (1,)), ((), ())), preferred_element_type=f32)

    @pl.loop(0, tiles, unroll=True)
    def _(k):
        lanes = pl.ds(pl.multiple_of(k * 128, 128), 128)
        low = (dd[:, lanes] * sg_ref[:, lanes]).astype(bf16)
        dt16[:, lanes] = low
        sum_ref[pl.ds(40, 8), lanes] = sum_ref[pl.ds(40, 8), lanes] + folded(low.astype(f32))

    rank16 = proj[:rank].astype(bf16)
    d_rank = lax.dot_general(dtw_ref[...], dt16[...], (((1,), (1,)), ((), ())), preferred_element_type=f32)
    proj16 = jnp.concatenate([d_rank, d_bc[:, :rows], d_bc[:, rows:]], axis=0).astype(bf16)
    off_ext[pl.ds(0, rows), :] = off_ref[...]

    @pl.loop(0, tiles // 2, unroll=True)
    def _(k):
        pair = pl.ds(pl.multiple_of(k * 256, 256), 256)
        dot = lambda a, b, c: lax.dot_general(a, b, ((c, (0,)), ((), ())), preferred_element_type=f32)
        gdt_ref[:, pair] = gdt_ref[:, pair] + dot(rank16, dt16[:, pair], (1,))
        gx_ref[:, pair] = gx_ref[:, pair] + dot(proj16, u16[:, pair], (1,))
        inner_grad = dot(proj16, xp_ref[:, pair], (0,)) + di[:, pair] + dy_ref[:, pair] * par_ref[SKIP : SKIP + 1, pair]
        ext[pl.ds(0, rows), pair] = inner_grad * ds_ref[:, pair]
        for j in range(2):
            lanes = pl.ds(pl.multiple_of(k * 256 + 128 * j, 128), 128)
            now, above = ext[pl.ds(0, rows), lanes], upper_ref[:, lanes]
            grad = par_ref[TAPS + 3 : TAPS + 4, lanes] * now
            sums = [now, now * above]
            for lag in range(1, 4):
                after = jnp.where(off_ext[pl.ds(lag, rows), :] >= lag, ext[pl.ds(lag, rows), lanes], 0.0)
                grad = grad + par_ref[TAPS + 3 - lag : TAPS + 4 - lag, lanes] * after
                sums.append(after * above)
            du_ref[:, lanes] = grad.astype(bf16)
            for at, value in zip((32, 24, 16, 8, 0), sums):
                sum_ref[pl.ds(at, 8), lanes] = sum_ref[pl.ds(at, 8), lanes] + folded(value)
            ext[pl.ds(rows, 8), lanes] = now[:8]

    off_ext[pl.ds(rows, 8), :] = off_ref[pl.ds(0, 8), :]

    @pl.when(pl.program_id(0) == pl.num_programs(0) - 1)
    def _():
        share = small_ref.shape[1]
        deep = small_ref.shape[0] // (inner // share)
        sums = [jnp.sum(sum_ref[pl.ds(8 * k, 8), :], axis=0, keepdims=True) for k in range(6)]
        sums += [jnp.sum(skip_ref[...], axis=0, keepdims=True), jnp.zeros((9, inner), f32)]
        blocks = [gx_ref[...], gdt_ref[...], ga_ref[...] * a_ref[...] * LN2, jnp.concatenate(sums, axis=0)]
        for f in range(inner // share):
            at = f * deep
            for block in blocks:
                small_ref[at : at + block.shape[0], :] = block[:, f * share : (f + 1) * share].astype(bf16)
                at += block.shape[0]
            small_ref[at : (f + 1) * deep, :] = jnp.zeros(((f + 1) * deep - at, share), bf16)
        plan.advance(everything, plan.steps - 1)
        plan.gone(everything)


def scan_backward(saved, both, offset, proj, wide_b, wide_c, bound, params, xp, dtw, rate, skip, chunk, width, grads, parts):
    T, DI = saved[0].shape
    n, states, cols, rank = T // chunk, rate.shape[0], xp.shape[0], dtw.shape[0]
    f32, bf16 = jnp.float32, jnp.bfloat16
    row = pl.BlockSpec((chunk, DI), lambda i: (n - 1 - i, 0))
    whole = lambda a: pl.BlockSpec(a.shape, lambda i: (0, 0))
    anywhere = pl.BlockSpec(memory_space=pl.ANY)
    plan, shaped, summed = reduction_of(grads, parts)
    outer, inner = lax.axis_size("fsdp"), lax.axis_size("dp")
    deep = -(-(states + rank + cols + 16) // (16 * inner)) * 16 * inner
    small = jax.ShapeDtypeStruct((outer * deep, DI // outer), bf16)
    pieces = pltpu.VMEM((width, chunk, 128), f32)
    eights = pltpu.VMEM((width, 64, 128), f32)
    tall = pltpu.VMEM((chunk * states, 128), f32)
    out = pl.pallas_call(
        functools.partial(backward_kernel, width=width, plan=plan, total=T),
        grid=(n,),
        in_specs=[row] * 6
        + [
            pl.BlockSpec((chunk, 128), lambda i: (n - 1 - i, 0)),
            pl.BlockSpec((1, cols, chunk), lambda i: (n - 1 - i, 0, 0)),
            pl.BlockSpec((chunk * states, 128), lambda i: (n - 1 - i, 0)),
            pl.BlockSpec((chunk * states, 128), lambda i: (n - 1 - i, 0)),
            pl.BlockSpec((1, states, DI), lambda i: (n - 1 - i, 0, 0)),
        ]
        + [whole(a) for a in (params, xp, dtw, rate, skip)]
        + [anywhere] * len(grads),
        out_specs=[row, whole(small)] + [anywhere] * len(grads),
        out_shape=[jax.ShapeDtypeStruct((T, DI), bf16), small] + summed,
        scratch_shapes=[pltpu.VMEM((r, DI), f32) for r in (states, rank, cols, 48)]
        + [
            pltpu.VMEM((states, DI), f32),
            pieces,
            pieces,
            pieces,
            pltpu.VMEM((chunk * states + states, 128 * width), f32),
            eights,
            eights,
            pltpu.VMEM((chunk, DI), f32),
            pltpu.VMEM((chunk, DI), f32),
            pltpu.VMEM((chunk, DI), bf16),
            pltpu.VMEM((chunk, DI), bf16),
            pltpu.VMEM((chunk + 8, DI), f32),
            pltpu.VMEM((chunk + 8, 128), jnp.int32),
            tall,
            tall,
            pltpu.VMEM((2 * chunk, states * 128), bf16),
        ]
        + plan.scratch(),
        compiler_params=pltpu.CompilerParams(
            dimension_semantics=("arbitrary",), collective_id=0, has_side_effects=True, vmem_limit_bytes=56 << 20
        ),
        name="scan_backward",
    )(*saved, both, offset, proj, wide_b, wide_c, bound, params, xp, dtw, rate, skip, *shaped)
    return out[:2], [o.reshape(-1, o.shape[-1]) for o in out[2:]]


def finish_kernel(
    grads_ref, small_ref, upper_ref, gate_ref, gated_ref, in_ref, wout_ref, x_ref, go_ref, gain_ref,
    total_ref, few_ref, layer_ref, left_ref,
    upper, gate, gated, win, wout, x, go, dn, layer, mine, gain_sum, loads, away, *rest, plan, gain_row
):
    f32, bf16 = jnp.float32, jnp.bfloat16
    rows, model = x.shape
    inner = upper.shape[1]
    plan.bind([grads_ref, mine], [total_ref, few_ref], rest)
    main = [p for p in range(len(plan.pieces)) if plan.pieces[p][0] == 0]
    late = [p for p in range(len(plan.pieces)) if plan.pieces[p][0] == 1]

    copies = [
        pltpu.make_async_copy(a, b, loads.at[i])
        for i, (a, b) in enumerate(
            (
                (upper_ref, upper), (in_ref.at[:, pl.ds(0, inner)], win.at[0]), (gate_ref, gate),
                (in_ref.at[:, pl.ds(inner, inner)], win.at[1]), (x_ref, x), (go_ref, go), (small_ref, mine),
                (gated_ref, gated), (wout_ref, wout),
            )
        )
    ]

    def product(left, k):
        @pl.loop(0, model // 256)
        def _(j):
            here = pl.ds(pl.multiple_of(j * 256, 256), 256)
            new = lax.dot_general(left[...], win[k, here, :], (((1,), (1,)), ((), ())), preferred_element_type=f32)
            dn[:, here] = new if k == 0 else dn[:, here] + new

    plan.barrier()
    plan.start(main)
    for c in copies:
        c.start()
    copies[0].wait()
    copies[1].wait()
    product(upper, 0)
    plan.advance(main, 0)
    copies[2].wait()
    copies[3].wait()
    product(gate, 1)
    copies[4].wait()
    copies[5].wait()
    gain_sum[...] = jnp.zeros_like(gain_sum)

    @pl.loop(0, rows // 32)
    def _(k):
        here = pl.ds(pl.multiple_of(k * 32, 32), 32)
        value, grad, gain = x[here, :].astype(f32), dn[here, :], gain_ref[0:1, :]
        scale = lax.rsqrt(jnp.mean(value * value, axis=-1, keepdims=True) + norm_eps)
        through = grad * value
        gain_sum[...] = gain_sum[...] + folded(through * scale)
        pull = jnp.mean(through * gain, axis=-1, keepdims=True) * (scale * scale * scale)
        dn[here, :] = go[here, :].astype(f32) + scale * (grad * gain) - value * pull

    leaving = [pltpu.make_async_copy(dn, left_ref, away.at[0]), pltpu.make_async_copy(layer, layer_ref, away.at[1])]
    leaving[0].start()
    copies[6].wait()
    gain_grad = jnp.sum(gain_sum[...], axis=0, keepdims=True)
    outer = plan.blocks // plan.inner
    deep, r = model // outer, mine.shape[1]
    for f in range(outer):
        block = f * plan.inner + gain_row // r
        old = mine[block, :, 0:deep].astype(f32)
        new = jnp.broadcast_to(gain_grad[:, f * deep : (f + 1) * deep], (r, deep))
        chosen = lax.broadcasted_iota(jnp.int32, (r, deep), 0) == gain_row % r
        mine[block, :, 0:deep] = jnp.where(chosen, new, old).astype(bf16)
    plan.start(late)
    plan.advance(main, 1)
    plan.advance(late, 0)
    copies[7].wait()
    copies[8].wait()

    @pl.loop(0, model // 256)
    def _(j):
        here = pl.ds(pl.multiple_of(j * 256, 256), 256)
        new = x[:, here].astype(f32) + jnp.dot(gated[...], wout[:, here], preferred_element_type=f32)
        layer[:, here] = new.astype(bf16)

    leaving[1].start()
    for step in range(2, plan.steps):
        plan.advance(main, step)
        plan.advance(late, step - 1)
    plan.advance(late, plan.steps - 1)
    plan.gone(main + late)
    for c in leaving:
        c.wait()


def finish(grads, small, upper16, gate16, gated16, w_in, w_out, x, go, gain, parts, gain_row):
    f32, bf16 = jnp.float32, jnp.bfloat16
    (rows, model), inner = x.shape, upper16.shape[1]
    plan, shaped, summed = reduction_of([grads, small], parts)
    anywhere = pl.BlockSpec(memory_space=pl.ANY)
    flat = pltpu.VMEM((rows, inner), bf16)
    thin = pltpu.VMEM((rows, model), bf16)
    total, few, layer_out, input_grad = pl.pallas_call(
        functools.partial(finish_kernel, plan=plan, gain_row=gain_row),
        out_shape=summed + [jax.ShapeDtypeStruct((rows, model), bf16), jax.ShapeDtypeStruct((rows, model), f32)],
        in_specs=[anywhere] * 9 + [pl.BlockSpec(memory_space=pltpu.VMEM)],
        out_specs=[anywhere] * 4,
        scratch_shapes=[
            flat,
            flat,
            flat,
            pltpu.VMEM((2, model, inner), bf16),
            pltpu.VMEM((inner, model), bf16),
            thin,
            thin,
            pltpu.VMEM((rows, model), f32),
            thin,
            pltpu.VMEM(plan.shapes[1], bf16),
            pltpu.VMEM((8, model), f32),
            pltpu.SemaphoreType.DMA((9,)),
            pltpu.SemaphoreType.DMA((2,)),
        ]
        + plan.scratch(),
        compiler_params=pltpu.CompilerParams(collective_id=1, has_side_effects=True, vmem_limit_bytes=56 << 20),
        name="finish",
    )(*shaped, upper16, gate16, gated16, w_in, w_out, x, go, gain)
    return total.reshape(-1, total.shape[-1]), few.reshape(-1, few.shape[-1]), layer_out, input_grad


def write_kernel(
    upper_ref, gate_ref, out_ref, small_ref, layer_ref, left_ref,
    in_to, out_to, x_to, dt_to, rate_to, taps_to, shift_to, bias_to, skip_to, gain_to, layer_to, left_to,
):
    f32 = jnp.float32
    wide = upper_ref.shape[1]
    in_to[:, 0:wide] = upper_ref[...].astype(f32)
    in_to[:, wide:] = gate_ref[...].astype(f32)
    out_to[...] = out_ref[...].astype(f32)
    layer_to[...] = layer_ref[...]
    left_to[...] = left_ref[...]

    @pl.when(pl.program_id(0) == 0)
    def _():
        at = 0
        for ref in (x_to, dt_to, rate_to):
            ref[...] = small_ref[at : at + ref.shape[0], :].astype(f32)
            at += ref.shape[0]
        few = small_ref[at : at + 16, :].astype(f32)
        at = 0
        for ref in (taps_to, shift_to, bias_to, skip_to, gain_to):
            ref[...] = few[at : at + ref.shape[0], : ref.shape[1]]
            at += ref.shape[0]


def write_outputs(upper, gate, out, small, layer, left, sizes):
    f32, share, steps = jnp.float32, small.shape[1], 4
    few = [(r, share) for r in sizes[:-1]] + [(1, sizes[-1])]
    part = lambda a: pl.BlockSpec((a.shape[0] // steps, a.shape[1]), lambda i: (i, 0))
    whole = lambda a: pl.BlockSpec(a.shape, lambda i: (0, 0))
    big = [jax.ShapeDtypeStruct((upper.shape[0], upper.shape[1] + gate.shape[1]), f32), jax.ShapeDtypeStruct(out.shape, f32)]
    few = [jax.ShapeDtypeStruct(a, f32) for a in few]
    last = [jax.ShapeDtypeStruct(a.shape, a.dtype) for a in (layer, left)]
    return pl.pallas_call(
        write_kernel,
        grid=(steps,),
        in_specs=[part(upper), part(gate), part(out), whole(small), part(layer), part(left)],
        out_specs=[part(a) for a in big] + [whole(a) for a in few] + [part(a) for a in last],
        out_shape=big + few + last,
        compiler_params=pltpu.CompilerParams(dimension_semantics=("arbitrary",), vmem_limit_bytes=62 << 20),
        name="write_outputs",
    )(upper, gate, out, small, layer, left)


def cluster_offsets(lengths, total_len):
    count = lengths.shape[1]
    ahead = jnp.arange(count)[:, None] < jnp.arange(count)[None, :]
    start_points = jnp.sum(jnp.where(ahead[None], lengths[:, :, None], 0), axis=1, dtype=jnp.int32)
    end_points = start_points + lengths
    where_at = jnp.arange(total_len, dtype=jnp.int32)
    inside = (where_at[None, None, :] >= start_points[:, :, None]) & (
        where_at[None, None, :] < end_points[:, :, None]
    )
    first_spot = jnp.sum(jnp.where(inside, start_points[:, :, None], 0), axis=1, dtype=jnp.int32)
    return where_at[None, :] - first_spot


def dot32(left, right, contract):
    return lax.dot_general(left, right, (contract, ((), ())), preferred_element_type=jnp.float32)


def thirds(columns, times=1):
    wide = columns // times // 1024 * 384
    return list(zip((wide, wide, columns // times - 2 * wide) * times, ORDERS * times))


def shards(
    hidden_in,
    cluster_lengths,
    norm_gain,
    in_proj,
    conv_weight,
    conv_bias,
    x_proj,
    dt_proj,
    dt_bias,
    a_log,
    skip_gain,
    out_proj,
    out_grad,
):
    f32, bf16 = jnp.float32, jnp.bfloat16
    taps, share = conv_weight.shape
    rank_dim = dt_proj.shape[0]
    state_dim = a_log.shape[0]
    contexts_here, total_len, model_dim = hidden_in.shape
    rows = contexts_here * total_len
    columns = rank_dim + 2 * state_dim
    offsets = cluster_offsets(cluster_lengths, total_len).reshape(rows)
    offset = jnp.broadcast_to(offsets[:, None], (rows, 128))
    grad_rows = out_grad.reshape(rows, model_dim)
    gain_part = jnp.pad(norm_gain, (0, share - norm_gain.shape[0]))
    vectors = jnp.concatenate([gain_part, conv_bias, dt_bias, skip_gain]).reshape(-1, 128)
    x = hidden_in.reshape(rows, model_dim)
    (normed16, w_dt, xp, rate2, params, gain), w_out, w_in, d_gated, both = gather_weights(
        x, grad_rows, (dt_proj, a_log, conv_weight, vectors, x_proj.T), out_proj, in_proj
    )
    inner_dim = params.shape[1]
    parts = lax.axis_size("fsdp")
    *saved, gated16, gate16, proj, b_wide, c_wide, boundary, skip_sums = scan_forward(
        both, d_gated, offset, params, xp, w_dt, rate2, CHUNK, WIDTH
    )
    g_w_out = dot32(gated16, grad_rows, ((0,), (0,))).astype(bf16)
    g_w_gate = dot32(normed16, gate16, ((0,), (0,))).astype(bf16)
    (upper16, small), (t_out, t_gate) = scan_backward(
        saved, both, offset, proj, b_wide, c_wide, boundary, params, xp, w_dt, rate2, skip_sums, CHUNK, WIDTH,
        [g_w_out, g_w_gate], [thirds(model_dim), thirds(inner_dim)],
    )
    g_w_upper = dot32(normed16, upper16, ((0,), (0,))).astype(bf16)
    gain_row = columns + rank_dim + state_dim + taps + 3
    t_upper, t_small, layer_out, input_grad = finish(
        g_w_upper, small, upper16, gate16, gated16, w_in, w_out, x, grad_rows,
        gain, [thirds(inner_dim, 2), [(inner_dim // parts, ORDERS[2])]], gain_row,
    )
    t_in, t_out, t_x, t_dt, t_alog, t_conv, t_b_conv, t_b_dt, t_skip, t_gain, layer_out, input_grad = write_outputs(
        t_upper, t_gate, t_out, t_small, layer_out, input_grad,
        (columns, rank_dim, state_dim, taps, 1, 1, 1, model_dim // parts),
    )
    return (
        layer_out.reshape(hidden_in.shape),
        input_grad.reshape(hidden_in.shape),
        t_gain[0],
        t_in,
        t_conv,
        t_b_conv[0],
        t_x.T,
        t_dt,
        t_b_dt[0],
        t_alog,
        t_skip[0],
        t_out,
    )


def solution(mesh):
    placed = (
        P(("dp", "fsdp"), None, None),
        P(("dp", "fsdp"), None),
        P("fsdp"),
        P("fsdp", None),
        P(None, "fsdp"),
        P("fsdp"),
        P("fsdp", None),
        P(None, "fsdp"),
        P("fsdp"),
        P(None, "fsdp"),
        P("fsdp"),
        P("fsdp", None),
        P(("dp", "fsdp"), None, None),
    )
    return jax.shard_map(
        shards,
        mesh=mesh,
        in_specs=placed,
        out_specs=(
            P(("dp", "fsdp"), None, None),
            P(("dp", "fsdp"), None, None),
            P("fsdp"),
            P("fsdp", None),
            P(None, "fsdp"),
            P("fsdp"),
            P("fsdp", None),
            P(None, "fsdp"),
            P("fsdp"),
            P(None, "fsdp"),
            P("fsdp"),
            P("fsdp", None),
        ),
        check_vma=False,
    )
```

```python
import functools
import math

import jax
import jax.numpy as jnp
from jax import lax
from jax.experimental import pallas as pl
from jax.experimental.pallas import tpu as pltpu
from jax.sharding import PartitionSpec as P

CHUNK = 64
WIDTH = 4
norm_eps = 1e-05
BIG = 1e30
LN2 = math.log(2.0)
LOG2E = 1.0 / LN2

def bits_of(size):
    return size.bit_length() - 1


ORDERS = ((0, 1, 2, 3), (1, 2, 0, 3), (2, 0, 1, 3))


class Reduction:
    def __init__(self, outer, inner, shapes, parts):
        self.outer_bits, self.inner_bits = bits_of(outer), bits_of(inner)
        self.blocks, self.inner = outer * inner, inner
        self.shapes = [(self.blocks, s[0] // self.blocks, s[1]) for s in shapes]
        self.stages = self.outer_bits + self.inner_bits
        self.steps = self.stages + self.inner_bits
        self.pieces = []
        for i, s in enumerate(shapes):
            at = 0
            for columns, order in parts[i]:
                order = [b for b in order if b < self.inner_bits] + list(range(len(order), self.inner_bits))
                self.pieces.append((i, pl.ds(at, columns), order))
                at += columns
            assert at == s[1]

    def axis_bit(self, piece, stage):
        if stage < self.outer_bits:
            return "fsdp", self.outer_bits - 1 - stage
        return "dp", self.pieces[piece][2][stage - self.outer_bits]

    def mine(self, piece, stage):
        axis, bit = self.axis_bit(piece, stage)
        return (lax.axis_index(axis) // (1 << bit)) % 2

    def partner(self, axis, bit):
        here = lax.axis_index(axis)
        return {axis: here + (1 << bit) - (here // (1 << bit)) % 2 * (2 << bit)}

    def barrier(self):
        sem = pltpu.get_barrier_semaphore()
        for axis, bits in (("fsdp", self.outer_bits), ("dp", self.inner_bits)):
            for bit in range(bits):
                pl.semaphore_signal(sem, inc=1, device_id=self.partner(axis, bit), device_id_type=pl.DeviceIdType.MESH)
        pl.semaphore_wait(sem, self.stages)

    def low(self, piece, stage):
        low = 0
        for s in range(1, stage):
            low = low + self.mine(piece, s) * (self.blocks >> (s + 1))
        return low

    def place(self, piece, stages):
        at = 0
        for j in range(stages):
            at = at + self.mine(piece, self.outer_bits + j) * (1 << (self.inner_bits - 1 - j))
        return at

    def bind(self, given, out, scratch):
        n = len(self.shapes)
        self.given, self.out = given, out
        self.work, self.inbox, self.result = scratch[:n], scratch[n : 2 * n], scratch[2 * n : 3 * n]
        self.send, self.recv, self.near = scratch[3 * n :]

    def scratch(self):
        b16, k = jnp.bfloat16, len(self.pieces)
        return (
            [pltpu.VMEM((b // 2, r, c), b16) for b, r, c in self.shapes]
            + [pltpu.VMEM((b, r, c), b16) for b, r, c in self.shapes]
            + [pltpu.VMEM((self.inner, r, c), b16) for b, r, c in self.shapes]
            + [pltpu.SemaphoreType.DMA((k, self.steps)), pltpu.SemaphoreType.DMA((k, self.steps)), pltpu.SemaphoreType.DMA((k,))]
        )

    def copy(self, piece, step):
        i, columns, _ = self.pieces[piece]
        if step < self.stages:
            stage = step
            half = self.blocks >> (step + 1)
            other = (1 - self.mine(piece, step)) * half
            if step == 0:
                source = self.given[i].at[pl.ds(other, half), :, columns]
            else:
                source = self.work[i].at[pl.ds(self.low(piece, step) + other, half), :, columns]
            target = self.inbox[i].at[pl.ds(self.blocks - 2 * half, half), :, columns]
        else:
            stage = self.steps - 1 - step + self.outer_bits
            j = stage - self.outer_bits
            many = 1 << (self.inner_bits - 1 - j)
            source = target = self.result[i].at[pl.ds(self.place(piece, j + 1), many), :, columns]
        return pltpu.make_async_remote_copy(
            src_ref=source,
            dst_ref=target,
            send_sem=self.send.at[piece, step],
            recv_sem=self.recv.at[piece, step],
            device_id=self.partner(*self.axis_bit(piece, stage)),
            device_id_type=pl.DeviceIdType.MESH,
        )

    def own(self, piece):
        i, columns, _ = self.pieces[piece]
        half = self.blocks // 2
        source = self.given[i].at[pl.ds(self.mine(piece, 0) * half, half), :, columns]
        return pltpu.make_async_copy(source, self.work[i].at[:, :, columns], self.near.at[piece])

    def leave(self, piece):
        i, columns, _ = self.pieces[piece]
        return pltpu.make_async_copy(self.result[i].at[:, :, columns], self.out[i].at[:, :, columns], self.near.at[piece])

    def add(self, piece, stage):
        i, columns, _ = self.pieces[piece]
        work, inbox, result = self.work[i], self.inbox[i], self.result[i]
        half = self.blocks >> (stage + 1)
        arrived = self.blocks - 2 * half
        base = 0 if stage == 0 else self.low(piece, stage) + self.mine(piece, stage) * half

        @pl.loop(0, half)
        def _(k):
            new = work[base + k, :, columns].astype(jnp.float32) + inbox[arrived + k, :, columns].astype(jnp.float32)
            if stage == self.stages - 1:
                result[self.place(piece, self.inner_bits), :, columns] = new.astype(jnp.bfloat16)
            else:
                work[base + k, :, columns] = new.astype(jnp.bfloat16)

    def start(self, pieces):
        for p in pieces:
            self.copy(p, 0).start()
        for p in pieces:
            self.own(p).start()

    def advance(self, pieces, step):
        for p in pieces:
            if step == 0:
                self.own(p).wait()
            self.copy(p, step).wait()
            if step < self.stages:
                self.add(p, step)
            if step + 1 < self.steps:
                self.copy(p, step + 1).start()
            else:
                self.leave(p).start()

    def gone(self, pieces):
        for p in pieces:
            self.leave(p).wait()

    def times(self, count):
        heavy = (18.0, 10.0, 6.5, 14.0)
        there = [heavy[min(j, 3)] for j in range(self.inner_bits)]
        loads = [11.0] * self.outer_bits + there + there[::-1]
        total, at, out = sum(loads), 0.0, []
        for load in loads[:-1]:
            at += load
            out.append(max(1, min(count - 1, round(at / total * count))))
        return out


def reduction_of(arrays, parts):
    plan = Reduction(lax.axis_size("fsdp"), lax.axis_size("dp"), [a.shape for a in arrays], parts)
    shaped = [a.reshape(s) for a, s in zip(arrays, plan.shapes)]
    out = [jax.ShapeDtypeStruct((plan.inner,) + s[1:], jnp.bfloat16) for s in plan.shapes]
    return plan, shaped, out


class Exchange:
    def __init__(self, size):
        self.size = size

    def owner(self, turn):
        return (lax.axis_index("fsdp") + self.size - turn) % self.size

    def peer(self, turn):
        return {"fsdp": (lax.axis_index("fsdp") + turn) % self.size}

    def barrier(self):
        sem = pltpu.get_barrier_semaphore()
        for turn in range(1, self.size):
            pl.semaphore_signal(sem, inc=1, device_id=self.peer(turn), device_id_type=pl.DeviceIdType.MESH)
        pl.semaphore_wait(sem, self.size - 1)

    def copy(self, source, target, sems, which, turn):
        if turn == 0:
            return pltpu.make_async_copy(source, target, sems[1].at[which, 0])
        return pltpu.make_async_remote_copy(
            src_ref=source,
            dst_ref=target,
            send_sem=sems[0].at[which, turn],
            recv_sem=sems[1].at[which, turn],
            device_id=self.peer(turn),
            device_id_type=pl.DeviceIdType.MESH,
        )


def gather_kernel(
    x_ref, go_ref, dt_ref, rate_ref, taps_ref, vec_ref, xp_ref, wout_ref, win_ref,
    normed_ref, dtw_ref, xpw_ref, decay_ref, par_ref, gain_ref, wout_out, win_out, dg_out, both_out,
    pack, wout, win, dg, both, packed, send, recv, leave, tiles, *, plan
):
    f32, bf16 = jnp.float32, jnp.bfloat16
    rows, model = x_ref.shape
    deep, wide, share = model // plan.size, both.shape[1], packed.shape[1]
    me = lax.axis_index("fsdp")
    sems = (send, recv)

    def copies(which, turn):
        source = (packed, wout_ref, win_ref)[which]
        if which == 0:
            target = pack.at[:, pl.ds(pl.multiple_of(me * share, 128), share)]
        else:
            target = (wout, win)[which - 1].at[me]
        return plan.copy(source, target, sems, which, turn)

    lines = share // 128
    vectors = vec_ref[...].astype(f32)
    line = [
        jnp.concatenate([vectors[k : k + 1] for k in range(v * lines, (v + 1) * lines)], axis=1) for v in range(4)
    ]
    few = [line[0], taps_ref[...].astype(f32)] + line[1:]
    depth, states, taps = dt_ref.shape[0], rate_ref.shape[0], taps_ref.shape[0]
    few.append(jnp.zeros((16 - 4 - taps, share), f32))
    packed[0:depth, :] = dt_ref[...]
    packed[depth : depth + states, :] = rate_ref[...]
    packed[depth + states : depth + states + 16, :] = jnp.concatenate(few, axis=0).astype(bf16)
    packed[depth + states + 16 :, :] = xp_ref[...]
    plan.barrier()
    for which in range(3):
        for turn in range(1, plan.size):
            copies(which, turn).start()
    for which in (1, 0, 2):
        copies(which, 0).start()

    def times_out(turn):
        at = plan.owner(turn)

        @pl.loop(0, share // 256)
        def _(k):
            here = pl.ds(pl.multiple_of(at * share + k * 256, 128), 256)
            dg[:, here] = lax.dot_general(
                go_ref[...], wout[at, pl.ds(pl.multiple_of(k * 256, 256), 256), :],
                (((1,), (1,)), ((), ())), preferred_element_type=f32,
            )
        pltpu.make_async_copy(wout.at[at], wout_out.at[at], leave.at[0, turn]).start()
        part = pl.ds(pl.multiple_of(at * share, 128), share)
        pltpu.make_async_copy(dg.at[:, part], dg_out.at[:, part], leave.at[2, turn]).start()

    def times_in(turn):
        at = plan.owner(turn)
        left = pl.ds(pl.multiple_of(at * deep, 128), deep)

        @pl.loop(0, wide // 256)
        def _(k):
            here = pl.ds(pl.multiple_of(k * 256, 256), 256)
            new = jnp.dot(normed_ref[:, left], win[at, :, here], preferred_element_type=f32)
            both[:, here] = new if turn == 0 else both[:, here] + new
            if turn == plan.size - 1:
                pltpu.make_async_copy(both.at[:, here], both_out.at[:, here], tiles.at[k]).start()
        pltpu.make_async_copy(win.at[at], win_out.at[at], leave.at[1, turn]).start()

    copies(1, 0).wait()
    times_out(0)
    for turn in range(plan.size):
        copies(0, turn).wait()
    dtw_ref[...] = pack[0:depth, :]
    xpw_ref[...] = pack[depth + states + 16 :, :]
    decay_ref[...] = -jnp.exp(pack[depth : depth + states, :].astype(f32)) * LOG2E
    few = pack[depth + states : depth + states + 16, :].astype(f32)
    par_ref[...] = few[1:9]
    gain = jnp.concatenate([few[:1, b * share : b * share + deep] for b in range(plan.size)], axis=1)
    gain_ref[...] = jnp.broadcast_to(gain, gain_ref.shape)

    @pl.loop(0, rows // 64)
    def _(k):
        here = pl.ds(pl.multiple_of(k * 64, 64), 64)
        x = x_ref[here, :].astype(f32)
        mean_sq = jnp.mean(x * x, axis=-1, keepdims=True)
        normed_ref[here, :] = (x * lax.rsqrt(mean_sq + norm_eps) * gain).astype(bf16)

    copies(2, 0).wait()
    times_in(0)
    for turn in range(1, plan.size):
        copies(1, turn).wait()
        times_out(turn)
    for turn in range(1, plan.size):
        copies(2, turn).wait()
        times_in(turn)
    for turn in range(plan.size):
        at = plan.owner(turn)
        part = pl.ds(pl.multiple_of(at * share, 128), share)
        pltpu.make_async_copy(wout.at[at], wout_out.at[at], leave.at[0, turn]).wait()
        pltpu.make_async_copy(win.at[at], win_out.at[at], leave.at[1, turn]).wait()
        pltpu.make_async_copy(dg.at[:, part], dg_out.at[:, part], leave.at[2, turn]).wait()

    @pl.loop(0, wide // 256)
    def _(k):
        here = pl.ds(pl.multiple_of(k * 256, 256), 256)
        pltpu.make_async_copy(both.at[:, here], both_out.at[:, here], tiles.at[k]).wait()


def gather_weights(x, grad_rows, small, w_out, w_in):
    f32, bf16 = jnp.float32, jnp.bfloat16
    plan = Exchange(lax.axis_size("fsdp"))
    n, (rows, model), wide = plan.size, x.shape, w_in.shape[1]
    (rank, share), states, cols = small[0].shape, small[1].shape[0], small[4].shape[0]
    inner = n * share
    anywhere = pl.BlockSpec(memory_space=pl.ANY)
    near = pl.BlockSpec(memory_space=pltpu.VMEM)
    shapes = [
        ((rank + states + 16 + cols, inner), bf16), ((n,) + w_out.shape, bf16), ((n,) + w_in.shape, bf16), ((rows, inner), f32), ((rows, wide), f32),
    ]
    outs = [
        (x.shape, bf16), ((rank, inner), bf16), ((cols, inner), bf16), ((states, inner), f32), ((8, inner), f32), ((8, model), f32),
    ]
    *made, out_all, in_all, d_gated, both = pl.pallas_call(
        functools.partial(gather_kernel, plan=plan),
        out_shape=[jax.ShapeDtypeStruct(*s) for s in outs + shapes[1:]],
        in_specs=[near] * 7 + [anywhere] * 2,
        out_specs=[near] * 6 + [anywhere] * 4,
        scratch_shapes=[pltpu.VMEM(*s) for s in shapes]
        + [
            pltpu.VMEM((shapes[0][0][0], share), bf16),
            pltpu.SemaphoreType.DMA((3, n)),
            pltpu.SemaphoreType.DMA((3, n)),
            pltpu.SemaphoreType.DMA((3, n)),
            pltpu.SemaphoreType.DMA((wide // 256,)),
        ],
        compiler_params=pltpu.CompilerParams(collective_id=2, has_side_effects=True, vmem_limit_bytes=56 << 20),
        name="gather_weights",
    )(x, grad_rows, *small, w_out, w_in)
    return made, out_all.reshape(-1, w_out.shape[1]), in_all.reshape(-1, wide), d_gated, both


TAPS, SHIFT, DT_BIAS, SKIP = 0, 4, 5, 6


def rows_of(ref, tile, row, width):
    return [ref[tile + j, pl.ds(row, 8, stride=0), :] for j in range(width)]


def by_eights(ref, tile):
    total = ref[tile, pl.ds(0, 8, stride=8), :]
    for s in range(1, 8):
        total = total + ref[tile, pl.ds(s, 8, stride=8), :]
    return total


def folded(x):
    total = x[:8]
    for s in range(8, x.shape[0], 8):
        total = total + x[s : s + 8]
    return total


def spread(proj, first, wide, states):
    for t in range(proj.shape[1]):
        wide[pl.ds(t * states, states), :] = jnp.broadcast_to(proj[first : first + states, t : t + 1], (states, 128))


def forward_kernel(
    upper_ref, z_ref, dg_ref, off_ref, par_ref, xp_ref, dtw_ref, a_ref,
    u_ref, ds_ref, dt_ref, sg_ref, dy_ref, gated_ref, gate_ref, proj_ref, wide_b, wide_c, kept_ref, end_ref, skip_ref,
    hs, ext, u16, dtm, dtu, ys, ybuf, *, width
):
    f32, bf16 = jnp.float32, jnp.bfloat16
    rows, inner = upper_ref.shape
    states, rank = a_ref.shape[0], dtw_ref.shape[0]
    tiles = inner // 128

    @pl.when(pl.program_id(0) == 0)
    def _():
        hs[...] = jnp.zeros_like(hs)
        skip_ref[...] = jnp.zeros_like(skip_ref)
        ext[pl.ds(0, 8), :] = jnp.zeros((8, inner), f32)

    @pl.loop(0, tiles, unroll=True)
    def _(k):
        lanes = pl.ds(pl.multiple_of(k * 128, 128), 128)
        now = upper_ref[:, lanes]
        ext[pl.ds(8, rows), lanes] = now
        conv = par_ref[SHIFT : SHIFT + 1, lanes] + par_ref[TAPS + 3 : TAPS + 4, lanes] * now
        for lag in range(1, 4):
            before = ext[pl.ds(8 - lag, rows), lanes]
            conv = conv + par_ref[TAPS + 3 - lag : TAPS + 4 - lag, lanes] * jnp.where(off_ref[...] >= lag, before, 0.0)
        sig = jax.nn.sigmoid(conv)
        act = conv * sig
        u_ref[:, lanes] = act
        u16[:, lanes] = act.astype(bf16)
        ds_ref[:, lanes] = sig * (1.0 + conv * (1.0 - sig))
        ext[pl.ds(0, 8), lanes] = now[rows - 8 :]

    proj = lax.dot_general(xp_ref[...], u16[...], (((1,), (1,)), ((), ())), preferred_element_type=f32)
    proj_ref[0] = proj
    spread(proj, rank, wide_b, states)
    spread(proj, rank + states, wide_c, states)
    rank16 = proj[:rank].astype(bf16)

    @pl.loop(0, tiles // 2, unroll=True)
    def _(k):
        pair = pl.ds(pl.multiple_of(k * 256, 256), 256)
        pre = lax.dot_general(rank16, dtw_ref[:, pair], (((0,), (0,)), ((), ())), preferred_element_type=f32)
        pre = pre + par_ref[DT_BIAS : DT_BIAS + 1, pair]
        small = jnp.exp(-jnp.abs(pre))
        delta = jnp.maximum(pre, 0.0) + jnp.log1p(small)
        dt_ref[:, pair] = delta
        sg_ref[:, pair] = jnp.where(pre >= 0, 1.0, small) / (1.0 + small)
        grown = delta * u_ref[:, pair]
        for j in range(2):
            part = slice(128 * j, 128 * j + 128)
            dtm[2 * k + j] = jnp.where(off_ref[...] > 0, delta[:, part], BIG)
            dtu[2 * k + j] = grown[:, part]

    @pl.loop(0, tiles // width)
    def _(cb):
        tile = cb * width
        base = pl.multiple_of(cb * 128 * width, 128 * width)
        rate = [[a_ref[pl.ds(8 * s, 8), pl.ds(base + 128 * j, 128)] for s in range(2)] for j in range(width)]

        def body(g, h):
            h = [list(p) for p in zip(h[:width], h[width:])]
            r0 = pl.multiple_of(g * 8, 8)
            for t in range(8):
                d = rows_of(dtm, tile, r0 + t, width)
                x = rows_of(dtu, tile, r0 + t, width)
                bt = [wide_b[pl.ds((r0 + t) * 16 + 8 * s, 8), :] for s in range(2)]
                ct = [wide_c[pl.ds((r0 + t) * 16 + 8 * s, 8), :] for s in range(2)]
                for j in range(width):
                    kept_ref[tile + j, pl.ds((r0 + t) * 16, 16), :] = jnp.concatenate(h[j], axis=0).astype(bf16)
                    for s in range(2):
                        h[j][s] = jnp.exp2(d[j] * rate[j][s]) * h[j][s] + x[j] * bt[s]
                    ybuf[j, pl.ds(t * 8, 8), :] = ct[0] * h[j][0] + ct[1] * h[j][1]
            for j in range(width):
                ys[tile + j, pl.ds(r0, 8), :] = by_eights(ybuf, j)
            return tuple(p[0] for p in h) + tuple(p[1] for p in h)

        h = tuple(hs[pl.ds(8 * s, 8), pl.ds(base + 128 * j, 128)] for s in range(2) for j in range(width))
        h = lax.fori_loop(0, rows // 8, body, h, unroll=4)
        for s in range(2):
            for j in range(width):
                hs[pl.ds(8 * s, 8), pl.ds(base + 128 * j, 128)] = h[s * width + j]
    end_ref[...] = hs[...]

    @pl.loop(0, tiles, unroll=True)
    def _(k):
        lanes = pl.ds(pl.multiple_of(k * 128, 128), 128)
        act, z, dg = u_ref[:, lanes], z_ref[:, lanes], dg_ref[:, lanes]
        full = ys[k] + par_ref[SKIP : SKIP + 1, lanes] * act
        sig = jax.nn.sigmoid(z)
        silu = z * sig
        gated_ref[:, lanes] = (full * silu).astype(bf16)
        dy = dg * silu
        dy_ref[:, lanes] = dy
        gate_ref[:, lanes] = (dg * full * sig * (1.0 + z * (1.0 - sig))).astype(bf16)
        skip_ref[:, lanes] = skip_ref[:, lanes] + folded(dy * act)


def scan_forward(both, d_gated, offset, params, xp, dtw, rate, chunk, width):
    T, DI = d_gated.shape
    n, states, cols = T // chunk, rate.shape[0], xp.shape[0]
    f32, bf16 = jnp.float32, jnp.bfloat16
    row = pl.BlockSpec((chunk, DI), lambda i: (i, 0))
    whole = lambda a: pl.BlockSpec(a.shape, lambda i: (0, 0))
    flat = lambda d: jax.ShapeDtypeStruct((T, DI), d)
    tile = lambda d: pltpu.VMEM((DI // 128, chunk, 128), d)
    return pl.pallas_call(
        functools.partial(forward_kernel, width=width),
        grid=(n,),
        in_specs=[row, pl.BlockSpec((chunk, DI), lambda i: (i, 1)), row, pl.BlockSpec((chunk, 128), lambda i: (i, 0))]
        + [whole(a) for a in (params, xp, dtw, rate)],
        out_specs=[row] * 7
        + [
            pl.BlockSpec((1, cols, chunk), lambda i: (i, 0, 0)),
            pl.BlockSpec((chunk * states, 128), lambda i: (i, 0)),
            pl.BlockSpec((chunk * states, 128), lambda i: (i, 0)),
            pl.BlockSpec((DI // 128, chunk * states, 128), lambda i: (0, i, 0)),
            pl.BlockSpec((states, DI), lambda i: (0, 0)),
            pl.BlockSpec((8, DI), lambda i: (0, 0)),
        ],
        out_shape=[flat(f32)] * 5
        + [flat(bf16)] * 2
        + [
            jax.ShapeDtypeStruct((n, cols, chunk), f32),
            jax.ShapeDtypeStruct((T * states, 128), f32),
            jax.ShapeDtypeStruct((T * states, 128), f32),
            jax.ShapeDtypeStruct((DI // 128, T * states, 128), bf16),
            jax.ShapeDtypeStruct((states, DI), f32),
            jax.ShapeDtypeStruct((8, DI), f32),
        ],
        scratch_shapes=[
            pltpu.VMEM((states, DI), f32),
            pltpu.VMEM((chunk + 8, DI), f32),
            pltpu.VMEM((chunk, DI), bf16),
            tile(f32),
            tile(f32),
            tile(f32),
            pltpu.VMEM((width, 64, 128), f32),
        ],
        compiler_params=pltpu.CompilerParams(dimension_semantics=("arbitrary",), vmem_limit_bytes=62 << 20),
        name="scan_forward",
    )(both, both, d_gated, offset, params, xp, dtw, rate)


def backward_kernel(
    u_ref, ds_ref, dt_ref, sg_ref, dy_ref, upper_ref, off_ref, proj_ref, wide_b, wide_c, kept_ref, end_ref, par_ref, xp_ref, dtw_ref, a_ref, skip_ref,
    *rest, width, plan, total
):
    f32, bf16 = jnp.float32, jnp.bfloat16
    n = len(plan.shapes)
    given, rest = rest[:n], rest[n:]
    (du_ref, small_ref), out, rest = rest[:2], rest[2 : 2 + n], rest[2 + n :]
    ga_ref, gdt_ref, gx_ref, sum_ref, *rest = rest
    ws, ns, dtm, dtu, dyb, sbuf, qbuf, dd, di, u16, dt16, ext, off_ext, wide_db, wide_dc, cols_ref = rest[:16]
    plan.bind(given, out, rest[16:])
    rows, inner = u_ref.shape
    states, rank = a_ref.shape[0], dtw_ref.shape[0]
    tiles = inner // 128
    everything = range(len(plan.pieces))
    times = plan.times(total // rows * (tiles // width))

    @pl.when(pl.program_id(0) == 0)
    def _():
        for ref in (ws, ga_ref, gdt_ref, gx_ref, sum_ref):
            ref[...] = jnp.zeros_like(ref)
        ns[...] = end_ref[...]
        ext[pl.ds(rows, 8), :] = jnp.zeros((8, inner), f32)
        off_ext[pl.ds(rows, 8), :] = jnp.full((8, 128), -1, jnp.int32)
        plan.barrier()
        plan.start(everything)

    proj = proj_ref[0]
    wide_db[...] = jnp.zeros_like(wide_db)
    wide_dc[...] = jnp.zeros_like(wide_dc)

    @pl.loop(0, tiles // width)
    def _(cb):
        tile = cb * width
        base = pl.multiple_of(cb * 128 * width, 128 * width)
        for at in sorted(set(times)):
            @pl.when(pl.program_id(0) * (tiles // width) + cb == at)
            def _():
                for step in range(plan.steps - 1):
                    if times[step] == at:
                        plan.advance(everything, step)

        for j in range(width):
            lanes = pl.ds(base + 128 * j, 128)
            d, act = dt_ref[:, lanes], u_ref[:, lanes]
            dtm[j] = jnp.where(off_ref[...] > 0, d, BIG)
            dtu[j] = d * act
            dyb[j] = dy_ref[:, lanes]
            u16[:, lanes] = act.astype(bf16)
        rate = [[a_ref[pl.ds(8 * s, 8), pl.ds(base + 128 * j, 128)] for s in range(2)] for j in range(width)]

        def body(k, carry):
            r0 = pl.multiple_of((rows // 8 - 1 - k) * 8, 8)
            w = [[carry[s * width + j] for s in range(2)] for j in range(width)]
            ga = [[carry[2 * width + s * width + j] for s in range(2)] for j in range(width)]
            newer = [[carry[4 * width + s * width + j] for s in range(2)] for j in range(width)]
            for t in range(7, -1, -1):
                d = rows_of(dtm, 0, r0 + t, width)
                x = rows_of(dtu, 0, r0 + t, width)
                v = rows_of(dyb, 0, r0 + t, width)
                bt = [wide_b[pl.ds((r0 + t) * 16 + 8 * s, 8), :] for s in range(2)]
                ct = [wide_c[pl.ds((r0 + t) * 16 + 8 * s, 8), :] for s in range(2)]
                db = [None, None]
                dc = [None, None]
                for j in range(width):
                    qs, ss = None, None
                    both = kept_ref[tile + j, pl.ds((r0 + t) * 16, 16), :].astype(f32)
                    for s in range(2):
                        later = newer[j][s]
                        prior = both[8 * s : 8 * s + 8]
                        newer[j][s] = prior
                        g = ct[s] * v[j] + w[j][s]
                        w[j][s] = jnp.exp2(d[j] * rate[j][s]) * g
                        q = w[j][s] * prior
                        ga[j][s] = ga[j][s] + q * d[j]
                        qa = q * rate[j][s]
                        sb = g * bt[s]
                        qs = qa if qs is None else qs + qa
                        ss = sb if ss is None else ss + sb
                        gx = g * x[j]
                        vh = v[j] * later
                        db[s] = gx if db[s] is None else db[s] + gx
                        dc[s] = vh if dc[s] is None else dc[s] + vh
                    qbuf[j, pl.ds(t * 8, 8), :] = qs
                    sbuf[j, pl.ds(t * 8, 8), :] = ss
                for s in range(2):
                    here = pl.ds((r0 + t) * 16 + 8 * s, 8)
                    wide_db[here, :] = wide_db[here, :] + db[s]
                    wide_dc[here, :] = wide_dc[here, :] + dc[s]
            for j in range(width):
                lanes = pl.ds(base + 128 * j, 128)
                here = pl.ds(r0, 8)
                s8 = by_eights(sbuf, j)
                dd[here, lanes] = LN2 * by_eights(qbuf, j) + u_ref[here, lanes] * s8
                di[here, lanes] = dt_ref[here, lanes] * s8
            return tuple(v[j][s] for v in (w, ga, newer) for s in range(2) for j in range(width))

        held = [(r, pl.ds(8 * s, 8), pl.ds(base + 128 * j, 128)) for r in (ws, ga_ref, ns) for s in range(2) for j in range(width)]
        end = lax.fori_loop(0, rows // 8, body, tuple(r[a, b] for r, a, b in held))
        for (r, a, b), value in zip(held, end):
            r[a, b] = value

    for i, ref in enumerate((wide_db, wide_dc)):
        for k in range(states):
            cols_ref[pl.ds(i * rows, rows), pl.ds(128 * k, 128)] = ref[pl.ds(k, rows, stride=states), :].astype(bf16)
    owner = lax.broadcasted_iota(jnp.int32, (states, states * 128), 1) // 128
    picks = jnp.where(owner == lax.broadcasted_iota(jnp.int32, (states, states * 128), 0), 1.0, 0.0).astype(bf16)
    d_bc = lax.dot_general(picks, cols_ref[...], (((1,), (1,)), ((), ())), preferred_element_type=f32)

    @pl.loop(0, tiles, unroll=True)
    def _(k):
        lanes = pl.ds(pl.multiple_of(k * 128, 128), 128)
        low = (dd[:, lanes] * sg_ref[:, lanes]).astype(bf16)
        dt16[:, lanes] = low
        sum_ref[pl.ds(40, 8), lanes] = sum_ref[pl.ds(40, 8), lanes] + folded(low.astype(f32))

    rank16 = proj[:rank].astype(bf16)
    d_rank = lax.dot_general(dtw_ref[...], dt16[...], (((1,), (1,)), ((), ())), preferred_element_type=f32)
    proj16 = jnp.concatenate([d_rank, d_bc[:, :rows], d_bc[:, rows:]], axis=0).astype(bf16)
    off_ext[pl.ds(0, rows), :] = off_ref[...]

    @pl.loop(0, tiles // 2, unroll=True)
    def _(k):
        pair = pl.ds(pl.multiple_of(k * 256, 256), 256)
        dot = lambda a, b, c: lax.dot_general(a, b, ((c, (0,)), ((), ())), preferred_element_type=f32)
        gdt_ref[:, pair] = gdt_ref[:, pair] + dot(rank16, dt16[:, pair], (1,))
        gx_ref[:, pair] = gx_ref[:, pair] + dot(proj16, u16[:, pair], (1,))
        inner_grad = dot(proj16, xp_ref[:, pair], (0,)) + di[:, pair] + dy_ref[:, pair] * par_ref[SKIP : SKIP + 1, pair]
        ext[pl.ds(0, rows), pair] = inner_grad * ds_ref[:, pair]
        for j in range(2):
            lanes = pl.ds(pl.multiple_of(k * 256 + 128 * j, 128), 128)
            now, above = ext[pl.ds(0, rows), lanes], upper_ref[:, lanes]
            grad = par_ref[TAPS + 3 : TAPS + 4, lanes] * now
            sums = [now, now * above]
            for lag in range(1, 4):
                after = jnp.where(off_ext[pl.ds(lag, rows), :] >= lag, ext[pl.ds(lag, rows), lanes], 0.0)
                grad = grad + par_ref[TAPS + 3 - lag : TAPS + 4 - lag, lanes] * after
                sums.append(after * above)
            du_ref[:, lanes] = grad.astype(bf16)
            for at, value in zip((32, 24, 16, 8, 0), sums):
                sum_ref[pl.ds(at, 8), lanes] = sum_ref[pl.ds(at, 8), lanes] + folded(value)
            ext[pl.ds(rows, 8), lanes] = now[:8]

    off_ext[pl.ds(rows, 8), :] = off_ref[pl.ds(0, 8), :]

    @pl.when(pl.program_id(0) == pl.num_programs(0) - 1)
    def _():
        share = small_ref.shape[1]
        deep = small_ref.shape[0] // (inner // share)
        sums = [jnp.sum(sum_ref[pl.ds(8 * k, 8), :], axis=0, keepdims=True) for k in range(6)]
        sums += [jnp.sum(skip_ref[...], axis=0, keepdims=True), jnp.zeros((9, inner), f32)]
        blocks = [gx_ref[...], gdt_ref[...], ga_ref[...] * a_ref[...] * LN2, jnp.concatenate(sums, axis=0)]
        for f in range(inner // share):
            at = f * deep
            for block in blocks:
                small_ref[at : at + block.shape[0], :] = block[:, f * share : (f + 1) * share].astype(bf16)
                at += block.shape[0]
            small_ref[at : (f + 1) * deep, :] = jnp.zeros(((f + 1) * deep - at, share), bf16)
        plan.advance(everything, plan.steps - 1)
        plan.gone(everything)


def scan_backward(saved, both, offset, proj, wide_b, wide_c, kept, end, params, xp, dtw, rate, skip, chunk, width, grads, parts):
    T, DI = saved[0].shape
    n, states, cols, rank = T // chunk, rate.shape[0], xp.shape[0], dtw.shape[0]
    f32, bf16 = jnp.float32, jnp.bfloat16
    row = pl.BlockSpec((chunk, DI), lambda i: (n - 1 - i, 0))
    whole = lambda a: pl.BlockSpec(a.shape, lambda i: (0, 0))
    anywhere = pl.BlockSpec(memory_space=pl.ANY)
    plan, shaped, summed = reduction_of(grads, parts)
    outer, inner = lax.axis_size("fsdp"), lax.axis_size("dp")
    deep = -(-(states + rank + cols + 16) // (16 * inner)) * 16 * inner
    small = jax.ShapeDtypeStruct((outer * deep, DI // outer), bf16)
    pieces = pltpu.VMEM((width, chunk, 128), f32)
    eights = pltpu.VMEM((width, 64, 128), f32)
    tall = pltpu.VMEM((chunk * states, 128), f32)
    out = pl.pallas_call(
        functools.partial(backward_kernel, width=width, plan=plan, total=T),
        grid=(n,),
        in_specs=[row] * 6
        + [
            pl.BlockSpec((chunk, 128), lambda i: (n - 1 - i, 0)),
            pl.BlockSpec((1, cols, chunk), lambda i: (n - 1 - i, 0, 0)),
            pl.BlockSpec((chunk * states, 128), lambda i: (n - 1 - i, 0)),
            pl.BlockSpec((chunk * states, 128), lambda i: (n - 1 - i, 0)),
            pl.BlockSpec((DI // 128, chunk * states, 128), lambda i: (0, n - 1 - i, 0)),
            whole(end),
        ]
        + [whole(a) for a in (params, xp, dtw, rate, skip)]
        + [anywhere] * len(grads),
        out_specs=[row, whole(small)] + [anywhere] * len(grads),
        out_shape=[jax.ShapeDtypeStruct((T, DI), bf16), small] + summed,
        scratch_shapes=[pltpu.VMEM((r, DI), f32) for r in (states, rank, cols, 48)]
        + [
            pltpu.VMEM((states, DI), f32),
            pltpu.VMEM((states, DI), f32),
            pieces,
            pieces,
            pieces,
            eights,
            eights,
            pltpu.VMEM((chunk, DI), f32),
            pltpu.VMEM((chunk, DI), f32),
            pltpu.VMEM((chunk, DI), bf16),
            pltpu.VMEM((chunk, DI), bf16),
            pltpu.VMEM((chunk + 8, DI), f32),
            pltpu.VMEM((chunk + 8, 128), jnp.int32),
            tall,
            tall,
            pltpu.VMEM((2 * chunk, states * 128), bf16),
        ]
        + plan.scratch(),
        compiler_params=pltpu.CompilerParams(
            dimension_semantics=("arbitrary",), collective_id=0, has_side_effects=True, vmem_limit_bytes=56 << 20
        ),
        name="scan_backward",
    )(*saved, both, offset, proj, wide_b, wide_c, kept, end, params, xp, dtw, rate, skip, *shaped)
    return out[:2], [o.reshape(-1, o.shape[-1]) for o in out[2:]]


def finish_kernel(
    grads_ref, small_ref, upper_ref, gate_ref, gated_ref, in_ref, wout_ref, x_ref, go_ref, gain_ref,
    total_ref, few_ref, layer_ref, left_ref,
    upper, gate, gated, win, wout, x, go, dn, layer, mine, gain_sum, loads, away, *rest, plan, gain_row
):
    f32, bf16 = jnp.float32, jnp.bfloat16
    rows, model = x.shape
    inner = upper.shape[1]
    plan.bind([grads_ref, mine], [total_ref, few_ref], rest)
    main = [p for p in range(len(plan.pieces)) if plan.pieces[p][0] == 0]
    late = [p for p in range(len(plan.pieces)) if plan.pieces[p][0] == 1]

    copies = [
        pltpu.make_async_copy(a, b, loads.at[i])
        for i, (a, b) in enumerate(
            (
                (upper_ref, upper), (in_ref.at[:, pl.ds(0, inner)], win.at[0]), (gate_ref, gate),
                (in_ref.at[:, pl.ds(inner, inner)], win.at[1]), (x_ref, x), (go_ref, go), (small_ref, mine),
                (gated_ref, gated), (wout_ref, wout),
            )
        )
    ]

    def product(left, k):
        @pl.loop(0, model // 256)
        def _(j):
            here = pl.ds(pl.multiple_of(j * 256, 256), 256)
            new = lax.dot_general(left[...], win[k, here, :], (((1,), (1,)), ((), ())), preferred_element_type=f32)
            dn[:, here] = new if k == 0 else dn[:, here] + new

    plan.barrier()
    plan.start(main)
    for c in copies:
        c.start()
    copies[0].wait()
    copies[1].wait()
    product(upper, 0)
    plan.advance(main, 0)
    copies[2].wait()
    copies[3].wait()
    product(gate, 1)
    copies[4].wait()
    copies[5].wait()
    gain_sum[...] = jnp.zeros_like(gain_sum)

    @pl.loop(0, rows // 32)
    def _(k):
        here = pl.ds(pl.multiple_of(k * 32, 32), 32)
        value, grad, gain = x[here, :].astype(f32), dn[here, :], gain_ref[0:1, :]
        scale = lax.rsqrt(jnp.mean(value * value, axis=-1, keepdims=True) + norm_eps)
        through = grad * value
        gain_sum[...] = gain_sum[...] + folded(through * scale)
        pull = jnp.mean(through * gain, axis=-1, keepdims=True) * (scale * scale * scale)
        dn[here, :] = go[here, :].astype(f32) + scale * (grad * gain) - value * pull

    leaving = [pltpu.make_async_copy(dn, left_ref, away.at[0]), pltpu.make_async_copy(layer, layer_ref, away.at[1])]
    leaving[0].start()
    copies[6].wait()
    gain_grad = jnp.sum(gain_sum[...], axis=0, keepdims=True)
    outer = plan.blocks // plan.inner
    deep, r = model // outer, mine.shape[1]
    for f in range(outer):
        block = f * plan.inner + gain_row // r
        old = mine[block, :, 0:deep].astype(f32)
        new = jnp.broadcast_to(gain_grad[:, f * deep : (f + 1) * deep], (r, deep))
        chosen = lax.broadcasted_iota(jnp.int32, (r, deep), 0) == gain_row % r
        mine[block, :, 0:deep] = jnp.where(chosen, new, old).astype(bf16)
    plan.start(late)
    plan.advance(main, 1)
    plan.advance(late, 0)
    copies[7].wait()
    copies[8].wait()

    @pl.loop(0, model // 256)
    def _(j):
        here = pl.ds(pl.multiple_of(j * 256, 256), 256)
        new = x[:, here].astype(f32) + jnp.dot(gated[...], wout[:, here], preferred_element_type=f32)
        layer[:, here] = new.astype(bf16)

    leaving[1].start()
    for step in range(2, plan.steps):
        plan.advance(main, step)
        plan.advance(late, step - 1)
    plan.advance(late, plan.steps - 1)
    plan.gone(main + late)
    for c in leaving:
        c.wait()


def finish(grads, small, upper16, gate16, gated16, w_in, w_out, x, go, gain, parts, gain_row):
    f32, bf16 = jnp.float32, jnp.bfloat16
    (rows, model), inner = x.shape, upper16.shape[1]
    plan, shaped, summed = reduction_of([grads, small], parts)
    anywhere = pl.BlockSpec(memory_space=pl.ANY)
    flat = pltpu.VMEM((rows, inner), bf16)
    thin = pltpu.VMEM((rows, model), bf16)
    total, few, layer_out, input_grad = pl.pallas_call(
        functools.partial(finish_kernel, plan=plan, gain_row=gain_row),
        out_shape=summed + [jax.ShapeDtypeStruct((rows, model), bf16), jax.ShapeDtypeStruct((rows, model), f32)],
        in_specs=[anywhere] * 9 + [pl.BlockSpec(memory_space=pltpu.VMEM)],
        out_specs=[anywhere] * 4,
        scratch_shapes=[
            flat,
            flat,
            flat,
            pltpu.VMEM((2, model, inner), bf16),
            pltpu.VMEM((inner, model), bf16),
            thin,
            thin,
            pltpu.VMEM((rows, model), f32),
            thin,
            pltpu.VMEM(plan.shapes[1], bf16),
            pltpu.VMEM((8, model), f32),
            pltpu.SemaphoreType.DMA((9,)),
            pltpu.SemaphoreType.DMA((2,)),
        ]
        + plan.scratch(),
        compiler_params=pltpu.CompilerParams(collective_id=1, has_side_effects=True, vmem_limit_bytes=56 << 20),
        name="finish",
    )(*shaped, upper16, gate16, gated16, w_in, w_out, x, go, gain)
    return total.reshape(-1, total.shape[-1]), few.reshape(-1, few.shape[-1]), layer_out, input_grad


def write_kernel(
    upper_ref, gate_ref, out_ref, small_ref, layer_ref, left_ref,
    in_to, out_to, x_to, dt_to, rate_to, taps_to, shift_to, bias_to, skip_to, gain_to, layer_to, left_to,
):
    f32 = jnp.float32
    wide = upper_ref.shape[1]
    in_to[:, 0:wide] = upper_ref[...].astype(f32)
    in_to[:, wide:] = gate_ref[...].astype(f32)
    out_to[...] = out_ref[...].astype(f32)
    layer_to[...] = layer_ref[...]
    left_to[...] = left_ref[...]

    @pl.when(pl.program_id(0) == 0)
    def _():
        at = 0
        for ref in (x_to, dt_to, rate_to):
            ref[...] = small_ref[at : at + ref.shape[0], :].astype(f32)
            at += ref.shape[0]
        few = small_ref[at : at + 16, :].astype(f32)
        at = 0
        for ref in (taps_to, shift_to, bias_to, skip_to, gain_to):
            ref[...] = few[at : at + ref.shape[0], : ref.shape[1]]
            at += ref.shape[0]


def write_outputs(upper, gate, out, small, layer, left, sizes):
    f32, share, steps = jnp.float32, small.shape[1], 4
    few = [(r, share) for r in sizes[:-1]] + [(1, sizes[-1])]
    part = lambda a: pl.BlockSpec((a.shape[0] // steps, a.shape[1]), lambda i: (i, 0))
    whole = lambda a: pl.BlockSpec(a.shape, lambda i: (0, 0))
    big = [jax.ShapeDtypeStruct((upper.shape[0], upper.shape[1] + gate.shape[1]), f32), jax.ShapeDtypeStruct(out.shape, f32)]
    few = [jax.ShapeDtypeStruct(a, f32) for a in few]
    last = [jax.ShapeDtypeStruct(a.shape, a.dtype) for a in (layer, left)]
    return pl.pallas_call(
        write_kernel,
        grid=(steps,),
        in_specs=[part(upper), part(gate), part(out), whole(small), part(layer), part(left)],
        out_specs=[part(a) for a in big] + [whole(a) for a in few] + [part(a) for a in last],
        out_shape=big + few + last,
        compiler_params=pltpu.CompilerParams(dimension_semantics=("arbitrary",), vmem_limit_bytes=62 << 20),
        name="write_outputs",
    )(upper, gate, out, small, layer, left)


def cluster_offsets(lengths, total_len):
    count = lengths.shape[1]
    ahead = jnp.arange(count)[:, None] < jnp.arange(count)[None, :]
    start_points = jnp.sum(jnp.where(ahead[None], lengths[:, :, None], 0), axis=1, dtype=jnp.int32)
    end_points = start_points + lengths
    where_at = jnp.arange(total_len, dtype=jnp.int32)
    inside = (where_at[None, None, :] >= start_points[:, :, None]) & (
        where_at[None, None, :] < end_points[:, :, None]
    )
    first_spot = jnp.sum(jnp.where(inside, start_points[:, :, None], 0), axis=1, dtype=jnp.int32)
    return where_at[None, :] - first_spot


def dot32(left, right, contract):
    return lax.dot_general(left, right, (contract, ((), ())), preferred_element_type=jnp.float32)


def thirds(columns, times=1):
    wide = columns // times // 1024 * 384
    return list(zip((wide, wide, columns // times - 2 * wide) * times, ORDERS * times))


def shards(
    hidden_in,
    cluster_lengths,
    norm_gain,
    in_proj,
    conv_weight,
    conv_bias,
    x_proj,
    dt_proj,
    dt_bias,
    a_log,
    skip_gain,
    out_proj,
    out_grad,
):
    f32, bf16 = jnp.float32, jnp.bfloat16
    taps, share = conv_weight.shape
    rank_dim = dt_proj.shape[0]
    state_dim = a_log.shape[0]
    contexts_here, total_len, model_dim = hidden_in.shape
    rows = contexts_here * total_len
    columns = rank_dim + 2 * state_dim
    offsets = cluster_offsets(cluster_lengths, total_len).reshape(rows)
    offset = jnp.broadcast_to(offsets[:, None], (rows, 128))
    grad_rows = out_grad.reshape(rows, model_dim)
    gain_part = jnp.pad(norm_gain, (0, share - norm_gain.shape[0]))
    vectors = jnp.concatenate([gain_part, conv_bias, dt_bias, skip_gain]).reshape(-1, 128)
    x = hidden_in.reshape(rows, model_dim)
    (normed16, w_dt, xp, rate2, params, gain), w_out, w_in, d_gated, both = gather_weights(
        x, grad_rows, (dt_proj, a_log, conv_weight, vectors, x_proj.T), out_proj, in_proj
    )
    inner_dim = params.shape[1]
    parts = lax.axis_size("fsdp")
    *saved, gated16, gate16, proj, b_wide, c_wide, kept, end, skip_sums = scan_forward(
        both, d_gated, offset, params, xp, w_dt, rate2, CHUNK, WIDTH
    )
    g_w_out = dot32(gated16, grad_rows, ((0,), (0,))).astype(bf16)
    g_w_gate = dot32(normed16, gate16, ((0,), (0,))).astype(bf16)
    (upper16, small), (t_out, t_gate) = scan_backward(
        saved, both, offset, proj, b_wide, c_wide, kept, end, params, xp, w_dt, rate2, skip_sums, CHUNK, WIDTH,
        [g_w_out, g_w_gate], [thirds(model_dim), thirds(inner_dim)],
    )
    g_w_upper = dot32(normed16, upper16, ((0,), (0,))).astype(bf16)
    gain_row = columns + rank_dim + state_dim + taps + 3
    t_upper, t_small, layer_out, input_grad = finish(
        g_w_upper, small, upper16, gate16, gated16, w_in, w_out, x, grad_rows,
        gain, [thirds(inner_dim, 2), [(inner_dim // parts, ORDERS[2])]], gain_row,
    )
    t_in, t_out, t_x, t_dt, t_alog, t_conv, t_b_conv, t_b_dt, t_skip, t_gain, layer_out, input_grad = write_outputs(
        t_upper, t_gate, t_out, t_small, layer_out, input_grad,
        (columns, rank_dim, state_dim, taps, 1, 1, 1, model_dim // parts),
    )
    return (
        layer_out.reshape(hidden_in.shape),
        input_grad.reshape(hidden_in.shape),
        t_gain[0],
        t_in,
        t_conv,
        t_b_conv[0],
        t_x.T,
        t_dt,
        t_b_dt[0],
        t_alog,
        t_skip[0],
        t_out,
    )


def solution(mesh):
    placed = (
        P(("dp", "fsdp"), None, None),
        P(("dp", "fsdp"), None),
        P("fsdp"),
        P("fsdp", None),
        P(None, "fsdp"),
        P("fsdp"),
        P("fsdp", None),
        P(None, "fsdp"),
        P("fsdp"),
        P(None, "fsdp"),
        P("fsdp"),
        P("fsdp", None),
        P(("dp", "fsdp"), None, None),
    )
    return jax.shard_map(
        shards,
        mesh=mesh,
        in_specs=placed,
        out_specs=(
            P(("dp", "fsdp"), None, None),
            P(("dp", "fsdp"), None, None),
            P("fsdp"),
            P("fsdp", None),
            P(None, "fsdp"),
            P("fsdp"),
            P("fsdp", None),
            P(None, "fsdp"),
            P("fsdp"),
            P(None, "fsdp"),
            P("fsdp"),
            P("fsdp", None),
        ),
        check_vma=False,
    )
```

```python
import functools
import math

import jax
import jax.numpy as jnp
from jax import lax
from jax.experimental import pallas as pl
from jax.experimental.pallas import tpu as pltpu
from jax.sharding import PartitionSpec as P

CHUNK = 64
WIDTH = 4
norm_eps = 1e-05
BIG = 1e30
LN2 = math.log(2.0)
LOG2E = 1.0 / LN2

def bits_of(size):
    return size.bit_length() - 1


ORDERS = ((0, 1, 2, 3), (1, 2, 0, 3), (2, 0, 1, 3))


class Reduction:
    def __init__(self, outer, inner, shapes, parts):
        self.outer_bits, self.inner_bits = bits_of(outer), bits_of(inner)
        self.blocks, self.inner = outer * inner, inner
        self.shapes = [(self.blocks, s[0] // self.blocks, s[1]) for s in shapes]
        self.stages = self.outer_bits + self.inner_bits
        self.steps = self.stages + self.inner_bits
        self.pieces = []
        for i, s in enumerate(shapes):
            at = 0
            for columns, order in parts[i]:
                order = [b for b in order if b < self.inner_bits] + list(range(len(order), self.inner_bits))
                self.pieces.append((i, pl.ds(at, columns), order))
                at += columns
            assert at == s[1]

    def axis_bit(self, piece, stage):
        if stage < self.outer_bits:
            return "fsdp", self.outer_bits - 1 - stage
        return "dp", self.pieces[piece][2][stage - self.outer_bits]

    def mine(self, piece, stage):
        axis, bit = self.axis_bit(piece, stage)
        return (lax.axis_index(axis) // (1 << bit)) % 2

    def partner(self, axis, bit):
        here = lax.axis_index(axis)
        return {axis: here + (1 << bit) - (here // (1 << bit)) % 2 * (2 << bit)}

    def barrier(self):
        sem = pltpu.get_barrier_semaphore()
        for axis, bits in (("fsdp", self.outer_bits), ("dp", self.inner_bits)):
            for bit in range(bits):
                pl.semaphore_signal(sem, inc=1, device_id=self.partner(axis, bit), device_id_type=pl.DeviceIdType.MESH)
        pl.semaphore_wait(sem, self.stages)

    def low(self, piece, stage):
        low = 0
        for s in range(1, stage):
            low = low + self.mine(piece, s) * (self.blocks >> (s + 1))
        return low

    def place(self, piece, stages):
        at = 0
        for j in range(stages):
            at = at + self.mine(piece, self.outer_bits + j) * (1 << (self.inner_bits - 1 - j))
        return at

    def bind(self, given, out, scratch):
        n = len(self.shapes)
        self.given, self.out = given, out
        self.work, self.inbox, self.result = scratch[:n], scratch[n : 2 * n], scratch[2 * n : 3 * n]
        self.send, self.recv, self.near = scratch[3 * n :]

    def scratch(self):
        b16, k = jnp.bfloat16, len(self.pieces)
        return (
            [pltpu.VMEM((b // 2, r, c), b16) for b, r, c in self.shapes]
            + [pltpu.VMEM((b, r, c), b16) for b, r, c in self.shapes]
            + [pltpu.VMEM((self.inner, r, c), b16) for b, r, c in self.shapes]
            + [pltpu.SemaphoreType.DMA((k, self.steps)), pltpu.SemaphoreType.DMA((k, self.steps)), pltpu.SemaphoreType.DMA((k,))]
        )

    def copy(self, piece, step):
        i, columns, _ = self.pieces[piece]
        if step < self.stages:
            stage = step
            half = self.blocks >> (step + 1)
            other = (1 - self.mine(piece, step)) * half
            if step == 0:
                source = self.given[i].at[pl.ds(other, half), :, columns]
            else:
                source = self.work[i].at[pl.ds(self.low(piece, step) + other, half), :, columns]
            target = self.inbox[i].at[pl.ds(self.blocks - 2 * half, half), :, columns]
        else:
            stage = self.steps - 1 - step + self.outer_bits
            j = stage - self.outer_bits
            many = 1 << (self.inner_bits - 1 - j)
            source = target = self.result[i].at[pl.ds(self.place(piece, j + 1), many), :, columns]
        return pltpu.make_async_remote_copy(
            src_ref=source,
            dst_ref=target,
            send_sem=self.send.at[piece, step],
            recv_sem=self.recv.at[piece, step],
            device_id=self.partner(*self.axis_bit(piece, stage)),
            device_id_type=pl.DeviceIdType.MESH,
        )

    def own(self, piece):
        i, columns, _ = self.pieces[piece]
        half = self.blocks // 2
        source = self.given[i].at[pl.ds(self.mine(piece, 0) * half, half), :, columns]
        return pltpu.make_async_copy(source, self.work[i].at[:, :, columns], self.near.at[piece])

    def leave(self, piece):
        i, columns, _ = self.pieces[piece]
        return pltpu.make_async_copy(self.result[i].at[:, :, columns], self.out[i].at[:, :, columns], self.near.at[piece])

    def add(self, piece, stage):
        i, columns, _ = self.pieces[piece]
        work, inbox, result = self.work[i], self.inbox[i], self.result[i]
        half = self.blocks >> (stage + 1)
        arrived = self.blocks - 2 * half
        base = 0 if stage == 0 else self.low(piece, stage) + self.mine(piece, stage) * half

        @pl.loop(0, half)
        def _(k):
            new = work[base + k, :, columns].astype(jnp.float32) + inbox[arrived + k, :, columns].astype(jnp.float32)
            if stage == self.stages - 1:
                result[self.place(piece, self.inner_bits), :, columns] = new.astype(jnp.bfloat16)
            else:
                work[base + k, :, columns] = new.astype(jnp.bfloat16)

    def start(self, pieces):
        for p in pieces:
            self.copy(p, 0).start()
        for p in pieces:
            self.own(p).start()

    def advance(self, pieces, step):
        for p in pieces:
            if step == 0:
                self.own(p).wait()
            self.copy(p, step).wait()
            if step < self.stages:
                self.add(p, step)
            if step + 1 < self.steps:
                self.copy(p, step + 1).start()
            else:
                self.leave(p).start()

    def gone(self, pieces):
        for p in pieces:
            self.leave(p).wait()

    def times(self, count):
        heavy = (18.0, 10.0, 6.5, 14.0)
        there = [heavy[min(j, 3)] for j in range(self.inner_bits)]
        loads = [11.0] * self.outer_bits + there + there[::-1]
        total, at, out = sum(loads), 0.0, []
        for load in loads[:-1]:
            at += load
            out.append(max(1, min(count - 1, round(at / total * count))))
        return out


def reduction_of(arrays, parts):
    plan = Reduction(lax.axis_size("fsdp"), lax.axis_size("dp"), [a.shape for a in arrays], parts)
    shaped = [a.reshape(s) for a, s in zip(arrays, plan.shapes)]
    out = [jax.ShapeDtypeStruct((plan.inner,) + s[1:], jnp.bfloat16) for s in plan.shapes]
    return plan, shaped, out


class Exchange:
    def __init__(self, size):
        self.size = size

    def owner(self, turn):
        return (lax.axis_index("fsdp") + self.size - turn) % self.size

    def peer(self, turn):
        return {"fsdp": (lax.axis_index("fsdp") + turn) % self.size}

    def barrier(self):
        sem = pltpu.get_barrier_semaphore()
        for turn in range(1, self.size):
            pl.semaphore_signal(sem, inc=1, device_id=self.peer(turn), device_id_type=pl.DeviceIdType.MESH)
        pl.semaphore_wait(sem, self.size - 1)

    def copy(self, source, target, sems, which, turn):
        if turn == 0:
            return pltpu.make_async_copy(source, target, sems[1].at[which, 0])
        return pltpu.make_async_remote_copy(
            src_ref=source,
            dst_ref=target,
            send_sem=sems[0].at[which, turn],
            recv_sem=sems[1].at[which, turn],
            device_id=self.peer(turn),
            device_id_type=pl.DeviceIdType.MESH,
        )


def gather_kernel(
    x_ref, go_ref, dt_ref, rate_ref, taps_ref, vec_ref, xp_ref, wout_ref, win_ref,
    normed_ref, dtw_ref, xpw_ref, decay_ref, par_ref, gain_ref, wout_out, win_out, dg_out, both_out,
    pack, wout, win, dg, both, packed, send, recv, leave, tiles, *, plan
):
    f32, bf16 = jnp.float32, jnp.bfloat16
    rows, model = x_ref.shape
    deep, wide, share = model // plan.size, both.shape[1], packed.shape[1]
    me = lax.axis_index("fsdp")
    sems = (send, recv)

    def copies(which, turn):
        source = (packed, wout_ref, win_ref)[which]
        if which == 0:
            target = pack.at[:, pl.ds(pl.multiple_of(me * share, 128), share)]
        else:
            target = (wout, win)[which - 1].at[me]
        return plan.copy(source, target, sems, which, turn)

    lines = share // 128
    vectors = vec_ref[...].astype(f32)
    line = [
        jnp.concatenate([vectors[k : k + 1] for k in range(v * lines, (v + 1) * lines)], axis=1) for v in range(4)
    ]
    few = [line[0], taps_ref[...].astype(f32)] + line[1:]
    depth, states, taps = dt_ref.shape[0], rate_ref.shape[0], taps_ref.shape[0]
    few.append(jnp.zeros((16 - 4 - taps, share), f32))
    packed[0:depth, :] = dt_ref[...]
    packed[depth : depth + states, :] = rate_ref[...]
    packed[depth + states : depth + states + 16, :] = jnp.concatenate(few, axis=0).astype(bf16)
    packed[depth + states + 16 :, :] = xp_ref[...]
    plan.barrier()
    for which in range(3):
        for turn in range(1, plan.size):
            copies(which, turn).start()
    for which in (1, 0, 2):
        copies(which, 0).start()

    def times_out(turn):
        at = plan.owner(turn)

        @pl.loop(0, share // 256)
        def _(k):
            here = pl.ds(pl.multiple_of(at * share + k * 256, 128), 256)
            dg[:, here] = lax.dot_general(
                go_ref[...], wout[at, pl.ds(pl.multiple_of(k * 256, 256), 256), :],
                (((1,), (1,)), ((), ())), preferred_element_type=f32,
            )
        pltpu.make_async_copy(wout.at[at], wout_out.at[at], leave.at[0, turn]).start()
        part = pl.ds(pl.multiple_of(at * share, 128), share)
        pltpu.make_async_copy(dg.at[:, part], dg_out.at[:, part], leave.at[2, turn]).start()

    def times_in(turn):
        at = plan.owner(turn)
        left = pl.ds(pl.multiple_of(at * deep, 128), deep)

        @pl.loop(0, wide // 256)
        def _(k):
            here = pl.ds(pl.multiple_of(k * 256, 256), 256)
            new = jnp.dot(normed_ref[:, left], win[at, :, here], preferred_element_type=f32)
            both[:, here] = new if turn == 0 else both[:, here] + new
            if turn == plan.size - 1:
                pltpu.make_async_copy(both.at[:, here], both_out.at[:, here], tiles.at[k]).start()
        pltpu.make_async_copy(win.at[at], win_out.at[at], leave.at[1, turn]).start()

    copies(1, 0).wait()
    times_out(0)
    for turn in range(plan.size):
        copies(0, turn).wait()
    dtw_ref[...] = pack[0:depth, :]
    xpw_ref[...] = pack[depth + states + 16 :, :]
    decay_ref[...] = -jnp.exp(pack[depth : depth + states, :].astype(f32)) * LOG2E
    few = pack[depth + states : depth + states + 16, :].astype(f32)
    par_ref[...] = few[1:9]
    gain = jnp.concatenate([few[:1, b * share : b * share + deep] for b in range(plan.size)], axis=1)
    gain_ref[...] = jnp.broadcast_to(gain, gain_ref.shape)

    @pl.loop(0, rows // 64)
    def _(k):
        here = pl.ds(pl.multiple_of(k * 64, 64), 64)
        x = x_ref[here, :].astype(f32)
        mean_sq = jnp.mean(x * x, axis=-1, keepdims=True)
        normed_ref[here, :] = (x * lax.rsqrt(mean_sq + norm_eps) * gain).astype(bf16)

    copies(2, 0).wait()
    times_in(0)
    for turn in range(1, plan.size):
        copies(1, turn).wait()
        times_out(turn)
    for turn in range(1, plan.size):
        copies(2, turn).wait()
        times_in(turn)
    for turn in range(plan.size):
        at = plan.owner(turn)
        part = pl.ds(pl.multiple_of(at * share, 128), share)
        pltpu.make_async_copy(wout.at[at], wout_out.at[at], leave.at[0, turn]).wait()
        pltpu.make_async_copy(win.at[at], win_out.at[at], leave.at[1, turn]).wait()
        pltpu.make_async_copy(dg.at[:, part], dg_out.at[:, part], leave.at[2, turn]).wait()

    @pl.loop(0, wide // 256)
    def _(k):
        here = pl.ds(pl.multiple_of(k * 256, 256), 256)
        pltpu.make_async_copy(both.at[:, here], both_out.at[:, here], tiles.at[k]).wait()


def gather_weights(x, grad_rows, small, w_out, w_in):
    f32, bf16 = jnp.float32, jnp.bfloat16
    plan = Exchange(lax.axis_size("fsdp"))
    n, (rows, model), wide = plan.size, x.shape, w_in.shape[1]
    (rank, share), states, cols = small[0].shape, small[1].shape[0], small[4].shape[0]
    inner = n * share
    anywhere = pl.BlockSpec(memory_space=pl.ANY)
    near = pl.BlockSpec(memory_space=pltpu.VMEM)
    shapes = [
        ((rank + states + 16 + cols, inner), bf16), ((n,) + w_out.shape, bf16), ((n,) + w_in.shape, bf16), ((rows, inner), f32), ((rows, wide), f32),
    ]
    outs = [
        (x.shape, bf16), ((rank, inner), bf16), ((cols, inner), bf16), ((states, inner), f32), ((8, inner), f32), ((8, model), f32),
    ]
    *made, out_all, in_all, d_gated, both = pl.pallas_call(
        functools.partial(gather_kernel, plan=plan),
        out_shape=[jax.ShapeDtypeStruct(*s) for s in outs + shapes[1:]],
        in_specs=[near] * 7 + [anywhere] * 2,
        out_specs=[near] * 6 + [anywhere] * 4,
        scratch_shapes=[pltpu.VMEM(*s) for s in shapes]
        + [
            pltpu.VMEM((shapes[0][0][0], share), bf16),
            pltpu.SemaphoreType.DMA((3, n)),
            pltpu.SemaphoreType.DMA((3, n)),
            pltpu.SemaphoreType.DMA((3, n)),
            pltpu.SemaphoreType.DMA((wide // 256,)),
        ],
        compiler_params=pltpu.CompilerParams(collective_id=2, has_side_effects=True, vmem_limit_bytes=56 << 20),
        name="gather_weights",
    )(x, grad_rows, *small, w_out, w_in)
    return made, out_all.reshape(-1, w_out.shape[1]), in_all.reshape(-1, wide), d_gated, both


TAPS, SHIFT, DT_BIAS, SKIP = 0, 4, 5, 6


def rows_of(ref, tile, row, width):
    return [ref[tile + j, pl.ds(row, 8, stride=0), :] for j in range(width)]


def by_eights(ref, tile):
    total = ref[tile, pl.ds(0, 8, stride=8), :]
    for s in range(1, 8):
        total = total + ref[tile, pl.ds(s, 8, stride=8), :]
    return total


def folded(x):
    total = x[:8]
    for s in range(8, x.shape[0], 8):
        total = total + x[s : s + 8]
    return total


def spread(proj, first, wide, states):
    for t in range(proj.shape[1]):
        wide[pl.ds(t * states, states), :] = jnp.broadcast_to(proj[first : first + states, t : t + 1], (states, 128))


def forward_kernel(
    upper_ref, z_ref, dg_ref, off_ref, par_ref, xp_ref, dtw_ref, a_ref,
    u_ref, ds_ref, dt_ref, sg_ref, dy_ref, gated_ref, gate_ref, proj_ref, wide_b, wide_c, kept_ref, end_ref, skip_ref,
    hs, ext, u16, dtm, dtu, ys, ybuf, *, width
):
    f32, bf16 = jnp.float32, jnp.bfloat16
    rows, inner = upper_ref.shape
    states, rank = a_ref.shape[0], dtw_ref.shape[0]
    tiles = inner // 128

    @pl.when(pl.program_id(0) == 0)
    def _():
        hs[...] = jnp.zeros_like(hs)
        skip_ref[...] = jnp.zeros_like(skip_ref)
        ext[pl.ds(0, 8), :] = jnp.zeros((8, inner), f32)

    @pl.loop(0, tiles, unroll=True)
    def _(k):
        lanes = pl.ds(pl.multiple_of(k * 128, 128), 128)
        now = upper_ref[:, lanes]
        ext[pl.ds(8, rows), lanes] = now
        conv = par_ref[SHIFT : SHIFT + 1, lanes] + par_ref[TAPS + 3 : TAPS + 4, lanes] * now
        for lag in range(1, 4):
            before = ext[pl.ds(8 - lag, rows), lanes]
            conv = conv + par_ref[TAPS + 3 - lag : TAPS + 4 - lag, lanes] * jnp.where(off_ref[...] >= lag, before, 0.0)
        sig = jax.nn.sigmoid(conv)
        act = conv * sig
        u_ref[:, lanes] = act
        u16[:, lanes] = act.astype(bf16)
        ds_ref[:, lanes] = sig * (1.0 + conv * (1.0 - sig))
        ext[pl.ds(0, 8), lanes] = now[rows - 8 :]

    proj = lax.dot_general(xp_ref[...], u16[...], (((1,), (1,)), ((), ())), preferred_element_type=f32)
    proj_ref[0] = proj
    spread(proj, rank, wide_b, states)
    spread(proj, rank + states, wide_c, states)
    rank16 = proj[:rank].astype(bf16)

    @pl.loop(0, tiles // 2, unroll=True)
    def _(k):
        pair = pl.ds(pl.multiple_of(k * 256, 256), 256)
        pre = lax.dot_general(rank16, dtw_ref[:, pair], (((0,), (0,)), ((), ())), preferred_element_type=f32)
        pre = pre + par_ref[DT_BIAS : DT_BIAS + 1, pair]
        small = jnp.exp(-jnp.abs(pre))
        delta = jnp.maximum(pre, 0.0) + jnp.log1p(small)
        dt_ref[:, pair] = delta
        sg_ref[:, pair] = jnp.where(pre >= 0, 1.0, small) / (1.0 + small)
        grown = delta * u_ref[:, pair]
        for j in range(2):
            part = slice(128 * j, 128 * j + 128)
            dtm[2 * k + j] = jnp.where(off_ref[...] > 0, delta[:, part], BIG)
            dtu[2 * k + j] = grown[:, part]

    @pl.loop(0, tiles // width)
    def _(cb):
        tile = cb * width
        base = pl.multiple_of(cb * 128 * width, 128 * width)
        rate = [[a_ref[pl.ds(8 * s, 8), pl.ds(base + 128 * j, 128)] for s in range(2)] for j in range(width)]

        def body(g, h):
            h = [list(p) for p in zip(h[:width], h[width:])]
            r0 = pl.multiple_of(g * 8, 8)
            for t in range(8):
                d = rows_of(dtm, tile, r0 + t, width)
                x = rows_of(dtu, tile, r0 + t, width)
                bt = [wide_b[pl.ds((r0 + t) * 16 + 8 * s, 8), :] for s in range(2)]
                ct = [wide_c[pl.ds((r0 + t) * 16 + 8 * s, 8), :] for s in range(2)]
                for j in range(width):
                    kept_ref[tile + j, pl.ds((r0 + t) * 16, 16), :] = jnp.concatenate(h[j], axis=0).astype(bf16)
                    for s in range(2):
                        h[j][s] = jnp.exp2(d[j] * rate[j][s]) * h[j][s] + x[j] * bt[s]
                    ybuf[j, pl.ds(t * 8, 8), :] = ct[0] * h[j][0] + ct[1] * h[j][1]
            for j in range(width):
                ys[tile + j, pl.ds(r0, 8), :] = by_eights(ybuf, j)
            return tuple(p[0] for p in h) + tuple(p[1] for p in h)

        h = tuple(hs[pl.ds(8 * s, 8), pl.ds(base + 128 * j, 128)] for s in range(2) for j in range(width))
        h = lax.fori_loop(0, rows // 8, body, h, unroll=4)
        for s in range(2):
            for j in range(width):
                hs[pl.ds(8 * s, 8), pl.ds(base + 128 * j, 128)] = h[s * width + j]
    end_ref[...] = hs[...]

    @pl.loop(0, tiles, unroll=True)
    def _(k):
        lanes = pl.ds(pl.multiple_of(k * 128, 128), 128)
        act, z, dg = u_ref[:, lanes], z_ref[:, lanes], dg_ref[:, lanes]
        full = ys[k] + par_ref[SKIP : SKIP + 1, lanes] * act
        sig = jax.nn.sigmoid(z)
        silu = z * sig
        gated_ref[:, lanes] = (full * silu).astype(bf16)
        dy = dg * silu
        dy_ref[:, lanes] = dy
        gate_ref[:, lanes] = (dg * full * sig * (1.0 + z * (1.0 - sig))).astype(bf16)
        skip_ref[:, lanes] = skip_ref[:, lanes] + folded(dy * act)


def scan_forward(both, d_gated, offset, params, xp, dtw, rate, chunk, width):
    T, DI = d_gated.shape
    n, states, cols = T // chunk, rate.shape[0], xp.shape[0]
    f32, bf16 = jnp.float32, jnp.bfloat16
    row = pl.BlockSpec((chunk, DI), lambda i: (i, 0))
    whole = lambda a: pl.BlockSpec(a.shape, lambda i: (0, 0))
    flat = lambda d: jax.ShapeDtypeStruct((T, DI), d)
    tile = lambda d: pltpu.VMEM((DI // 128, chunk, 128), d)
    return pl.pallas_call(
        functools.partial(forward_kernel, width=width),
        grid=(n,),
        in_specs=[row, pl.BlockSpec((chunk, DI), lambda i: (i, 1)), row, pl.BlockSpec((chunk, 128), lambda i: (i, 0))]
        + [whole(a) for a in (params, xp, dtw, rate)],
        out_specs=[row] * 7
        + [
            pl.BlockSpec((1, cols, chunk), lambda i: (i, 0, 0)),
            pl.BlockSpec((chunk * states, 128), lambda i: (i, 0)),
            pl.BlockSpec((chunk * states, 128), lambda i: (i, 0)),
            pl.BlockSpec((DI // 128, chunk * states, 128), lambda i: (0, i, 0)),
            pl.BlockSpec((states, DI), lambda i: (0, 0)),
            pl.BlockSpec((8, DI), lambda i: (0, 0)),
        ],
        out_shape=[flat(f32)] * 5
        + [flat(bf16)] * 2
        + [
            jax.ShapeDtypeStruct((n, cols, chunk), f32),
            jax.ShapeDtypeStruct((T * states, 128), f32),
            jax.ShapeDtypeStruct((T * states, 128), f32),
            jax.ShapeDtypeStruct((DI // 128, T * states, 128), bf16),
            jax.ShapeDtypeStruct((states, DI), f32),
            jax.ShapeDtypeStruct((8, DI), f32),
        ],
        scratch_shapes=[
            pltpu.VMEM((states, DI), f32),
            pltpu.VMEM((chunk + 8, DI), f32),
            pltpu.VMEM((chunk, DI), bf16),
            tile(f32),
            tile(f32),
            tile(f32),
            pltpu.VMEM((width, 64, 128), f32),
        ],
        compiler_params=pltpu.CompilerParams(dimension_semantics=("arbitrary",), vmem_limit_bytes=62 << 20),
        name="scan_forward",
    )(both, both, d_gated, offset, params, xp, dtw, rate)


def backward_kernel(
    u_ref, ds_ref, dt_ref, sg_ref, dy_ref, upper_ref, off_ref, proj_ref, wide_b, wide_c, kept_ref, end_ref, par_ref, xp_ref, dtw_ref, a_ref, skip_ref,
    *rest, width, plan, total
):
    f32, bf16 = jnp.float32, jnp.bfloat16
    n = len(plan.shapes)
    given, rest = rest[:n], rest[n:]
    (du_ref, small_ref), out, rest = rest[:2], rest[2 : 2 + n], rest[2 + n :]
    ga_ref, gdt_ref, gx_ref, sum_ref, *rest = rest
    ws, ns, dtm, dtu, dyb, sbuf, qbuf, dd, di, u16, dt16, ext, off_ext, wide_db, wide_dc, cols_ref = rest[:16]
    plan.bind(given, out, rest[16:])
    rows, inner = u_ref.shape
    states, rank = a_ref.shape[0], dtw_ref.shape[0]
    tiles = inner // 128
    everything = range(len(plan.pieces))
    times = plan.times(total // rows * (tiles // width))

    @pl.when(pl.program_id(0) == 0)
    def _():
        for ref in (ws, ga_ref, gdt_ref, gx_ref, sum_ref):
            ref[...] = jnp.zeros_like(ref)
        ns[...] = end_ref[...]
        ext[pl.ds(rows, 8), :] = jnp.zeros((8, inner), f32)
        off_ext[pl.ds(rows, 8), :] = jnp.full((8, 128), -1, jnp.int32)
        plan.barrier()
        plan.start(everything)

    proj = proj_ref[0]
    wide_db[...] = jnp.zeros_like(wide_db)
    wide_dc[...] = jnp.zeros_like(wide_dc)

    @pl.loop(0, tiles // width)
    def _(cb):
        tile = cb * width
        base = pl.multiple_of(cb * 128 * width, 128 * width)
        for at in sorted(set(times)):
            @pl.when(pl.program_id(0) * (tiles // width) + cb == at)
            def _():
                for step in range(plan.steps - 1):
                    if times[step] == at:
                        plan.advance(everything, step)

        for j in range(width):
            lanes = pl.ds(base + 128 * j, 128)
            d, act = dt_ref[:, lanes], u_ref[:, lanes]
            dtm[j] = jnp.where(off_ref[...] > 0, d, BIG)
            dtu[j] = d * act
            dyb[j] = dy_ref[:, lanes]
            u16[:, lanes] = act.astype(bf16)
        rate = [[a_ref[pl.ds(8 * s, 8), pl.ds(base + 128 * j, 128)] for s in range(2)] for j in range(width)]

        def body(k, carry):
            r0 = pl.multiple_of((rows // 8 - 1 - k) * 8, 8)
            w = [[carry[s * width + j] for s in range(2)] for j in range(width)]
            ga = [[carry[2 * width + s * width + j] for s in range(2)] for j in range(width)]
            newer = [[carry[4 * width + s * width + j] for s in range(2)] for j in range(width)]
            for t in range(7, -1, -1):
                d = rows_of(dtm, 0, r0 + t, width)
                x = rows_of(dtu, 0, r0 + t, width)
                v = rows_of(dyb, 0, r0 + t, width)
                bt = [wide_b[pl.ds((r0 + t) * 16 + 8 * s, 8), :] for s in range(2)]
                ct = [wide_c[pl.ds((r0 + t) * 16 + 8 * s, 8), :] for s in range(2)]
                db = [None, None]
                dc = [None, None]
                for j in range(width):
                    qs, ss = None, None
                    both = kept_ref[tile + j, pl.ds((r0 + t) * 16, 16), :].astype(f32)
                    for s in range(2):
                        later = newer[j][s]
                        prior = both[8 * s : 8 * s + 8]
                        newer[j][s] = prior
                        g = ct[s] * v[j] + w[j][s]
                        w[j][s] = jnp.exp2(d[j] * rate[j][s]) * g
                        q = w[j][s] * prior
                        ga[j][s] = ga[j][s] + q * d[j]
                        qa = q * rate[j][s]
                        sb = g * bt[s]
                        qs = qa if qs is None else qs + qa
                        ss = sb if ss is None else ss + sb
                        gx = g * x[j]
                        vh = v[j] * later
                        db[s] = gx if db[s] is None else db[s] + gx
                        dc[s] = vh if dc[s] is None else dc[s] + vh
                    qbuf[j, pl.ds(t * 8, 8), :] = qs
                    sbuf[j, pl.ds(t * 8, 8), :] = ss
                for s in range(2):
                    here = pl.ds((r0 + t) * 16 + 8 * s, 8)
                    wide_db[here, :] = wide_db[here, :] + db[s]
                    wide_dc[here, :] = wide_dc[here, :] + dc[s]
            for j in range(width):
                lanes = pl.ds(base + 128 * j, 128)
                here = pl.ds(r0, 8)
                s8 = by_eights(sbuf, j)
                dd[here, lanes] = LN2 * by_eights(qbuf, j) + u_ref[here, lanes] * s8
                di[here, lanes] = dt_ref[here, lanes] * s8
            return tuple(v[j][s] for v in (w, ga, newer) for s in range(2) for j in range(width))

        held = [(r, pl.ds(8 * s, 8), pl.ds(base + 128 * j, 128)) for r in (ws, ga_ref, ns) for s in range(2) for j in range(width)]
        end = lax.fori_loop(0, rows // 8, body, tuple(r[a, b] for r, a, b in held))
        for (r, a, b), value in zip(held, end):
            r[a, b] = value

    for i, ref in enumerate((wide_db, wide_dc)):
        for k in range(states):
            cols_ref[pl.ds(i * rows, rows), pl.ds(128 * k, 128)] = ref[pl.ds(k, rows, stride=states), :].astype(bf16)
    owner = lax.broadcasted_iota(jnp.int32, (states, states * 128), 1) // 128
    picks = jnp.where(owner == lax.broadcasted_iota(jnp.int32, (states, states * 128), 0), 1.0, 0.0).astype(bf16)
    d_bc = lax.dot_general(picks, cols_ref[...], (((1,), (1,)), ((), ())), preferred_element_type=f32)

    @pl.loop(0, tiles, unroll=True)
    def _(k):
        lanes = pl.ds(pl.multiple_of(k * 128, 128), 128)
        low = (dd[:, lanes] * sg_ref[:, lanes]).astype(bf16)
        dt16[:, lanes] = low
        sum_ref[pl.ds(40, 8), lanes] = sum_ref[pl.ds(40, 8), lanes] + folded(low.astype(f32))

    rank16 = proj[:rank].astype(bf16)
    d_rank = lax.dot_general(dtw_ref[...], dt16[...], (((1,), (1,)), ((), ())), preferred_element_type=f32)
    proj16 = jnp.concatenate([d_rank, d_bc[:, :rows], d_bc[:, rows:]], axis=0).astype(bf16)
    off_ext[pl.ds(0, rows), :] = off_ref[...]

    @pl.loop(0, tiles // 2, unroll=True)
    def _(k):
        pair = pl.ds(pl.multiple_of(k * 256, 256), 256)
        dot = lambda a, b, c: lax.dot_general(a, b, ((c, (0,)), ((), ())), preferred_element_type=f32)
        gdt_ref[:, pair] = gdt_ref[:, pair] + dot(rank16, dt16[:, pair], (1,))
        gx_ref[:, pair] = gx_ref[:, pair] + dot(proj16, u16[:, pair], (1,))
        inner_grad = dot(proj16, xp_ref[:, pair], (0,)) + di[:, pair] + dy_ref[:, pair] * par_ref[SKIP : SKIP + 1, pair]
        ext[pl.ds(0, rows), pair] = inner_grad * ds_ref[:, pair]
        for j in range(2):
            lanes = pl.ds(pl.multiple_of(k * 256 + 128 * j, 128), 128)
            now, above = ext[pl.ds(0, rows), lanes], upper_ref[:, lanes]
            grad = par_ref[TAPS + 3 : TAPS + 4, lanes] * now
            sums = [now, now * above]
            for lag in range(1, 4):
                after = jnp.where(off_ext[pl.ds(lag, rows), :] >= lag, ext[pl.ds(lag, rows), lanes], 0.0)
                grad = grad + par_ref[TAPS + 3 - lag : TAPS + 4 - lag, lanes] * after
                sums.append(after * above)
            du_ref[:, lanes] = grad.astype(bf16)
            for at, value in zip((32, 24, 16, 8, 0), sums):
                sum_ref[pl.ds(at, 8), lanes] = sum_ref[pl.ds(at, 8), lanes] + folded(value)
            ext[pl.ds(rows, 8), lanes] = now[:8]

    off_ext[pl.ds(rows, 8), :] = off_ref[pl.ds(0, 8), :]

    @pl.when(pl.program_id(0) == pl.num_programs(0) - 1)
    def _():
        share = small_ref.shape[1]
        deep = small_ref.shape[0] // (inner // share)
        sums = [jnp.sum(sum_ref[pl.ds(8 * k, 8), :], axis=0, keepdims=True) for k in range(6)]
        sums += [jnp.sum(skip_ref[...], axis=0, keepdims=True), jnp.zeros((9, inner), f32)]
        blocks = [gx_ref[...], gdt_ref[...], ga_ref[...] * a_ref[...] * LN2, jnp.concatenate(sums, axis=0)]
        for f in range(inner // share):
            at = f * deep
            for block in blocks:
                small_ref[at : at + block.shape[0], :] = block[:, f * share : (f + 1) * share].astype(bf16)
                at += block.shape[0]
            small_ref[at : (f + 1) * deep, :] = jnp.zeros(((f + 1) * deep - at, share), bf16)
        plan.advance(everything, plan.steps - 1)
        plan.gone(everything)


def scan_backward(saved, both, offset, proj, wide_b, wide_c, kept, end, params, xp, dtw, rate, skip, chunk, width, grads, parts):
    T, DI = saved[0].shape
    n, states, cols, rank = T // chunk, rate.shape[0], xp.shape[0], dtw.shape[0]
    f32, bf16 = jnp.float32, jnp.bfloat16
    row = pl.BlockSpec((chunk, DI), lambda i: (n - 1 - i, 0))
    whole = lambda a: pl.BlockSpec(a.shape, lambda i: (0, 0))
    anywhere = pl.BlockSpec(memory_space=pl.ANY)
    plan, shaped, summed = reduction_of(grads, parts)
    outer, inner = lax.axis_size("fsdp"), lax.axis_size("dp")
    deep = -(-(states + rank + cols + 16) // (16 * inner)) * 16 * inner
    small = jax.ShapeDtypeStruct((outer * deep, DI // outer), bf16)
    pieces = pltpu.VMEM((width, chunk, 128), f32)
    eights = pltpu.VMEM((width, 64, 128), f32)
    tall = pltpu.VMEM((chunk * states, 128), f32)
    out = pl.pallas_call(
        functools.partial(backward_kernel, width=width, plan=plan, total=T),
        grid=(n,),
        in_specs=[row] * 6
        + [
            pl.BlockSpec((chunk, 128), lambda i: (n - 1 - i, 0)),
            pl.BlockSpec((1, cols, chunk), lambda i: (n - 1 - i, 0, 0)),
            pl.BlockSpec((chunk * states, 128), lambda i: (n - 1 - i, 0)),
            pl.BlockSpec((chunk * states, 128), lambda i: (n - 1 - i, 0)),
            pl.BlockSpec((DI // 128, chunk * states, 128), lambda i: (0, n - 1 - i, 0)),
            whole(end),
        ]
        + [whole(a) for a in (params, xp, dtw, rate, skip)]
        + [anywhere] * len(grads),
        out_specs=[row, whole(small)] + [anywhere] * len(grads),
        out_shape=[jax.ShapeDtypeStruct((T, DI), bf16), small] + summed,
        scratch_shapes=[pltpu.VMEM((r, DI), f32) for r in (states, rank, cols, 48)]
        + [
            pltpu.VMEM((states, DI), f32),
            pltpu.VMEM((states, DI), f32),
            pieces,
            pieces,
            pieces,
            eights,
            eights,
            pltpu.VMEM((chunk, DI), f32),
            pltpu.VMEM((chunk, DI), f32),
            pltpu.VMEM((chunk, DI), bf16),
            pltpu.VMEM((chunk, DI), bf16),
            pltpu.VMEM((chunk + 8, DI), f32),
            pltpu.VMEM((chunk + 8, 128), jnp.int32),
            tall,
            tall,
            pltpu.VMEM((2 * chunk, states * 128), bf16),
        ]
        + plan.scratch(),
        compiler_params=pltpu.CompilerParams(
            dimension_semantics=("arbitrary",), collective_id=0, has_side_effects=True, vmem_limit_bytes=56 << 20
        ),
        name="scan_backward",
    )(*saved, both, offset, proj, wide_b, wide_c, kept, end, params, xp, dtw, rate, skip, *shaped)
    return out[:2], [o.reshape(-1, o.shape[-1]) for o in out[2:]]


def finish_kernel(
    small_ref, normed_ref, upper_ref, gate_ref, gated_ref, in_ref, wout_ref, x_ref, go_ref, gain_ref,
    total_ref, few_ref, layer_ref, left_ref, gain_out,
    normed, upper, gate, gated, win, wout, x, go, dn, layer, grads, gain_sum, gain_in, loads, away, gain_send, gain_recv,
    *rest, plan
):
    f32, bf16 = jnp.float32, jnp.bfloat16
    rows, model = x.shape
    inner = upper.shape[1]
    plan.bind([grads, small_ref], [total_ref, few_ref], rest)
    everything = range(len(plan.pieces))
    few = [p for p in everything if plan.pieces[p][0] == 1]
    main = [p for p in everything if plan.pieces[p][0] == 0]
    halves = [main[: len(main) // 2], main[len(main) // 2 :]]

    copies = [
        pltpu.make_async_copy(a, b, loads.at[i])
        for i, (a, b) in enumerate(
            (
                (normed_ref, normed), (upper_ref, upper), (in_ref.at[:, pl.ds(0, inner)], win.at[0]), (gate_ref, gate),
                (in_ref.at[:, pl.ds(inner, inner)], win.at[1]), (x_ref, x), (go_ref, go), (gated_ref, gated), (wout_ref, wout),
            )
        )
    ]

    def gradient(half):
        columns = pl.ds(half * (inner // 2), inner // 2)
        deep = grads.shape[1]

        @pl.loop(0, model // 256)
        def _(k):
            part = normed[:, pl.ds(pl.multiple_of(k * 256, 256), 256)]
            new = lax.dot_general(part, upper[:, columns], (((0,), (0,)), ((), ())), preferred_element_type=f32).astype(bf16)
            for b in range(256 // deep):
                grads[k * (256 // deep) + b, :, columns] = new[b * deep : (b + 1) * deep]

    def product(left, k):
        @pl.loop(0, model // 256)
        def _(j):
            here = pl.ds(pl.multiple_of(j * 256, 256), 256)
            new = lax.dot_general(left[...], win[k, here, :], (((1,), (1,)), ((), ())), preferred_element_type=f32)
            dn[:, here] = new if k == 0 else dn[:, here] + new

    def gain_copy(stage):
        axis, bit = ("fsdp", stage) if stage < plan.outer_bits else ("dp", stage - plan.outer_bits)
        return pltpu.make_async_remote_copy(
            src_ref=gain_sum.at[stage],
            dst_ref=gain_in.at[stage],
            send_sem=gain_send.at[stage],
            recv_sem=gain_recv.at[stage],
            device_id=plan.partner(axis, bit),
            device_id_type=pl.DeviceIdType.MESH,
        )

    def gain_step(stage):
        gain_copy(stage).wait()
        gain_sum[stage + 1] = gain_sum[stage] + gain_in[stage]
        if stage + 1 < plan.stages:
            gain_copy(stage + 1).start()

    for c in copies:
        c.start()
    plan.barrier()
    plan.start(few)
    copies[0].wait()
    copies[1].wait()
    gradient(0)
    plan.start(halves[0])
    gradient(1)
    plan.start(halves[1])
    copies[2].wait()
    plan.advance(halves[0], 0)
    plan.advance(few, 0)
    product(upper, 0)
    plan.advance(halves[1], 0)
    copies[3].wait()
    copies[4].wait()
    product(gate, 1)
    copies[5].wait()
    copies[6].wait()
    plan.advance(halves[0], 1)
    plan.advance(halves[1], 1)
    plan.advance(few, 1)
    gain_sum[0] = jnp.zeros(gain_sum.shape[1:], f32)

    @pl.loop(0, rows // 32)
    def _(k):
        here = pl.ds(pl.multiple_of(k * 32, 32), 32)
        value, grad, gain = x[here, :].astype(f32), dn[here, :], gain_ref[0:1, :]
        scale = lax.rsqrt(jnp.mean(value * value, axis=-1, keepdims=True) + norm_eps)
        through = grad * value
        gain_sum[0] = gain_sum[0] + folded(through * scale)
        pull = jnp.mean(through * gain, axis=-1, keepdims=True) * (scale * scale * scale)
        dn[here, :] = go[here, :].astype(f32) + scale * (grad * gain) - value * pull

    gain_copy(0).start()
    leaving = [pltpu.make_async_copy(dn, left_ref, away.at[0]), pltpu.make_async_copy(layer, layer_ref, away.at[1])]
    leaving[0].start()
    plan.advance(everything, 2)
    copies[7].wait()
    copies[8].wait()

    @pl.loop(0, model // 256)
    def _(j):
        here = pl.ds(pl.multiple_of(j * 256, 256), 256)
        new = x[:, here].astype(f32) + jnp.dot(gated[...], wout[:, here], preferred_element_type=f32)
        layer[:, here] = new.astype(bf16)

    leaving[1].start()
    stage = 0
    for step in range(3, plan.steps):
        plan.advance(everything, step)
        if stage < plan.stages:
            gain_step(stage)
            stage += 1
    while stage < plan.stages:
        gain_step(stage)
        stage += 1
    deep = gain_out.shape[1]
    own = pl.ds(pl.multiple_of(lax.axis_index("fsdp") * deep, 128), deep)
    gain_out[...] = jnp.broadcast_to(jnp.sum(gain_sum[plan.stages, :, own], axis=0, keepdims=True), gain_out.shape)
    plan.gone(everything)
    for c in leaving:
        c.wait()


def finish(small, normed16, upper16, gate16, gated16, w_in, w_out, x, go, gain, parts):
    f32, bf16 = jnp.float32, jnp.bfloat16
    (rows, model), inner = x.shape, upper16.shape[1]
    grads = jax.ShapeDtypeStruct((model, inner), bf16)
    outer = lax.axis_size("fsdp")
    plan = Reduction(outer, lax.axis_size("dp"), [grads.shape, small.shape], parts)
    summed = [jax.ShapeDtypeStruct((plan.inner,) + s[1:], bf16) for s in plan.shapes]
    anywhere = pl.BlockSpec(memory_space=pl.ANY)
    near = pl.BlockSpec(memory_space=pltpu.VMEM)
    flat = pltpu.VMEM((rows, inner), bf16)
    thin = pltpu.VMEM((rows, model), bf16)
    total, few, layer_out, input_grad, gain_total = pl.pallas_call(
        functools.partial(finish_kernel, plan=plan),
        out_shape=summed
        + [
            jax.ShapeDtypeStruct((rows, model), bf16),
            jax.ShapeDtypeStruct((rows, model), f32),
            jax.ShapeDtypeStruct((8, model // outer), f32),
        ],
        in_specs=[anywhere] * 9 + [near],
        out_specs=[anywhere] * 4 + [near],
        scratch_shapes=[
            thin,
            flat,
            flat,
            flat,
            pltpu.VMEM((2, model, inner), bf16),
            pltpu.VMEM((inner, model), bf16),
            thin,
            thin,
            pltpu.VMEM((rows, model), f32),
            thin,
            pltpu.VMEM(plan.shapes[0], bf16),
            pltpu.VMEM((plan.stages + 1, 8, model), f32),
            pltpu.VMEM((plan.stages, 8, model), f32),
            pltpu.SemaphoreType.DMA((9,)),
            pltpu.SemaphoreType.DMA((2,)),
            pltpu.SemaphoreType.DMA((plan.stages,)),
            pltpu.SemaphoreType.DMA((plan.stages,)),
        ]
        + plan.scratch(),
        compiler_params=pltpu.CompilerParams(collective_id=1, has_side_effects=True, vmem_limit_bytes=60 << 20),
        name="finish",
    )(small.reshape(plan.shapes[1]), normed16, upper16, gate16, gated16, w_in, w_out, x, go, gain)
    return total.reshape(-1, total.shape[-1]), few.reshape(-1, few.shape[-1]), layer_out, input_grad, gain_total


def write_kernel(
    upper_ref, gate_ref, out_ref, small_ref, layer_ref, left_ref, gain_ref,
    in_to, out_to, x_to, dt_to, rate_to, taps_to, shift_to, bias_to, skip_to, gain_to, layer_to, left_to,
):
    f32 = jnp.float32
    wide = upper_ref.shape[1]
    in_to[:, 0:wide] = upper_ref[...].astype(f32)
    in_to[:, wide:] = gate_ref[...].astype(f32)
    out_to[...] = out_ref[...].astype(f32)
    layer_to[...] = layer_ref[...]
    left_to[...] = left_ref[...]

    @pl.when(pl.program_id(0) == 0)
    def _():
        at = 0
        for ref in (x_to, dt_to, rate_to):
            ref[...] = small_ref[at : at + ref.shape[0], :].astype(f32)
            at += ref.shape[0]
        few = small_ref[at : at + 16, :].astype(f32)
        at = 0
        gain_to[...] = gain_ref[0:1, :]
        for ref in (taps_to, shift_to, bias_to, skip_to):
            ref[...] = few[at : at + ref.shape[0], : ref.shape[1]]
            at += ref.shape[0]


def write_outputs(upper, gate, out, small, layer, left, gain, sizes):
    f32, share, steps = jnp.float32, small.shape[1], 4
    few = [(r, share) for r in sizes[:-1]] + [(1, sizes[-1])]
    part = lambda a: pl.BlockSpec((a.shape[0] // steps, a.shape[1]), lambda i: (i, 0))
    whole = lambda a: pl.BlockSpec(a.shape, lambda i: (0, 0))
    big = [jax.ShapeDtypeStruct((upper.shape[0], upper.shape[1] + gate.shape[1]), f32), jax.ShapeDtypeStruct(out.shape, f32)]
    few = [jax.ShapeDtypeStruct(a, f32) for a in few]
    last = [jax.ShapeDtypeStruct(a.shape, a.dtype) for a in (layer, left)]
    return pl.pallas_call(
        write_kernel,
        grid=(steps,),
        in_specs=[part(upper), part(gate), part(out), whole(small), part(layer), part(left), whole(gain)],
        out_specs=[part(a) for a in big] + [whole(a) for a in few] + [part(a) for a in last],
        out_shape=big + few + last,
        compiler_params=pltpu.CompilerParams(dimension_semantics=("arbitrary",), vmem_limit_bytes=62 << 20),
        name="write_outputs",
    )(upper, gate, out, small, layer, left, gain)


def cluster_offsets(lengths, total_len):
    count = lengths.shape[1]
    ahead = jnp.arange(count)[:, None] < jnp.arange(count)[None, :]
    start_points = jnp.sum(jnp.where(ahead[None], lengths[:, :, None], 0), axis=1, dtype=jnp.int32)
    end_points = start_points + lengths
    where_at = jnp.arange(total_len, dtype=jnp.int32)
    inside = (where_at[None, None, :] >= start_points[:, :, None]) & (
        where_at[None, None, :] < end_points[:, :, None]
    )
    first_spot = jnp.sum(jnp.where(inside, start_points[:, :, None], 0), axis=1, dtype=jnp.int32)
    return where_at[None, :] - first_spot


def dot32(left, right, contract):
    return lax.dot_general(left, right, (contract, ((), ())), preferred_element_type=jnp.float32)


def thirds(columns, times=1):
    wide = columns // times // 1024 * 384
    return list(zip((wide, wide, columns // times - 2 * wide) * times, ORDERS * times))


def shards(
    hidden_in,
    cluster_lengths,
    norm_gain,
    in_proj,
    conv_weight,
    conv_bias,
    x_proj,
    dt_proj,
    dt_bias,
    a_log,
    skip_gain,
    out_proj,
    out_grad,
):
    f32, bf16 = jnp.float32, jnp.bfloat16
    taps, share = conv_weight.shape
    rank_dim = dt_proj.shape[0]
    state_dim = a_log.shape[0]
    contexts_here, total_len, model_dim = hidden_in.shape
    rows = contexts_here * total_len
    columns = rank_dim + 2 * state_dim
    offsets = cluster_offsets(cluster_lengths, total_len).reshape(rows)
    offset = jnp.broadcast_to(offsets[:, None], (rows, 128))
    grad_rows = out_grad.reshape(rows, model_dim)
    gain_part = jnp.pad(norm_gain, (0, share - norm_gain.shape[0]))
    vectors = jnp.concatenate([gain_part, conv_bias, dt_bias, skip_gain]).reshape(-1, 128)
    x = hidden_in.reshape(rows, model_dim)
    (normed16, w_dt, xp, rate2, params, gain), w_out, w_in, d_gated, both = gather_weights(
        x, grad_rows, (dt_proj, a_log, conv_weight, vectors, x_proj.T), out_proj, in_proj
    )
    inner_dim = params.shape[1]
    parts = lax.axis_size("fsdp")
    *saved, gated16, gate16, proj, b_wide, c_wide, kept, end, skip_sums = scan_forward(
        both, d_gated, offset, params, xp, w_dt, rate2, CHUNK, WIDTH
    )
    g_w_out = dot32(gated16, grad_rows, ((0,), (0,))).astype(bf16)
    g_w_gate = dot32(normed16, gate16, ((0,), (0,))).astype(bf16)
    (upper16, small), (t_out, t_gate) = scan_backward(
        saved, both, offset, proj, b_wide, c_wide, kept, end, params, xp, w_dt, rate2, skip_sums, CHUNK, WIDTH,
        [g_w_out, g_w_gate], [thirds(model_dim), thirds(inner_dim)],
    )
    t_upper, t_small, layer_out, input_grad, t_gain = finish(
        small, normed16, upper16, gate16, gated16, w_in, w_out, x, grad_rows, gain,
        [thirds(inner_dim, 2), [(inner_dim // parts, ORDERS[2])]],
    )
    t_in, t_out, t_x, t_dt, t_alog, t_conv, t_b_conv, t_b_dt, t_skip, t_gain, layer_out, input_grad = write_outputs(
        t_upper, t_gate, t_out, t_small, layer_out, input_grad, t_gain,
        (columns, rank_dim, state_dim, taps, 1, 1, 1, model_dim // parts),
    )
    return (
        layer_out.reshape(hidden_in.shape),
        input_grad.reshape(hidden_in.shape),
        t_gain[0],
        t_in,
        t_conv,
        t_b_conv[0],
        t_x.T,
        t_dt,
        t_b_dt[0],
        t_alog,
        t_skip[0],
        t_out,
    )


def solution(mesh):
    placed = (
        P(("dp", "fsdp"), None, None),
        P(("dp", "fsdp"), None),
        P("fsdp"),
        P("fsdp", None),
        P(None, "fsdp"),
        P("fsdp"),
        P("fsdp", None),
        P(None, "fsdp"),
        P("fsdp"),
        P(None, "fsdp"),
        P("fsdp"),
        P("fsdp", None),
        P(("dp", "fsdp"), None, None),
    )
    return jax.shard_map(
        shards,
        mesh=mesh,
        in_specs=placed,
        out_specs=(
            P(("dp", "fsdp"), None, None),
            P(("dp", "fsdp"), None, None),
            P("fsdp"),
            P("fsdp", None),
            P(None, "fsdp"),
            P("fsdp"),
            P("fsdp", None),
            P(None, "fsdp"),
            P("fsdp"),
            P(None, "fsdp"),
            P("fsdp"),
            P("fsdp", None),
        ),
        check_vma=False,
    )
```

```python
import functools
import math

import jax
import jax.numpy as jnp
from jax import lax
from jax.experimental import pallas as pl
from jax.experimental.pallas import tpu as pltpu
from jax.sharding import PartitionSpec as P

CHUNK = 64
WIDTH = 4
norm_eps = 1e-05
BIG = 1e30
LN2 = math.log(2.0)
LOG2E = 1.0 / LN2

def bits_of(size):
    return size.bit_length() - 1


ORDERS = ((0, 1, 2, 3), (1, 2, 0, 3), (2, 0, 1, 3))


class Reduction:
    def __init__(self, outer, inner, shapes, parts):
        self.outer_bits, self.inner_bits = bits_of(outer), bits_of(inner)
        self.blocks, self.inner = outer * inner, inner
        self.shapes = [(self.blocks, s[0] // self.blocks, s[1]) for s in shapes]
        self.stages = self.outer_bits + self.inner_bits
        self.steps = self.stages + self.inner_bits
        self.pieces = []
        for i, s in enumerate(shapes):
            at = 0
            for columns, order in parts[i]:
                order = [b for b in order if b < self.inner_bits] + list(range(len(order), self.inner_bits))
                self.pieces.append((i, pl.ds(at, columns), order))
                at += columns
            assert at == s[1]

    def axis_bit(self, piece, stage):
        if stage < self.outer_bits:
            return "fsdp", self.outer_bits - 1 - stage
        return "dp", self.pieces[piece][2][stage - self.outer_bits]

    def mine(self, piece, stage):
        axis, bit = self.axis_bit(piece, stage)
        return (lax.axis_index(axis) // (1 << bit)) % 2

    def partner(self, axis, bit):
        here = lax.axis_index(axis)
        return {axis: here + (1 << bit) - (here // (1 << bit)) % 2 * (2 << bit)}

    def barrier(self):
        sem = pltpu.get_barrier_semaphore()
        for axis, bits in (("fsdp", self.outer_bits), ("dp", self.inner_bits)):
            for bit in range(bits):
                pl.semaphore_signal(sem, inc=1, device_id=self.partner(axis, bit), device_id_type=pl.DeviceIdType.MESH)
        pl.semaphore_wait(sem, self.stages)

    def low(self, piece, stage):
        low = 0
        for s in range(1, stage):
            low = low + self.mine(piece, s) * (self.blocks >> (s + 1))
        return low

    def place(self, piece, stages):
        at = 0
        for j in range(stages):
            at = at + self.mine(piece, self.outer_bits + j) * (1 << (self.inner_bits - 1 - j))
        return at

    def bind(self, given, out, scratch):
        n = len(self.shapes)
        self.given, self.out = given, out
        self.work, self.inbox, self.result = scratch[:n], scratch[n : 2 * n], scratch[2 * n : 3 * n]
        self.send, self.recv, self.near = scratch[3 * n :]

    def scratch(self):
        b16, k = jnp.bfloat16, len(self.pieces)
        return (
            [pltpu.VMEM((b // 2, r, c), b16) for b, r, c in self.shapes]
            + [pltpu.VMEM((b, r, c), b16) for b, r, c in self.shapes]
            + [pltpu.VMEM((self.inner, r, c), b16) for b, r, c in self.shapes]
            + [pltpu.SemaphoreType.DMA((k, self.steps)), pltpu.SemaphoreType.DMA((k, self.steps)), pltpu.SemaphoreType.DMA((k,))]
        )

    def copy(self, piece, step):
        i, columns, _ = self.pieces[piece]
        if step < self.stages:
            stage = step
            half = self.blocks >> (step + 1)
            other = (1 - self.mine(piece, step)) * half
            if step == 0:
                source = self.given[i].at[pl.ds(other, half), :, columns]
            else:
                source = self.work[i].at[pl.ds(self.low(piece, step) + other, half), :, columns]
            target = self.inbox[i].at[pl.ds(self.blocks - 2 * half, half), :, columns]
        else:
            stage = self.steps - 1 - step + self.outer_bits
            j = stage - self.outer_bits
            many = 1 << (self.inner_bits - 1 - j)
            source = target = self.result[i].at[pl.ds(self.place(piece, j + 1), many), :, columns]
        return pltpu.make_async_remote_copy(
            src_ref=source,
            dst_ref=target,
            send_sem=self.send.at[piece, step],
            recv_sem=self.recv.at[piece, step],
            device_id=self.partner(*self.axis_bit(piece, stage)),
            device_id_type=pl.DeviceIdType.MESH,
        )

    def own(self, piece):
        i, columns, _ = self.pieces[piece]
        half = self.blocks // 2
        source = self.given[i].at[pl.ds(self.mine(piece, 0) * half, half), :, columns]
        return pltpu.make_async_copy(source, self.work[i].at[:, :, columns], self.near.at[piece])

    def leave(self, piece):
        i, columns, _ = self.pieces[piece]
        return pltpu.make_async_copy(self.result[i].at[:, :, columns], self.out[i].at[:, :, columns], self.near.at[piece])

    def add(self, piece, stage):
        i, columns, _ = self.pieces[piece]
        work, inbox, result = self.work[i], self.inbox[i], self.result[i]
        half = self.blocks >> (stage + 1)
        arrived = self.blocks - 2 * half
        base = 0 if stage == 0 else self.low(piece, stage) + self.mine(piece, stage) * half

        @pl.loop(0, half)
        def _(k):
            new = work[base + k, :, columns].astype(jnp.float32) + inbox[arrived + k, :, columns].astype(jnp.float32)
            if stage == self.stages - 1:
                result[self.place(piece, self.inner_bits), :, columns] = new.astype(jnp.bfloat16)
            else:
                work[base + k, :, columns] = new.astype(jnp.bfloat16)

    def start(self, pieces):
        for p in pieces:
            self.copy(p, 0).start()
        for p in pieces:
            self.own(p).start()

    def advance(self, pieces, step):
        for p in pieces:
            if step == 0:
                self.own(p).wait()
            self.copy(p, step).wait()
            if step < self.stages:
                self.add(p, step)
            if step + 1 < self.steps:
                self.copy(p, step + 1).start()
            else:
                self.leave(p).start()

    def gone(self, pieces):
        for p in pieces:
            self.leave(p).wait()

    def times(self, count):
        heavy = (18.0, 10.0, 6.5, 14.0)
        there = [heavy[min(j, 3)] for j in range(self.inner_bits)]
        loads = [11.0] * self.outer_bits + there + there[::-1]
        total, at, out = sum(loads), 0.0, []
        for load in loads[:-1]:
            at += load
            out.append(max(1, min(count - 1, round(at / total * count))))
        return out


def reduction_of(arrays, parts):
    plan = Reduction(lax.axis_size("fsdp"), lax.axis_size("dp"), [a.shape for a in arrays], parts)
    shaped = [a.reshape(s) for a, s in zip(arrays, plan.shapes)]
    out = [jax.ShapeDtypeStruct((plan.inner,) + s[1:], jnp.bfloat16) for s in plan.shapes]
    return plan, shaped, out


class Exchange:
    def __init__(self, size):
        self.size = size

    def owner(self, turn):
        return (lax.axis_index("fsdp") + self.size - turn) % self.size

    def peer(self, turn):
        return {"fsdp": (lax.axis_index("fsdp") + turn) % self.size}

    def barrier(self):
        sem = pltpu.get_barrier_semaphore()
        for turn in range(1, self.size):
            pl.semaphore_signal(sem, inc=1, device_id=self.peer(turn), device_id_type=pl.DeviceIdType.MESH)
        pl.semaphore_wait(sem, self.size - 1)

    def copy(self, source, target, sems, which, turn):
        if turn == 0:
            return pltpu.make_async_copy(source, target, sems[1].at[which, 0])
        return pltpu.make_async_remote_copy(
            src_ref=source,
            dst_ref=target,
            send_sem=sems[0].at[which, turn],
            recv_sem=sems[1].at[which, turn],
            device_id=self.peer(turn),
            device_id_type=pl.DeviceIdType.MESH,
        )


def gather_kernel(
    x_ref, go_ref, dt_ref, rate_ref, taps_ref, vec_ref, xp_ref, wout_ref, win_ref,
    normed_ref, dtw_ref, xpw_ref, decay_ref, par_ref, gain_ref, wout_out, win_out, dg_out, both_out,
    pack, wout, win, dg, both, packed, send, recv, leave, tiles, *, plan
):
    f32, bf16 = jnp.float32, jnp.bfloat16
    rows, model = x_ref.shape
    deep, wide, share = model // plan.size, both.shape[1], packed.shape[1]
    me = lax.axis_index("fsdp")
    sems = (send, recv)

    def copies(which, turn):
        source = (packed, wout_ref, win_ref)[which]
        if which == 0:
            target = pack.at[:, pl.ds(pl.multiple_of(me * share, 128), share)]
        else:
            target = (wout, win)[which - 1].at[me]
        return plan.copy(source, target, sems, which, turn)

    lines = share // 128
    vectors = vec_ref[...].astype(f32)
    line = [
        jnp.concatenate([vectors[k : k + 1] for k in range(v * lines, (v + 1) * lines)], axis=1) for v in range(4)
    ]
    few = [line[0], taps_ref[...].astype(f32)] + line[1:]
    depth, states, taps = dt_ref.shape[0], rate_ref.shape[0], taps_ref.shape[0]
    few.append(jnp.zeros((16 - 4 - taps, share), f32))
    packed[0:depth, :] = dt_ref[...]
    packed[depth : depth + states, :] = rate_ref[...]
    packed[depth + states : depth + states + 16, :] = jnp.concatenate(few, axis=0).astype(bf16)
    packed[depth + states + 16 :, :] = xp_ref[...]
    plan.barrier()
    for which in range(3):
        for turn in range(1, plan.size):
            copies(which, turn).start()
    for which in (1, 0, 2):
        copies(which, 0).start()

    def times_out(turn):
        at = plan.owner(turn)

        @pl.loop(0, share // 256)
        def _(k):
            here = pl.ds(pl.multiple_of(at * share + k * 256, 128), 256)
            dg[:, here] = lax.dot_general(
                go_ref[...], wout[at, pl.ds(pl.multiple_of(k * 256, 256), 256), :],
                (((1,), (1,)), ((), ())), preferred_element_type=f32,
            )
        pltpu.make_async_copy(wout.at[at], wout_out.at[at], leave.at[0, turn]).start()
        part = pl.ds(pl.multiple_of(at * share, 128), share)
        pltpu.make_async_copy(dg.at[:, part], dg_out.at[:, part], leave.at[2, turn]).start()

    def times_in(turn):
        at = plan.owner(turn)
        left = pl.ds(pl.multiple_of(at * deep, 128), deep)

        @pl.loop(0, wide // 256)
        def _(k):
            here = pl.ds(pl.multiple_of(k * 256, 256), 256)
            new = jnp.dot(normed_ref[:, left], win[at, :, here], preferred_element_type=f32)
            both[:, here] = new if turn == 0 else both[:, here] + new
            if turn == plan.size - 1:
                pltpu.make_async_copy(both.at[:, here], both_out.at[:, here], tiles.at[k]).start()
        pltpu.make_async_copy(win.at[at], win_out.at[at], leave.at[1, turn]).start()

    copies(1, 0).wait()
    times_out(0)
    for turn in range(plan.size):
        copies(0, turn).wait()
    dtw_ref[...] = pack[0:depth, :]
    xpw_ref[...] = pack[depth + states + 16 :, :]
    decay_ref[...] = -jnp.exp(pack[depth : depth + states, :].astype(f32)) * LOG2E
    few = pack[depth + states : depth + states + 16, :].astype(f32)
    par_ref[...] = few[1:9]
    gain = jnp.concatenate([few[:1, b * share : b * share + deep] for b in range(plan.size)], axis=1)
    gain_ref[...] = jnp.broadcast_to(gain, gain_ref.shape)

    @pl.loop(0, rows // 64)
    def _(k):
        here = pl.ds(pl.multiple_of(k * 64, 64), 64)
        x = x_ref[here, :].astype(f32)
        mean_sq = jnp.mean(x * x, axis=-1, keepdims=True)
        normed_ref[here, :] = (x * lax.rsqrt(mean_sq + norm_eps) * gain).astype(bf16)

    copies(2, 0).wait()
    times_in(0)
    for turn in range(1, plan.size):
        copies(1, turn).wait()
        times_out(turn)
    for turn in range(1, plan.size):
        copies(2, turn).wait()
        times_in(turn)
    for turn in range(plan.size):
        at = plan.owner(turn)
        part = pl.ds(pl.multiple_of(at * share, 128), share)
        pltpu.make_async_copy(wout.at[at], wout_out.at[at], leave.at[0, turn]).wait()
        pltpu.make_async_copy(win.at[at], win_out.at[at], leave.at[1, turn]).wait()
        pltpu.make_async_copy(dg.at[:, part], dg_out.at[:, part], leave.at[2, turn]).wait()

    @pl.loop(0, wide // 256)
    def _(k):
        here = pl.ds(pl.multiple_of(k * 256, 256), 256)
        pltpu.make_async_copy(both.at[:, here], both_out.at[:, here], tiles.at[k]).wait()


def gather_weights(x, grad_rows, small, w_out, w_in):
    f32, bf16 = jnp.float32, jnp.bfloat16
    plan = Exchange(lax.axis_size("fsdp"))
    n, (rows, model), wide = plan.size, x.shape, w_in.shape[1]
    (rank, share), states, cols = small[0].shape, small[1].shape[0], small[4].shape[0]
    inner = n * share
    anywhere = pl.BlockSpec(memory_space=pl.ANY)
    near = pl.BlockSpec(memory_space=pltpu.VMEM)
    shapes = [
        ((rank + states + 16 + cols, inner), bf16), ((n,) + w_out.shape, bf16), ((n,) + w_in.shape, bf16), ((rows, inner), f32), ((rows, wide), f32),
    ]
    outs = [
        (x.shape, bf16), ((rank, inner), bf16), ((cols, inner), bf16), ((states, inner), f32), ((8, inner), f32), ((8, model), f32),
    ]
    *made, out_all, in_all, d_gated, both = pl.pallas_call(
        functools.partial(gather_kernel, plan=plan),
        out_shape=[jax.ShapeDtypeStruct(*s) for s in outs + shapes[1:]],
        in_specs=[near] * 7 + [anywhere] * 2,
        out_specs=[near] * 6 + [anywhere] * 4,
        scratch_shapes=[pltpu.VMEM(*s) for s in shapes]
        + [
            pltpu.VMEM((shapes[0][0][0], share), bf16),
            pltpu.SemaphoreType.DMA((3, n)),
            pltpu.SemaphoreType.DMA((3, n)),
            pltpu.SemaphoreType.DMA((3, n)),
            pltpu.SemaphoreType.DMA((wide // 256,)),
        ],
        compiler_params=pltpu.CompilerParams(collective_id=2, has_side_effects=True, vmem_limit_bytes=56 << 20),
        name="gather_weights",
    )(x, grad_rows, *small, w_out, w_in)
    return made, out_all.reshape(-1, w_out.shape[1]), in_all.reshape(-1, wide), d_gated, both


TAPS, SHIFT, DT_BIAS, SKIP = 0, 4, 5, 6


def rows_of(ref, tile, row, width):
    return [ref[tile + j, pl.ds(row, 8, stride=0), :] for j in range(width)]


def by_eights(ref, tile):
    total = ref[tile, pl.ds(0, 8, stride=8), :]
    for s in range(1, 8):
        total = total + ref[tile, pl.ds(s, 8, stride=8), :]
    return total


def folded(x):
    total = x[:8]
    for s in range(8, x.shape[0], 8):
        total = total + x[s : s + 8]
    return total


def spread(proj, first, wide, states):
    for t in range(proj.shape[1]):
        wide[pl.ds(t * states, states), :] = jnp.broadcast_to(proj[first : first + states, t : t + 1], (states, 128))


def forward_kernel(
    upper_ref, z_ref, dg_ref, off_ref, par_ref, xp_ref, dtw_ref, a_ref,
    u_ref, ds_ref, dt_ref, sg_ref, dy_ref, gated_ref, gate_ref, proj_ref, wide_b, wide_c, kept_ref, end_ref, skip_ref,
    hs, ext, u16, dtm, dtu, ys, mix, *, width
):
    f32, bf16 = jnp.float32, jnp.bfloat16
    rows, inner = upper_ref.shape
    states, rank = a_ref.shape[0], dtw_ref.shape[0]
    tiles = inner // 128

    @pl.when(pl.program_id(0) == 0)
    def _():
        hs[...] = jnp.zeros_like(hs)
        skip_ref[...] = jnp.zeros_like(skip_ref)
        ext[pl.ds(0, 8), :] = jnp.zeros((8, inner), f32)

    @pl.loop(0, tiles, unroll=True)
    def _(k):
        lanes = pl.ds(pl.multiple_of(k * 128, 128), 128)
        now = upper_ref[:, lanes]
        ext[pl.ds(8, rows), lanes] = now
        conv = par_ref[SHIFT : SHIFT + 1, lanes] + par_ref[TAPS + 3 : TAPS + 4, lanes] * now
        for lag in range(1, 4):
            before = ext[pl.ds(8 - lag, rows), lanes]
            conv = conv + par_ref[TAPS + 3 - lag : TAPS + 4 - lag, lanes] * jnp.where(off_ref[...] >= lag, before, 0.0)
        sig = jax.nn.sigmoid(conv)
        act = conv * sig
        u_ref[:, lanes] = act
        u16[:, lanes] = act.astype(bf16)
        ds_ref[:, lanes] = sig * (1.0 + conv * (1.0 - sig))
        ext[pl.ds(0, 8), lanes] = now[rows - 8 :]

    proj = lax.dot_general(xp_ref[...], u16[...], (((1,), (1,)), ((), ())), preferred_element_type=f32)
    proj_ref[0] = proj
    spread(proj, rank, wide_b, states)
    spread(proj, rank + states, wide_c, states)
    rank16 = proj[:rank].astype(bf16)
    column = lax.broadcasted_iota(jnp.int32, (states, 8 * states), 1) % states
    tiled = jnp.where(column == lax.broadcasted_iota(jnp.int32, (states, 8 * states), 0), 1.0, 0.0).astype(bf16)
    many = lax.dot_general(
        proj[rank + states :].astype(bf16), tiled, (((0,), (0,)), ((), ())), preferred_element_type=f32
    )
    token = lax.broadcasted_iota(jnp.int32, (rows, 8 * states), 0) % 8
    mine = lax.broadcasted_iota(jnp.int32, (rows, 8 * states), 1) // states == token
    mix[...] = jnp.where(mine, many, 0.0)

    @pl.loop(0, tiles // 2, unroll=True)
    def _(k):
        pair = pl.ds(pl.multiple_of(k * 256, 256), 256)
        pre = lax.dot_general(rank16, dtw_ref[:, pair], (((0,), (0,)), ((), ())), preferred_element_type=f32)
        pre = pre + par_ref[DT_BIAS : DT_BIAS + 1, pair]
        small = jnp.exp(-jnp.abs(pre))
        delta = jnp.maximum(pre, 0.0) + jnp.log1p(small)
        dt_ref[:, pair] = delta
        sg_ref[:, pair] = jnp.where(pre >= 0, 1.0, small) / (1.0 + small)
        grown = delta * u_ref[:, pair]
        for j in range(2):
            part = slice(128 * j, 128 * j + 128)
            dtm[2 * k + j] = jnp.where(off_ref[...] > 0, delta[:, part], BIG)
            dtu[2 * k + j] = grown[:, part]

    @pl.loop(0, tiles // width)
    def _(cb):
        tile = cb * width
        base = pl.multiple_of(cb * 128 * width, 128 * width)
        rate = [[a_ref[pl.ds(8 * s, 8), pl.ds(base + 128 * j, 128)] for s in range(2)] for j in range(width)]

        def body(g, h):
            h = [list(p) for p in zip(h[:width], h[width:])]
            r0 = pl.multiple_of(g * 8, 8)
            low = [jnp.concatenate(h[j], axis=0).astype(bf16) for j in range(width)]
            seen = [[] for _ in range(width)]
            for t in range(8):
                d = rows_of(dtm, tile, r0 + t, width)
                x = rows_of(dtu, tile, r0 + t, width)
                bt = [wide_b[pl.ds((r0 + t) * 16 + 8 * s, 8), :] for s in range(2)]
                for j in range(width):
                    kept_ref[tile + j, pl.ds((r0 + t) * 16, 16), :] = low[j]
                    for s in range(2):
                        h[j][s] = jnp.exp2(d[j] * rate[j][s]) * h[j][s] + x[j] * bt[s]
                    low[j] = jnp.concatenate(h[j], axis=0).astype(bf16)
                    seen[j].append(low[j])
            left = mix[pl.ds(r0, 8), :].astype(bf16)
            for j in range(0, width, 2):
                right = jnp.concatenate([jnp.concatenate(seen[j + k], axis=0) for k in range(2)], axis=1)
                part = jnp.dot(left, right, preferred_element_type=f32)
                for k in range(2):
                    ys[tile + j + k, pl.ds(r0, 8), :] = part[:, 128 * k : 128 * k + 128]
            return tuple(p[0] for p in h) + tuple(p[1] for p in h)

        h = tuple(hs[pl.ds(8 * s, 8), pl.ds(base + 128 * j, 128)] for s in range(2) for j in range(width))
        h = lax.fori_loop(0, rows // 8, body, h, unroll=8)
        for s in range(2):
            for j in range(width):
                hs[pl.ds(8 * s, 8), pl.ds(base + 128 * j, 128)] = h[s * width + j]
    end_ref[...] = hs[...]

    @pl.loop(0, tiles, unroll=True)
    def _(k):
        lanes = pl.ds(pl.multiple_of(k * 128, 128), 128)
        act, z, dg = u_ref[:, lanes], z_ref[:, lanes], dg_ref[:, lanes]
        full = ys[k] + par_ref[SKIP : SKIP + 1, lanes] * act
        sig = jax.nn.sigmoid(z)
        silu = z * sig
        gated_ref[:, lanes] = (full * silu).astype(bf16)
        dy = dg * silu
        dy_ref[:, lanes] = dy
        gate_ref[:, lanes] = (dg * full * sig * (1.0 + z * (1.0 - sig))).astype(bf16)
        skip_ref[:, lanes] = skip_ref[:, lanes] + folded(dy * act)


def scan_forward(both, d_gated, offset, params, xp, dtw, rate, chunk, width):
    T, DI = d_gated.shape
    n, states, cols = T // chunk, rate.shape[0], xp.shape[0]
    f32, bf16 = jnp.float32, jnp.bfloat16
    row = pl.BlockSpec((chunk, DI), lambda i: (i, 0))
    whole = lambda a: pl.BlockSpec(a.shape, lambda i: (0, 0))
    flat = lambda d: jax.ShapeDtypeStruct((T, DI), d)
    tile = lambda d: pltpu.VMEM((DI // 128, chunk, 128), d)
    return pl.pallas_call(
        functools.partial(forward_kernel, width=width),
        grid=(n,),
        in_specs=[row, pl.BlockSpec((chunk, DI), lambda i: (i, 1)), row, pl.BlockSpec((chunk, 128), lambda i: (i, 0))]
        + [whole(a) for a in (params, xp, dtw, rate)],
        out_specs=[row] * 7
        + [
            pl.BlockSpec((1, cols, chunk), lambda i: (i, 0, 0)),
            pl.BlockSpec((chunk * states, 128), lambda i: (i, 0)),
            pl.BlockSpec((chunk * states, 128), lambda i: (i, 0)),
            pl.BlockSpec((DI // 128, chunk * states, 128), lambda i: (0, i, 0)),
            pl.BlockSpec((states, DI), lambda i: (0, 0)),
            pl.BlockSpec((8, DI), lambda i: (0, 0)),
        ],
        out_shape=[flat(f32)] * 5
        + [flat(bf16)] * 2
        + [
            jax.ShapeDtypeStruct((n, cols, chunk), f32),
            jax.ShapeDtypeStruct((T * states, 128), f32),
            jax.ShapeDtypeStruct((T * states, 128), f32),
            jax.ShapeDtypeStruct((DI // 128, T * states, 128), bf16),
            jax.ShapeDtypeStruct((states, DI), f32),
            jax.ShapeDtypeStruct((8, DI), f32),
        ],
        scratch_shapes=[
            pltpu.VMEM((states, DI), f32),
            pltpu.VMEM((chunk + 8, DI), f32),
            pltpu.VMEM((chunk, DI), bf16),
            tile(f32),
            tile(f32),
            tile(f32),
            pltpu.VMEM((chunk, 8 * states), f32),
        ],
        compiler_params=pltpu.CompilerParams(dimension_semantics=("arbitrary",), vmem_limit_bytes=62 << 20),
        name="scan_forward",
    )(both, both, d_gated, offset, params, xp, dtw, rate)


def backward_kernel(
    u_ref, ds_ref, dt_ref, sg_ref, dy_ref, upper_ref, off_ref, proj_ref, wide_b, wide_c, kept_ref, end_ref, par_ref, xp_ref, dtw_ref, a_ref, skip_ref,
    *rest, width, plan, total
):
    f32, bf16 = jnp.float32, jnp.bfloat16
    n = len(plan.shapes)
    given, rest = rest[:n], rest[n:]
    (du_ref, small_ref), out, rest = rest[:2], rest[2 : 2 + n], rest[2 + n :]
    ga_ref, gdt_ref, gx_ref, sum_ref, *rest = rest
    ws, ns, dtm, dtu, dyb, sbuf, qbuf, dd, di, u16, dt16, ext, off_ext, wide_db, wide_dc, cols_ref = rest[:16]
    plan.bind(given, out, rest[16:])
    rows, inner = u_ref.shape
    states, rank = a_ref.shape[0], dtw_ref.shape[0]
    tiles = inner // 128
    everything = range(len(plan.pieces))
    times = plan.times(total // rows * (tiles // width))

    @pl.when(pl.program_id(0) == 0)
    def _():
        for ref in (ws, ga_ref, gdt_ref, gx_ref, sum_ref):
            ref[...] = jnp.zeros_like(ref)
        ns[...] = end_ref[...]
        ext[pl.ds(rows, 8), :] = jnp.zeros((8, inner), f32)
        off_ext[pl.ds(rows, 8), :] = jnp.full((8, 128), -1, jnp.int32)
        plan.barrier()
        plan.start(everything)

    proj = proj_ref[0]
    wide_db[...] = jnp.zeros_like(wide_db)
    wide_dc[...] = jnp.zeros_like(wide_dc)

    @pl.loop(0, tiles // width)
    def _(cb):
        tile = cb * width
        base = pl.multiple_of(cb * 128 * width, 128 * width)
        for at in sorted(set(times)):
            @pl.when(pl.program_id(0) * (tiles // width) + cb == at)
            def _():
                for step in range(plan.steps - 1):
                    if times[step] == at:
                        plan.advance(everything, step)

        for j in range(width):
            lanes = pl.ds(base + 128 * j, 128)
            d, act = dt_ref[:, lanes], u_ref[:, lanes]
            dtm[j] = jnp.where(off_ref[...] > 0, d, BIG)
            dtu[j] = d * act
            dyb[j] = dy_ref[:, lanes]
            u16[:, lanes] = act.astype(bf16)
        rate = [[a_ref[pl.ds(8 * s, 8), pl.ds(base + 128 * j, 128)] for s in range(2)] for j in range(width)]

        def body(k, carry):
            r0 = pl.multiple_of((rows // 8 - 1 - k) * 8, 8)
            w = [[carry[s * width + j] for s in range(2)] for j in range(width)]
            ga = [[carry[2 * width + s * width + j] for s in range(2)] for j in range(width)]
            newer = [[carry[4 * width + s * width + j] for s in range(2)] for j in range(width)]
            for t in range(7, -1, -1):
                d = rows_of(dtm, 0, r0 + t, width)
                x = rows_of(dtu, 0, r0 + t, width)
                v = rows_of(dyb, 0, r0 + t, width)
                bt = [wide_b[pl.ds((r0 + t) * 16 + 8 * s, 8), :] for s in range(2)]
                ct = [wide_c[pl.ds((r0 + t) * 16 + 8 * s, 8), :] for s in range(2)]
                db = [None, None]
                dc = [None, None]
                for j in range(width):
                    qs, ss = None, None
                    both = kept_ref[tile + j, pl.ds((r0 + t) * 16, 16), :].astype(f32)
                    for s in range(2):
                        later = newer[j][s]
                        prior = both[8 * s : 8 * s + 8]
                        newer[j][s] = prior
                        g = ct[s] * v[j] + w[j][s]
                        w[j][s] = jnp.exp2(d[j] * rate[j][s]) * g
                        q = w[j][s] * prior
                        ga[j][s] = ga[j][s] + q * d[j]
                        qa = q * rate[j][s]
                        sb = g * bt[s]
                        qs = qa if qs is None else qs + qa
                        ss = sb if ss is None else ss + sb
                        gx = g * x[j]
                        vh = v[j] * later
                        db[s] = gx if db[s] is None else db[s] + gx
                        dc[s] = vh if dc[s] is None else dc[s] + vh
                    qbuf[j, pl.ds(t * 8, 8), :] = qs
                    sbuf[j, pl.ds(t * 8, 8), :] = ss
                for s in range(2):
                    here = pl.ds((r0 + t) * 16 + 8 * s, 8)
                    wide_db[here, :] = wide_db[here, :] + db[s]
                    wide_dc[here, :] = wide_dc[here, :] + dc[s]
            for j in range(width):
                lanes = pl.ds(base + 128 * j, 128)
                here = pl.ds(r0, 8)
                s8 = by_eights(sbuf, j)
                dd[here, lanes] = LN2 * by_eights(qbuf, j) + u_ref[here, lanes] * s8
                di[here, lanes] = dt_ref[here, lanes] * s8
            return tuple(v[j][s] for v in (w, ga, newer) for s in range(2) for j in range(width))

        held = [(r, pl.ds(8 * s, 8), pl.ds(base + 128 * j, 128)) for r in (ws, ga_ref, ns) for s in range(2) for j in range(width)]
        end = lax.fori_loop(0, rows // 8, body, tuple(r[a, b] for r, a, b in held))
        for (r, a, b), value in zip(held, end):
            r[a, b] = value

    for i, ref in enumerate((wide_db, wide_dc)):
        for k in range(states):
            cols_ref[pl.ds(i * rows, rows), pl.ds(128 * k, 128)] = ref[pl.ds(k, rows, stride=states), :].astype(bf16)
    owner = lax.broadcasted_iota(jnp.int32, (states, states * 128), 1) // 128
    picks = jnp.where(owner == lax.broadcasted_iota(jnp.int32, (states, states * 128), 0), 1.0, 0.0).astype(bf16)
    d_bc = lax.dot_general(picks, cols_ref[...], (((1,), (1,)), ((), ())), preferred_element_type=f32)

    @pl.loop(0, tiles, unroll=True)
    def _(k):
        lanes = pl.ds(pl.multiple_of(k * 128, 128), 128)
        low = (dd[:, lanes] * sg_ref[:, lanes]).astype(bf16)
        dt16[:, lanes] = low
        sum_ref[pl.ds(40, 8), lanes] = sum_ref[pl.ds(40, 8), lanes] + folded(low.astype(f32))

    rank16 = proj[:rank].astype(bf16)
    d_rank = lax.dot_general(dtw_ref[...], dt16[...], (((1,), (1,)), ((), ())), preferred_element_type=f32)
    proj16 = jnp.concatenate([d_rank, d_bc[:, :rows], d_bc[:, rows:]], axis=0).astype(bf16)
    off_ext[pl.ds(0, rows), :] = off_ref[...]

    @pl.loop(0, tiles // 2, unroll=True)
    def _(k):
        pair = pl.ds(pl.multiple_of(k * 256, 256), 256)
        dot = lambda a, b, c: lax.dot_general(a, b, ((c, (0,)), ((), ())), preferred_element_type=f32)
        gdt_ref[:, pair] = gdt_ref[:, pair] + dot(rank16, dt16[:, pair], (1,))
        gx_ref[:, pair] = gx_ref[:, pair] + dot(proj16, u16[:, pair], (1,))
        inner_grad = dot(proj16, xp_ref[:, pair], (0,)) + di[:, pair] + dy_ref[:, pair] * par_ref[SKIP : SKIP + 1, pair]
        ext[pl.ds(0, rows), pair] = inner_grad * ds_ref[:, pair]
        for j in range(2):
            lanes = pl.ds(pl.multiple_of(k * 256 + 128 * j, 128), 128)
            now, above = ext[pl.ds(0, rows), lanes], upper_ref[:, lanes]
            grad = par_ref[TAPS + 3 : TAPS + 4, lanes] * now
            sums = [now, now * above]
            for lag in range(1, 4):
                after = jnp.where(off_ext[pl.ds(lag, rows), :] >= lag, ext[pl.ds(lag, rows), lanes], 0.0)
                grad = grad + par_ref[TAPS + 3 - lag : TAPS + 4 - lag, lanes] * after
                sums.append(after * above)
            du_ref[:, lanes] = grad.astype(bf16)
            for at, value in zip((32, 24, 16, 8, 0), sums):
                sum_ref[pl.ds(at, 8), lanes] = sum_ref[pl.ds(at, 8), lanes] + folded(value)
            ext[pl.ds(rows, 8), lanes] = now[:8]

    off_ext[pl.ds(rows, 8), :] = off_ref[pl.ds(0, 8), :]

    @pl.when(pl.program_id(0) == pl.num_programs(0) - 1)
    def _():
        share = small_ref.shape[1]
        deep = small_ref.shape[0] // (inner // share)
        sums = [jnp.sum(sum_ref[pl.ds(8 * k, 8), :], axis=0, keepdims=True) for k in range(6)]
        sums += [jnp.sum(skip_ref[...], axis=0, keepdims=True), jnp.zeros((9, inner), f32)]
        blocks = [gx_ref[...], gdt_ref[...], ga_ref[...] * a_ref[...] * LN2, jnp.concatenate(sums, axis=0)]
        for f in range(inner // share):
            at = f * deep
            for block in blocks:
                small_ref[at : at + block.shape[0], :] = block[:, f * share : (f + 1) * share].astype(bf16)
                at += block.shape[0]
            small_ref[at : (f + 1) * deep, :] = jnp.zeros(((f + 1) * deep - at, share), bf16)
        plan.advance(everything, plan.steps - 1)
        plan.gone(everything)


def scan_backward(saved, both, offset, proj, wide_b, wide_c, kept, end, params, xp, dtw, rate, skip, chunk, width, grads, parts):
    T, DI = saved[0].shape
    n, states, cols, rank = T // chunk, rate.shape[0], xp.shape[0], dtw.shape[0]
    f32, bf16 = jnp.float32, jnp.bfloat16
    row = pl.BlockSpec((chunk, DI), lambda i: (n - 1 - i, 0))
    whole = lambda a: pl.BlockSpec(a.shape, lambda i: (0, 0))
    anywhere = pl.BlockSpec(memory_space=pl.ANY)
    plan, shaped, summed = reduction_of(grads, parts)
    outer, inner = lax.axis_size("fsdp"), lax.axis_size("dp")
    deep = -(-(states + rank + cols + 16) // (16 * inner)) * 16 * inner
    small = jax.ShapeDtypeStruct((outer * deep, DI // outer), bf16)
    pieces = pltpu.VMEM((width, chunk, 128), f32)
    eights = pltpu.VMEM((width, 64, 128), f32)
    tall = pltpu.VMEM((chunk * states, 128), f32)
    out = pl.pallas_call(
        functools.partial(backward_kernel, width=width, plan=plan, total=T),
        grid=(n,),
        in_specs=[row] * 6
        + [
            pl.BlockSpec((chunk, 128), lambda i: (n - 1 - i, 0)),
            pl.BlockSpec((1, cols, chunk), lambda i: (n - 1 - i, 0, 0)),
            pl.BlockSpec((chunk * states, 128), lambda i: (n - 1 - i, 0)),
            pl.BlockSpec((chunk * states, 128), lambda i: (n - 1 - i, 0)),
            pl.BlockSpec((DI // 128, chunk * states, 128), lambda i: (0, n - 1 - i, 0)),
            whole(end),
        ]
        + [whole(a) for a in (params, xp, dtw, rate, skip)]
        + [anywhere] * len(grads),
        out_specs=[row, whole(small)] + [anywhere] * len(grads),
        out_shape=[jax.ShapeDtypeStruct((T, DI), bf16), small] + summed,
        scratch_shapes=[pltpu.VMEM((r, DI), f32) for r in (states, rank, cols, 48)]
        + [
            pltpu.VMEM((states, DI), f32),
            pltpu.VMEM((states, DI), f32),
            pieces,
            pieces,
            pieces,
            eights,
            eights,
            pltpu.VMEM((chunk, DI), f32),
            pltpu.VMEM((chunk, DI), f32),
            pltpu.VMEM((chunk, DI), bf16),
            pltpu.VMEM((chunk, DI), bf16),
            pltpu.VMEM((chunk + 8, DI), f32),
            pltpu.VMEM((chunk + 8, 128), jnp.int32),
            tall,
            tall,
            pltpu.VMEM((2 * chunk, states * 128), bf16),
        ]
        + plan.scratch(),
        compiler_params=pltpu.CompilerParams(
            dimension_semantics=("arbitrary",), collective_id=0, has_side_effects=True, vmem_limit_bytes=56 << 20
        ),
        name="scan_backward",
    )(*saved, both, offset, proj, wide_b, wide_c, kept, end, params, xp, dtw, rate, skip, *shaped)
    return out[:2], [o.reshape(-1, o.shape[-1]) for o in out[2:]]


def finish_kernel(
    small_ref, normed_ref, upper_ref, gate_ref, gated_ref, in_ref, wout_ref, x_ref, go_ref, gain_ref,
    total_ref, few_ref, layer_ref, left_ref, gain_out,
    normed, upper, gate, gated, win, wout, x, go, dn, layer, grads, gain_sum, gain_in, loads, away, gain_send, gain_recv,
    *rest, plan
):
    f32, bf16 = jnp.float32, jnp.bfloat16
    rows, model = x.shape
    inner = upper.shape[1]
    plan.bind([grads, small_ref], [total_ref, few_ref], rest)
    everything = range(len(plan.pieces))
    few = [p for p in everything if plan.pieces[p][0] == 1]
    main = [p for p in everything if plan.pieces[p][0] == 0]
    halves = [main[: len(main) // 2], main[len(main) // 2 :]]

    copies = [
        pltpu.make_async_copy(a, b, loads.at[i])
        for i, (a, b) in enumerate(
            (
                (normed_ref, normed), (upper_ref, upper), (in_ref.at[:, pl.ds(0, inner)], win.at[0]), (gate_ref, gate),
                (in_ref.at[:, pl.ds(inner, inner)], win.at[1]), (x_ref, x), (go_ref, go), (gated_ref, gated), (wout_ref, wout),
            )
        )
    ]

    def gradient(half):
        columns = pl.ds(half * (inner // 2), inner // 2)
        deep = grads.shape[1]

        @pl.loop(0, model // 256)
        def _(k):
            part = normed[:, pl.ds(pl.multiple_of(k * 256, 256), 256)]
            new = lax.dot_general(part, upper[:, columns], (((0,), (0,)), ((), ())), preferred_element_type=f32).astype(bf16)
            for b in range(256 // deep):
                grads[k * (256 // deep) + b, :, columns] = new[b * deep : (b + 1) * deep]

    def product(left, k, start=0, stop=model // 256):
        @pl.loop(start, stop)
        def _(j):
            here = pl.ds(pl.multiple_of(j * 256, 256), 256)
            new = lax.dot_general(left[...], win[k, here, :], (((1,), (1,)), ((), ())), preferred_element_type=f32)
            dn[:, here] = new if k == 0 else dn[:, here] + new

    def gain_copy(stage):
        axis, bit = ("fsdp", stage) if stage < plan.outer_bits else ("dp", stage - plan.outer_bits)
        return pltpu.make_async_remote_copy(
            src_ref=gain_sum.at[stage],
            dst_ref=gain_in.at[stage],
            send_sem=gain_send.at[stage],
            recv_sem=gain_recv.at[stage],
            device_id=plan.partner(axis, bit),
            device_id_type=pl.DeviceIdType.MESH,
        )

    def gain_step(stage):
        gain_copy(stage).wait()
        gain_sum[stage + 1] = gain_sum[stage] + gain_in[stage]
        if stage + 1 < plan.stages:
            gain_copy(stage + 1).start()

    for c in copies:
        c.start()
    plan.barrier()
    plan.start(few)
    copies[0].wait()
    copies[1].wait()
    gradient(0)
    plan.start(halves[0])
    gradient(1)
    plan.start(halves[1])
    copies[2].wait()
    plan.advance(halves[0], 0)
    plan.advance(few, 0)
    product(upper, 0, 0, model // 512)
    plan.advance(halves[1], 0)
    product(upper, 0, model // 512, model // 256)
    copies[3].wait()
    copies[4].wait()
    product(gate, 1)
    copies[5].wait()
    copies[6].wait()
    plan.advance(halves[0], 1)
    plan.advance(halves[1], 1)
    plan.advance(few, 1)
    gain_sum[0] = jnp.zeros(gain_sum.shape[1:], f32)

    @pl.loop(0, rows // 32)
    def _(k):
        here = pl.ds(pl.multiple_of(k * 32, 32), 32)
        value, grad, gain = x[here, :].astype(f32), dn[here, :], gain_ref[0:1, :]
        scale = lax.rsqrt(jnp.mean(value * value, axis=-1, keepdims=True) + norm_eps)
        through = grad * value
        gain_sum[0] = gain_sum[0] + folded(through * scale)
        pull = jnp.mean(through * gain, axis=-1, keepdims=True) * (scale * scale * scale)
        dn[here, :] = go[here, :].astype(f32) + scale * (grad * gain) - value * pull

    gain_copy(0).start()
    leaving = [pltpu.make_async_copy(dn, left_ref, away.at[0]), pltpu.make_async_copy(layer, layer_ref, away.at[1])]
    leaving[0].start()
    plan.advance(everything, 2)
    copies[7].wait()
    copies[8].wait()

    @pl.loop(0, model // 256)
    def _(j):
        here = pl.ds(pl.multiple_of(j * 256, 256), 256)
        new = x[:, here].astype(f32) + jnp.dot(gated[...], wout[:, here], preferred_element_type=f32)
        layer[:, here] = new.astype(bf16)

    leaving[1].start()
    stage = 0
    for step in range(3, plan.steps):
        plan.advance(everything, step)
        if stage < plan.stages:
            gain_step(stage)
            stage += 1
    while stage < plan.stages:
        gain_step(stage)
        stage += 1
    deep = gain_out.shape[1]
    own = pl.ds(pl.multiple_of(lax.axis_index("fsdp") * deep, 128), deep)
    gain_out[...] = jnp.broadcast_to(jnp.sum(gain_sum[plan.stages, :, own], axis=0, keepdims=True), gain_out.shape)
    plan.gone(everything)
    for c in leaving:
        c.wait()


def finish(small, normed16, upper16, gate16, gated16, w_in, w_out, x, go, gain, parts):
    f32, bf16 = jnp.float32, jnp.bfloat16
    (rows, model), inner = x.shape, upper16.shape[1]
    grads = jax.ShapeDtypeStruct((model, inner), bf16)
    outer = lax.axis_size("fsdp")
    plan = Reduction(outer, lax.axis_size("dp"), [grads.shape, small.shape], parts)
    summed = [jax.ShapeDtypeStruct((plan.inner,) + s[1:], bf16) for s in plan.shapes]
    anywhere = pl.BlockSpec(memory_space=pl.ANY)
    near = pl.BlockSpec(memory_space=pltpu.VMEM)
    flat = pltpu.VMEM((rows, inner), bf16)
    thin = pltpu.VMEM((rows, model), bf16)
    total, few, layer_out, input_grad, gain_total = pl.pallas_call(
        functools.partial(finish_kernel, plan=plan),
        out_shape=summed
        + [
            jax.ShapeDtypeStruct((rows, model), bf16),
            jax.ShapeDtypeStruct((rows, model), f32),
            jax.ShapeDtypeStruct((8, model // outer), f32),
        ],
        in_specs=[anywhere] * 9 + [near],
        out_specs=[anywhere] * 4 + [near],
        scratch_shapes=[
            thin,
            flat,
            flat,
            flat,
            pltpu.VMEM((2, model, inner), bf16),
            pltpu.VMEM((inner, model), bf16),
            thin,
            thin,
            pltpu.VMEM((rows, model), f32),
            thin,
            pltpu.VMEM(plan.shapes[0], bf16),
            pltpu.VMEM((plan.stages + 1, 8, model), f32),
            pltpu.VMEM((plan.stages, 8, model), f32),
            pltpu.SemaphoreType.DMA((9,)),
            pltpu.SemaphoreType.DMA((2,)),
            pltpu.SemaphoreType.DMA((plan.stages,)),
            pltpu.SemaphoreType.DMA((plan.stages,)),
        ]
        + plan.scratch(),
        compiler_params=pltpu.CompilerParams(collective_id=1, has_side_effects=True, vmem_limit_bytes=60 << 20),
        name="finish",
    )(small.reshape(plan.shapes[1]), normed16, upper16, gate16, gated16, w_in, w_out, x, go, gain)
    return total.reshape(-1, total.shape[-1]), few.reshape(-1, few.shape[-1]), layer_out, input_grad, gain_total


def write_kernel(
    upper_ref, gate_ref, out_ref, small_ref, layer_ref, left_ref, gain_ref,
    in_to, out_to, x_to, dt_to, rate_to, taps_to, shift_to, bias_to, skip_to, gain_to, layer_to, left_to,
):
    f32 = jnp.float32
    wide = upper_ref.shape[1]
    in_to[:, 0:wide] = upper_ref[...].astype(f32)
    in_to[:, wide:] = gate_ref[...].astype(f32)
    out_to[...] = out_ref[...].astype(f32)
    layer_to[...] = layer_ref[...]
    left_to[...] = left_ref[...]

    @pl.when(pl.program_id(0) == 0)
    def _():
        at = 0
        for ref in (x_to, dt_to, rate_to):
            ref[...] = small_ref[at : at + ref.shape[0], :].astype(f32)
            at += ref.shape[0]
        few = small_ref[at : at + 16, :].astype(f32)
        at = 0
        gain_to[...] = gain_ref[0:1, :]
        for ref in (taps_to, shift_to, bias_to, skip_to):
            ref[...] = few[at : at + ref.shape[0], : ref.shape[1]]
            at += ref.shape[0]


def write_outputs(upper, gate, out, small, layer, left, gain, sizes):
    f32, share, steps = jnp.float32, small.shape[1], 4
    few = [(r, share) for r in sizes[:-1]] + [(1, sizes[-1])]
    part = lambda a: pl.BlockSpec((a.shape[0] // steps, a.shape[1]), lambda i: (i, 0))
    whole = lambda a: pl.BlockSpec(a.shape, lambda i: (0, 0))
    big = [jax.ShapeDtypeStruct((upper.shape[0], upper.shape[1] + gate.shape[1]), f32), jax.ShapeDtypeStruct(out.shape, f32)]
    few = [jax.ShapeDtypeStruct(a, f32) for a in few]
    last = [jax.ShapeDtypeStruct(a.shape, a.dtype) for a in (layer, left)]
    return pl.pallas_call(
        write_kernel,
        grid=(steps,),
        in_specs=[part(upper), part(gate), part(out), whole(small), part(layer), part(left), whole(gain)],
        out_specs=[part(a) for a in big] + [whole(a) for a in few] + [part(a) for a in last],
        out_shape=big + few + last,
        compiler_params=pltpu.CompilerParams(dimension_semantics=("arbitrary",), vmem_limit_bytes=62 << 20),
        name="write_outputs",
    )(upper, gate, out, small, layer, left, gain)


def cluster_offsets(lengths, total_len):
    count = lengths.shape[1]
    ahead = jnp.arange(count)[:, None] < jnp.arange(count)[None, :]
    start_points = jnp.sum(jnp.where(ahead[None], lengths[:, :, None], 0), axis=1, dtype=jnp.int32)
    end_points = start_points + lengths
    where_at = jnp.arange(total_len, dtype=jnp.int32)
    inside = (where_at[None, None, :] >= start_points[:, :, None]) & (
        where_at[None, None, :] < end_points[:, :, None]
    )
    first_spot = jnp.sum(jnp.where(inside, start_points[:, :, None], 0), axis=1, dtype=jnp.int32)
    return where_at[None, :] - first_spot


def dot32(left, right, contract):
    return lax.dot_general(left, right, (contract, ((), ())), preferred_element_type=jnp.float32)


def thirds(columns, times=1):
    wide = columns // times // 1024 * 384
    return list(zip((wide, wide, columns // times - 2 * wide) * times, ORDERS * times))


def shards(
    hidden_in,
    cluster_lengths,
    norm_gain,
    in_proj,
    conv_weight,
    conv_bias,
    x_proj,
    dt_proj,
    dt_bias,
    a_log,
    skip_gain,
    out_proj,
    out_grad,
):
    f32, bf16 = jnp.float32, jnp.bfloat16
    taps, share = conv_weight.shape
    rank_dim = dt_proj.shape[0]
    state_dim = a_log.shape[0]
    contexts_here, total_len, model_dim = hidden_in.shape
    rows = contexts_here * total_len
    columns = rank_dim + 2 * state_dim
    offsets = cluster_offsets(cluster_lengths, total_len).reshape(rows)
    offset = jnp.broadcast_to(offsets[:, None], (rows, 128))
    grad_rows = out_grad.reshape(rows, model_dim)
    gain_part = jnp.pad(norm_gain, (0, share - norm_gain.shape[0]))
    vectors = jnp.concatenate([gain_part, conv_bias, dt_bias, skip_gain]).reshape(-1, 128)
    x = hidden_in.reshape(rows, model_dim)
    (normed16, w_dt, xp, rate2, params, gain), w_out, w_in, d_gated, both = gather_weights(
        x, grad_rows, (dt_proj, a_log, conv_weight, vectors, x_proj.T), out_proj, in_proj
    )
    inner_dim = params.shape[1]
    parts = lax.axis_size("fsdp")
    *saved, gated16, gate16, proj, b_wide, c_wide, kept, end, skip_sums = scan_forward(
        both, d_gated, offset, params, xp, w_dt, rate2, CHUNK, WIDTH
    )
    g_w_out = dot32(gated16, grad_rows, ((0,), (0,))).astype(bf16)
    g_w_gate = dot32(normed16, gate16, ((0,), (0,))).astype(bf16)
    (upper16, small), (t_out, t_gate) = scan_backward(
        saved, both, offset, proj, b_wide, c_wide, kept, end, params, xp, w_dt, rate2, skip_sums, CHUNK, WIDTH,
        [g_w_out, g_w_gate], [thirds(model_dim), thirds(inner_dim)],
    )
    t_upper, t_small, layer_out, input_grad, t_gain = finish(
        small, normed16, upper16, gate16, gated16, w_in, w_out, x, grad_rows, gain,
        [thirds(inner_dim, 2), [(inner_dim // parts, ORDERS[2])]],
    )
    t_in, t_out, t_x, t_dt, t_alog, t_conv, t_b_conv, t_b_dt, t_skip, t_gain, layer_out, input_grad = write_outputs(
        t_upper, t_gate, t_out, t_small, layer_out, input_grad, t_gain,
        (columns, rank_dim, state_dim, taps, 1, 1, 1, model_dim // parts),
    )
    return (
        layer_out.reshape(hidden_in.shape),
        input_grad.reshape(hidden_in.shape),
        t_gain[0],
        t_in,
        t_conv,
        t_b_conv[0],
        t_x.T,
        t_dt,
        t_b_dt[0],
        t_alog,
        t_skip[0],
        t_out,
    )


def solution(mesh):
    placed = (
        P(("dp", "fsdp"), None, None),
        P(("dp", "fsdp"), None),
        P("fsdp"),
        P("fsdp", None),
        P(None, "fsdp"),
        P("fsdp"),
        P("fsdp", None),
        P(None, "fsdp"),
        P("fsdp"),
        P(None, "fsdp"),
        P("fsdp"),
        P("fsdp", None),
        P(("dp", "fsdp"), None, None),
    )
    return jax.shard_map(
        shards,
        mesh=mesh,
        in_specs=placed,
        out_specs=(
            P(("dp", "fsdp"), None, None),
            P(("dp", "fsdp"), None, None),
            P("fsdp"),
            P("fsdp", None),
            P(None, "fsdp"),
            P("fsdp"),
            P("fsdp", None),
            P(None, "fsdp"),
            P("fsdp"),
            P(None, "fsdp"),
            P("fsdp"),
            P("fsdp", None),
        ),
        check_vma=False,
    )
```

```python
import functools
import math

import jax
import jax.numpy as jnp
from jax import lax
from jax.experimental import pallas as pl
from jax.experimental.pallas import tpu as pltpu
from jax.sharding import PartitionSpec as P

CHUNK = 64
WIDTH = 4
norm_eps = 1e-05
BIG = 1e30
LN2 = math.log(2.0)
LOG2E = 1.0 / LN2

def bits_of(size):
    return size.bit_length() - 1


ORDERS = ((0, 1, 2, 3), (1, 2, 0, 3), (2, 0, 1, 3))


class Reduction:
    def __init__(self, outer, inner, shapes, parts):
        self.outer_bits, self.inner_bits = bits_of(outer), bits_of(inner)
        self.blocks, self.inner = outer * inner, inner
        self.shapes = [(self.blocks, s[0] // self.blocks, s[1]) for s in shapes]
        self.stages = self.outer_bits + self.inner_bits
        self.steps = self.stages + self.inner_bits
        self.pieces = []
        for i, s in enumerate(shapes):
            at = 0
            for columns, order in parts[i]:
                order = [b for b in order if b < self.inner_bits] + list(range(len(order), self.inner_bits))
                self.pieces.append((i, pl.ds(at, columns), order))
                at += columns
            assert at == s[1]

    def axis_bit(self, piece, stage):
        if stage < self.outer_bits:
            return "fsdp", self.outer_bits - 1 - stage
        return "dp", self.pieces[piece][2][stage - self.outer_bits]

    def mine(self, piece, stage):
        axis, bit = self.axis_bit(piece, stage)
        return (lax.axis_index(axis) // (1 << bit)) % 2

    def partner(self, axis, bit):
        here = lax.axis_index(axis)
        return {axis: here + (1 << bit) - (here // (1 << bit)) % 2 * (2 << bit)}

    def barrier(self):
        sem = pltpu.get_barrier_semaphore()
        for axis, bits in (("fsdp", self.outer_bits), ("dp", self.inner_bits)):
            for bit in range(bits):
                pl.semaphore_signal(sem, inc=1, device_id=self.partner(axis, bit), device_id_type=pl.DeviceIdType.MESH)
        pl.semaphore_wait(sem, self.stages)

    def low(self, piece, stage):
        low = 0
        for s in range(1, stage):
            low = low + self.mine(piece, s) * (self.blocks >> (s + 1))
        return low

    def place(self, piece, stages):
        at = 0
        for j in range(stages):
            at = at + self.mine(piece, self.outer_bits + j) * (1 << (self.inner_bits - 1 - j))
        return at

    def bind(self, given, out, scratch):
        n = len(self.shapes)
        self.given, self.out = given, out
        self.work, self.inbox, self.result = scratch[:n], scratch[n : 2 * n], scratch[2 * n : 3 * n]
        self.send, self.recv, self.near = scratch[3 * n :]

    def scratch(self):
        b16, k = jnp.bfloat16, len(self.pieces)
        return (
            [pltpu.VMEM((b // 2, r, c), b16) for b, r, c in self.shapes]
            + [pltpu.VMEM((b, r, c), b16) for b, r, c in self.shapes]
            + [pltpu.VMEM((self.inner, r, c), b16) for b, r, c in self.shapes]
            + [pltpu.SemaphoreType.DMA((k, self.steps)), pltpu.SemaphoreType.DMA((k, self.steps)), pltpu.SemaphoreType.DMA((k,))]
        )

    def copy(self, piece, step):
        i, columns, _ = self.pieces[piece]
        if step < self.stages:
            stage = step
            half = self.blocks >> (step + 1)
            other = (1 - self.mine(piece, step)) * half
            if step == 0:
                source = self.given[i].at[pl.ds(other, half), :, columns]
            else:
                source = self.work[i].at[pl.ds(self.low(piece, step) + other, half), :, columns]
            target = self.inbox[i].at[pl.ds(self.blocks - 2 * half, half), :, columns]
        else:
            stage = self.steps - 1 - step + self.outer_bits
            j = stage - self.outer_bits
            many = 1 << (self.inner_bits - 1 - j)
            source = target = self.result[i].at[pl.ds(self.place(piece, j + 1), many), :, columns]
        return pltpu.make_async_remote_copy(
            src_ref=source,
            dst_ref=target,
            send_sem=self.send.at[piece, step],
            recv_sem=self.recv.at[piece, step],
            device_id=self.partner(*self.axis_bit(piece, stage)),
            device_id_type=pl.DeviceIdType.MESH,
        )

    def own(self, piece):
        i, columns, _ = self.pieces[piece]
        half = self.blocks // 2
        source = self.given[i].at[pl.ds(self.mine(piece, 0) * half, half), :, columns]
        return pltpu.make_async_copy(source, self.work[i].at[:, :, columns], self.near.at[piece])

    def leave(self, piece):
        i, columns, _ = self.pieces[piece]
        return pltpu.make_async_copy(self.result[i].at[:, :, columns], self.out[i].at[:, :, columns], self.near.at[piece])

    def add(self, piece, stage):
        i, columns, _ = self.pieces[piece]
        work, inbox, result = self.work[i], self.inbox[i], self.result[i]
        half = self.blocks >> (stage + 1)
        arrived = self.blocks - 2 * half
        base = 0 if stage == 0 else self.low(piece, stage) + self.mine(piece, stage) * half

        @pl.loop(0, half)
        def _(k):
            new = work[base + k, :, columns].astype(jnp.float32) + inbox[arrived + k, :, columns].astype(jnp.float32)
            if stage == self.stages - 1:
                result[self.place(piece, self.inner_bits), :, columns] = new.astype(jnp.bfloat16)
            else:
                work[base + k, :, columns] = new.astype(jnp.bfloat16)

    def start(self, pieces):
        for p in pieces:
            self.copy(p, 0).start()
        for p in pieces:
            self.own(p).start()

    def advance(self, pieces, step):
        for p in pieces:
            if step == 0:
                self.own(p).wait()
            self.copy(p, step).wait()
            if step < self.stages:
                self.add(p, step)
            if step + 1 < self.steps:
                self.copy(p, step + 1).start()
            else:
                self.leave(p).start()

    def gone(self, pieces):
        for p in pieces:
            self.leave(p).wait()

    def times(self, count):
        heavy = (18.0, 10.0, 6.5, 14.0)
        there = [heavy[min(j, 3)] for j in range(self.inner_bits)]
        loads = [11.0] * self.outer_bits + there + there[::-1]
        total, at, out = sum(loads), 0.0, []
        for load in loads[:-1]:
            at += load
            out.append(max(1, min(count - 1, round(at / total * count))))
        return out


def reduction_of(arrays, parts):
    plan = Reduction(lax.axis_size("fsdp"), lax.axis_size("dp"), [a.shape for a in arrays], parts)
    shaped = [a.reshape(s) for a, s in zip(arrays, plan.shapes)]
    out = [jax.ShapeDtypeStruct((plan.inner,) + s[1:], jnp.bfloat16) for s in plan.shapes]
    return plan, shaped, out


class Exchange:
    def __init__(self, size):
        self.size = size

    def owner(self, turn):
        return (lax.axis_index("fsdp") + self.size - turn) % self.size

    def peer(self, turn):
        return {"fsdp": (lax.axis_index("fsdp") + turn) % self.size}

    def barrier(self):
        sem = pltpu.get_barrier_semaphore()
        for turn in range(1, self.size):
            pl.semaphore_signal(sem, inc=1, device_id=self.peer(turn), device_id_type=pl.DeviceIdType.MESH)
        pl.semaphore_wait(sem, self.size - 1)

    def copy(self, source, target, sems, which, turn):
        if turn == 0:
            return pltpu.make_async_copy(source, target, sems[1].at[which, 0])
        return pltpu.make_async_remote_copy(
            src_ref=source,
            dst_ref=target,
            send_sem=sems[0].at[which, turn],
            recv_sem=sems[1].at[which, turn],
            device_id=self.peer(turn),
            device_id_type=pl.DeviceIdType.MESH,
        )


def gather_kernel(
    x_ref, go_ref, dt_ref, rate_ref, taps_ref, vec_ref, xp_ref, len_ref, wout_ref, win_ref,
    normed_ref, dtw_ref, xpw_ref, decay_ref, par_ref, gain_ref, off_ref, wout_out, win_out, dg_out, both_out,
    pack, wout, win, dg, both, packed, send, recv, leave, tiles, *, plan
):
    f32, bf16 = jnp.float32, jnp.bfloat16
    rows, model = x_ref.shape
    deep, wide, share = model // plan.size, both.shape[1], packed.shape[1]
    me = lax.axis_index("fsdp")
    sems = (send, recv)

    def copies(which, turn):
        source = (packed, wout_ref, win_ref)[which]
        if which == 0:
            target = pack.at[:, pl.ds(pl.multiple_of(me * share, 128), share)]
        else:
            target = (wout, win)[which - 1].at[me]
        return plan.copy(source, target, sems, which, turn)

    lines = share // 128
    vectors = vec_ref[...].astype(f32)
    line = [
        jnp.concatenate([vectors[k : k + 1] for k in range(v * lines, (v + 1) * lines)], axis=1) for v in range(4)
    ]
    few = [line[0], taps_ref[...].astype(f32)] + line[1:]
    depth, states, taps = dt_ref.shape[0], rate_ref.shape[0], taps_ref.shape[0]
    few.append(jnp.zeros((16 - 4 - taps, share), f32))
    packed[0:depth, :] = dt_ref[...]
    packed[depth : depth + states, :] = rate_ref[...]
    packed[depth + states : depth + states + 16, :] = jnp.concatenate(few, axis=0).astype(bf16)
    packed[depth + states + 16 :, :] = xp_ref[...]
    plan.barrier()
    for which in range(3):
        for turn in range(1, plan.size):
            copies(which, turn).start()
    for which in (1, 0, 2):
        copies(which, 0).start()

    def times_out(turn):
        at = plan.owner(turn)

        @pl.loop(0, share // 256)
        def _(k):
            here = pl.ds(pl.multiple_of(at * share + k * 256, 128), 256)
            dg[:, here] = lax.dot_general(
                go_ref[...], wout[at, pl.ds(pl.multiple_of(k * 256, 256), 256), :],
                (((1,), (1,)), ((), ())), preferred_element_type=f32,
            )
        pltpu.make_async_copy(wout.at[at], wout_out.at[at], leave.at[0, turn]).start()
        part = pl.ds(pl.multiple_of(at * share, 128), share)
        pltpu.make_async_copy(dg.at[:, part], dg_out.at[:, part], leave.at[2, turn]).start()

    def times_in(turn):
        at = plan.owner(turn)
        left = pl.ds(pl.multiple_of(at * deep, 128), deep)

        @pl.loop(0, wide // 256)
        def _(k):
            here = pl.ds(pl.multiple_of(k * 256, 256), 256)
            new = jnp.dot(normed_ref[:, left], win[at, :, here], preferred_element_type=f32)
            both[:, here] = new if turn == 0 else both[:, here] + new
            if turn == plan.size - 1:
                pltpu.make_async_copy(both.at[:, here], both_out.at[:, here], tiles.at[k]).start()
        pltpu.make_async_copy(win.at[at], win_out.at[at], leave.at[1, turn]).start()

    contexts, clusters = len_ref.shape
    span = rows // contexts
    for c in range(contexts):
        starts = [jnp.int32(0)]
        for k in range(clusters - 1):
            starts.append(starts[-1] + len_ref[c, k])

        @pl.loop(0, span // 64)
        def _(k):
            spot = lax.broadcasted_iota(jnp.int32, (64, 128), 0) + k * 64
            value = spot
            for first in starts[1:]:
                value = jnp.where(spot >= first, spot - first, value)
            off_ref[pl.ds(pl.multiple_of(c * span + k * 64, 64), 64), :] = value

    copies(1, 0).wait()
    times_out(0)
    for turn in range(plan.size):
        copies(0, turn).wait()
    dtw_ref[...] = pack[0:depth, :]
    xpw_ref[...] = pack[depth + states + 16 :, :]
    decay_ref[...] = -jnp.exp(pack[depth : depth + states, :].astype(f32)) * LOG2E
    few = pack[depth + states : depth + states + 16, :].astype(f32)
    par_ref[...] = few[1:9]
    gain = jnp.concatenate([few[:1, b * share : b * share + deep] for b in range(plan.size)], axis=1)
    gain_ref[...] = jnp.broadcast_to(gain, gain_ref.shape)

    @pl.loop(0, rows // 64)
    def _(k):
        here = pl.ds(pl.multiple_of(k * 64, 64), 64)
        x = x_ref[here, :].astype(f32)
        mean_sq = jnp.mean(x * x, axis=-1, keepdims=True)
        normed_ref[here, :] = (x * lax.rsqrt(mean_sq + norm_eps) * gain).astype(bf16)

    copies(2, 0).wait()
    times_in(0)
    for turn in range(1, plan.size):
        copies(1, turn).wait()
        times_out(turn)
    for turn in range(1, plan.size):
        copies(2, turn).wait()
        times_in(turn)
    for turn in range(plan.size):
        at = plan.owner(turn)
        part = pl.ds(pl.multiple_of(at * share, 128), share)
        pltpu.make_async_copy(wout.at[at], wout_out.at[at], leave.at[0, turn]).wait()
        pltpu.make_async_copy(win.at[at], win_out.at[at], leave.at[1, turn]).wait()
        pltpu.make_async_copy(dg.at[:, part], dg_out.at[:, part], leave.at[2, turn]).wait()

    @pl.loop(0, wide // 256)
    def _(k):
        here = pl.ds(pl.multiple_of(k * 256, 256), 256)
        pltpu.make_async_copy(both.at[:, here], both_out.at[:, here], tiles.at[k]).wait()


def gather_weights(x, grad_rows, small, lengths, w_out, w_in):
    f32, bf16 = jnp.float32, jnp.bfloat16
    plan = Exchange(lax.axis_size("fsdp"))
    n, (rows, model), wide = plan.size, x.shape, w_in.shape[1]
    (rank, share), states, cols = small[0].shape, small[1].shape[0], small[4].shape[0]
    inner = n * share
    anywhere = pl.BlockSpec(memory_space=pl.ANY)
    near = pl.BlockSpec(memory_space=pltpu.VMEM)
    shapes = [
        ((rank + states + 16 + cols, inner), bf16), ((n,) + w_out.shape, bf16), ((n,) + w_in.shape, bf16), ((rows, inner), f32), ((rows, wide), f32),
    ]
    outs = [
        (x.shape, bf16), ((rank, inner), bf16), ((cols, inner), bf16), ((states, inner), f32), ((8, inner), f32), ((8, model), f32), ((rows, 128), jnp.int32),
    ]
    *made, out_all, in_all, d_gated, both = pl.pallas_call(
        functools.partial(gather_kernel, plan=plan),
        out_shape=[jax.ShapeDtypeStruct(*s) for s in outs + shapes[1:]],
        in_specs=[near] * 7 + [pl.BlockSpec(memory_space=pltpu.SMEM)] + [anywhere] * 2,
        out_specs=[near] * 7 + [anywhere] * 4,
        scratch_shapes=[pltpu.VMEM(*s) for s in shapes]
        + [
            pltpu.VMEM((shapes[0][0][0], share), bf16),
            pltpu.SemaphoreType.DMA((3, n)),
            pltpu.SemaphoreType.DMA((3, n)),
            pltpu.SemaphoreType.DMA((3, n)),
            pltpu.SemaphoreType.DMA((wide // 256,)),
        ],
        compiler_params=pltpu.CompilerParams(collective_id=2, has_side_effects=True, vmem_limit_bytes=56 << 20),
        name="gather_weights",
    )(x, grad_rows, *small, lengths, w_out, w_in)
    return made, out_all.reshape(-1, w_out.shape[1]), in_all.reshape(-1, wide), d_gated, both


TAPS, SHIFT, DT_BIAS, SKIP = 0, 4, 5, 6


def rows_of(ref, tile, row, width):
    return [ref[tile + j, pl.ds(row, 8, stride=0), :] for j in range(width)]


def by_eights(ref, tile):
    total = ref[tile, pl.ds(0, 8, stride=8), :]
    for s in range(1, 8):
        total = total + ref[tile, pl.ds(s, 8, stride=8), :]
    return total


def folded(x):
    total = x[:8]
    for s in range(8, x.shape[0], 8):
        total = total + x[s : s + 8]
    return total


def spread(proj, first, wide, states):
    for t in range(proj.shape[1]):
        wide[pl.ds(t * states, states), :] = jnp.broadcast_to(proj[first : first + states, t : t + 1], (states, 128))


def forward_kernel(
    upper_ref, z_ref, dg_ref, off_ref, par_ref, xp_ref, dtw_ref, a_ref,
    u_ref, ds_ref, dt_ref, sg_ref, dy_ref, gated_ref, gate_ref, proj_ref, wide_b, wide_c, kept_ref, end_ref, skip_ref,
    hs, ext, u16, dtm, dtu, ys, mix, *, width
):
    f32, bf16 = jnp.float32, jnp.bfloat16
    rows, inner = upper_ref.shape
    states, rank = a_ref.shape[0], dtw_ref.shape[0]
    tiles = inner // 128

    @pl.when(pl.program_id(0) == 0)
    def _():
        hs[...] = jnp.zeros_like(hs)
        skip_ref[...] = jnp.zeros_like(skip_ref)
        ext[pl.ds(0, 8), :] = jnp.zeros((8, inner), f32)

    @pl.loop(0, tiles, unroll=True)
    def _(k):
        lanes = pl.ds(pl.multiple_of(k * 128, 128), 128)
        now = upper_ref[:, lanes]
        ext[pl.ds(8, rows), lanes] = now
        conv = par_ref[SHIFT : SHIFT + 1, lanes] + par_ref[TAPS + 3 : TAPS + 4, lanes] * now
        for lag in range(1, 4):
            before = ext[pl.ds(8 - lag, rows), lanes]
            conv = conv + par_ref[TAPS + 3 - lag : TAPS + 4 - lag, lanes] * jnp.where(off_ref[...] >= lag, before, 0.0)
        sig = jax.nn.sigmoid(conv)
        act = conv * sig
        u_ref[:, lanes] = act
        u16[:, lanes] = act.astype(bf16)
        ds_ref[:, lanes] = sig * (1.0 + conv * (1.0 - sig))
        ext[pl.ds(0, 8), lanes] = now[rows - 8 :]

    proj = lax.dot_general(xp_ref[...], u16[...], (((1,), (1,)), ((), ())), preferred_element_type=f32)
    proj_ref[0] = proj
    spread(proj, rank, wide_b, states)
    spread(proj, rank + states, wide_c, states)
    rank16 = proj[:rank].astype(bf16)
    column = lax.broadcasted_iota(jnp.int32, (states, 8 * states), 1) % states
    tiled = jnp.where(column == lax.broadcasted_iota(jnp.int32, (states, 8 * states), 0), 1.0, 0.0).astype(bf16)
    many = lax.dot_general(
        proj[rank + states :].astype(bf16), tiled, (((0,), (0,)), ((), ())), preferred_element_type=f32
    )
    token = lax.broadcasted_iota(jnp.int32, (rows, 8 * states), 0) % 8
    mine = lax.broadcasted_iota(jnp.int32, (rows, 8 * states), 1) // states == token
    mix[...] = jnp.where(mine, many, 0.0)

    @pl.loop(0, tiles // 2, unroll=True)
    def _(k):
        pair = pl.ds(pl.multiple_of(k * 256, 256), 256)
        pre = lax.dot_general(rank16, dtw_ref[:, pair], (((0,), (0,)), ((), ())), preferred_element_type=f32)
        pre = pre + par_ref[DT_BIAS : DT_BIAS + 1, pair]
        small = jnp.exp(-jnp.abs(pre))
        delta = jnp.maximum(pre, 0.0) + jnp.log1p(small)
        dt_ref[:, pair] = delta
        sg_ref[:, pair] = jnp.where(pre >= 0, 1.0, small) / (1.0 + small)
        grown = delta * u_ref[:, pair]
        for j in range(2):
            part = slice(128 * j, 128 * j + 128)
            dtm[2 * k + j] = jnp.where(off_ref[...] > 0, delta[:, part], BIG)
            dtu[2 * k + j] = grown[:, part]

    @pl.loop(0, tiles // width, unroll=2)
    def _(cb):
        tile = cb * width
        base = pl.multiple_of(cb * 128 * width, 128 * width)
        rate = [[a_ref[pl.ds(8 * s, 8), pl.ds(base + 128 * j, 128)] for s in range(2)] for j in range(width)]

        def body(g, h):
            h = [list(p) for p in zip(h[:width], h[width:])]
            r0 = pl.multiple_of(g * 8, 8)
            low = [jnp.concatenate(h[j], axis=0).astype(bf16) for j in range(width)]
            seen = [[] for _ in range(width)]
            for t in range(8):
                d = rows_of(dtm, tile, r0 + t, width)
                x = rows_of(dtu, tile, r0 + t, width)
                bt = [wide_b[pl.ds((r0 + t) * 16 + 8 * s, 8), :] for s in range(2)]
                for j in range(width):
                    kept_ref[tile + j, pl.ds((r0 + t) * 16, 16), :] = low[j]
                    for s in range(2):
                        h[j][s] = jnp.exp2(d[j] * rate[j][s]) * h[j][s] + x[j] * bt[s]
                    low[j] = jnp.concatenate(h[j], axis=0).astype(bf16)
                    seen[j].append(low[j])
            left = mix[pl.ds(r0, 8), :].astype(bf16)
            for j in range(0, width, 2):
                right = jnp.concatenate([jnp.concatenate(seen[j + k], axis=0) for k in range(2)], axis=1)
                part = jnp.dot(left, right, preferred_element_type=f32)
                for k in range(2):
                    ys[tile + j + k, pl.ds(r0, 8), :] = part[:, 128 * k : 128 * k + 128]
            return tuple(p[0] for p in h) + tuple(p[1] for p in h)

        h = tuple(hs[pl.ds(8 * s, 8), pl.ds(base + 128 * j, 128)] for s in range(2) for j in range(width))
        h = lax.fori_loop(0, rows // 8, body, h, unroll=8)
        for s in range(2):
            for j in range(width):
                hs[pl.ds(8 * s, 8), pl.ds(base + 128 * j, 128)] = h[s * width + j]
    end_ref[...] = hs[...]

    @pl.loop(0, tiles, unroll=True)
    def _(k):
        lanes = pl.ds(pl.multiple_of(k * 128, 128), 128)
        act, z, dg = u_ref[:, lanes], z_ref[:, lanes], dg_ref[:, lanes]
        full = ys[k] + par_ref[SKIP : SKIP + 1, lanes] * act
        sig = jax.nn.sigmoid(z)
        silu = z * sig
        gated_ref[:, lanes] = (full * silu).astype(bf16)
        dy = dg * silu
        dy_ref[:, lanes] = dy
        gate_ref[:, lanes] = (dg * full * sig * (1.0 + z * (1.0 - sig))).astype(bf16)
        skip_ref[:, lanes] = skip_ref[:, lanes] + folded(dy * act)


def scan_forward(both, d_gated, offset, params, xp, dtw, rate, chunk, width):
    T, DI = d_gated.shape
    n, states, cols = T // chunk, rate.shape[0], xp.shape[0]
    f32, bf16 = jnp.float32, jnp.bfloat16
    row = pl.BlockSpec((chunk, DI), lambda i: (i, 0))
    whole = lambda a: pl.BlockSpec(a.shape, lambda i: (0, 0))
    flat = lambda d: jax.ShapeDtypeStruct((T, DI), d)
    tile = lambda d: pltpu.VMEM((DI // 128, chunk, 128), d)
    return pl.pallas_call(
        functools.partial(forward_kernel, width=width),
        grid=(n,),
        in_specs=[row, pl.BlockSpec((chunk, DI), lambda i: (i, 1)), row, pl.BlockSpec((chunk, 128), lambda i: (i, 0))]
        + [whole(a) for a in (params, xp, dtw, rate)],
        out_specs=[row] * 7
        + [
            pl.BlockSpec((1, cols, chunk), lambda i: (i, 0, 0)),
            pl.BlockSpec((chunk * states, 128), lambda i: (i, 0)),
            pl.BlockSpec((chunk * states, 128), lambda i: (i, 0)),
            pl.BlockSpec((DI // 128, chunk * states, 128), lambda i: (0, i, 0)),
            pl.BlockSpec((states, DI), lambda i: (0, 0)),
            pl.BlockSpec((8, DI), lambda i: (0, 0)),
        ],
        out_shape=[flat(f32)] * 5
        + [flat(bf16)] * 2
        + [
            jax.ShapeDtypeStruct((n, cols, chunk), f32),
            jax.ShapeDtypeStruct((T * states, 128), f32),
            jax.ShapeDtypeStruct((T * states, 128), f32),
            jax.ShapeDtypeStruct((DI // 128, T * states, 128), bf16),
            jax.ShapeDtypeStruct((states, DI), f32),
            jax.ShapeDtypeStruct((8, DI), f32),
        ],
        scratch_shapes=[
            pltpu.VMEM((states, DI), f32),
            pltpu.VMEM((chunk + 8, DI), f32),
            pltpu.VMEM((chunk, DI), bf16),
            tile(f32),
            tile(f32),
            tile(f32),
            pltpu.VMEM((chunk, 8 * states), f32),
        ],
        compiler_params=pltpu.CompilerParams(dimension_semantics=("arbitrary",), vmem_limit_bytes=62 << 20),
        name="scan_forward",
    )(both, both, d_gated, offset, params, xp, dtw, rate)


def backward_kernel(
    u_ref, ds_ref, dt_ref, sg_ref, dy_ref, upper_ref, off_ref, proj_ref, wide_b, wide_c, kept_ref, end_ref, par_ref, xp_ref, dtw_ref, a_ref, skip_ref,
    *rest, width, plan, total
):
    f32, bf16 = jnp.float32, jnp.bfloat16
    n = len(plan.shapes)
    given, rest = rest[:n], rest[n:]
    (du_ref, small_ref), out, rest = rest[:2], rest[2 : 2 + n], rest[2 + n :]
    ga_ref, gdt_ref, gx_ref, sum_ref, *rest = rest
    ws, ns, dtm, dtu, dyb, sbuf, qbuf, dd, di, u16, dt16, ext, off_ext, wide_db, wide_dc, cols_ref = rest[:16]
    plan.bind(given, out, rest[16:])
    rows, inner = u_ref.shape
    states, rank = a_ref.shape[0], dtw_ref.shape[0]
    tiles = inner // 128
    everything = range(len(plan.pieces))
    times = plan.times(total // rows * (tiles // width))

    @pl.when(pl.program_id(0) == 0)
    def _():
        for ref in (ws, ga_ref, gdt_ref, gx_ref, sum_ref):
            ref[...] = jnp.zeros_like(ref)
        ns[...] = end_ref[...]
        ext[pl.ds(rows, 8), :] = jnp.zeros((8, inner), f32)
        off_ext[pl.ds(rows, 8), :] = jnp.full((8, 128), -1, jnp.int32)
        plan.barrier()
        plan.start(everything)

    proj = proj_ref[0]
    wide_db[...] = jnp.zeros_like(wide_db)
    wide_dc[...] = jnp.zeros_like(wide_dc)

    @pl.loop(0, tiles // width)
    def _(cb):
        tile = cb * width
        base = pl.multiple_of(cb * 128 * width, 128 * width)
        for at in sorted(set(times)):
            @pl.when(pl.program_id(0) * (tiles // width) + cb == at)
            def _():
                for step in range(plan.steps - 1):
                    if times[step] == at:
                        plan.advance(everything, step)

        for j in range(width):
            lanes = pl.ds(base + 128 * j, 128)
            d, act = dt_ref[:, lanes], u_ref[:, lanes]
            dtm[j] = jnp.where(off_ref[...] > 0, d, BIG)
            dtu[j] = d * act
            dyb[j] = dy_ref[:, lanes]
            u16[:, lanes] = act.astype(bf16)
        rate = [[a_ref[pl.ds(8 * s, 8), pl.ds(base + 128 * j, 128)] for s in range(2)] for j in range(width)]

        def body(k, carry):
            r0 = pl.multiple_of((rows // 8 - 1 - k) * 8, 8)
            w = [[carry[s * width + j] for s in range(2)] for j in range(width)]
            ga = [[carry[2 * width + s * width + j] for s in range(2)] for j in range(width)]
            newer = [[carry[4 * width + s * width + j] for s in range(2)] for j in range(width)]
            for t in range(7, -1, -1):
                d = rows_of(dtm, 0, r0 + t, width)
                x = rows_of(dtu, 0, r0 + t, width)
                v = rows_of(dyb, 0, r0 + t, width)
                bt = [wide_b[pl.ds((r0 + t) * 16 + 8 * s, 8), :] for s in range(2)]
                ct = [wide_c[pl.ds((r0 + t) * 16 + 8 * s, 8), :] for s in range(2)]
                db = [None, None]
                dc = [None, None]
                for j in range(width):
                    qs, ss = None, None
                    both = kept_ref[tile + j, pl.ds((r0 + t) * 16, 16), :].astype(f32)
                    for s in range(2):
                        later = newer[j][s]
                        prior = both[8 * s : 8 * s + 8]
                        newer[j][s] = prior
                        g = ct[s] * v[j] + w[j][s]
                        w[j][s] = jnp.exp2(d[j] * rate[j][s]) * g
                        q = w[j][s] * prior
                        ga[j][s] = ga[j][s] + q * d[j]
                        qa = q * rate[j][s]
                        sb = g * bt[s]
                        qs = qa if qs is None else qs + qa
                        ss = sb if ss is None else ss + sb
                        gx = g * x[j]
                        vh = v[j] * later
                        db[s] = gx if db[s] is None else db[s] + gx
                        dc[s] = vh if dc[s] is None else dc[s] + vh
                    qbuf[j, pl.ds(t * 8, 8), :] = qs
                    sbuf[j, pl.ds(t * 8, 8), :] = ss
                for s in range(2):
                    here = pl.ds((r0 + t) * 16 + 8 * s, 8)
                    wide_db[here, :] = wide_db[here, :] + db[s]
                    wide_dc[here, :] = wide_dc[here, :] + dc[s]
            for j in range(width):
                lanes = pl.ds(base + 128 * j, 128)
                here = pl.ds(r0, 8)
                s8 = by_eights(sbuf, j)
                dd[here, lanes] = LN2 * by_eights(qbuf, j) + u_ref[here, lanes] * s8
                di[here, lanes] = dt_ref[here, lanes] * s8
            return tuple(v[j][s] for v in (w, ga, newer) for s in range(2) for j in range(width))

        held = [(r, pl.ds(8 * s, 8), pl.ds(base + 128 * j, 128)) for r in (ws, ga_ref, ns) for s in range(2) for j in range(width)]
        end = lax.fori_loop(0, rows // 8, body, tuple(r[a, b] for r, a, b in held))
        for (r, a, b), value in zip(held, end):
            r[a, b] = value

    for i, ref in enumerate((wide_db, wide_dc)):
        for k in range(states):
            cols_ref[pl.ds(i * rows, rows), pl.ds(128 * k, 128)] = ref[pl.ds(k, rows, stride=states), :].astype(bf16)
    owner = lax.broadcasted_iota(jnp.int32, (states, states * 128), 1) // 128
    picks = jnp.where(owner == lax.broadcasted_iota(jnp.int32, (states, states * 128), 0), 1.0, 0.0).astype(bf16)
    d_bc = lax.dot_general(picks, cols_ref[...], (((1,), (1,)), ((), ())), preferred_element_type=f32)

    @pl.loop(0, tiles, unroll=True)
    def _(k):
        lanes = pl.ds(pl.multiple_of(k * 128, 128), 128)
        low = (dd[:, lanes] * sg_ref[:, lanes]).astype(bf16)
        dt16[:, lanes] = low
        sum_ref[pl.ds(40, 8), lanes] = sum_ref[pl.ds(40, 8), lanes] + folded(low.astype(f32))

    rank16 = proj[:rank].astype(bf16)
    d_rank = lax.dot_general(dtw_ref[...], dt16[...], (((1,), (1,)), ((), ())), preferred_element_type=f32)
    proj16 = jnp.concatenate([d_rank, d_bc[:, :rows], d_bc[:, rows:]], axis=0).astype(bf16)
    off_ext[pl.ds(0, rows), :] = off_ref[...]

    @pl.loop(0, tiles // 2, unroll=True)
    def _(k):
        pair = pl.ds(pl.multiple_of(k * 256, 256), 256)
        dot = lambda a, b, c: lax.dot_general(a, b, ((c, (0,)), ((), ())), preferred_element_type=f32)
        gdt_ref[:, pair] = gdt_ref[:, pair] + dot(rank16, dt16[:, pair], (1,))
        gx_ref[:, pair] = gx_ref[:, pair] + dot(proj16, u16[:, pair], (1,))
        inner_grad = dot(proj16, xp_ref[:, pair], (0,)) + di[:, pair] + dy_ref[:, pair] * par_ref[SKIP : SKIP + 1, pair]
        ext[pl.ds(0, rows), pair] = inner_grad * ds_ref[:, pair]
        for j in range(2):
            lanes = pl.ds(pl.multiple_of(k * 256 + 128 * j, 128), 128)
            now, above = ext[pl.ds(0, rows), lanes], upper_ref[:, lanes]
            grad = par_ref[TAPS + 3 : TAPS + 4, lanes] * now
            sums = [now, now * above]
            for lag in range(1, 4):
                after = jnp.where(off_ext[pl.ds(lag, rows), :] >= lag, ext[pl.ds(lag, rows), lanes], 0.0)
                grad = grad + par_ref[TAPS + 3 - lag : TAPS + 4 - lag, lanes] * after
                sums.append(after * above)
            du_ref[:, lanes] = grad.astype(bf16)
            for at, value in zip((32, 24, 16, 8, 0), sums):
                sum_ref[pl.ds(at, 8), lanes] = sum_ref[pl.ds(at, 8), lanes] + folded(value)
            ext[pl.ds(rows, 8), lanes] = now[:8]

    off_ext[pl.ds(rows, 8), :] = off_ref[pl.ds(0, 8), :]

    @pl.when(pl.program_id(0) == pl.num_programs(0) - 1)
    def _():
        share = small_ref.shape[1]
        deep = small_ref.shape[0] // (inner // share)
        sums = [jnp.sum(sum_ref[pl.ds(8 * k, 8), :], axis=0, keepdims=True) for k in range(6)]
        sums += [jnp.sum(skip_ref[...], axis=0, keepdims=True), jnp.zeros((9, inner), f32)]
        blocks = [gx_ref[...], gdt_ref[...], ga_ref[...] * a_ref[...] * LN2, jnp.concatenate(sums, axis=0)]
        for f in range(inner // share):
            at = f * deep
            for block in blocks:
                small_ref[at : at + block.shape[0], :] = block[:, f * share : (f + 1) * share].astype(bf16)
                at += block.shape[0]
            small_ref[at : (f + 1) * deep, :] = jnp.zeros(((f + 1) * deep - at, share), bf16)
        plan.advance(everything, plan.steps - 1)
        plan.gone(everything)


def scan_backward(saved, both, offset, proj, wide_b, wide_c, kept, end, params, xp, dtw, rate, skip, chunk, width, grads, parts):
    T, DI = saved[0].shape
    n, states, cols, rank = T // chunk, rate.shape[0], xp.shape[0], dtw.shape[0]
    f32, bf16 = jnp.float32, jnp.bfloat16
    row = pl.BlockSpec((chunk, DI), lambda i: (n - 1 - i, 0))
    whole = lambda a: pl.BlockSpec(a.shape, lambda i: (0, 0))
    anywhere = pl.BlockSpec(memory_space=pl.ANY)
    plan, shaped, summed = reduction_of(grads, parts)
    outer, inner = lax.axis_size("fsdp"), lax.axis_size("dp")
    deep = -(-(states + rank + cols + 16) // (16 * inner)) * 16 * inner
    small = jax.ShapeDtypeStruct((outer * deep, DI // outer), bf16)
    pieces = pltpu.VMEM((width, chunk, 128), f32)
    eights = pltpu.VMEM((width, 64, 128), f32)
    tall = pltpu.VMEM((chunk * states, 128), f32)
    out = pl.pallas_call(
        functools.partial(backward_kernel, width=width, plan=plan, total=T),
        grid=(n,),
        in_specs=[row] * 6
        + [
            pl.BlockSpec((chunk, 128), lambda i: (n - 1 - i, 0)),
            pl.BlockSpec((1, cols, chunk), lambda i: (n - 1 - i, 0, 0)),
            pl.BlockSpec((chunk * states, 128), lambda i: (n - 1 - i, 0)),
            pl.BlockSpec((chunk * states, 128), lambda i: (n - 1 - i, 0)),
            pl.BlockSpec((DI // 128, chunk * states, 128), lambda i: (0, n - 1 - i, 0)),
            whole(end),
        ]
        + [whole(a) for a in (params, xp, dtw, rate, skip)]
        + [anywhere] * len(grads),
        out_specs=[row, whole(small)] + [anywhere] * len(grads),
        out_shape=[jax.ShapeDtypeStruct((T, DI), bf16), small] + summed,
        scratch_shapes=[pltpu.VMEM((r, DI), f32) for r in (states, rank, cols, 48)]
        + [
            pltpu.VMEM((states, DI), f32),
            pltpu.VMEM((states, DI), f32),
            pieces,
            pieces,
            pieces,
            eights,
            eights,
            pltpu.VMEM((chunk, DI), f32),
            pltpu.VMEM((chunk, DI), f32),
            pltpu.VMEM((chunk, DI), bf16),
            pltpu.VMEM((chunk, DI), bf16),
            pltpu.VMEM((chunk + 8, DI), f32),
            pltpu.VMEM((chunk + 8, 128), jnp.int32),
            tall,
            tall,
            pltpu.VMEM((2 * chunk, states * 128), bf16),
        ]
        + plan.scratch(),
        compiler_params=pltpu.CompilerParams(
            dimension_semantics=("arbitrary",), collective_id=0, has_side_effects=True, vmem_limit_bytes=56 << 20
        ),
        name="scan_backward",
    )(*saved, both, offset, proj, wide_b, wide_c, kept, end, params, xp, dtw, rate, skip, *shaped)
    return out[:2], [o.reshape(-1, o.shape[-1]) for o in out[2:]]


def finish_kernel(
    small_ref, normed_ref, upper_ref, gate_ref, gated_ref, in_ref, wout_ref, x_ref, go_ref, gain_ref,
    total_ref, few_ref, layer_ref, left_ref, gain_out,
    normed, upper, gate, gated, win, wout, x, go, dn, layer, grads, gain_sum, gain_in, loads, away, gain_send, gain_recv,
    *rest, plan
):
    f32, bf16 = jnp.float32, jnp.bfloat16
    rows, model = x.shape
    inner = upper.shape[1]
    plan.bind([grads, small_ref], [total_ref, few_ref], rest)
    everything = range(len(plan.pieces))
    few = [p for p in everything if plan.pieces[p][0] == 1]
    main = [p for p in everything if plan.pieces[p][0] == 0]
    halves = [main[: len(main) // 2], main[len(main) // 2 :]]

    copies = [
        pltpu.make_async_copy(a, b, loads.at[i])
        for i, (a, b) in enumerate(
            (
                (normed_ref, normed), (upper_ref, upper), (in_ref.at[:, pl.ds(0, inner)], win.at[0]), (gate_ref, gate),
                (in_ref.at[:, pl.ds(inner, inner)], win.at[1]), (x_ref, x), (go_ref, go), (gated_ref, gated), (wout_ref, wout),
            )
        )
    ]

    def gradient(half):
        columns = pl.ds(half * (inner // 2), inner // 2)
        deep = grads.shape[1]

        @pl.loop(0, model // 256)
        def _(k):
            part = normed[:, pl.ds(pl.multiple_of(k * 256, 256), 256)]
            new = lax.dot_general(part, upper[:, columns], (((0,), (0,)), ((), ())), preferred_element_type=f32).astype(bf16)
            for b in range(256 // deep):
                grads[k * (256 // deep) + b, :, columns] = new[b * deep : (b + 1) * deep]

    def product(left, k, start=0, stop=model // 256):
        @pl.loop(start, stop)
        def _(j):
            here = pl.ds(pl.multiple_of(j * 256, 256), 256)
            new = lax.dot_general(left[...], win[k, here, :], (((1,), (1,)), ((), ())), preferred_element_type=f32)
            dn[:, here] = new if k == 0 else dn[:, here] + new

    def gain_copy(stage):
        axis, bit = ("fsdp", stage) if stage < plan.outer_bits else ("dp", stage - plan.outer_bits)
        return pltpu.make_async_remote_copy(
            src_ref=gain_sum.at[stage],
            dst_ref=gain_in.at[stage],
            send_sem=gain_send.at[stage],
            recv_sem=gain_recv.at[stage],
            device_id=plan.partner(axis, bit),
            device_id_type=pl.DeviceIdType.MESH,
        )

    def gain_step(stage):
        gain_copy(stage).wait()
        gain_sum[stage + 1] = gain_sum[stage] + gain_in[stage]
        if stage + 1 < plan.stages:
            gain_copy(stage + 1).start()

    for c in copies:
        c.start()
    plan.barrier()
    plan.start(few)
    copies[0].wait()
    copies[1].wait()
    gradient(0)
    plan.start(halves[0])
    gradient(1)
    plan.start(halves[1])
    copies[2].wait()
    plan.advance(halves[0], 0)
    plan.advance(few, 0)
    product(upper, 0, 0, model // 512)
    plan.advance(halves[1], 0)
    product(upper, 0, model // 512, model // 256)
    copies[3].wait()
    copies[4].wait()
    product(gate, 1)
    copies[5].wait()
    copies[6].wait()
    plan.advance(halves[0], 1)
    plan.advance(halves[1], 1)
    plan.advance(few, 1)
    gain_sum[0] = jnp.zeros(gain_sum.shape[1:], f32)

    @pl.loop(0, rows // 32)
    def _(k):
        here = pl.ds(pl.multiple_of(k * 32, 32), 32)
        value, grad, gain = x[here, :].astype(f32), dn[here, :], gain_ref[0:1, :]
        scale = lax.rsqrt(jnp.mean(value * value, axis=-1, keepdims=True) + norm_eps)
        through = grad * value
        gain_sum[0] = gain_sum[0] + folded(through * scale)
        pull = jnp.mean(through * gain, axis=-1, keepdims=True) * (scale * scale * scale)
        dn[here, :] = go[here, :].astype(f32) + scale * (grad * gain) - value * pull

    gain_copy(0).start()
    leaving = [pltpu.make_async_copy(dn, left_ref, away.at[0]), pltpu.make_async_copy(layer, layer_ref, away.at[1])]
    leaving[0].start()
    plan.advance(everything, 2)
    copies[7].wait()
    copies[8].wait()

    @pl.loop(0, model // 256)
    def _(j):
        here = pl.ds(pl.multiple_of(j * 256, 256), 256)
        new = x[:, here].astype(f32) + jnp.dot(gated[...], wout[:, here], preferred_element_type=f32)
        layer[:, here] = new.astype(bf16)

    leaving[1].start()
    stage = 0
    for step in range(3, plan.steps):
        plan.advance(everything, step)
        if stage < plan.stages:
            gain_step(stage)
            stage += 1
    while stage < plan.stages:
        gain_step(stage)
        stage += 1
    deep = gain_out.shape[1]
    own = pl.ds(pl.multiple_of(lax.axis_index("fsdp") * deep, 128), deep)
    gain_out[...] = jnp.broadcast_to(jnp.sum(gain_sum[plan.stages, :, own], axis=0, keepdims=True), gain_out.shape)
    plan.gone(everything)
    for c in leaving:
        c.wait()


def finish(small, normed16, upper16, gate16, gated16, w_in, w_out, x, go, gain, parts):
    f32, bf16 = jnp.float32, jnp.bfloat16
    (rows, model), inner = x.shape, upper16.shape[1]
    grads = jax.ShapeDtypeStruct((model, inner), bf16)
    outer = lax.axis_size("fsdp")
    plan = Reduction(outer, lax.axis_size("dp"), [grads.shape, small.shape], parts)
    summed = [jax.ShapeDtypeStruct((plan.inner,) + s[1:], bf16) for s in plan.shapes]
    anywhere = pl.BlockSpec(memory_space=pl.ANY)
    near = pl.BlockSpec(memory_space=pltpu.VMEM)
    flat = pltpu.VMEM((rows, inner), bf16)
    thin = pltpu.VMEM((rows, model), bf16)
    total, few, layer_out, input_grad, gain_total = pl.pallas_call(
        functools.partial(finish_kernel, plan=plan),
        out_shape=summed
        + [
            jax.ShapeDtypeStruct((rows, model), bf16),
            jax.ShapeDtypeStruct((rows, model), f32),
            jax.ShapeDtypeStruct((8, model // outer), f32),
        ],
        in_specs=[anywhere] * 9 + [near],
        out_specs=[anywhere] * 4 + [near],
        scratch_shapes=[
            thin,
            flat,
            flat,
            flat,
            pltpu.VMEM((2, model, inner), bf16),
            pltpu.VMEM((inner, model), bf16),
            thin,
            thin,
            pltpu.VMEM((rows, model), f32),
            thin,
            pltpu.VMEM(plan.shapes[0], bf16),
            pltpu.VMEM((plan.stages + 1, 8, model), f32),
            pltpu.VMEM((plan.stages, 8, model), f32),
            pltpu.SemaphoreType.DMA((9,)),
            pltpu.SemaphoreType.DMA((2,)),
            pltpu.SemaphoreType.DMA((plan.stages,)),
            pltpu.SemaphoreType.DMA((plan.stages,)),
        ]
        + plan.scratch(),
        compiler_params=pltpu.CompilerParams(collective_id=1, has_side_effects=True, vmem_limit_bytes=60 << 20),
        name="finish",
    )(small.reshape(plan.shapes[1]), normed16, upper16, gate16, gated16, w_in, w_out, x, go, gain)
    return total.reshape(-1, total.shape[-1]), few.reshape(-1, few.shape[-1]), layer_out, input_grad, gain_total


def write_kernel(
    upper_ref, gate_ref, out_ref, small_ref, layer_ref, left_ref, gain_ref,
    in_to, out_to, x_to, dt_to, rate_to, taps_to, shift_to, bias_to, skip_to, gain_to, layer_to, left_to,
):
    f32 = jnp.float32
    wide = upper_ref.shape[1]
    in_to[:, 0:wide] = upper_ref[...].astype(f32)
    in_to[:, wide:] = gate_ref[...].astype(f32)
    out_to[...] = out_ref[...].astype(f32)
    layer_to[...] = layer_ref[...]
    left_to[...] = left_ref[...]

    @pl.when(pl.program_id(0) == 0)
    def _():
        at = 0
        for ref in (x_to, dt_to, rate_to):
            ref[...] = small_ref[at : at + ref.shape[0], :].astype(f32)
            at += ref.shape[0]
        few = small_ref[at : at + 16, :].astype(f32)
        at = 0
        gain_to[...] = gain_ref[0:1, :]
        for ref in (taps_to, shift_to, bias_to, skip_to):
            ref[...] = few[at : at + ref.shape[0], : ref.shape[1]]
            at += ref.shape[0]


def write_outputs(upper, gate, out, small, layer, left, gain, sizes):
    f32, share, steps = jnp.float32, small.shape[1], 4
    few = [(r, share) for r in sizes[:-1]] + [(1, sizes[-1])]
    part = lambda a: pl.BlockSpec((a.shape[0] // steps, a.shape[1]), lambda i: (i, 0))
    whole = lambda a: pl.BlockSpec(a.shape, lambda i: (0, 0))
    big = [jax.ShapeDtypeStruct((upper.shape[0], upper.shape[1] + gate.shape[1]), f32), jax.ShapeDtypeStruct(out.shape, f32)]
    few = [jax.ShapeDtypeStruct(a, f32) for a in few]
    last = [jax.ShapeDtypeStruct(a.shape, a.dtype) for a in (layer, left)]
    return pl.pallas_call(
        write_kernel,
        grid=(steps,),
        in_specs=[part(upper), part(gate), part(out), whole(small), part(layer), part(left), whole(gain)],
        out_specs=[part(a) for a in big] + [whole(a) for a in few] + [part(a) for a in last],
        out_shape=big + few + last,
        compiler_params=pltpu.CompilerParams(dimension_semantics=("arbitrary",), vmem_limit_bytes=62 << 20),
        name="write_outputs",
    )(upper, gate, out, small, layer, left, gain)


def dot32(left, right, contract):
    return lax.dot_general(left, right, (contract, ((), ())), preferred_element_type=jnp.float32)


def thirds(columns, times=1):
    wide = columns // times // 1024 * 384
    return list(zip((wide, wide, columns // times - 2 * wide) * times, ORDERS * times))


def shards(
    hidden_in,
    cluster_lengths,
    norm_gain,
    in_proj,
    conv_weight,
    conv_bias,
    x_proj,
    dt_proj,
    dt_bias,
    a_log,
    skip_gain,
    out_proj,
    out_grad,
):
    f32, bf16 = jnp.float32, jnp.bfloat16
    taps, share = conv_weight.shape
    rank_dim = dt_proj.shape[0]
    state_dim = a_log.shape[0]
    contexts_here, total_len, model_dim = hidden_in.shape
    rows = contexts_here * total_len
    columns = rank_dim + 2 * state_dim
    grad_rows = out_grad.reshape(rows, model_dim)
    gain_part = jnp.pad(norm_gain, (0, share - norm_gain.shape[0]))
    vectors = jnp.concatenate([gain_part, conv_bias, dt_bias, skip_gain]).reshape(-1, 128)
    x = hidden_in.reshape(rows, model_dim)
    (normed16, w_dt, xp, rate2, params, gain, offset), w_out, w_in, d_gated, both = gather_weights(
        x, grad_rows, (dt_proj, a_log, conv_weight, vectors, x_proj.T), cluster_lengths, out_proj, in_proj
    )
    inner_dim = params.shape[1]
    parts = lax.axis_size("fsdp")
    *saved, gated16, gate16, proj, b_wide, c_wide, kept, end, skip_sums = scan_forward(
        both, d_gated, offset, params, xp, w_dt, rate2, CHUNK, WIDTH
    )
    g_w_out = dot32(gated16, grad_rows, ((0,), (0,))).astype(bf16)
    g_w_gate = dot32(normed16, gate16, ((0,), (0,))).astype(bf16)
    (upper16, small), (t_out, t_gate) = scan_backward(
        saved, both, offset, proj, b_wide, c_wide, kept, end, params, xp, w_dt, rate2, skip_sums, CHUNK, WIDTH,
        [g_w_out, g_w_gate], [thirds(model_dim), thirds(inner_dim)],
    )
    t_upper, t_small, layer_out, input_grad, t_gain = finish(
        small, normed16, upper16, gate16, gated16, w_in, w_out, x, grad_rows, gain,
        [thirds(inner_dim, 2), [(inner_dim // parts, ORDERS[2])]],
    )
    t_in, t_out, t_x, t_dt, t_alog, t_conv, t_b_conv, t_b_dt, t_skip, t_gain, layer_out, input_grad = write_outputs(
        t_upper, t_gate, t_out, t_small, layer_out, input_grad, t_gain,
        (columns, rank_dim, state_dim, taps, 1, 1, 1, model_dim // parts),
    )
    return (
        layer_out.reshape(hidden_in.shape),
        input_grad.reshape(hidden_in.shape),
        t_gain[0],
        t_in,
        t_conv,
        t_b_conv[0],
        t_x.T,
        t_dt,
        t_b_dt[0],
        t_alog,
        t_skip[0],
        t_out,
    )


def solution(mesh):
    placed = (
        P(("dp", "fsdp"), None, None),
        P(("dp", "fsdp"), None),
        P("fsdp"),
        P("fsdp", None),
        P(None, "fsdp"),
        P("fsdp"),
        P("fsdp", None),
        P(None, "fsdp"),
        P("fsdp"),
        P(None, "fsdp"),
        P("fsdp"),
        P("fsdp", None),
        P(("dp", "fsdp"), None, None),
    )
    return jax.shard_map(
        shards,
        mesh=mesh,
        in_specs=placed,
        out_specs=(
            P(("dp", "fsdp"), None, None),
            P(("dp", "fsdp"), None, None),
            P("fsdp"),
            P("fsdp", None),
            P(None, "fsdp"),
            P("fsdp"),
            P("fsdp", None),
            P(None, "fsdp"),
            P("fsdp"),
            P(None, "fsdp"),
            P("fsdp"),
            P("fsdp", None),
        ),
        check_vma=False,
    )
```
